32 devices in a mesh: fsdp: 4 (over x, core), ctx: 8 (over z, y).
Axes of the slice: x: 2, y: 2, z: 4, core: 2. Of those that a mesh axis runs over, the one named last changes fastest.
Arguments:
- layer_in: bfloat16 [8, 4, 128, 1024], P('ctx', 'fsdp'), may hold values from -6 to 6
- grad_out: bfloat16 [8, 4, 128, 1024], P('ctx', 'fsdp'), may hold values from -6 to 6
- pair_of_rank: int32 [8], replicated, may hold values from 0 to 7, each once
- ln1_gain: bfloat16 [1024], P(('fsdp', 'ctx')), may hold values from 0.5 to 1.5
- ln1_bias: bfloat16 [1024], P(('fsdp', 'ctx')), may hold values from -1.5 to 1.5
- ln2_gain: bfloat16 [1024], P(('fsdp', 'ctx')), may hold values from 0.5 to 1.5
- ln2_bias: bfloat16 [1024], P(('fsdp', 'ctx')), may hold values from -1.5 to 1.5
- w_qkv: bfloat16 [1024, 3072], P(('fsdp', 'ctx')), may hold values from -4 to 4
- b_qkv: bfloat16 [3072], P(('fsdp', 'ctx')), may hold values from -2.5 to 2.5
- w_out: bfloat16 [1024, 1024], P(('fsdp', 'ctx')), may hold values from -3 to 3
- b_out: bfloat16 [1024], P(('fsdp', 'ctx')), may hold values from -2.5 to 2.5
- w_up: bfloat16 [1024, 4096], P(('fsdp', 'ctx')), may hold values from -0.1875 to 0.1875
- b_up: bfloat16 [4096], P(('fsdp', 'ctx')), may hold values from -2.5 to 2.5
- w_down: bfloat16 [1024, 4096], P(('fsdp', 'ctx')), may hold values from -0.09375 to 0.09375
- b_down: bfloat16 [1024], P(('fsdp', 'ctx')), may hold values from -2.5 to 2.5
Outputs:
- layer_out: bfloat16 [8, 4, 128, 1024], P('ctx', 'fsdp')
- grad_x: bfloat16 [8, 4, 128, 1024], P('ctx', 'fsdp')
- grad_ln1_gain: float32 [1024], P(('fsdp', 'ctx'))
- grad_ln1_bias: float32 [1024], P(('fsdp', 'ctx'))
- grad_ln2_gain: float32 [1024], P(('fsdp', 'ctx'))
- grad_ln2_bias: float32 [1024], P(('fsdp', 'ctx'))
- grad_w_qkv: float32 [1024, 3072], P(('fsdp', 'ctx'))
- grad_b_qkv: float32 [3072], P(('fsdp', 'ctx'))
- grad_w_out: float32 [1024, 1024], P(('fsdp', 'ctx'))
- grad_b_out: float32 [1024], P(('fsdp', 'ctx'))
- grad_w_up: float32 [1024, 4096], P(('fsdp', 'ctx'))
- grad_b_up: float32 [4096], P(('fsdp', 'ctx'))
- grad_w_down: float32 [1024, 4096], P(('fsdp', 'ctx'))
- grad_b_down: float32 [1024], P(('fsdp', 'ctx'))
The draws below stay inside these ranges and needn't reach their ends.
Inputs may be any that keep to these rules, and one draw needn't show every extreme that they name: `pair_of_rank`: a permutation: each slot holds a different block pair, so block pairs 0 to 7 each appear once.
All inputs are finite; a program needn't handle non-finite values.
Results may differ from the reference program's by a relative error of at most 0.011.
Values may be sent and summed in bfloat16 or wider, within the bound.
A program may use at most 512 MiB of HBM per device.

```python
import math
import jax
import jax.numpy as jnp
from jax import lax

D = 1024
H = 16
HD = 64
FF = 4096
ROT = 16
BLK = 64
BATCH = 4
N_CTX = 8


def draw_w_qkv(key, part):
    base = jax.random.normal(key, (D, 3 * D), jnp.float32) / math.sqrt(D)
    return base.astype(jnp.bfloat16)


def raised(values, stream_key, source, target, parts, factor):
    def block_of(position):
        return (jnp.arange(values.shape[position]) // (values.shape[position] // parts)).reshape((-1,) + (1,) * (values.ndim - 1 - position))

    one_side = jax.random.permutation(stream_key, parts)[block_of(target)]
    second = (block_of(target) + parts // 2) % parts
    return jnp.where((block_of(source) == one_side) | (block_of(source) == second), factor * values, values)


def shard_levels(rng, shape, shards, low, high):
    def one(dim, blocks):
        draws = jax.random.uniform(jax.random.fold_in(jax.random.fold_in(rng, 6), dim), (blocks,), jnp.float32, low / len(shards), high / len(shards))
        return jnp.repeat(jnp.exp(draws), shape[dim] // blocks).reshape((-1,) + (1,) * (len(shape) - dim - 1))

    loudness = one(*shards[0])
    for cut in shards[1:]:
        loudness = loudness * one(*cut)
    return loudness


def scatter_about(rng, shape, spread, bound, split=(), kind=jnp.bfloat16):
    entries = spread * jax.random.normal(rng, shape, jnp.float32)
    if split:
        entries = entries * shard_levels(rng, shape, split, -0.22, 0.18)
    return jnp.clip(entries, -bound, bound).astype(kind)


def heavy_noise(own_key, extent, spread, most, shards, heavy, held_as=jnp.bfloat16):
    values = spread * jax.random.normal(own_key, extent, jnp.float32)
    if shards:
        values = values * shard_levels(own_key, extent, shards, -0.22, 0.18)
    return jnp.clip(raised(values, jax.random.fold_in(own_key, 3), *heavy), -most, most).astype(held_as)


def setup_inputs(seed: int = 0) -> dict:
    seeds = jax.random.split(jax.random.key(seed), 16)
    return {
        "layer_in": scatter_about(seeds[0], (N_CTX, BATCH, 2 * BLK, D), 1.0, 6.0, ((0, 8), (1, 4))),
        "grad_out": heavy_noise(seeds[1], (N_CTX, BATCH, 2 * BLK, D), 1.0, 6.0, ((0, 8), (1, 4)), (0, 3, 8, 2.0)),
        "pair_of_rank": jax.random.permutation(seeds[2], N_CTX).astype(jnp.int32),
        "ln1_gain": jnp.clip(1.0 + 0.1 * jax.random.normal(seeds[3], (D,), jnp.float32), 0.5, 1.5).astype(jnp.bfloat16),
        "ln1_bias": scatter_about(seeds[4], (D,), 0.3, 1.5, ((0, 32),)),
        "ln2_gain": jnp.clip(1.0 + 0.1 * jax.random.normal(seeds[5], (D,), jnp.float32), 0.5, 1.5).astype(jnp.bfloat16),
        "ln2_bias": scatter_about(seeds[6], (D,), 0.3, 1.5, ((0, 32),)),
        "w_qkv": draw_w_qkv(jax.random.fold_in(seeds[15], 71), 0),
        "b_qkv": scatter_about(seeds[8], (3 * D,), 0.5, 2.5, ((0, 32),)),
        "w_out": scatter_about(seeds[9], (D, D), (max(D // 256, 1)) ** -0.5, 3.0, ((0, 32),)),
        "b_out": scatter_about(seeds[10], (D,), 0.5, 2.5, ((0, 32),)),
        "w_up": scatter_about(seeds[11], (D, FF), D ** -0.5, 0.1875, ((0, 32),)),
        "b_up": scatter_about(seeds[12], (FF,), 0.5, 2.5, ((0, 32),)),
        "w_down": scatter_about(seeds[13], (D, FF), FF ** -0.5, 0.09375, ((0, 32),)),
        "b_down": scatter_about(seeds[14], (D,), 0.5, 2.5, ((0, 32),)),
    }


EPS = 1e-05
NEG = -1e+30
ROOT_HALF = 0.7071067811865476
INV_ROOT_TAU = 0.3989422804014327

def norm_parts(xf, scale_weight, shift_bias):
    row_mean = lax.optimization_barrier(jnp.mean(xf, axis=-1, keepdims=True))
    centred_input = xf - row_mean
    inverse_deviation = lax.rsqrt(lax.optimization_barrier(jnp.mean(centred_input * centred_input, axis=-1, keepdims=True)) + EPS)
    normalized_input = centred_input * inverse_deviation
    return (normalized_input * scale_weight.astype(jnp.float32) + shift_bias.astype(jnp.float32), normalized_input, inverse_deviation)

def layer_norm_backward(norm_output_gradient, normalized_input, inverse_deviation, scale_weight):
    normalized_gradient = norm_output_gradient * scale_weight.astype(jnp.float32)
    return inverse_deviation * (normalized_gradient - lax.optimization_barrier(jnp.mean(normalized_gradient, axis=-1, keepdims=True)) - normalized_input * lax.optimization_barrier(jnp.mean(normalized_gradient * normalized_input, axis=-1, keepdims=True)))

def gelu_value(u):
    return 0.5 * u * (1.0 + lax.erf(u * ROOT_HALF))

def gelu_slope(u):
    return 0.5 * (1.0 + lax.erf(u * ROOT_HALF)) + u * jnp.exp(-0.5 * u * u) * INV_ROOT_TAU

def rotate(field, place, sign):
    half = ROT // 2
    freqs = jnp.exp(jnp.arange(half).astype(jnp.float32) * (-2.0 * math.log(10000.0) / ROT))
    angle = place.astype(jnp.float32)[..., None] * freqs
    cosine = jnp.cos(angle)[..., None, :]
    sine = sign * jnp.sin(angle)[..., None, :]
    first = field[..., :half]
    second = field[..., half:ROT]
    return jnp.concatenate([first * cosine - second * sine, second * cosine + first * sine, field[..., ROT:]], axis=-1)

def slot_places(pairs):
    offsets = jnp.arange(BLK, dtype=jnp.int32)
    early = pairs[:, None] * BLK + offsets[None, :]
    late = (2 * N_CTX - 1 - pairs)[:, None] * BLK + offsets[None, :]
    return jnp.concatenate([early, late], axis=1).astype(jnp.int32)

def reference(layer_in, grad_out, pair_of_rank, ln1_gain, ln1_bias, ln2_gain, ln2_bias, w_qkv, b_qkv, w_out, b_out, w_up, b_up, w_down, b_down):
    f32 = jnp.float32
    bf = jnp.bfloat16
    length = 2 * BLK * N_CTX
    scale = 1.0 / math.sqrt(HD)
    places = slot_places(pair_of_rank).reshape(length)
    qblock = 512 if length % 512 == 0 else length
    nblocks = length // qblock
    pblocks = places.reshape(nblocks, qblock)

    def one_sequence(grads, inputs):
        xs, gs = inputs
        xf = xs.reshape(length, D).astype(f32)
        norm1, hat1, rstd1 = norm_parts(xf, ln1_gain, ln1_bias)
        norm2, hat2, rstd2 = norm_parts(xf, ln2_gain, ln2_bias)
        norm1 = norm1.astype(bf)
        norm2 = norm2.astype(bf)
        qkv = jnp.dot(norm1, w_qkv, preferred_element_type=f32) + b_qkv.astype(f32)
        query = rotate(qkv[:, :D].reshape(length, H, HD), places, 1.0).astype(bf)
        key = rotate(qkv[:, D:2 * D].reshape(length, H, HD), places, 1.0).astype(bf)
        value = qkv[:, 2 * D:].reshape(length, H, HD).astype(bf)
        keyf = key.astype(f32)
        valuef = value.astype(f32)
        qblocks = query.reshape(nblocks, qblock, H, HD)

        def attend(args):
            qpart, qplace = args
            visible = places[None, None, :] <= qplace[None, :, None]
            score = jnp.einsum('qhd,khd->hqk', qpart.astype(f32), keyf) * scale
            score = jnp.where(visible, score, NEG)
            top = lax.optimization_barrier(jnp.max(score, axis=-1))
            weight = jnp.where(visible, jnp.exp(score - top[..., None]), 0.0)
            total = lax.optimization_barrier(jnp.sum(weight, axis=-1))
            mixed = jnp.einsum('hqk,khd->hqd', weight.astype(bf).astype(f32), valuef)
            return ((mixed / total[..., None]).transpose(1, 0, 2), (top + jnp.log(total)).T)
        ctx_blocks, lse_blocks = lax.map(attend, (qblocks, pblocks))
        context = ctx_blocks.reshape(length, D).astype(bf)
        lse = lse_blocks.reshape(length, H)
        attn = jnp.dot(context, w_out, preferred_element_type=f32) + b_out.astype(f32)
        pre = jnp.dot(norm2, w_up, preferred_element_type=f32) + b_up.astype(f32)
        hidden = gelu_value(pre).astype(bf)
        mlp = jnp.dot(hidden, w_down.T, preferred_element_type=f32) + b_down.astype(f32)
        out = (xf + attn + mlp).astype(bf)
        grad_b = gs.reshape(length, D)
        grad_f = grad_b.astype(f32)
        dhidden = jnp.dot(grad_b, w_down, preferred_element_type=f32)
        dpre = dhidden * gelu_slope(pre)
        dpre_b = dpre.astype(bf)
        dnorm2 = jnp.dot(dpre_b, w_up.T, preferred_element_type=f32)
        dcontext = jnp.dot(grad_b, w_out.T, preferred_element_type=f32).astype(bf)
        dctx3 = dcontext.reshape(length, H, HD)
        delta = lax.optimization_barrier(jnp.sum(dctx3.astype(f32) * context.reshape(length, H, HD).astype(f32), axis=-1))

        def back(carry, args):
            dkey, dvalue = carry
            qpart, dpart, lpart, delpart, qplace = args
            visible = places[None, None, :] <= qplace[None, :, None]
            score = jnp.einsum('qhd,khd->hqk', qpart.astype(f32), keyf) * scale
            score = jnp.where(visible, score, NEG)
            prob = jnp.where(visible, jnp.exp(score - lpart.T[..., None]), 0.0)
            dvalue = dvalue + jnp.einsum('hqk,qhd->khd', prob.astype(bf).astype(f32), dpart.astype(f32))
            dprob = jnp.einsum('qhd,khd->hqk', dpart.astype(f32), valuef)
            dscore = (scale * prob * (dprob - delpart.T[..., None])).astype(bf).astype(f32)
            dquery = jnp.einsum('hqk,khd->qhd', dscore, keyf)
            dkey = dkey + jnp.einsum('hqk,qhd->khd', dscore, qpart.astype(f32))
            return ((dkey, dvalue), dquery)
        zero = jnp.zeros((length, H, HD), f32)
        (dkey, dvalue), dquery = lax.scan(back, (zero, zero), (qblocks, dctx3.reshape(nblocks, qblock, H, HD), lse.reshape(nblocks, qblock, H), delta.reshape(nblocks, qblock, H), pblocks))
        dquery = dquery.reshape(length, H, HD)
        dqkv = jnp.concatenate([rotate(dquery, places, -1.0).reshape(length, D), rotate(dkey, places, -1.0).reshape(length, D), dvalue.reshape(length, D)], axis=1)
        dqkv_b = dqkv.astype(bf)
        dnorm1 = jnp.dot(dqkv_b, w_qkv.T, preferred_element_type=f32)
        dx = (grad_f + layer_norm_backward(dnorm1, hat1, rstd1, ln1_gain) + layer_norm_backward(dnorm2, hat2, rstd2, ln2_gain)).astype(bf)
        new = (grads[0] + lax.optimization_barrier(jnp.sum(dnorm1 * hat1, axis=0)), grads[1] + lax.optimization_barrier(jnp.sum(dnorm1, axis=0)), grads[2] + lax.optimization_barrier(jnp.sum(dnorm2 * hat2, axis=0)), grads[3] + lax.optimization_barrier(jnp.sum(dnorm2, axis=0)), grads[4] + jnp.dot(norm1.T, dqkv_b, preferred_element_type=f32), grads[5] + lax.optimization_barrier(jnp.sum(dqkv, axis=0)), grads[6] + jnp.dot(context.T, grad_b, preferred_element_type=f32), grads[7] + lax.optimization_barrier(jnp.sum(grad_f, axis=0)), grads[8] + jnp.dot(norm2.T, dpre_b, preferred_element_type=f32), grads[9] + lax.optimization_barrier(jnp.sum(dpre, axis=0)), grads[10] + jnp.dot(grad_b.T, hidden, preferred_element_type=f32))
        return (new, (out.reshape(N_CTX, 2 * BLK, D), dx.reshape(N_CTX, 2 * BLK, D)))
    start = (jnp.zeros((D,), f32), jnp.zeros((D,), f32), jnp.zeros((D,), f32), jnp.zeros((D,), f32), jnp.zeros((D, 3 * D), f32), jnp.zeros((3 * D,), f32), jnp.zeros((D, D), f32), jnp.zeros((D,), f32), jnp.zeros((D, FF), f32), jnp.zeros((FF,), f32), jnp.zeros((D, FF), f32))
    grads, (outs, dxs) = lax.scan(one_sequence, start, (layer_in.transpose(1, 0, 2, 3), grad_out.transpose(1, 0, 2, 3)))
    layer_out = outs.transpose(1, 0, 2, 3)
    grad_x = dxs.transpose(1, 0, 2, 3)
    return (layer_out, grad_x, grads[0], grads[1], grads[2], grads[3], grads[4], grads[5], grads[6], grads[7], grads[8], grads[9], grads[10], grads[7])
```

```python
import functools
import math

import jax
import jax.numpy as jnp
from jax import lax
from jax.experimental import pallas as pl
from jax.experimental.pallas import tpu as pltpu
from jax.sharding import PartitionSpec as P

HD = 64
ROT = 16
LANES = 128


EPS = 1e-05
NEG = -1e30
ROOT_HALF = 0.7071067811865476
INV_ROOT_TAU = 0.3989422804014327


def norm_parts(xf, scale_weight, shift_bias):
    row_mean = jnp.mean(xf, axis=-1, keepdims=True)
    centred_input = xf - row_mean
    inverse_deviation = lax.rsqrt(
        jnp.mean(centred_input * centred_input, axis=-1, keepdims=True) + EPS
    )
    normalized_input = centred_input * inverse_deviation
    return (
        normalized_input * scale_weight.astype(jnp.float32) + shift_bias.astype(jnp.float32),
        normalized_input,
        inverse_deviation,
    )


def layer_norm_backward(norm_output_gradient, normalized_input, inverse_deviation, scale_weight):
    normalized_gradient = norm_output_gradient * scale_weight.astype(jnp.float32)
    return inverse_deviation * (
        normalized_gradient
        - jnp.mean(normalized_gradient, axis=-1, keepdims=True)
        - normalized_input
        * jnp.mean(normalized_gradient * normalized_input, axis=-1, keepdims=True)
    )


def gelu_value(u):
    return 0.5 * u * (1.0 + lax.erf(u * ROOT_HALF))


def gelu_slope(u):
    return 0.5 * (1.0 + lax.erf(u * ROOT_HALF)) + u * jnp.exp(-0.5 * u * u) * INV_ROOT_TAU


def rotate(field, place, sign):
    half = ROT // 2
    freqs = jnp.exp(jnp.arange(half).astype(jnp.float32) * (-2.0 * math.log(10000.0) / ROT))
    angle = place.astype(jnp.float32)[..., None] * freqs
    cosine = jnp.cos(angle)[..., None, :]
    sine = sign * jnp.sin(angle)[..., None, :]
    first = field[..., :half]
    second = field[..., half:ROT]
    return jnp.concatenate(
        [first * cosine - second * sine, second * cosine + first * sine, field[..., rot_end() :]],
        axis=-1,
    )


def rot_end():
    return ROT


def leading(field, letters):
    return "n" + letters if field.ndim == 5 else letters


def product(left, left_letters, right, right_letters, result):
    form = leading(left, left_letters) + "," + leading(right, right_letters) + "->" + result
    return jnp.einsum(form, left, right, preferred_element_type=jnp.float32)


def selectors(sel):
    return (sel[:, None, None, None, None], sel[:, None, None, None], sel[:, None])


def visibility(sel, qpa, qpb, kpa, kpb):
    chosen = sel[:, None]
    key_place = jnp.where(chosen, kpa, kpb)
    query_place = jnp.where(chosen, qpa, qpb)
    return (key_place[:, None, :] <= query_place[:, :, None])[:, None, None]


def online_update(state, qa, qb, ka, kb, va, vb, qpa, qpb, kpa, kpb, sel, with_first, scale):
    top_a, total_a, acc_a, top_b, total_b, acc_b = state
    sel5, sel4, sel2 = selectors(sel)
    query_two = jnp.where(sel5, qa, qb)
    key_two = jnp.where(sel5, ka, kb)
    value_two = jnp.where(sel5, va, vb)
    visible = visibility(sel, qpa, qpb, kpa, kpb)
    score = jnp.where(visible, product(query_two, "sqhd", key_two, "skhd", "nshqk") * scale, NEG)
    peak_a = jnp.max(jnp.where(sel5, score, NEG), axis=(0, 4))
    peak_b = jnp.max(jnp.where(sel5, NEG, score), axis=(0, 4))
    if with_first:
        score_one = product(qb, "sqhd", ka, "skhd", "nshqk") * scale
        peak_b = jnp.maximum(peak_b, jnp.max(score_one, axis=(0, 4)))
    new_a = jnp.maximum(top_a, peak_a)
    new_b = jnp.maximum(top_b, peak_b)
    lifted = jnp.where(sel5, new_a[..., None], new_b[..., None])
    weight = jnp.where(visible, jnp.exp(score - lifted), 0.0)
    mixed = product(weight.astype(jnp.bfloat16), "shqk", value_two, "skhd", "nshqd")
    mass = jnp.sum(weight, axis=4)
    add_total_a = jnp.sum(jnp.where(sel4, mass, 0.0), axis=0)
    add_total_b = jnp.sum(jnp.where(sel4, 0.0, mass), axis=0)
    add_acc_a = jnp.sum(jnp.where(sel5, mixed, 0.0), axis=0)
    add_acc_b = jnp.sum(jnp.where(sel5, 0.0, mixed), axis=0)
    if with_first:
        weight_one = jnp.exp(score_one - new_b[..., None])
        add_total_b = add_total_b + jnp.sum(weight_one, axis=(0, 4))
        add_acc_b = add_acc_b + product(weight_one.astype(jnp.bfloat16), "shqk", va, "skhd", "shqd")
    decay_a = jnp.exp(top_a - new_a)
    decay_b = jnp.exp(top_b - new_b)
    return (
        new_a,
        total_a * decay_a + add_total_a,
        acc_a * decay_a[..., None] + add_acc_a,
        new_b,
        total_b * decay_b + add_total_b,
        acc_b * decay_b[..., None] + add_acc_b,
    )


def pair_terms(
    qa,
    qb,
    ka,
    kb,
    va,
    vb,
    da,
    db,
    lsea,
    lseb,
    dela,
    delb,
    qpa,
    qpb,
    kpa,
    kpb,
    sel,
    with_first,
    scale,
):
    sel5, sel4, sel2 = selectors(sel)
    query_two = jnp.where(sel5, qa, qb)
    key_two = jnp.where(sel5, ka, kb)
    value_two = jnp.where(sel5, va, vb)
    dctx_two = jnp.where(sel5, da, db)
    lse_two = jnp.where(sel4, lsea, lseb)
    delta_two = jnp.where(sel4, dela, delb)
    visible = visibility(sel, qpa, qpb, kpa, kpb)
    score = jnp.where(visible, product(query_two, "sqhd", key_two, "skhd", "nshqk") * scale, NEG)
    prob = jnp.exp(score - lse_two[..., None])
    dprob = product(dctx_two, "sqhd", value_two, "skhd", "nshqk")
    dscore = (scale * prob * (dprob - delta_two[..., None])).astype(jnp.bfloat16)
    first_ds = None
    first_prob = None
    if with_first:
        score_one = product(qb, "sqhd", ka, "skhd", "nshqk") * scale
        prob_one = jnp.exp(score_one - lseb[..., None])
        dprob_one = product(db, "sqhd", va, "skhd", "nshqk")
        first_ds = (scale * prob_one * (dprob_one - delb[..., None])).astype(jnp.bfloat16)
        first_prob = prob_one.astype(jnp.bfloat16)
    return (first_ds, first_prob, dscore, prob.astype(jnp.bfloat16))


def query_grads(terms, ka, kb, sel):
    sel5, sel4, sel2 = selectors(sel)
    key_two = jnp.where(sel5, ka, kb)
    dq_two = product(terms[2], "shqk", key_two, "skhd", "nsqhd")
    dq_a = jnp.where(sel5, dq_two, 0.0)
    dq_b = jnp.where(sel5, 0.0, dq_two)
    if terms[0] is not None:
        dq_b = dq_b + product(terms[0], "shqk", ka, "skhd", "nsqhd")
    return (dq_a, dq_b)


def key_grads(terms, qa, qb, da, db, sel):
    sel5, sel4, sel2 = selectors(sel)
    query_two = jnp.where(sel5, qa, qb)
    dctx_two = jnp.where(sel5, da, db)
    dk_two = product(terms[2], "shqk", query_two, "sqhd", "nskhd")
    dv_two = product(terms[3], "shqk", dctx_two, "sqhd", "nskhd")
    dk_a = jnp.where(sel5, dk_two, 0.0)
    dk_b = jnp.where(sel5, 0.0, dk_two)
    dv_a = jnp.where(sel5, dv_two, 0.0)
    dv_b = jnp.where(sel5, 0.0, dv_two)
    if terms[0] is not None:
        dk_a = dk_a + product(terms[0], "shqk", qb, "sqhd", "nskhd")
        dv_a = dv_a + product(terms[1], "shqk", db, "sqhd", "nskhd")
    return (dk_a, dk_b, dv_a, dv_b)


def tdot(left, right):
    return lax.dot_general(
        left, right, (((0,), (0,)), ((), ())), preferred_element_type=jnp.float32
    )


def rdot(left, right):
    return lax.dot_general(
        left, right, (((1,), (1,)), ((), ())), preferred_element_type=jnp.float32
    )


def shards(
    layer_in,
    grad_out,
    pair_of_rank,
    ln1_gain,
    ln1_bias,
    ln2_gain,
    ln2_bias,
    w_qkv,
    b_qkv,
    w_out,
    b_out,
    w_up,
    b_up,
    w_down,
    b_down,
):
    f32 = jnp.float32
    bf = jnp.bfloat16
    nctx = lax.axis_size("ctx")
    mine = pair_of_rank[lax.axis_index("ctx")]
    seqs = layer_in.shape[1]
    width2 = layer_in.shape[2]
    dmodel = layer_in.shape[3]
    blk = width2 // 2
    rows = seqs * width2
    heads = dmodel // HD
    scale = 1.0 / math.sqrt(HD)
    offsets = jnp.arange(blk, dtype=jnp.int32)
    place_a = mine * blk + offsets
    place_b = (2 * nctx - 1 - mine) * blk + offsets
    places = jnp.concatenate([place_a, place_b])
    params = (
        ln1_gain,
        ln1_bias,
        ln2_gain,
        ln2_bias,
        w_qkv,
        b_qkv,
        w_out,
        b_out,
        w_up,
        b_up,
        w_down,
        b_down,
    )
    full = (
        lax.all_gather(params[0], ("fsdp", "ctx"), axis=0, tiled=True),
        lax.all_gather(params[1], ("fsdp", "ctx"), axis=0, tiled=True),
        lax.all_gather(params[2], ("fsdp", "ctx"), axis=0, tiled=True),
        lax.all_gather(params[3], ("fsdp", "ctx"), axis=0, tiled=True),
        lax.all_gather(params[4], ("fsdp", "ctx"), axis=0, tiled=True),
        lax.all_gather(params[5], ("fsdp", "ctx"), axis=0, tiled=True),
        lax.all_gather(params[6], ("fsdp", "ctx"), axis=0, tiled=True),
        lax.all_gather(params[7], ("fsdp", "ctx"), axis=0, tiled=True),
        lax.all_gather(params[8], ("fsdp", "ctx"), axis=0, tiled=True),
        lax.all_gather(params[9], ("fsdp", "ctx"), axis=0, tiled=True),
        lax.all_gather(params[10], ("fsdp", "ctx"), axis=0, tiled=True),
        lax.all_gather(params[11], ("fsdp", "ctx"), axis=0, tiled=True),
    )
    xf = layer_in.reshape(rows, dmodel).astype(f32)
    norm1, hat1, rstd1 = norm_parts(xf, full[0], full[1])
    norm2, hat2, rstd2 = norm_parts(xf, full[2], full[3])
    norm1 = norm1.astype(bf)
    norm2 = norm2.astype(bf)
    qkv = jnp.dot(norm1, full[4], preferred_element_type=f32) + full[5].astype(f32)
    query = rotate(qkv[:, :dmodel].reshape(seqs, width2, heads, HD), places, 1.0).astype(bf)
    key = rotate(qkv[:, dmodel : 2 * dmodel].reshape(seqs, width2, heads, HD), places, 1.0).astype(
        bf
    )
    value = qkv[:, 2 * dmodel :].reshape(seqs, width2, heads, HD).astype(bf)
    query_a = query[:, :blk]
    query_b = query[:, blk:]
    key_b = key[:, blk:]
    value_b = value[:, blk:]
    lone = jnp.zeros((1,), dtype=bool)
    empty_top = jnp.full((seqs, heads, blk), NEG, f32)
    empty_total = jnp.zeros((seqs, heads, blk), f32)
    empty_acc = jnp.zeros((seqs, heads, blk, HD), f32)
    state = (empty_top, empty_total, empty_acc, empty_top, empty_total, empty_acc)
    state = online_update(
        state,
        query_a,
        query_b,
        key_b[None],
        key_b[None],
        value_b[None],
        value_b[None],
        place_a,
        place_b,
        place_b[None],
        place_b[None],
        lone,
        False,
        scale,
    )

    def key_parts(kpiece, vpiece, first):
        count = kpiece.shape[0]
        pairs = lax.dynamic_slice_in_dim(pair_of_rank, first, count)
        keys = kpiece.reshape(count, seqs, width2, heads, HD)
        values = vpiece.reshape(count, seqs, width2, heads, HD)
        kplace_a = pairs[:, None] * blk + offsets[None, :]
        kplace_b = (2 * nctx - 1 - pairs)[:, None] * blk + offsets[None, :]
        return (
            keys[:, :, :blk],
            keys[:, :, blk:],
            values[:, :, :blk],
            values[:, :, blk:],
            kplace_a,
            kplace_b,
            pairs,
        )

    key_send = key.reshape(1, seqs, width2, dmodel)
    value_send = value.reshape(1, seqs, width2, dmodel)
    ka, kb, va, vb, kpa, kpb, pairs = key_parts(
        lax.all_gather(key_send, "ctx", axis=0, tiled=True),
        lax.all_gather(value_send, "ctx", axis=0, tiled=True),
        jnp.int32(0),
    )
    state = online_update(
        state,
        query_a,
        query_b,
        ka,
        kb,
        va,
        vb,
        place_a,
        place_b,
        kpa,
        kpb,
        pairs <= mine,
        True,
        scale,
    )
    top_a, total_a, acc_a, top_b, total_b, acc_b = state
    context4 = jnp.concatenate([acc_a / total_a[..., None], acc_b / total_b[..., None]], axis=2)
    lse = jnp.concatenate([top_a + jnp.log(total_a), top_b + jnp.log(total_b)], axis=2)
    context = context4.transpose(0, 2, 1, 3).reshape(rows, dmodel).astype(bf)
    attn = jnp.dot(context, full[6], preferred_element_type=f32) + full[7].astype(f32)
    pre = jnp.dot(norm2, full[8], preferred_element_type=f32) + full[9].astype(f32)
    hidden = gelu_value(pre).astype(bf)
    mlp = rdot(hidden, full[10]) + full[11].astype(f32)
    layer_out = (xf + attn + mlp).astype(bf).reshape(layer_in.shape)
    again = (
        lax.all_gather(params[0], ("fsdp", "ctx"), axis=0, tiled=True),
        lax.all_gather(params[1], ("fsdp", "ctx"), axis=0, tiled=True),
        lax.all_gather(params[2], ("fsdp", "ctx"), axis=0, tiled=True),
        lax.all_gather(params[3], ("fsdp", "ctx"), axis=0, tiled=True),
        lax.all_gather(params[4], ("fsdp", "ctx"), axis=0, tiled=True),
        lax.all_gather(params[5], ("fsdp", "ctx"), axis=0, tiled=True),
        lax.all_gather(params[6], ("fsdp", "ctx"), axis=0, tiled=True),
        lax.all_gather(params[7], ("fsdp", "ctx"), axis=0, tiled=True),
        lax.all_gather(params[8], ("fsdp", "ctx"), axis=0, tiled=True),
        lax.all_gather(params[9], ("fsdp", "ctx"), axis=0, tiled=True),
        lax.all_gather(params[10], ("fsdp", "ctx"), axis=0, tiled=True),
        lax.all_gather(params[11], ("fsdp", "ctx"), axis=0, tiled=True),
    )
    grad_b = grad_out.reshape(rows, dmodel)
    grad_f = grad_b.astype(f32)
    dhidden = jnp.dot(grad_b, again[10], preferred_element_type=f32)
    dpre = dhidden * gelu_slope(pre)
    dpre_b = dpre.astype(bf)
    dnorm2 = rdot(dpre_b, again[8])
    dcontext = rdot(grad_b, again[6]).astype(bf)
    dctx4 = dcontext.reshape(seqs, width2, heads, HD)
    delta = jnp.sum(
        dctx4.astype(f32) * context.reshape(seqs, width2, heads, HD).astype(f32), axis=-1
    ).transpose(0, 2, 1)
    dctx_a = dctx4[:, :blk]
    dctx_b = dctx4[:, blk:]
    lse_a = lse[..., :blk]
    lse_b = lse[..., blk:]
    delta_a = delta[..., :blk]
    delta_b = delta[..., blk:]
    own = pair_terms(
        query_b,
        query_b,
        key_b[None],
        key_b[None],
        value_b[None],
        value_b[None],
        dctx_b,
        dctx_b,
        lse_b,
        lse_b,
        delta_b,
        delta_b,
        place_b,
        place_b,
        place_b[None],
        place_b[None],
        lone,
        False,
        scale,
    )
    own_dq = query_grads(own, key_b[None], key_b[None], lone)[1][0]
    own_keys = key_grads(own, query_b, query_b, dctx_b, dctx_b, lone)
    gathered = (
        lax.all_gather(key_send, "ctx", axis=0, tiled=True),
        lax.all_gather(value_send, "ctx", axis=0, tiled=True),
    )
    groups = math.gcd(nctx, 8)
    per = nctx // groups

    def group_terms(args):
        kpiece, vpiece, first = args
        ka, kb, va, vb, kpa, kpb, pairs = key_parts(kpiece, vpiece, first)
        sel = pairs <= mine
        terms = pair_terms(
            query_a,
            query_b,
            ka,
            kb,
            va,
            vb,
            dctx_a,
            dctx_b,
            lse_a,
            lse_b,
            delta_a,
            delta_b,
            place_a,
            place_b,
            kpa,
            kpb,
            sel,
            True,
            scale,
        )
        dq_a, dq_b = query_grads(terms, ka, kb, sel)
        return (terms, jnp.sum(dq_a, axis=0), jnp.sum(dq_b, axis=0))

    grouped = lax.map(
        group_terms,
        (
            gathered[0].reshape(groups, per, seqs, width2, dmodel),
            gathered[1].reshape(groups, per, seqs, width2, dmodel),
            jnp.arange(groups, dtype=jnp.int32) * per,
        ),
    )
    terms_all = tuple((part.reshape((nctx,) + part.shape[2:]) for part in grouped[0]))
    dq_a = jnp.sum(grouped[1], axis=0)
    dq_b = jnp.sum(grouped[2], axis=0)
    pairs = pair_of_rank
    sliced = tuple(
        (lax.slice_in_dim(part, 0, 1 * lax.axis_size("ctx"), axis=0) for part in terms_all)
    )
    dk_a, dk_b, dv_a, dv_b = key_grads(sliced, query_a, query_b, dctx_a, dctx_b, pairs <= mine)
    dkey = jnp.concatenate([dk_a, dk_b], axis=2).reshape(
        1 * lax.axis_size("ctx"), seqs, width2, dmodel
    )
    dval = jnp.concatenate([dv_a, dv_b], axis=2).reshape(
        1 * lax.axis_size("ctx"), seqs, width2, dmodel
    )
    kv_grad = lax.psum_scatter(
        jnp.concatenate([dkey, dval], axis=-1), "ctx", scatter_dimension=0, tiled=True
    )
    dkey = kv_grad[0, :, :, :dmodel].reshape(seqs, width2, heads, HD)
    dval = kv_grad[0, :, :, dmodel:].reshape(seqs, width2, heads, HD)
    zero_half = jnp.zeros((seqs, blk, heads, HD), f32)
    dquery = jnp.concatenate([dq_a, dq_b + own_dq], axis=1)
    dkey = dkey + jnp.concatenate([zero_half, own_keys[1][0]], axis=1)
    dval = dval + jnp.concatenate([zero_half, own_keys[3][0]], axis=1)
    dqkv = jnp.concatenate(
        [
            rotate(dquery, places, -1.0).reshape(rows, dmodel),
            rotate(dkey, places, -1.0).reshape(rows, dmodel),
            dval.reshape(rows, dmodel),
        ],
        axis=1,
    )
    dqkv_b = dqkv.astype(bf)
    dnorm1 = rdot(dqkv_b, again[4])
    grad_x = (
        (
            grad_f
            + layer_norm_backward(dnorm1, hat1, rstd1, again[0])
            + layer_norm_backward(dnorm2, hat2, rstd2, again[2])
        )
        .astype(bf)
        .reshape(layer_in.shape)
    )
    vectors = (
        lax.psum_scatter(
            jnp.sum(dnorm1 * hat1, axis=0), ("fsdp", "ctx"), scatter_dimension=0, tiled=True
        ),
        lax.psum_scatter(jnp.sum(dnorm1, axis=0), ("fsdp", "ctx"), scatter_dimension=0, tiled=True),
        lax.psum_scatter(
            jnp.sum(dnorm2 * hat2, axis=0), ("fsdp", "ctx"), scatter_dimension=0, tiled=True
        ),
        lax.psum_scatter(jnp.sum(dnorm2, axis=0), ("fsdp", "ctx"), scatter_dimension=0, tiled=True),
        lax.psum_scatter(jnp.sum(dqkv, axis=0), ("fsdp", "ctx"), scatter_dimension=0, tiled=True),
        lax.psum_scatter(jnp.sum(grad_f, axis=0), ("fsdp", "ctx"), scatter_dimension=0, tiled=True),
        lax.psum_scatter(jnp.sum(dpre, axis=0), ("fsdp", "ctx"), scatter_dimension=0, tiled=True),
    )
    weights = (
        lax.psum_scatter(tdot(norm1, dqkv_b), ("fsdp", "ctx"), scatter_dimension=0, tiled=True),
        lax.psum_scatter(tdot(context, grad_b), ("fsdp", "ctx"), scatter_dimension=0, tiled=True),
        lax.psum_scatter(tdot(norm2, dpre_b), ("fsdp", "ctx"), scatter_dimension=0, tiled=True),
        lax.psum_scatter(tdot(grad_b, hidden), ("fsdp", "ctx"), scatter_dimension=0, tiled=True),
    )
    return (
        layer_out,
        grad_x,
        vectors[0],
        vectors[1],
        vectors[2],
        vectors[3],
        weights[0],
        vectors[4],
        weights[1],
        vectors[5],
        weights[2],
        vectors[6],
        weights[3],
        vectors[5],
    )


def span(lead, cols):
    return jnp.arange(lead, dtype=jnp.int32)[:, None] if cols else jnp.arange(lead, dtype=jnp.int32)


def turn(field, cosine, sine_low, sine_high):
    half = ROT // 2
    down = jnp.concatenate([field[:, half:], field[:, :half]], axis=1)
    up = jnp.concatenate([field[:, -half:], field[:, :-half]], axis=1)
    return field * cosine + down * sine_low + up * sine_high


def turn_tables(places, width):
    half = ROT // 2
    lane = jnp.arange(width, dtype=jnp.int32) % HD
    freqs = jnp.exp((lane % half).astype(jnp.float32) * (-2.0 * math.log(10000.0) / ROT))
    angle = places.astype(jnp.float32)[:, None] * freqs[None, :]
    cosine = jnp.where(lane < ROT, jnp.cos(angle), 1.0)
    sine = jnp.sin(angle)
    sine_low = jnp.where(lane < half, -sine, 0.0)
    sine_high = jnp.where((lane >= half) & (lane < ROT), sine, 0.0)
    return cosine, sine_low, sine_high


def headed(field, count):
    return field.reshape(field.shape[0], count, HD).transpose(1, 0, 2)


def joined(field):
    return field.transpose(1, 0, 2).reshape(field.shape[1], -1)


def bdot(form, left, right):
    return jnp.einsum(form, left, right, preferred_element_type=jnp.float32)


def head_shards(
    layer_in,
    grad_out,
    pair_of_rank,
    ln1_gain,
    ln1_bias,
    ln2_gain,
    ln2_bias,
    w_qkv,
    b_qkv,
    w_out,
    b_out,
    w_up,
    b_up,
    w_down,
    b_down,
):
    f32 = jnp.float32
    bf = jnp.bfloat16
    both = ("fsdp", "ctx")
    nctx = lax.axis_size("ctx")
    nf = lax.axis_size("fsdp")
    ndev = nctx * nf
    c = lax.axis_index("ctx")
    seqs, width2, dmodel = layer_in.shape[1:]
    blk = width2 // 2
    own_rows = seqs * width2
    ff = w_up.shape[1]
    hloc = dmodel // HD // nctx
    qw = hloc * HD
    fw = ff // nctx
    piece = dmodel // ndev
    scale = 1.0 / math.sqrt(HD)

    x_all = lax.all_gather(layer_in.reshape(own_rows, dmodel), "ctx", axis=0, tiled=True)
    def columns(parts):
        packed = jnp.concatenate([p.reshape(piece, nctx, -1) for p in parts], axis=-1)
        packed = packed.transpose(1, 0, 2)
        got = lax.all_to_all(packed, "ctx", split_axis=0, concat_axis=0, tiled=True)
        return got.reshape(nctx * piece, -1)

    wq = w_qkv.reshape(piece, 3, nctx, qw).transpose(0, 2, 1, 3)
    vec = jnp.concatenate([ln1_gain, ln1_bias, ln2_gain, ln2_bias, b_out, b_down, b_qkv, b_up])
    vw = LANES * -(-vec.shape[0] // (piece * LANES))
    vec_pad = jnp.pad(vec, (0, piece * vw - vec.shape[0])).reshape(piece, 1, vw)
    vec_pad = jnp.broadcast_to(vec_pad, (piece, nctx, vw))
    cols = lax.all_gather(columns([wq, w_up, w_down, vec_pad]), "fsdp", axis=0, tiled=True)
    g_own = grad_out.reshape(own_rows, dmodel)
    cols, g_send = lax.optimization_barrier((cols, g_own))
    got = cols[:, 3 * qw + 2 * fw :].reshape(ndev, piece * vw)
    cuts = [piece] * 6 + [b_qkv.shape[0], b_up.shape[0]]
    fulls = []
    at = 0
    for cut in cuts:
        fulls.append(got[:, at : at + cut].reshape(-1).astype(f32))
        at += cut
    gain1, bias1, gain2, bias2, bo, bd, bq, bu = fulls
    bq_c = lax.dynamic_slice_in_dim(bq.reshape(3, nctx, qw), c, 1, axis=1).reshape(1, 3 * qw)
    bu_c = lax.dynamic_slice_in_dim(bu, c * fw, fw).reshape(1, fw)
    wq_c = cols[:, : 3 * qw]
    wu_c = cols[:, 3 * qw : 3 * qw + fw]
    wd_c = cols[:, 3 * qw + fw : 3 * qw + 2 * fw]
    there = [((nf * cc + f) , f * nctx + cc) for f in range(nf) for cc in range(nctx)]
    back = [(b, a) for a, b in there]
    wo_c = lax.all_gather(lax.ppermute(w_out, both, there), "fsdp", axis=0, tiled=True)
    g_all = lax.all_gather(g_send, "ctx", axis=0, tiled=True)

    rows = x_all.shape[0]
    offsets = jnp.arange(blk, dtype=jnp.int32)
    slot_a = pair_of_rank[:, None] * blk + offsets[None, :]
    slot_b = (2 * nctx - 1 - pair_of_rank)[:, None] * blk + offsets[None, :]
    slots = jnp.concatenate([slot_a, slot_b], axis=1)[:, None, :]
    places = jnp.broadcast_to(slots, (nctx, seqs, width2)).reshape(rows)
    group = jnp.broadcast_to(span(seqs, False)[None, :, None], (nctx, seqs, width2)).reshape(rows)

    def hat_of(xf):
        row_mean = jnp.mean(xf, axis=-1, keepdims=True)
        centred = xf - row_mean
        rstd = lax.rsqrt(jnp.mean(centred * centred, axis=-1, keepdims=True) + EPS)
        return centred * rstd, rstd

    hat, _ = hat_of(x_all.astype(f32))
    norm1 = (hat * gain1 + bias1).astype(bf)
    norm2 = (hat * gain2 + bias2).astype(bf)
    qkv = jnp.dot(norm1, wq_c, preferred_element_type=f32) + bq_c
    cosine, sine_low, sine_high = turn_tables(places, qw)
    query = headed(turn(qkv[:, :qw], cosine, sine_low, sine_high).astype(bf), hloc)
    key = headed(turn(qkv[:, qw : 2 * qw], cosine, sine_low, sine_high).astype(bf), hloc)
    value = headed(qkv[:, 2 * qw :].astype(bf), hloc)
    visible = places[None, :] <= places[:, None]
    if seqs > 1:
        visible = visible & (group[None, :] == group[:, None])
    score = jnp.where(visible[None], bdot("hqd,hkd->hqk", query, key) * scale, NEG)
    top = jnp.max(score, axis=-1, keepdims=True)
    weight = jnp.exp(score - top)
    total = jnp.sum(weight, axis=-1, keepdims=True)
    mixed = bdot("hqk,hkd->hqd", weight.astype(bf), value)
    context = (mixed / total).astype(bf)
    lse = top + jnp.log(total)
    ctx_c = joined(context)

    pre = jnp.dot(norm2, wu_c, preferred_element_type=f32) + bu_c
    hidden = gelu_value(pre).astype(bf)
    part = rdot(hidden, wd_c) + jnp.dot(ctx_c, wo_c, preferred_element_type=f32)
    fwd = lax.all_to_all(
        part.astype(bf).reshape(nctx, own_rows, dmodel), "ctx", split_axis=0, concat_axis=0, tiled=True
    )
    fwd = jnp.sum(fwd.astype(f32), axis=0)
    x_own = layer_in.reshape(own_rows, dmodel).astype(f32)
    layer_out = (x_own + fwd + (bo + bd)).astype(bf).reshape(layer_in.shape)

    dhidden = jnp.dot(g_all, wd_c, preferred_element_type=f32)
    dpre = dhidden * gelu_slope(pre)
    dpre_b = dpre.astype(bf)
    dnorm2 = rdot(dpre_b, wu_c)
    dctx = headed(rdot(g_all, wo_c).astype(bf), hloc)
    delta = jnp.sum(dctx.astype(f32) * context.astype(f32), axis=-1, keepdims=True)
    prob = jnp.exp(score - lse)
    dprob = bdot("hqd,hkd->hqk", dctx, value)
    ds = (scale * prob * (dprob - delta)).astype(bf)
    dquery = joined(bdot("hqk,hkd->hqd", ds, key))
    dkey = joined(bdot("hqk,hqd->hkd", ds, query))
    dvalue = joined(bdot("hqk,hqd->hkd", prob.astype(bf), dctx))
    dqkv = jnp.concatenate(
        [
            turn(dquery, cosine, -sine_low, -sine_high),
            turn(dkey, cosine, -sine_low, -sine_high),
            dvalue,
        ],
        axis=1,
    )
    dqkv_b = dqkv.astype(bf)
    dnorm1 = rdot(dqkv_b, wq_c)
    gsum = (dnorm1 * gain1 + dnorm2 * gain2).astype(bf)
    gsum = lax.psum_scatter(gsum, "ctx", scatter_dimension=0, tiled=True).astype(f32)
    hat_own, rstd_own = hat_of(x_own)
    g_ownf = g_own.astype(f32)
    grad_x = (
        g_ownf
        + rstd_own
        * (
            gsum
            - jnp.mean(gsum, axis=-1, keepdims=True)
            - hat_own * jnp.mean(gsum * hat_own, axis=-1, keepdims=True)
        )
    ).astype(bf).reshape(layer_in.shape)

    sum_q = jnp.zeros((3, nctx, qw), f32)
    sum_q = lax.dynamic_update_slice_in_dim(
        sum_q, jnp.sum(dqkv, axis=0).reshape(3, 1, qw), c, axis=1
    ).reshape(ndev, -1)
    sum_u = lax.dynamic_update_slice_in_dim(
        jnp.zeros((ff,), f32), jnp.sum(dpre, axis=0), c * fw, axis=0
    ).reshape(ndev, -1)
    sums = [
        jnp.sum(dnorm1 * hat, axis=0).reshape(ndev, -1),
        jnp.sum(dnorm1, axis=0).reshape(ndev, -1),
        jnp.sum(dnorm2 * hat, axis=0).reshape(ndev, -1),
        jnp.sum(dnorm2, axis=0).reshape(ndev, -1),
        jnp.sum(g_ownf, axis=0).reshape(ndev, -1),
        sum_q,
        sum_u,
    ]
    sums = jnp.concatenate(sums, axis=1)
    sw = LANES * -(-sums.shape[1] // (piece * LANES))
    sums_pad = jnp.pad(sums, ((0, 0), (0, piece * sw - sums.shape[1]))).reshape(ndev * piece, sw)
    rows_out = tdot(ctx_c, g_all).astype(bf)
    wide = jnp.concatenate(
        [
            tdot(norm1, dqkv_b).astype(bf),
            tdot(norm2, dpre_b).astype(bf),
            tdot(g_all, hidden).astype(bf),
            sums_pad.astype(bf),
            rows_out.reshape(ndev * piece, -1),
        ],
        axis=1,
    )
    wide = lax.psum_scatter(wide, "fsdp", scatter_dimension=0, tiled=True)
    split = 3 * qw + 2 * fw + sw
    grad_wout = lax.ppermute(wide[:, split:].reshape(piece, dmodel), both, back).astype(f32)
    wide = lax.all_to_all(
        wide[:, :split].reshape(nctx, piece, split), "ctx", split_axis=0, concat_axis=0, tiled=True
    )
    sums = jnp.sum(wide[:, :, split - sw :].astype(f32), axis=0).reshape(-1)[: sums.shape[1]]
    wide = wide.transpose(1, 0, 2).astype(f32)
    grad_qkv = (
        wide[:, :, : 3 * qw].reshape(piece, nctx, 3, qw).transpose(0, 2, 1, 3).reshape(piece, -1)
    )
    grad_up = wide[:, :, 3 * qw : 3 * qw + fw].reshape(piece, ff)
    grad_down = wide[:, :, 3 * qw + fw : 3 * qw + 2 * fw].reshape(piece, ff)
    ends = [piece * i for i in range(6)] + [5 * piece + b_qkv.shape[0], sums.shape[0]]
    vs = [sums[a:b] for a, b in zip(ends[:-1], ends[1:])]
    return (
        layer_out,
        grad_x,
        vs[0],
        vs[1],
        vs[2],
        vs[3],
        grad_qkv,
        vs[5],
        grad_wout,
        vs[4],
        grad_up,
        vs[6],
        grad_down,
        vs[4],
    )


def mod_less(a, n):
    return jnp.where(a >= n, a - n, a)


def mesh_dev(xi, ki, zi, yi):
    return {"fsdp": xi * 2 + ki, "ctx": zi * 2 + yi}


def rcopy(src, dst, send, recv, where):
    return pltpu.make_async_remote_copy(
        src_ref=src,
        dst_ref=dst,
        send_sem=send,
        recv_sem=recv,
        device_id=where,
        device_id_type=pl.DeviceIdType.MESH,
    )


def coordinates():
    f = lax.axis_index("fsdp")
    c = lax.axis_index("ctx")
    xi, ki = lax.div(f, 2), lax.rem(f, 2)
    zi, yi = lax.div(c, 2), lax.rem(c, 2)
    return xi, ki, zi, yi


def greet(nz, xi, ki, zi, yi):
    t = ki * nz + zi
    nt = 2 * nz
    barrier = pltpu.get_barrier_semaphore()

    def hello(where):
        pl.semaphore_signal(barrier, inc=1, device_id=where, device_id_type=pl.DeviceIdType.MESH)

    for d in range(1, nt):
        o = mod_less(t + d, nt)
        hello(mesh_dev(xi, lax.div(o, nz), lax.rem(o, nz), yi))
    hello(mesh_dev(1 - xi, ki, zi, yi))
    hello(mesh_dev(xi, ki, zi, 1 - yi))

    @pl.when(ki != yi)
    def _():
        hello(mesh_dev(xi, yi, zi, ki))

    pl.semaphore_wait(barrier, jnp.where(ki != yi, nt + 2, nt + 1))


def gather_kernel(
    nz,
    x_ref,
    g_ref,
    wq_ref,
    wu_ref,
    wd_ref,
    wo_ref,
    xb,
    gb,
    wq,
    wu,
    wd,
    wo,
    pq,
    pu,
    pd,
    sw_s,
    sw_r,
    up_s,
    up_r,
    dn_s,
    dn_r,
    cc_s,
    cc_r,
    w1_s,
    w1_r,
    xs_s,
    xs_r,
    ys_s,
    ys_r,
    fx_s,
    fx_r,
    fy_s,
    fy_r,
):
    xi, ki, zi, yi = coordinates()
    nt = 2 * nz
    t = ki * nz + zi
    dm = x_ref.shape[1]
    fw = wu_ref.shape[1] // nt
    half = dm // 2

    for o in range(nt):
        cols = []
        for part in range(3):
            base = part * dm + o * HD
            cols += [wq_ref[:, base : base + HD], wq_ref[:, base + half : base + half + HD]]
        for j in range(3):
            pq[o, :, j * 2 * HD : (j + 1) * 2 * HD] = jnp.concatenate(cols[2 * j : 2 * j + 2], axis=1)
        pu[o] = wu_ref[:, o * fw : (o + 1) * fw]
        pd[o] = wd_ref[:, o * fw : (o + 1) * fw]

    greet(nz, xi, ki, zi, yi)

    xpeer = mesh_dev(1 - xi, ki, zi, yi)
    ypeer = mesh_dev(xi, ki, zi, 1 - yi)
    cpeer = mesh_dev(xi, 1 - ki, zi, yi)
    acts = ((x_ref, xb), (g_ref, gb))
    packs = ((pq, wq), (pu, wu), (pd, wd))
    mats = (wq, wu, wd)
    c_own = zi * 2 + yi

    def swap(i):
        src, dst = acts[i]
        return rcopy(src, dst.at[c_own], sw_s.at[i], sw_r.at[i], mesh_dev(xi, yi, zi, ki))

    def swap_start(i):
        @pl.when(ki != yi)
        def _():
            swap(i).start()

        @pl.when(ki == yi)
        def _():
            acts[i][1][c_own] = acts[i][0][...]

    def swap_wait(i):
        @pl.when(ki != yi)
        def _():
            dst = acts[i][1]
            rcopy(
                acts[i][0], dst.at[zi * 2 + ki], sw_s.at[i], sw_r.at[i], mesh_dev(xi, yi, zi, ki)
            ).wait_recv()

    def line(i, z, up):
        slot = acts[i][1].at[z * 2 + ki]
        return slot

    def up_copy(i, d, z):
        slot = line(i, z, True)
        return rcopy(slot, slot, up_s.at[i, d], up_r.at[i, d], mesh_dev(xi, ki, zi + 1, yi))

    def dn_copy(i, d, z):
        slot = line(i, z, False)
        return rcopy(slot, slot, dn_s.at[i, d], dn_r.at[i, d], mesh_dev(xi, ki, zi - 1, yi))

    def cc_copy(i, z, k):
        slot = acts[i][1].at[z * 2 + k]
        return rcopy(slot, slot, cc_s.at[i, z], cc_r.at[i, z], cpeer)

    def hop_send(i, d):
        @pl.when((zi - (d - 1) >= 0) & (zi + 1 < nz))
        def _():
            up_copy(i, d, zi - (d - 1)).start()

        @pl.when((zi + (d - 1) < nz) & (zi >= 1))
        def _():
            dn_copy(i, d, zi + (d - 1)).start()

    def hop_recv(i, d):
        @pl.when(zi - d >= 0)
        def _():
            up_copy(i, d, zi - d).wait_recv()

        @pl.when(zi + d < nz)
        def _():
            dn_copy(i, d, zi + d).wait_recv()

    def hop_share(i, d):
        @pl.when(zi - d >= 0)
        def _():
            cc_copy(i, zi - d, ki).start()

        if d > 0:

            @pl.when(zi + d < nz)
            def _():
                cc_copy(i, zi + d, ki).start()

    def w1(w, d, own):
        pack, dst = packs[w]
        o = mod_less(t + d, nt) if own else t
        s = t if own else mod_less(t + nt - d, nt)
        return rcopy(
            pack.at[o],
            dst.at[xi, s, yi],
            w1_s.at[w, d],
            w1_r.at[w, d],
            mesh_dev(xi, lax.div(o, nz), lax.rem(o, nz), yi) if own else xpeer,
        )

    def w1_start(w):
        for d in range(1, nt):
            w1(w, d, True).start()
        packs[w][1][xi, t, yi] = packs[w][0][t]

    def w1_wait(w):
        for d in range(1, nt):
            w1(w, d, False).wait_recv()

    def own_view(w, xx, yy):
        return mats[w].at[xx, :, yy] if w < 3 else wo.at[xx, yy]

    def half_view(w, h, xx, yy):
        if w < 3:
            return mats[w].at[xx, h * nz : (h + 1) * nz, yy]
        return wo.at[xx, yy, :, h * half : (h + 1) * half]

    def plane_x(w, xx):
        v = own_view(w, xx, yi)
        return rcopy(v, v, xs_s.at[w], xs_r.at[w], xpeer)

    def plane_y(w, yy):
        v = own_view(w, xi, yy)
        return rcopy(v, v, ys_s.at[w], ys_r.at[w], ypeer)

    def forward_y(w, xx, yy):
        v = half_view(w, 0, xx, yy)
        return rcopy(v, v, fy_s.at[w], fy_r.at[w], ypeer)

    def forward_x(w, xx, yy):
        v = half_view(w, 1, xx, yy)
        return rcopy(v, v, fx_s.at[w], fx_r.at[w], xpeer)

    def plane_start(w):
        plane_x(w, xi).start()
        plane_y(w, yi).start()

    def plane_forward(w):
        plane_x(w, 1 - xi).wait_recv()
        forward_y(w, 1 - xi, yi).start()
        plane_y(w, 1 - yi).wait_recv()
        forward_x(w, xi, 1 - yi).start()

    def plane_wait(w):
        forward_y(w, 1 - xi, 1 - yi).wait_recv()
        forward_x(w, 1 - xi, 1 - yi).wait_recv()

    swap_start(0)
    wo[xi, yi] = wo_ref[...]
    w1_start(0)
    swap_wait(0)
    hop_send(0, 1)
    hop_share(0, 0)
    swap_start(1)
    plane_start(3)
    w1_wait(0)
    plane_start(0)
    w1_start(1)
    for d in range(1, nz):
        hop_recv(0, d)
        if d + 1 < nz:
            hop_send(0, d + 1)
        hop_share(0, d)
    plane_forward(0)
    w1_start(2)
    w1_wait(1)
    plane_start(1)
    swap_wait(1)
    hop_send(1, 1)
    hop_share(1, 0)
    plane_forward(3)
    w1_wait(2)
    plane_start(2)
    plane_forward(1)
    for d in range(1, nz):
        hop_recv(1, d)
        if d + 1 < nz:
            hop_send(1, d + 1)
        hop_share(1, d)
    plane_forward(2)
    for w in range(4):
        plane_wait(w)
    for i in range(2):
        for z in range(nz):
            cc_copy(i, z, 1 - ki).wait_recv()

    for i in range(2):

        @pl.when(ki != yi)
        def _():
            swap(i).wait_send()

        for d in range(1, nz):

            @pl.when((zi - (d - 1) >= 0) & (zi + 1 < nz))
            def _():
                up_copy(i, d, zi - (d - 1)).wait_send()

            @pl.when((zi + (d - 1) < nz) & (zi >= 1))
            def _():
                dn_copy(i, d, zi + (d - 1)).wait_send()

        for z in range(nz):
            cc_copy(i, z, ki).wait_send()
    for w in range(3):
        for d in range(1, nt):
            w1(w, d, True).wait_send()
    for w in range(4):
        plane_x(w, xi).wait_send()
        plane_y(w, yi).wait_send()
        forward_y(w, 1 - xi, yi).wait_send()
        forward_x(w, xi, 1 - yi).wait_send()


def gather_all(nz, x, g, w_qkv, w_up, w_down, w_out):
    bf = jnp.bfloat16
    nt = 2 * nz
    rows, dm = x.shape
    piece = w_qkv.shape[0]
    qw = 3 * 2 * HD
    fw = w_up.shape[1] // nt
    vm = pl.BlockSpec(memory_space=pltpu.VMEM)
    dma = pltpu.SemaphoreType.DMA
    shape = jax.ShapeDtypeStruct
    return pl.pallas_call(
        functools.partial(gather_kernel, nz),
        out_shape=(
            shape((nt, rows, dm), bf),
            shape((nt, rows, dm), bf),
            shape((2, nt, 2, piece, qw), bf),
            shape((2, nt, 2, piece, fw), bf),
            shape((2, nt, 2, piece, fw), bf),
            shape((2, 2, piece, dm), bf),
        ),
        in_specs=[vm] * 6,
        out_specs=(vm,) * 6,
        scratch_shapes=[
            pltpu.VMEM((nt, piece, qw), bf),
            pltpu.VMEM((nt, piece, fw), bf),
            pltpu.VMEM((nt, piece, fw), bf),
            dma((2,)),
            dma((2,)),
            dma((2, nz)),
            dma((2, nz)),
            dma((2, nz)),
            dma((2, nz)),
            dma((2, nz)),
            dma((2, nz)),
            dma((3, nt)),
            dma((3, nt)),
        ]
        + [dma((4,)) for _ in range(8)],
        compiler_params=pltpu.CompilerParams(
            collective_id=0, has_side_effects=True, vmem_limit_bytes=48 * 1024 * 1024
        ),
    )(x, g, w_qkv, w_up, w_down, w_out)


def scatter_kernel(
    nz,
    nb,
    *refs,
):
    (a0, a1, mq, mu, md, mo, o0, o1, oq, ou, od, oo) = refs[:12]
    (ex, ru, rd, fin) = refs[12:16]
    (rq, ruu, rdd) = refs[16:19]
    (q2, u2, d2) = refs[19:22]
    (cq, cu, cd) = refs[22:25]
    (ro, so) = refs[25:27]
    (
        cc_s,
        cc_r,
        up_s,
        up_r,
        dn_s,
        dn_r,
        sw_s,
        sw_r,
        x1_s,
        x1_r,
        y1_s,
        y1_r,
        x2_s,
        x2_r,
        y2_s,
        y2_r,
        t_s,
        t_r,
    ) = refs[27:]
    f32 = jnp.float32
    bf = jnp.bfloat16
    xi, ki, zi, yi = coordinates()
    nt = 2 * nz
    t = ki * nz + zi
    greet(nz, xi, ki, zi, yi)
    xpeer = mesh_dev(1 - xi, ki, zi, yi)
    ypeer = mesh_dev(xi, ki, zi, 1 - yi)
    cpeer = mesh_dev(xi, 1 - ki, zi, yi)
    acts = (a0, a1)
    outs = (o0, o1)
    mats = (mq, mu, md)
    got1 = (rq, ruu, rdd)
    got2 = (q2, u2, d2)
    chunks = (cq, cu, cd)

    def plus(a, b):
        return (a.astype(f32) + b.astype(f32)).astype(bf)

    def share(i, z, k):
        return rcopy(acts[i].at[z * 2 + k], ex.at[i, z], cc_s.at[i, z], cc_r.at[i, z], cpeer)

    def up_copy(i, z):
        return rcopy(
            ex.at[i, z], ru.at[i, z], up_s.at[i, z], up_r.at[i, z], mesh_dev(xi, ki, zi + 1, yi)
        )

    def dn_copy(i, z):
        return rcopy(
            ex.at[i, z], rd.at[i, z], dn_s.at[i, z], dn_r.at[i, z], mesh_dev(xi, ki, zi - 1, yi)
        )

    def swap(i):
        return rcopy(fin.at[i], outs[i], sw_s.at[i], sw_r.at[i], mesh_dev(xi, yi, zi, ki))

    def x1(w, mine):
        xx = 1 - xi if mine else xi
        return rcopy(mats[w].at[xx, 0:nz], got1[w].at[0], x1_s.at[w], x1_r.at[w], xpeer)

    def y1(w, y):
        out = [
            rcopy(
                mats[w].at[xx, nz:nt, y],
                got1[w].at[1, :, xx],
                y1_s.at[w, xx],
                y1_r.at[w, xx],
                ypeer,
            )
            for xx in range(2)
        ]
        return out

    def y2(w):
        return rcopy(
            got1[w].at[0, :, 1 - yi], got2[w].at[0:nz], y2_s.at[w], y2_r.at[w], ypeer
        )

    def x2(w):
        return rcopy(
            got1[w].at[1, :, 1 - xi], got2[w].at[nz:nt], x2_s.at[w], x2_r.at[w], xpeer
        )

    def tp(w, d, own):
        o = mod_less(t + d, nt) if own else t
        s = t if own else mod_less(t + nt - d, nt)
        return rcopy(
            got2[w].at[o],
            chunks[w].at[s],
            t_s.at[w, d],
            t_r.at[w, d],
            mesh_dev(xi, lax.div(o, nz), lax.rem(o, nz), yi) if own else xpeer,
        )

    dm = mo.shape[3]
    hw = dm // 2

    def ox1():
        return rcopy(mo.at[1 - xi, :, :, 0:hw], ro.at[0], x1_s.at[3], x1_r.at[3], xpeer)

    def oy1():
        return rcopy(mo.at[:, 1 - yi, :, hw:dm], ro.at[1], y1_s.at[3, 0], y1_r.at[3, 0], ypeer)

    def oy2():
        return rcopy(ro.at[0, 1 - yi], so.at[0], y2_s.at[3], y2_r.at[3], ypeer)

    def ox2():
        return rcopy(ro.at[1, 1 - xi], so.at[1], x2_s.at[3], x2_r.at[3], xpeer)

    for z in range(nz):
        for i in range(2):
            share(i, z, 1 - ki).start()
    for w in range(3):
        x1(w, True).start()
        for c in y1(w, 1 - yi):
            c.start()
    ox1().start()
    oy1().start()

    def fold(i, z):
        share(i, z, 1 - ki).wait_recv()
        ex[i, z] = plus(ex[i, z], acts[i][z * 2 + ki])

    for z in range(nz):
        for i in range(2):
            fold(i, z)

    def hop(i, d):
        @pl.when(zi + d < nz)
        def _():
            z = zi + d

            @pl.when(zi > 0)
            def _():
                up_copy(i, z).wait_recv()
                ex[i, z] = plus(ex[i, z], ru[i, z])

            up_copy(i, z).start()

        @pl.when(zi - d >= 0)
        def _():
            z = zi - d

            @pl.when(zi < nz - 1)
            def _():
                dn_copy(i, z).wait_recv()
                ex[i, z] = plus(ex[i, z], rd[i, z])

            dn_copy(i, z).start()

    def fold1(w):
        x1(w, True).wait_recv()
        got1[w][0] = plus(got1[w][0], mats[w][xi, 0:nz])
        y2(w).start()
        for c in y1(w, 1 - yi):
            c.wait_recv()
        for xx in range(2):
            got1[w][1, :, xx] = plus(got1[w][1, :, xx], mats[w][xx, nz:nt, yi])
        x2(w).start()

    def fold2(w):
        y2(w).wait_recv()
        got2[w][0:nz] = plus(got2[w][0:nz], got1[w][0, :, yi])
        x2(w).wait_recv()
        got2[w][nz:nt] = plus(got2[w][nz:nt], got1[w][1, :, xi])
        for d in range(1, nt):
            tp(w, d, True).start()
        chunks[w][t] = got2[w][t]

    def end(i):
        @pl.when(zi > 0)
        def _():
            up_copy(i, zi).wait_recv()
            ex[i, zi] = plus(ex[i, zi], ru[i, zi])

        @pl.when(zi < nz - 1)
        def _():
            dn_copy(i, zi).wait_recv()
            ex[i, zi] = plus(ex[i, zi], rd[i, zi])

        @pl.when(ki != yi)
        def _():
            fin[i] = ex[i, zi]
            swap(i).start()

        @pl.when(ki == yi)
        def _():
            outs[i][...] = ex[i, zi]

    for d in range(nz - 1, 0, -1):
        for i in range(2):
            hop(i, d)
        if nz - 1 - d < 3:
            fold1(nz - 1 - d)
    for w in range(nz - 1, 3):
        fold1(w)
    ox1().wait_recv()
    ro[0] = plus(ro[0], mo[xi, :, :, 0:hw])
    oy2().start()
    oy1().wait_recv()
    ro[1] = plus(ro[1], mo[:, yi, :, hw:dm])
    ox2().start()
    for i in range(2):
        end(i)
    for w in range(3):
        fold2(w)
    oy2().wait_recv()
    oo[:, 0:hw] = so[0].astype(f32) + ro[0, yi].astype(f32)
    ox2().wait_recv()
    oo[:, hw:dm] = so[1].astype(f32) + ro[1, xi].astype(f32)

    fw = cu.shape[2]
    for w in range(3):
        for d in range(1, nt):
            tp(w, d, False).wait_recv()
    for j in range(3):
        for h in range(2):
            for o in range(0, nt, 2):
                lo = j * 2 * HD + h * HD
                both = jnp.concatenate([cq[o, :, lo : lo + HD], cq[o + 1, :, lo : lo + HD]], axis=1)
                at = j * dm + h * hw + o * HD
                oq[:, at : at + 2 * HD] = both.astype(f32)
    for o in range(nt):
        ou[:, o * fw : (o + 1) * fw] = cu[o].astype(f32)
        od[:, o * fw : (o + 1) * fw] = cd[o].astype(f32)

    for i in range(2):

        @pl.when(ki != yi)
        def _():
            swap(i).wait()

        for z in range(nz):
            share(i, z, 1 - ki).wait_send()
        for d in range(1, nz):

            @pl.when(zi + d < nz)
            def _():
                up_copy(i, zi + d).wait_send()

            @pl.when(zi - d >= 0)
            def _():
                dn_copy(i, zi - d).wait_send()

    for w in range(3):
        x1(w, True).wait_send()
        for c in y1(w, 1 - yi):
            c.wait_send()
        y2(w).wait_send()
        x2(w).wait_send()
        for d in range(1, nt):
            tp(w, d, True).wait_send()
    ox1().wait_send()
    oy1().wait_send()
    oy2().wait_send()
    ox2().wait_send()


def scatter_all(nz, a0, a1, mq, mu, md, mo):
    bf, f32 = jnp.bfloat16, jnp.float32
    nt, rows, dm = a0.shape
    piece, qw = mq.shape[3:]
    fw = mu.shape[4]
    vm = pl.BlockSpec(memory_space=pltpu.VMEM)
    dma = pltpu.SemaphoreType.DMA
    shape = jax.ShapeDtypeStruct
    widths = (qw, fw, fw)
    return pl.pallas_call(
        functools.partial(scatter_kernel, nz, 2),
        out_shape=(
            shape((rows, dm), bf),
            shape((rows, dm), bf),
            shape((piece, 3 * dm), f32),
            shape((piece, fw * nt), f32),
            shape((piece, fw * nt), f32),
            shape((piece, dm), f32),
        ),
        in_specs=[vm] * 6,
        out_specs=(vm,) * 6,
        scratch_shapes=[
            pltpu.VMEM((2, nz, rows, dm), bf),
            pltpu.VMEM((2, nz, rows, dm), bf),
            pltpu.VMEM((2, nz, rows, dm), bf),
            pltpu.VMEM((2, rows, dm), bf),
        ]
        + [pltpu.VMEM((2, nz, 2, piece, w), bf) for w in widths]
        + [pltpu.VMEM((nt, piece, w), bf) for w in widths]
        + [pltpu.VMEM((nt, piece, w), bf) for w in widths]
        + [pltpu.VMEM((2, 2, piece, dm // 2), bf), pltpu.VMEM((2, piece, dm // 2), bf)]
        + [dma((2, nz)) for _ in range(6)]
        + [dma((2,)), dma((2,))]
        + [dma((4,)), dma((4,)), dma((4, 2)), dma((4, 2))]
        + [dma((4,)) for _ in range(4)]
        + [dma((3, nt)), dma((3, nt))],
        compiler_params=pltpu.CompilerParams(
            collective_id=1, has_side_effects=True, vmem_limit_bytes=56 * 1024 * 1024
        ),
    )(a0, a1, mq, mu, md, mo)


def routed(
    layer_in,
    grad_out,
    pair_of_rank,
    ln1_gain,
    ln1_bias,
    ln2_gain,
    ln2_bias,
    w_qkv,
    b_qkv,
    w_out,
    b_out,
    w_up,
    b_up,
    w_down,
    b_down,
):
    f32 = jnp.float32
    bf = jnp.bfloat16
    both = ("fsdp", "ctx")
    nctx = lax.axis_size("ctx")
    ndev = nctx * lax.axis_size("fsdp")
    nz = nctx // 2
    t = lax.rem(lax.axis_index("fsdp"), 2) * nz + lax.div(lax.axis_index("ctx"), 2)
    width2, dmodel = layer_in.shape[2:]
    blk = width2 // 2
    ff = w_up.shape[1]
    qw = 2 * HD
    fw = ff // nctx
    piece = dmodel // ndev
    scale = 1.0 / math.sqrt(HD)

    vec = jnp.concatenate([ln1_gain, ln1_bias, ln2_gain, ln2_bias, b_out, b_down, b_qkv, b_up])
    got = lax.all_gather(vec, both, axis=0, tiled=True).reshape(ndev, -1)
    x_own = layer_in.reshape(width2, dmodel)
    g_own = grad_out.reshape(width2, dmodel)
    x_all, g_all, wq, wu, wd, wo = gather_all(nz, x_own, g_own, w_qkv, w_up, w_down, w_out)
    rows = nctx * width2
    x_all = x_all.reshape(rows, dmodel)
    g_all = g_all.reshape(rows, dmodel)
    wq_c = wq.reshape(dmodel, 3 * qw)
    wu_c = wu.reshape(dmodel, fw)
    wd_c = wd.reshape(dmodel, fw)
    wo_c = wo.reshape(qw, dmodel)

    cuts = [piece] * 6 + [b_qkv.shape[0], b_up.shape[0]]
    fulls = []
    at = 0
    for cut in cuts:
        fulls.append(got[:, at : at + cut].reshape(-1).astype(f32))
        at += cut
    gain1, bias1, gain2, bias2, bo, bd, bq, bu = fulls
    bq_c = lax.dynamic_slice_in_dim(bq.reshape(3, 2, nctx, HD), t, 1, axis=2).reshape(1, 3 * qw)
    bu_c = lax.dynamic_slice_in_dim(bu, t * fw, fw).reshape(1, fw)

    offsets = jnp.arange(blk, dtype=jnp.int32)
    slot_a = pair_of_rank[:, None] * blk + offsets[None, :]
    slot_b = (2 * nctx - 1 - pair_of_rank)[:, None] * blk + offsets[None, :]
    places = jnp.concatenate([slot_a, slot_b], axis=1).reshape(rows)

    def hat_of(xf):
        row_mean = jnp.mean(xf, axis=-1, keepdims=True)
        centred = xf - row_mean
        rstd = lax.rsqrt(jnp.mean(centred * centred, axis=-1, keepdims=True) + EPS)
        return centred * rstd, rstd

    hat, _ = hat_of(x_all.astype(f32))
    norm1 = (hat * gain1 + bias1).astype(bf)
    norm2 = (hat * gain2 + bias2).astype(bf)
    qkv = jnp.dot(norm1, wq_c, preferred_element_type=f32) + bq_c
    cosine, sine_low, sine_high = turn_tables(places, qw)
    query = headed(turn(qkv[:, :qw], cosine, sine_low, sine_high).astype(bf), 2)
    key = headed(turn(qkv[:, qw : 2 * qw], cosine, sine_low, sine_high).astype(bf), 2)
    value = headed(qkv[:, 2 * qw :].astype(bf), 2)
    visible = places[None, :] <= places[:, None]
    score = jnp.where(visible[None], bdot("hqd,hkd->hqk", query, key) * scale, NEG)
    top = jnp.max(score, axis=-1, keepdims=True)
    weight = jnp.exp(score - top)
    total = jnp.sum(weight, axis=-1, keepdims=True)
    mixed = bdot("hqk,hkd->hqd", weight.astype(bf), value)
    context = (mixed / total).astype(bf)
    lse = top + jnp.log(total)
    ctx_c = joined(context)

    pre = jnp.dot(norm2, wu_c, preferred_element_type=f32) + bu_c
    hidden = gelu_value(pre).astype(bf)
    part = rdot(hidden, wd_c) + jnp.dot(ctx_c, wo_c, preferred_element_type=f32)

    dhidden = jnp.dot(g_all, wd_c, preferred_element_type=f32)
    dpre = dhidden * gelu_slope(pre)
    dpre_b = dpre.astype(bf)
    dnorm2 = rdot(dpre_b, wu_c)
    dctx = headed(rdot(g_all, wo_c).astype(bf), 2)
    delta = jnp.sum(dctx.astype(f32) * context.astype(f32), axis=-1, keepdims=True)
    prob = jnp.exp(score - lse)
    dprob = bdot("hqd,hkd->hqk", dctx, value)
    ds = (scale * prob * (dprob - delta)).astype(bf)
    dquery = joined(bdot("hqk,hkd->hqd", ds, key))
    dkey = joined(bdot("hqk,hqd->hkd", ds, query))
    dvalue = joined(bdot("hqk,hqd->hkd", prob.astype(bf), dctx))
    dqkv = jnp.concatenate(
        [
            turn(dquery, cosine, -sine_low, -sine_high),
            turn(dkey, cosine, -sine_low, -sine_high),
            dvalue,
        ],
        axis=1,
    )
    dqkv_b = dqkv.astype(bf)
    dnorm1 = rdot(dqkv_b, wq_c)
    gsum = (dnorm1 * gain1 + dnorm2 * gain2).astype(bf)
    g_ownf = g_own.astype(f32)

    sum_q = lax.dynamic_update_slice_in_dim(
        jnp.zeros((3, 2, nctx, HD), f32), jnp.sum(dqkv, axis=0).reshape(3, 2, 1, HD), t, axis=2
    ).reshape(ndev, -1)
    sum_u = lax.dynamic_update_slice_in_dim(
        jnp.zeros((ff,), f32), jnp.sum(dpre, axis=0), t * fw, axis=0
    ).reshape(ndev, -1)
    sums = [
        jnp.sum(dnorm1 * hat, axis=0).reshape(ndev, -1),
        jnp.sum(dnorm1, axis=0).reshape(ndev, -1),
        jnp.sum(dnorm2 * hat, axis=0).reshape(ndev, -1),
        jnp.sum(dnorm2, axis=0).reshape(ndev, -1),
        jnp.sum(g_ownf, axis=0).reshape(ndev, -1),
        sum_q,
        sum_u,
    ]
    sums = jnp.concatenate(sums, axis=1).reshape(-1)
    sums = lax.psum_scatter(sums, both, scatter_dimension=0, tiled=True)

    lead = (2, nctx, 2, piece)
    fwd, gsum, grad_qkv, grad_up, grad_down, grad_wout = scatter_all(
        nz,
        part.astype(bf).reshape(nctx, width2, dmodel),
        gsum.reshape(nctx, width2, dmodel),
        tdot(norm1, dqkv_b).astype(bf).reshape(lead + (3 * qw,)),
        tdot(norm2, dpre_b).astype(bf).reshape(lead + (fw,)),
        tdot(g_all, hidden).astype(bf).reshape(lead + (fw,)),
        tdot(ctx_c, g_all).astype(bf).reshape(2, 2, piece, dmodel),
    )
    x_ownf = x_own.astype(f32)
    layer_out = (x_ownf + fwd.astype(f32) + (bo + bd)).astype(bf).reshape(layer_in.shape)
    gsum = gsum.astype(f32)
    hat_own, rstd_own = hat_of(x_ownf)
    grad_x = (
        g_ownf
        + rstd_own
        * (
            gsum
            - jnp.mean(gsum, axis=-1, keepdims=True)
            - hat_own * jnp.mean(gsum * hat_own, axis=-1, keepdims=True)
        )
    ).astype(bf).reshape(layer_in.shape)
    ends = [piece * i for i in range(6)] + [5 * piece + b_qkv.shape[0], sums.shape[0]]
    vs = [sums[a:b] for a, b in zip(ends[:-1], ends[1:])]
    return (
        layer_out,
        grad_x,
        vs[0],
        vs[1],
        vs[2],
        vs[3],
        grad_qkv,
        vs[5],
        grad_wout,
        vs[4],
        grad_up,
        vs[6],
        grad_down,
        vs[4],
    )


def solution(mesh):
    nctx = mesh.shape["ctx"]

    def pick(layer_in, *rest):
        heads = layer_in.shape[-1] // HD
        whole = heads % nctx == 0
        square = nctx % 2 == 0 and mesh.shape["fsdp"] == 4 and heads == 2 * nctx
        if square and layer_in.shape[1] == 1 and layer_in.shape[2] % 16 == 0:
            return routed(layer_in, *rest)
        return (head_shards if whole else shards)(layer_in, *rest)

    return jax.shard_map(
        pick,
        mesh=mesh,
        in_specs=(
            P("ctx", "fsdp", None, None),
            P("ctx", "fsdp", None, None),
            P(),
            P(("fsdp", "ctx")),
            P(("fsdp", "ctx")),
            P(("fsdp", "ctx")),
            P(("fsdp", "ctx")),
            P(("fsdp", "ctx"), None),
            P(("fsdp", "ctx")),
            P(("fsdp", "ctx"), None),
            P(("fsdp", "ctx")),
            P(("fsdp", "ctx"), None),
            P(("fsdp", "ctx")),
            P(("fsdp", "ctx"), None),
            P(("fsdp", "ctx")),
        ),
        out_specs=(
            P("ctx", "fsdp", None, None),
            P("ctx", "fsdp", None, None),
            P(("fsdp", "ctx")),
            P(("fsdp", "ctx")),
            P(("fsdp", "ctx")),
            P(("fsdp", "ctx")),
            P(("fsdp", "ctx"), None),
            P(("fsdp", "ctx")),
            P(("fsdp", "ctx"), None),
            P(("fsdp", "ctx")),
            P(("fsdp", "ctx"), None),
            P(("fsdp", "ctx")),
            P(("fsdp", "ctx"), None),
            P(("fsdp", "ctx")),
        ),
        check_vma=False,
    )
```

```python
import functools
import math

import jax
import jax.numpy as jnp
from jax import lax
from jax.experimental import pallas as pl
from jax.experimental.pallas import tpu as pltpu
from jax.sharding import PartitionSpec as P

HD = 64
ROT = 16
LANES = 128


EPS = 1e-05
NEG = -1e30
ROOT_HALF = 0.7071067811865476
INV_ROOT_TAU = 0.3989422804014327


def norm_parts(xf, scale_weight, shift_bias):
    row_mean = jnp.mean(xf, axis=-1, keepdims=True)
    centred_input = xf - row_mean
    inverse_deviation = lax.rsqrt(
        jnp.mean(centred_input * centred_input, axis=-1, keepdims=True) + EPS
    )
    normalized_input = centred_input * inverse_deviation
    return (
        normalized_input * scale_weight.astype(jnp.float32) + shift_bias.astype(jnp.float32),
        normalized_input,
        inverse_deviation,
    )


def layer_norm_backward(norm_output_gradient, normalized_input, inverse_deviation, scale_weight):
    normalized_gradient = norm_output_gradient * scale_weight.astype(jnp.float32)
    return inverse_deviation * (
        normalized_gradient
        - jnp.mean(normalized_gradient, axis=-1, keepdims=True)
        - normalized_input
        * jnp.mean(normalized_gradient * normalized_input, axis=-1, keepdims=True)
    )


def gelu_value(u):
    return 0.5 * u * (1.0 + lax.erf(u * ROOT_HALF))


def gelu_slope(u):
    return 0.5 * (1.0 + lax.erf(u * ROOT_HALF)) + u * jnp.exp(-0.5 * u * u) * INV_ROOT_TAU


def rotate(field, place, sign):
    half = ROT // 2
    freqs = jnp.exp(jnp.arange(half).astype(jnp.float32) * (-2.0 * math.log(10000.0) / ROT))
    angle = place.astype(jnp.float32)[..., None] * freqs
    cosine = jnp.cos(angle)[..., None, :]
    sine = sign * jnp.sin(angle)[..., None, :]
    first = field[..., :half]
    second = field[..., half:ROT]
    return jnp.concatenate(
        [first * cosine - second * sine, second * cosine + first * sine, field[..., rot_end() :]],
        axis=-1,
    )


def rot_end():
    return ROT


def leading(field, letters):
    return "n" + letters if field.ndim == 5 else letters


def product(left, left_letters, right, right_letters, result):
    form = leading(left, left_letters) + "," + leading(right, right_letters) + "->" + result
    return jnp.einsum(form, left, right, preferred_element_type=jnp.float32)


def selectors(sel):
    return (sel[:, None, None, None, None], sel[:, None, None, None], sel[:, None])


def visibility(sel, qpa, qpb, kpa, kpb):
    chosen = sel[:, None]
    key_place = jnp.where(chosen, kpa, kpb)
    query_place = jnp.where(chosen, qpa, qpb)
    return (key_place[:, None, :] <= query_place[:, :, None])[:, None, None]


def online_update(state, qa, qb, ka, kb, va, vb, qpa, qpb, kpa, kpb, sel, with_first, scale):
    top_a, total_a, acc_a, top_b, total_b, acc_b = state
    sel5, sel4, sel2 = selectors(sel)
    query_two = jnp.where(sel5, qa, qb)
    key_two = jnp.where(sel5, ka, kb)
    value_two = jnp.where(sel5, va, vb)
    visible = visibility(sel, qpa, qpb, kpa, kpb)
    score = jnp.where(visible, product(query_two, "sqhd", key_two, "skhd", "nshqk") * scale, NEG)
    peak_a = jnp.max(jnp.where(sel5, score, NEG), axis=(0, 4))
    peak_b = jnp.max(jnp.where(sel5, NEG, score), axis=(0, 4))
    if with_first:
        score_one = product(qb, "sqhd", ka, "skhd", "nshqk") * scale
        peak_b = jnp.maximum(peak_b, jnp.max(score_one, axis=(0, 4)))
    new_a = jnp.maximum(top_a, peak_a)
    new_b = jnp.maximum(top_b, peak_b)
    lifted = jnp.where(sel5, new_a[..., None], new_b[..., None])
    weight = jnp.where(visible, jnp.exp(score - lifted), 0.0)
    mixed = product(weight.astype(jnp.bfloat16), "shqk", value_two, "skhd", "nshqd")
    mass = jnp.sum(weight, axis=4)
    add_total_a = jnp.sum(jnp.where(sel4, mass, 0.0), axis=0)
    add_total_b = jnp.sum(jnp.where(sel4, 0.0, mass), axis=0)
    add_acc_a = jnp.sum(jnp.where(sel5, mixed, 0.0), axis=0)
    add_acc_b = jnp.sum(jnp.where(sel5, 0.0, mixed), axis=0)
    if with_first:
        weight_one = jnp.exp(score_one - new_b[..., None])
        add_total_b = add_total_b + jnp.sum(weight_one, axis=(0, 4))
        add_acc_b = add_acc_b + product(weight_one.astype(jnp.bfloat16), "shqk", va, "skhd", "shqd")
    decay_a = jnp.exp(top_a - new_a)
    decay_b = jnp.exp(top_b - new_b)
    return (
        new_a,
        total_a * decay_a + add_total_a,
        acc_a * decay_a[..., None] + add_acc_a,
        new_b,
        total_b * decay_b + add_total_b,
        acc_b * decay_b[..., None] + add_acc_b,
    )


def pair_terms(
    qa,
    qb,
    ka,
    kb,
    va,
    vb,
    da,
    db,
    lsea,
    lseb,
    dela,
    delb,
    qpa,
    qpb,
    kpa,
    kpb,
    sel,
    with_first,
    scale,
):
    sel5, sel4, sel2 = selectors(sel)
    query_two = jnp.where(sel5, qa, qb)
    key_two = jnp.where(sel5, ka, kb)
    value_two = jnp.where(sel5, va, vb)
    dctx_two = jnp.where(sel5, da, db)
    lse_two = jnp.where(sel4, lsea, lseb)
    delta_two = jnp.where(sel4, dela, delb)
    visible = visibility(sel, qpa, qpb, kpa, kpb)
    score = jnp.where(visible, product(query_two, "sqhd", key_two, "skhd", "nshqk") * scale, NEG)
    prob = jnp.exp(score - lse_two[..., None])
    dprob = product(dctx_two, "sqhd", value_two, "skhd", "nshqk")
    dscore = (scale * prob * (dprob - delta_two[..., None])).astype(jnp.bfloat16)
    first_ds = None
    first_prob = None
    if with_first:
        score_one = product(qb, "sqhd", ka, "skhd", "nshqk") * scale
        prob_one = jnp.exp(score_one - lseb[..., None])
        dprob_one = product(db, "sqhd", va, "skhd", "nshqk")
        first_ds = (scale * prob_one * (dprob_one - delb[..., None])).astype(jnp.bfloat16)
        first_prob = prob_one.astype(jnp.bfloat16)
    return (first_ds, first_prob, dscore, prob.astype(jnp.bfloat16))


def query_grads(terms, ka, kb, sel):
    sel5, sel4, sel2 = selectors(sel)
    key_two = jnp.where(sel5, ka, kb)
    dq_two = product(terms[2], "shqk", key_two, "skhd", "nsqhd")
    dq_a = jnp.where(sel5, dq_two, 0.0)
    dq_b = jnp.where(sel5, 0.0, dq_two)
    if terms[0] is not None:
        dq_b = dq_b + product(terms[0], "shqk", ka, "skhd", "nsqhd")
    return (dq_a, dq_b)


def key_grads(terms, qa, qb, da, db, sel):
    sel5, sel4, sel2 = selectors(sel)
    query_two = jnp.where(sel5, qa, qb)
    dctx_two = jnp.where(sel5, da, db)
    dk_two = product(terms[2], "shqk", query_two, "sqhd", "nskhd")
    dv_two = product(terms[3], "shqk", dctx_two, "sqhd", "nskhd")
    dk_a = jnp.where(sel5, dk_two, 0.0)
    dk_b = jnp.where(sel5, 0.0, dk_two)
    dv_a = jnp.where(sel5, dv_two, 0.0)
    dv_b = jnp.where(sel5, 0.0, dv_two)
    if terms[0] is not None:
        dk_a = dk_a + product(terms[0], "shqk", qb, "sqhd", "nskhd")
        dv_a = dv_a + product(terms[1], "shqk", db, "sqhd", "nskhd")
    return (dk_a, dk_b, dv_a, dv_b)


def tdot(left, right):
    return lax.dot_general(
        left, right, (((0,), (0,)), ((), ())), preferred_element_type=jnp.float32
    )


def rdot(left, right):
    return lax.dot_general(
        left, right, (((1,), (1,)), ((), ())), preferred_element_type=jnp.float32
    )


def shards(
    layer_in,
    grad_out,
    pair_of_rank,
    ln1_gain,
    ln1_bias,
    ln2_gain,
    ln2_bias,
    w_qkv,
    b_qkv,
    w_out,
    b_out,
    w_up,
    b_up,
    w_down,
    b_down,
):
    f32 = jnp.float32
    bf = jnp.bfloat16
    nctx = lax.axis_size("ctx")
    mine = pair_of_rank[lax.axis_index("ctx")]
    seqs = layer_in.shape[1]
    width2 = layer_in.shape[2]
    dmodel = layer_in.shape[3]
    blk = width2 // 2
    rows = seqs * width2
    heads = dmodel // HD
    scale = 1.0 / math.sqrt(HD)
    offsets = jnp.arange(blk, dtype=jnp.int32)
    place_a = mine * blk + offsets
    place_b = (2 * nctx - 1 - mine) * blk + offsets
    places = jnp.concatenate([place_a, place_b])
    params = (
        ln1_gain,
        ln1_bias,
        ln2_gain,
        ln2_bias,
        w_qkv,
        b_qkv,
        w_out,
        b_out,
        w_up,
        b_up,
        w_down,
        b_down,
    )
    full = (
        lax.all_gather(params[0], ("fsdp", "ctx"), axis=0, tiled=True),
        lax.all_gather(params[1], ("fsdp", "ctx"), axis=0, tiled=True),
        lax.all_gather(params[2], ("fsdp", "ctx"), axis=0, tiled=True),
        lax.all_gather(params[3], ("fsdp", "ctx"), axis=0, tiled=True),
        lax.all_gather(params[4], ("fsdp", "ctx"), axis=0, tiled=True),
        lax.all_gather(params[5], ("fsdp", "ctx"), axis=0, tiled=True),
        lax.all_gather(params[6], ("fsdp", "ctx"), axis=0, tiled=True),
        lax.all_gather(params[7], ("fsdp", "ctx"), axis=0, tiled=True),
        lax.all_gather(params[8], ("fsdp", "ctx"), axis=0, tiled=True),
        lax.all_gather(params[9], ("fsdp", "ctx"), axis=0, tiled=True),
        lax.all_gather(params[10], ("fsdp", "ctx"), axis=0, tiled=True),
        lax.all_gather(params[11], ("fsdp", "ctx"), axis=0, tiled=True),
    )
    xf = layer_in.reshape(rows, dmodel).astype(f32)
    norm1, hat1, rstd1 = norm_parts(xf, full[0], full[1])
    norm2, hat2, rstd2 = norm_parts(xf, full[2], full[3])
    norm1 = norm1.astype(bf)
    norm2 = norm2.astype(bf)
    qkv = jnp.dot(norm1, full[4], preferred_element_type=f32) + full[5].astype(f32)
    query = rotate(qkv[:, :dmodel].reshape(seqs, width2, heads, HD), places, 1.0).astype(bf)
    key = rotate(qkv[:, dmodel : 2 * dmodel].reshape(seqs, width2, heads, HD), places, 1.0).astype(
        bf
    )
    value = qkv[:, 2 * dmodel :].reshape(seqs, width2, heads, HD).astype(bf)
    query_a = query[:, :blk]
    query_b = query[:, blk:]
    key_b = key[:, blk:]
    value_b = value[:, blk:]
    lone = jnp.zeros((1,), dtype=bool)
    empty_top = jnp.full((seqs, heads, blk), NEG, f32)
    empty_total = jnp.zeros((seqs, heads, blk), f32)
    empty_acc = jnp.zeros((seqs, heads, blk, HD), f32)
    state = (empty_top, empty_total, empty_acc, empty_top, empty_total, empty_acc)
    state = online_update(
        state,
        query_a,
        query_b,
        key_b[None],
        key_b[None],
        value_b[None],
        value_b[None],
        place_a,
        place_b,
        place_b[None],
        place_b[None],
        lone,
        False,
        scale,
    )

    def key_parts(kpiece, vpiece, first):
        count = kpiece.shape[0]
        pairs = lax.dynamic_slice_in_dim(pair_of_rank, first, count)
        keys = kpiece.reshape(count, seqs, width2, heads, HD)
        values = vpiece.reshape(count, seqs, width2, heads, HD)
        kplace_a = pairs[:, None] * blk + offsets[None, :]
        kplace_b = (2 * nctx - 1 - pairs)[:, None] * blk + offsets[None, :]
        return (
            keys[:, :, :blk],
            keys[:, :, blk:],
            values[:, :, :blk],
            values[:, :, blk:],
            kplace_a,
            kplace_b,
            pairs,
        )

    key_send = key.reshape(1, seqs, width2, dmodel)
    value_send = value.reshape(1, seqs, width2, dmodel)
    ka, kb, va, vb, kpa, kpb, pairs = key_parts(
        lax.all_gather(key_send, "ctx", axis=0, tiled=True),
        lax.all_gather(value_send, "ctx", axis=0, tiled=True),
        jnp.int32(0),
    )
    state = online_update(
        state,
        query_a,
        query_b,
        ka,
        kb,
        va,
        vb,
        place_a,
        place_b,
        kpa,
        kpb,
        pairs <= mine,
        True,
        scale,
    )
    top_a, total_a, acc_a, top_b, total_b, acc_b = state
    context4 = jnp.concatenate([acc_a / total_a[..., None], acc_b / total_b[..., None]], axis=2)
    lse = jnp.concatenate([top_a + jnp.log(total_a), top_b + jnp.log(total_b)], axis=2)
    context = context4.transpose(0, 2, 1, 3).reshape(rows, dmodel).astype(bf)
    attn = jnp.dot(context, full[6], preferred_element_type=f32) + full[7].astype(f32)
    pre = jnp.dot(norm2, full[8], preferred_element_type=f32) + full[9].astype(f32)
    hidden = gelu_value(pre).astype(bf)
    mlp = rdot(hidden, full[10]) + full[11].astype(f32)
    layer_out = (xf + attn + mlp).astype(bf).reshape(layer_in.shape)
    again = (
        lax.all_gather(params[0], ("fsdp", "ctx"), axis=0, tiled=True),
        lax.all_gather(params[1], ("fsdp", "ctx"), axis=0, tiled=True),
        lax.all_gather(params[2], ("fsdp", "ctx"), axis=0, tiled=True),
        lax.all_gather(params[3], ("fsdp", "ctx"), axis=0, tiled=True),
        lax.all_gather(params[4], ("fsdp", "ctx"), axis=0, tiled=True),
        lax.all_gather(params[5], ("fsdp", "ctx"), axis=0, tiled=True),
        lax.all_gather(params[6], ("fsdp", "ctx"), axis=0, tiled=True),
        lax.all_gather(params[7], ("fsdp", "ctx"), axis=0, tiled=True),
        lax.all_gather(params[8], ("fsdp", "ctx"), axis=0, tiled=True),
        lax.all_gather(params[9], ("fsdp", "ctx"), axis=0, tiled=True),
        lax.all_gather(params[10], ("fsdp", "ctx"), axis=0, tiled=True),
        lax.all_gather(params[11], ("fsdp", "ctx"), axis=0, tiled=True),
    )
    grad_b = grad_out.reshape(rows, dmodel)
    grad_f = grad_b.astype(f32)
    dhidden = jnp.dot(grad_b, again[10], preferred_element_type=f32)
    dpre = dhidden * gelu_slope(pre)
    dpre_b = dpre.astype(bf)
    dnorm2 = rdot(dpre_b, again[8])
    dcontext = rdot(grad_b, again[6]).astype(bf)
    dctx4 = dcontext.reshape(seqs, width2, heads, HD)
    delta = jnp.sum(
        dctx4.astype(f32) * context.reshape(seqs, width2, heads, HD).astype(f32), axis=-1
    ).transpose(0, 2, 1)
    dctx_a = dctx4[:, :blk]
    dctx_b = dctx4[:, blk:]
    lse_a = lse[..., :blk]
    lse_b = lse[..., blk:]
    delta_a = delta[..., :blk]
    delta_b = delta[..., blk:]
    own = pair_terms(
        query_b,
        query_b,
        key_b[None],
        key_b[None],
        value_b[None],
        value_b[None],
        dctx_b,
        dctx_b,
        lse_b,
        lse_b,
        delta_b,
        delta_b,
        place_b,
        place_b,
        place_b[None],
        place_b[None],
        lone,
        False,
        scale,
    )
    own_dq = query_grads(own, key_b[None], key_b[None], lone)[1][0]
    own_keys = key_grads(own, query_b, query_b, dctx_b, dctx_b, lone)
    gathered = (
        lax.all_gather(key_send, "ctx", axis=0, tiled=True),
        lax.all_gather(value_send, "ctx", axis=0, tiled=True),
    )
    groups = math.gcd(nctx, 8)
    per = nctx // groups

    def group_terms(args):
        kpiece, vpiece, first = args
        ka, kb, va, vb, kpa, kpb, pairs = key_parts(kpiece, vpiece, first)
        sel = pairs <= mine
        terms = pair_terms(
            query_a,
            query_b,
            ka,
            kb,
            va,
            vb,
            dctx_a,
            dctx_b,
            lse_a,
            lse_b,
            delta_a,
            delta_b,
            place_a,
            place_b,
            kpa,
            kpb,
            sel,
            True,
            scale,
        )
        dq_a, dq_b = query_grads(terms, ka, kb, sel)
        return (terms, jnp.sum(dq_a, axis=0), jnp.sum(dq_b, axis=0))

    grouped = lax.map(
        group_terms,
        (
            gathered[0].reshape(groups, per, seqs, width2, dmodel),
            gathered[1].reshape(groups, per, seqs, width2, dmodel),
            jnp.arange(groups, dtype=jnp.int32) * per,
        ),
    )
    terms_all = tuple((part.reshape((nctx,) + part.shape[2:]) for part in grouped[0]))
    dq_a = jnp.sum(grouped[1], axis=0)
    dq_b = jnp.sum(grouped[2], axis=0)
    pairs = pair_of_rank
    sliced = tuple(
        (lax.slice_in_dim(part, 0, 1 * lax.axis_size("ctx"), axis=0) for part in terms_all)
    )
    dk_a, dk_b, dv_a, dv_b = key_grads(sliced, query_a, query_b, dctx_a, dctx_b, pairs <= mine)
    dkey = jnp.concatenate([dk_a, dk_b], axis=2).reshape(
        1 * lax.axis_size("ctx"), seqs, width2, dmodel
    )
    dval = jnp.concatenate([dv_a, dv_b], axis=2).reshape(
        1 * lax.axis_size("ctx"), seqs, width2, dmodel
    )
    kv_grad = lax.psum_scatter(
        jnp.concatenate([dkey, dval], axis=-1), "ctx", scatter_dimension=0, tiled=True
    )
    dkey = kv_grad[0, :, :, :dmodel].reshape(seqs, width2, heads, HD)
    dval = kv_grad[0, :, :, dmodel:].reshape(seqs, width2, heads, HD)
    zero_half = jnp.zeros((seqs, blk, heads, HD), f32)
    dquery = jnp.concatenate([dq_a, dq_b + own_dq], axis=1)
    dkey = dkey + jnp.concatenate([zero_half, own_keys[1][0]], axis=1)
    dval = dval + jnp.concatenate([zero_half, own_keys[3][0]], axis=1)
    dqkv = jnp.concatenate(
        [
            rotate(dquery, places, -1.0).reshape(rows, dmodel),
            rotate(dkey, places, -1.0).reshape(rows, dmodel),
            dval.reshape(rows, dmodel),
        ],
        axis=1,
    )
    dqkv_b = dqkv.astype(bf)
    dnorm1 = rdot(dqkv_b, again[4])
    grad_x = (
        (
            grad_f
            + layer_norm_backward(dnorm1, hat1, rstd1, again[0])
            + layer_norm_backward(dnorm2, hat2, rstd2, again[2])
        )
        .astype(bf)
        .reshape(layer_in.shape)
    )
    vectors = (
        lax.psum_scatter(
            jnp.sum(dnorm1 * hat1, axis=0), ("fsdp", "ctx"), scatter_dimension=0, tiled=True
        ),
        lax.psum_scatter(jnp.sum(dnorm1, axis=0), ("fsdp", "ctx"), scatter_dimension=0, tiled=True),
        lax.psum_scatter(
            jnp.sum(dnorm2 * hat2, axis=0), ("fsdp", "ctx"), scatter_dimension=0, tiled=True
        ),
        lax.psum_scatter(jnp.sum(dnorm2, axis=0), ("fsdp", "ctx"), scatter_dimension=0, tiled=True),
        lax.psum_scatter(jnp.sum(dqkv, axis=0), ("fsdp", "ctx"), scatter_dimension=0, tiled=True),
        lax.psum_scatter(jnp.sum(grad_f, axis=0), ("fsdp", "ctx"), scatter_dimension=0, tiled=True),
        lax.psum_scatter(jnp.sum(dpre, axis=0), ("fsdp", "ctx"), scatter_dimension=0, tiled=True),
    )
    weights = (
        lax.psum_scatter(tdot(norm1, dqkv_b), ("fsdp", "ctx"), scatter_dimension=0, tiled=True),
        lax.psum_scatter(tdot(context, grad_b), ("fsdp", "ctx"), scatter_dimension=0, tiled=True),
        lax.psum_scatter(tdot(norm2, dpre_b), ("fsdp", "ctx"), scatter_dimension=0, tiled=True),
        lax.psum_scatter(tdot(grad_b, hidden), ("fsdp", "ctx"), scatter_dimension=0, tiled=True),
    )
    return (
        layer_out,
        grad_x,
        vectors[0],
        vectors[1],
        vectors[2],
        vectors[3],
        weights[0],
        vectors[4],
        weights[1],
        vectors[5],
        weights[2],
        vectors[6],
        weights[3],
        vectors[5],
    )


def span(lead, cols):
    return jnp.arange(lead, dtype=jnp.int32)[:, None] if cols else jnp.arange(lead, dtype=jnp.int32)


def turn(field, cosine, sine_low, sine_high):
    half = ROT // 2
    down = jnp.concatenate([field[:, half:], field[:, :half]], axis=1)
    up = jnp.concatenate([field[:, -half:], field[:, :-half]], axis=1)
    return field * cosine + down * sine_low + up * sine_high


def turn_tables(places, width):
    half = ROT // 2
    lane = jnp.arange(width, dtype=jnp.int32) % HD
    freqs = jnp.exp((lane % half).astype(jnp.float32) * (-2.0 * math.log(10000.0) / ROT))
    angle = places.astype(jnp.float32)[:, None] * freqs[None, :]
    cosine = jnp.where(lane < ROT, jnp.cos(angle), 1.0)
    sine = jnp.sin(angle)
    sine_low = jnp.where(lane < half, -sine, 0.0)
    sine_high = jnp.where((lane >= half) & (lane < ROT), sine, 0.0)
    return cosine, sine_low, sine_high


def headed(field, count):
    return field.reshape(field.shape[0], count, HD).transpose(1, 0, 2)


def joined(field):
    return field.transpose(1, 0, 2).reshape(field.shape[1], -1)


def bdot(form, left, right):
    return jnp.einsum(form, left, right, preferred_element_type=jnp.float32)


def head_shards(
    layer_in,
    grad_out,
    pair_of_rank,
    ln1_gain,
    ln1_bias,
    ln2_gain,
    ln2_bias,
    w_qkv,
    b_qkv,
    w_out,
    b_out,
    w_up,
    b_up,
    w_down,
    b_down,
):
    f32 = jnp.float32
    bf = jnp.bfloat16
    both = ("fsdp", "ctx")
    nctx = lax.axis_size("ctx")
    nf = lax.axis_size("fsdp")
    ndev = nctx * nf
    c = lax.axis_index("ctx")
    seqs, width2, dmodel = layer_in.shape[1:]
    blk = width2 // 2
    own_rows = seqs * width2
    ff = w_up.shape[1]
    hloc = dmodel // HD // nctx
    qw = hloc * HD
    fw = ff // nctx
    piece = dmodel // ndev
    scale = 1.0 / math.sqrt(HD)

    x_all = lax.all_gather(layer_in.reshape(own_rows, dmodel), "ctx", axis=0, tiled=True)
    def columns(parts):
        packed = jnp.concatenate([p.reshape(piece, nctx, -1) for p in parts], axis=-1)
        packed = packed.transpose(1, 0, 2)
        got = lax.all_to_all(packed, "ctx", split_axis=0, concat_axis=0, tiled=True)
        return got.reshape(nctx * piece, -1)

    wq = w_qkv.reshape(piece, 3, nctx, qw).transpose(0, 2, 1, 3)
    vec = jnp.concatenate([ln1_gain, ln1_bias, ln2_gain, ln2_bias, b_out, b_down, b_qkv, b_up])
    vw = LANES * -(-vec.shape[0] // (piece * LANES))
    vec_pad = jnp.pad(vec, (0, piece * vw - vec.shape[0])).reshape(piece, 1, vw)
    vec_pad = jnp.broadcast_to(vec_pad, (piece, nctx, vw))
    cols = lax.all_gather(columns([wq, w_up, w_down, vec_pad]), "fsdp", axis=0, tiled=True)
    g_own = grad_out.reshape(own_rows, dmodel)
    cols, g_send = lax.optimization_barrier((cols, g_own))
    got = cols[:, 3 * qw + 2 * fw :].reshape(ndev, piece * vw)
    cuts = [piece] * 6 + [b_qkv.shape[0], b_up.shape[0]]
    fulls = []
    at = 0
    for cut in cuts:
        fulls.append(got[:, at : at + cut].reshape(-1).astype(f32))
        at += cut
    gain1, bias1, gain2, bias2, bo, bd, bq, bu = fulls
    bq_c = lax.dynamic_slice_in_dim(bq.reshape(3, nctx, qw), c, 1, axis=1).reshape(1, 3 * qw)
    bu_c = lax.dynamic_slice_in_dim(bu, c * fw, fw).reshape(1, fw)
    wq_c = cols[:, : 3 * qw]
    wu_c = cols[:, 3 * qw : 3 * qw + fw]
    wd_c = cols[:, 3 * qw + fw : 3 * qw + 2 * fw]
    there = [((nf * cc + f) , f * nctx + cc) for f in range(nf) for cc in range(nctx)]
    back = [(b, a) for a, b in there]
    wo_c = lax.all_gather(lax.ppermute(w_out, both, there), "fsdp", axis=0, tiled=True)
    g_all = lax.all_gather(g_send, "ctx", axis=0, tiled=True)

    rows = x_all.shape[0]
    offsets = jnp.arange(blk, dtype=jnp.int32)
    slot_a = pair_of_rank[:, None] * blk + offsets[None, :]
    slot_b = (2 * nctx - 1 - pair_of_rank)[:, None] * blk + offsets[None, :]
    slots = jnp.concatenate([slot_a, slot_b], axis=1)[:, None, :]
    places = jnp.broadcast_to(slots, (nctx, seqs, width2)).reshape(rows)
    group = jnp.broadcast_to(span(seqs, False)[None, :, None], (nctx, seqs, width2)).reshape(rows)

    def hat_of(xf):
        row_mean = jnp.mean(xf, axis=-1, keepdims=True)
        centred = xf - row_mean
        rstd = lax.rsqrt(jnp.mean(centred * centred, axis=-1, keepdims=True) + EPS)
        return centred * rstd, rstd

    hat, _ = hat_of(x_all.astype(f32))
    norm1 = (hat * gain1 + bias1).astype(bf)
    norm2 = (hat * gain2 + bias2).astype(bf)
    qkv = jnp.dot(norm1, wq_c, preferred_element_type=f32) + bq_c
    cosine, sine_low, sine_high = turn_tables(places, qw)
    query = headed(turn(qkv[:, :qw], cosine, sine_low, sine_high).astype(bf), hloc)
    key = headed(turn(qkv[:, qw : 2 * qw], cosine, sine_low, sine_high).astype(bf), hloc)
    value = headed(qkv[:, 2 * qw :].astype(bf), hloc)
    visible = places[None, :] <= places[:, None]
    if seqs > 1:
        visible = visible & (group[None, :] == group[:, None])
    score = jnp.where(visible[None], bdot("hqd,hkd->hqk", query, key) * scale, NEG)
    top = jnp.max(score, axis=-1, keepdims=True)
    weight = jnp.exp(score - top)
    total = jnp.sum(weight, axis=-1, keepdims=True)
    mixed = bdot("hqk,hkd->hqd", weight.astype(bf), value)
    context = (mixed / total).astype(bf)
    lse = top + jnp.log(total)
    ctx_c = joined(context)

    pre = jnp.dot(norm2, wu_c, preferred_element_type=f32) + bu_c
    hidden = gelu_value(pre).astype(bf)
    part = rdot(hidden, wd_c) + jnp.dot(ctx_c, wo_c, preferred_element_type=f32)
    fwd = lax.all_to_all(
        part.astype(bf).reshape(nctx, own_rows, dmodel), "ctx", split_axis=0, concat_axis=0, tiled=True
    )
    fwd = jnp.sum(fwd.astype(f32), axis=0)
    x_own = layer_in.reshape(own_rows, dmodel).astype(f32)
    layer_out = (x_own + fwd + (bo + bd)).astype(bf).reshape(layer_in.shape)

    dhidden = jnp.dot(g_all, wd_c, preferred_element_type=f32)
    dpre = dhidden * gelu_slope(pre)
    dpre_b = dpre.astype(bf)
    dnorm2 = rdot(dpre_b, wu_c)
    dctx = headed(rdot(g_all, wo_c).astype(bf), hloc)
    delta = jnp.sum(dctx.astype(f32) * context.astype(f32), axis=-1, keepdims=True)
    prob = jnp.exp(score - lse)
    dprob = bdot("hqd,hkd->hqk", dctx, value)
    ds = (scale * prob * (dprob - delta)).astype(bf)
    dquery = joined(bdot("hqk,hkd->hqd", ds, key))
    dkey = joined(bdot("hqk,hqd->hkd", ds, query))
    dvalue = joined(bdot("hqk,hqd->hkd", prob.astype(bf), dctx))
    dqkv = jnp.concatenate(
        [
            turn(dquery, cosine, -sine_low, -sine_high),
            turn(dkey, cosine, -sine_low, -sine_high),
            dvalue,
        ],
        axis=1,
    )
    dqkv_b = dqkv.astype(bf)
    dnorm1 = rdot(dqkv_b, wq_c)
    gsum = (dnorm1 * gain1 + dnorm2 * gain2).astype(bf)
    gsum = lax.psum_scatter(gsum, "ctx", scatter_dimension=0, tiled=True).astype(f32)
    hat_own, rstd_own = hat_of(x_own)
    g_ownf = g_own.astype(f32)
    grad_x = (
        g_ownf
        + rstd_own
        * (
            gsum
            - jnp.mean(gsum, axis=-1, keepdims=True)
            - hat_own * jnp.mean(gsum * hat_own, axis=-1, keepdims=True)
        )
    ).astype(bf).reshape(layer_in.shape)

    sum_q = jnp.zeros((3, nctx, qw), f32)
    sum_q = lax.dynamic_update_slice_in_dim(
        sum_q, jnp.sum(dqkv, axis=0).reshape(3, 1, qw), c, axis=1
    ).reshape(ndev, -1)
    sum_u = lax.dynamic_update_slice_in_dim(
        jnp.zeros((ff,), f32), jnp.sum(dpre, axis=0), c * fw, axis=0
    ).reshape(ndev, -1)
    sums = [
        jnp.sum(dnorm1 * hat, axis=0).reshape(ndev, -1),
        jnp.sum(dnorm1, axis=0).reshape(ndev, -1),
        jnp.sum(dnorm2 * hat, axis=0).reshape(ndev, -1),
        jnp.sum(dnorm2, axis=0).reshape(ndev, -1),
        jnp.sum(g_ownf, axis=0).reshape(ndev, -1),
        sum_q,
        sum_u,
    ]
    sums = jnp.concatenate(sums, axis=1)
    sw = LANES * -(-sums.shape[1] // (piece * LANES))
    sums_pad = jnp.pad(sums, ((0, 0), (0, piece * sw - sums.shape[1]))).reshape(ndev * piece, sw)
    rows_out = tdot(ctx_c, g_all).astype(bf)
    wide = jnp.concatenate(
        [
            tdot(norm1, dqkv_b).astype(bf),
            tdot(norm2, dpre_b).astype(bf),
            tdot(g_all, hidden).astype(bf),
            sums_pad.astype(bf),
            rows_out.reshape(ndev * piece, -1),
        ],
        axis=1,
    )
    wide = lax.psum_scatter(wide, "fsdp", scatter_dimension=0, tiled=True)
    split = 3 * qw + 2 * fw + sw
    grad_wout = lax.ppermute(wide[:, split:].reshape(piece, dmodel), both, back).astype(f32)
    wide = lax.all_to_all(
        wide[:, :split].reshape(nctx, piece, split), "ctx", split_axis=0, concat_axis=0, tiled=True
    )
    sums = jnp.sum(wide[:, :, split - sw :].astype(f32), axis=0).reshape(-1)[: sums.shape[1]]
    wide = wide.transpose(1, 0, 2).astype(f32)
    grad_qkv = (
        wide[:, :, : 3 * qw].reshape(piece, nctx, 3, qw).transpose(0, 2, 1, 3).reshape(piece, -1)
    )
    grad_up = wide[:, :, 3 * qw : 3 * qw + fw].reshape(piece, ff)
    grad_down = wide[:, :, 3 * qw + fw : 3 * qw + 2 * fw].reshape(piece, ff)
    ends = [piece * i for i in range(6)] + [5 * piece + b_qkv.shape[0], sums.shape[0]]
    vs = [sums[a:b] for a, b in zip(ends[:-1], ends[1:])]
    return (
        layer_out,
        grad_x,
        vs[0],
        vs[1],
        vs[2],
        vs[3],
        grad_qkv,
        vs[5],
        grad_wout,
        vs[4],
        grad_up,
        vs[6],
        grad_down,
        vs[4],
    )


def mod_less(a, n):
    return jnp.where(a >= n, a - n, a)


def mesh_dev(xi, ki, zi, yi):
    return {"fsdp": xi * 2 + ki, "ctx": zi * 2 + yi}


def rcopy(src, dst, send, recv, where):
    return pltpu.make_async_remote_copy(
        src_ref=src,
        dst_ref=dst,
        send_sem=send,
        recv_sem=recv,
        device_id=where,
        device_id_type=pl.DeviceIdType.MESH,
    )


def coordinates():
    f = lax.axis_index("fsdp")
    c = lax.axis_index("ctx")
    xi, ki = lax.div(f, 2), lax.rem(f, 2)
    zi, yi = lax.div(c, 2), lax.rem(c, 2)
    return xi, ki, zi, yi


def greet(nz, xi, ki, zi, yi):
    t = ki * nz + zi
    nt = 2 * nz
    barrier = pltpu.get_barrier_semaphore()

    def hello(where):
        pl.semaphore_signal(barrier, inc=1, device_id=where, device_id_type=pl.DeviceIdType.MESH)

    for d in range(1, nt):
        o = mod_less(t + d, nt)
        hello(mesh_dev(xi, lax.div(o, nz), lax.rem(o, nz), yi))
    hello(mesh_dev(1 - xi, ki, zi, yi))
    hello(mesh_dev(xi, ki, zi, 1 - yi))

    @pl.when(ki != yi)
    def _():
        hello(mesh_dev(xi, yi, zi, ki))

    pl.semaphore_wait(barrier, jnp.where(ki != yi, nt + 2, nt + 1))


def gather_kernel(
    nz,
    x_ref,
    g_ref,
    wq_ref,
    wu_ref,
    wd_ref,
    wo_ref,
    v0,
    v1,
    v2,
    v3,
    v4,
    v5,
    v6,
    v7,
    xb,
    gb,
    wq,
    wu,
    wd,
    wo,
    pq,
    pu,
    pd,
    vs,
    sw_s,
    sw_r,
    up_s,
    up_r,
    dn_s,
    dn_r,
    cc_s,
    cc_r,
    w1_s,
    w1_r,
    xs_s,
    xs_r,
    ys_s,
    ys_r,
    fx_s,
    fx_r,
    fy_s,
    fy_r,
):
    xi, ki, zi, yi = coordinates()
    nt = 2 * nz
    t = ki * nz + zi
    dm = x_ref.shape[1]
    fw = wu_ref.shape[1] // nt
    half = dm // 2

    vs[...] = jnp.zeros_like(vs)
    for i, v in enumerate((v0, v1, v2, v3, v4, v5, v6, v7)):
        vs[i : i + 1, 0 : v.shape[1]] = v[...].astype(jnp.float32)
    small = vs[...].astype(jnp.bfloat16)
    for o in range(nt):
        pq[o, :, 6 * HD :] = small
        cols = []
        for part in range(3):
            base = part * dm + o * HD
            cols += [wq_ref[:, base : base + HD], wq_ref[:, base + half : base + half + HD]]
        for j in range(3):
            pq[o, :, j * 2 * HD : (j + 1) * 2 * HD] = jnp.concatenate(cols[2 * j : 2 * j + 2], axis=1)
        pu[o] = wu_ref[:, o * fw : (o + 1) * fw]
        pd[o] = wd_ref[:, o * fw : (o + 1) * fw]

    greet(nz, xi, ki, zi, yi)

    xpeer = mesh_dev(1 - xi, ki, zi, yi)
    ypeer = mesh_dev(xi, ki, zi, 1 - yi)
    cpeer = mesh_dev(xi, 1 - ki, zi, yi)
    acts = ((x_ref, xb), (g_ref, gb))
    packs = ((pq, wq), (pu, wu), (pd, wd))
    mats = (wq, wu, wd)
    c_own = zi * 2 + yi

    def swap(i):
        src, dst = acts[i]
        return rcopy(src, dst.at[c_own], sw_s.at[i], sw_r.at[i], mesh_dev(xi, yi, zi, ki))

    def swap_start(i):
        @pl.when(ki != yi)
        def _():
            swap(i).start()

        @pl.when(ki == yi)
        def _():
            acts[i][1][c_own] = acts[i][0][...]

    def swap_wait(i):
        @pl.when(ki != yi)
        def _():
            dst = acts[i][1]
            rcopy(
                acts[i][0], dst.at[zi * 2 + ki], sw_s.at[i], sw_r.at[i], mesh_dev(xi, yi, zi, ki)
            ).wait_recv()

    def line(i, z, up):
        slot = acts[i][1].at[z * 2 + ki]
        return slot

    def up_copy(i, d, z):
        slot = line(i, z, True)
        return rcopy(slot, slot, up_s.at[i, d], up_r.at[i, d], mesh_dev(xi, ki, zi + 1, yi))

    def dn_copy(i, d, z):
        slot = line(i, z, False)
        return rcopy(slot, slot, dn_s.at[i, d], dn_r.at[i, d], mesh_dev(xi, ki, zi - 1, yi))

    def cc_copy(i, z, k):
        slot = acts[i][1].at[z * 2 + k]
        return rcopy(slot, slot, cc_s.at[i, z], cc_r.at[i, z], cpeer)

    def hop_send(i, d):
        @pl.when((zi - (d - 1) >= 0) & (zi + 1 < nz))
        def _():
            up_copy(i, d, zi - (d - 1)).start()

        @pl.when((zi + (d - 1) < nz) & (zi >= 1))
        def _():
            dn_copy(i, d, zi + (d - 1)).start()

    def hop_recv(i, d):
        @pl.when(zi - d >= 0)
        def _():
            up_copy(i, d, zi - d).wait_recv()

        @pl.when(zi + d < nz)
        def _():
            dn_copy(i, d, zi + d).wait_recv()

    def hop_share(i, d):
        @pl.when(zi - d >= 0)
        def _():
            cc_copy(i, zi - d, ki).start()

        if d > 0:

            @pl.when(zi + d < nz)
            def _():
                cc_copy(i, zi + d, ki).start()

    def w1(w, d, own):
        pack, dst = packs[w]
        o = mod_less(t + d, nt) if own else t
        s = t if own else mod_less(t + nt - d, nt)
        return rcopy(
            pack.at[o],
            dst.at[xi, s, yi],
            w1_s.at[w, d],
            w1_r.at[w, d],
            mesh_dev(xi, lax.div(o, nz), lax.rem(o, nz), yi) if own else xpeer,
        )

    def w1_start(w):
        for d in range(1, nt):
            w1(w, d, True).start()
        packs[w][1][xi, t, yi] = packs[w][0][t]

    def w1_wait(w):
        for d in range(1, nt):
            w1(w, d, False).wait_recv()

    def own_view(w, xx, yy):
        return mats[w].at[xx, :, yy] if w < 3 else wo.at[xx, yy]

    def half_view(w, h, xx, yy):
        if w < 3:
            return mats[w].at[xx, h * nz : (h + 1) * nz, yy]
        return wo.at[xx, yy, :, h * half : (h + 1) * half]

    def plane_x(w, xx):
        v = own_view(w, xx, yi)
        return rcopy(v, v, xs_s.at[w], xs_r.at[w], xpeer)

    def plane_y(w, yy):
        v = own_view(w, xi, yy)
        return rcopy(v, v, ys_s.at[w], ys_r.at[w], ypeer)

    def forward_y(w, xx, yy):
        v = half_view(w, 0, xx, yy)
        return rcopy(v, v, fy_s.at[w], fy_r.at[w], ypeer)

    def forward_x(w, xx, yy):
        v = half_view(w, 1, xx, yy)
        return rcopy(v, v, fx_s.at[w], fx_r.at[w], xpeer)

    def plane_start(w):
        plane_x(w, xi).start()
        plane_y(w, yi).start()

    def plane_forward(w):
        plane_x(w, 1 - xi).wait_recv()
        forward_y(w, 1 - xi, yi).start()
        plane_y(w, 1 - yi).wait_recv()
        forward_x(w, xi, 1 - yi).start()

    def plane_wait(w):
        forward_y(w, 1 - xi, 1 - yi).wait_recv()
        forward_x(w, 1 - xi, 1 - yi).wait_recv()

    swap_start(0)
    wo[xi, yi] = wo_ref[...]
    w1_start(0)
    swap_wait(0)
    hop_send(0, 1)
    hop_share(0, 0)
    swap_start(1)
    plane_start(3)
    w1_wait(0)
    plane_start(0)
    w1_start(1)
    for d in range(1, nz):
        hop_recv(0, d)
        if d + 1 < nz:
            hop_send(0, d + 1)
        hop_share(0, d)
    plane_forward(0)
    w1_start(2)
    w1_wait(1)
    plane_start(1)
    swap_wait(1)
    hop_send(1, 1)
    hop_share(1, 0)
    plane_forward(3)
    w1_wait(2)
    plane_start(2)
    plane_forward(1)
    for d in range(1, nz):
        hop_recv(1, d)
        if d + 1 < nz:
            hop_send(1, d + 1)
        hop_share(1, d)
    plane_forward(2)
    for w in range(4):
        plane_wait(w)
    for i in range(2):
        for z in range(nz):
            cc_copy(i, z, 1 - ki).wait_recv()

    for i in range(2):

        @pl.when(ki != yi)
        def _():
            swap(i).wait_send()

        for d in range(1, nz):

            @pl.when((zi - (d - 1) >= 0) & (zi + 1 < nz))
            def _():
                up_copy(i, d, zi - (d - 1)).wait_send()

            @pl.when((zi + (d - 1) < nz) & (zi >= 1))
            def _():
                dn_copy(i, d, zi + (d - 1)).wait_send()

        for z in range(nz):
            cc_copy(i, z, ki).wait_send()
    for w in range(3):
        for d in range(1, nt):
            w1(w, d, True).wait_send()
    for w in range(4):
        plane_x(w, xi).wait_send()
        plane_y(w, yi).wait_send()
        forward_y(w, 1 - xi, yi).wait_send()
        forward_x(w, xi, 1 - yi).wait_send()


def gather_all(nz, x, g, w_qkv, w_up, w_down, w_out, *vectors):
    bf = jnp.bfloat16
    nt = 2 * nz
    rows, dm = x.shape
    piece = w_qkv.shape[0]
    qw = 3 * 2 * HD + LANES
    fw = w_up.shape[1] // nt
    vm = pl.BlockSpec(memory_space=pltpu.VMEM)
    dma = pltpu.SemaphoreType.DMA
    shape = jax.ShapeDtypeStruct
    return pl.pallas_call(
        functools.partial(gather_kernel, nz),
        out_shape=(
            shape((nt, rows, dm), bf),
            shape((nt, rows, dm), bf),
            shape((2, nt, 2, piece, qw), bf),
            shape((2, nt, 2, piece, fw), bf),
            shape((2, nt, 2, piece, fw), bf),
            shape((2, 2, piece, dm), bf),
        ),
        in_specs=[vm] * 14,
        out_specs=(vm,) * 6,
        scratch_shapes=[
            pltpu.VMEM((nt, piece, qw), bf),
            pltpu.VMEM((nt, piece, fw), bf),
            pltpu.VMEM((nt, piece, fw), bf),
            pltpu.VMEM((piece, LANES), jnp.float32),
            dma((2,)),
            dma((2,)),
            dma((2, nz)),
            dma((2, nz)),
            dma((2, nz)),
            dma((2, nz)),
            dma((2, nz)),
            dma((2, nz)),
            dma((3, nt)),
            dma((3, nt)),
        ]
        + [dma((4,)) for _ in range(8)],
        compiler_params=pltpu.CompilerParams(
            collective_id=0, has_side_effects=True, vmem_limit_bytes=48 * 1024 * 1024
        ),
    )(x, g, w_qkv, w_up, w_down, w_out, *[v.reshape(1, -1) for v in vectors])


def scatter_kernel(
    nz,
    nb,
    *refs,
):
    (a0, a1, mq, mu, md, mo, o0, o1, oq, ou, od, oo, osum) = refs[:13]
    (ex, ru, rd, fin) = refs[13:17]
    (rq, ruu, rdd) = refs[17:20]
    (q2, u2, d2) = refs[20:23]
    (cq, cu, cd) = refs[23:26]
    (ro, so) = refs[26:28]
    (
        cc_s,
        cc_r,
        up_s,
        up_r,
        dn_s,
        dn_r,
        sw_s,
        sw_r,
        x1_s,
        x1_r,
        y1_s,
        y1_r,
        x2_s,
        x2_r,
        y2_s,
        y2_r,
        t_s,
        t_r,
    ) = refs[28:]
    f32 = jnp.float32
    bf = jnp.bfloat16
    xi, ki, zi, yi = coordinates()
    nt = 2 * nz
    t = ki * nz + zi
    greet(nz, xi, ki, zi, yi)
    xpeer = mesh_dev(1 - xi, ki, zi, yi)
    ypeer = mesh_dev(xi, ki, zi, 1 - yi)
    cpeer = mesh_dev(xi, 1 - ki, zi, yi)
    acts = (a0, a1)
    outs = (o0, o1)
    mats = (mq, mu, md)
    got1 = (rq, ruu, rdd)
    got2 = (q2, u2, d2)
    chunks = (cq, cu, cd)

    def plus(a, b):
        return (a.astype(f32) + b.astype(f32)).astype(bf)

    def share(i, z, k):
        return rcopy(acts[i].at[z * 2 + k], ex.at[i, z], cc_s.at[i, z], cc_r.at[i, z], cpeer)

    def up_copy(i, z):
        return rcopy(
            ex.at[i, z], ru.at[i, z], up_s.at[i, z], up_r.at[i, z], mesh_dev(xi, ki, zi + 1, yi)
        )

    def dn_copy(i, z):
        return rcopy(
            ex.at[i, z], rd.at[i, z], dn_s.at[i, z], dn_r.at[i, z], mesh_dev(xi, ki, zi - 1, yi)
        )

    def swap(i):
        return rcopy(fin.at[i], outs[i], sw_s.at[i], sw_r.at[i], mesh_dev(xi, yi, zi, ki))

    def x1(w, mine):
        xx = 1 - xi if mine else xi
        return rcopy(mats[w].at[xx, 0:nz], got1[w].at[0], x1_s.at[w], x1_r.at[w], xpeer)

    def y1(w, y):
        out = [
            rcopy(
                mats[w].at[xx, nz:nt, y],
                got1[w].at[1, :, xx],
                y1_s.at[w, xx],
                y1_r.at[w, xx],
                ypeer,
            )
            for xx in range(2)
        ]
        return out

    def y2(w):
        return rcopy(
            got1[w].at[0, :, 1 - yi], got2[w].at[0:nz], y2_s.at[w], y2_r.at[w], ypeer
        )

    def x2(w):
        return rcopy(
            got1[w].at[1, :, 1 - xi], got2[w].at[nz:nt], x2_s.at[w], x2_r.at[w], xpeer
        )

    def tp(w, d, own):
        o = mod_less(t + d, nt) if own else t
        s = t if own else mod_less(t + nt - d, nt)
        return rcopy(
            got2[w].at[o],
            chunks[w].at[s],
            t_s.at[w, d],
            t_r.at[w, d],
            mesh_dev(xi, lax.div(o, nz), lax.rem(o, nz), yi) if own else xpeer,
        )

    dm = mo.shape[3]
    hw = dm // 2

    def ox1():
        return rcopy(mo.at[1 - xi, :, :, 0:hw], ro.at[0], x1_s.at[3], x1_r.at[3], xpeer)

    def oy1():
        return rcopy(mo.at[:, 1 - yi, :, hw:dm], ro.at[1], y1_s.at[3, 0], y1_r.at[3, 0], ypeer)

    def oy2():
        return rcopy(ro.at[0, 1 - yi], so.at[0], y2_s.at[3], y2_r.at[3], ypeer)

    def ox2():
        return rcopy(ro.at[1, 1 - xi], so.at[1], x2_s.at[3], x2_r.at[3], xpeer)

    for z in range(nz):
        for i in range(2):
            share(i, z, 1 - ki).start()
    for w in range(3):
        x1(w, True).start()
        for c in y1(w, 1 - yi):
            c.start()
    ox1().start()
    oy1().start()

    def fold(i, z):
        share(i, z, 1 - ki).wait_recv()
        ex[i, z] = plus(ex[i, z], acts[i][z * 2 + ki])

    for z in range(nz):
        for i in range(2):
            fold(i, z)

    def hop(i, d):
        @pl.when(zi + d < nz)
        def _():
            z = zi + d

            @pl.when(zi > 0)
            def _():
                up_copy(i, z).wait_recv()
                ex[i, z] = plus(ex[i, z], ru[i, z])

            up_copy(i, z).start()

        @pl.when(zi - d >= 0)
        def _():
            z = zi - d

            @pl.when(zi < nz - 1)
            def _():
                dn_copy(i, z).wait_recv()
                ex[i, z] = plus(ex[i, z], rd[i, z])

            dn_copy(i, z).start()

    def fold1(w):
        x1(w, True).wait_recv()
        got1[w][0] = plus(got1[w][0], mats[w][xi, 0:nz])
        y2(w).start()
        for c in y1(w, 1 - yi):
            c.wait_recv()
        for xx in range(2):
            got1[w][1, :, xx] = plus(got1[w][1, :, xx], mats[w][xx, nz:nt, yi])
        x2(w).start()

    def fold2(w):
        y2(w).wait_recv()
        got2[w][0:nz] = plus(got2[w][0:nz], got1[w][0, :, yi])
        x2(w).wait_recv()
        got2[w][nz:nt] = plus(got2[w][nz:nt], got1[w][1, :, xi])
        for d in range(1, nt):
            tp(w, d, True).start()
        chunks[w][t] = got2[w][t]

    def end(i):
        @pl.when(zi > 0)
        def _():
            up_copy(i, zi).wait_recv()
            ex[i, zi] = plus(ex[i, zi], ru[i, zi])

        @pl.when(zi < nz - 1)
        def _():
            dn_copy(i, zi).wait_recv()
            ex[i, zi] = plus(ex[i, zi], rd[i, zi])

        @pl.when(ki != yi)
        def _():
            fin[i] = ex[i, zi]
            swap(i).start()

        @pl.when(ki == yi)
        def _():
            outs[i][...] = ex[i, zi]

    for d in range(nz - 1, 0, -1):
        for i in range(2):
            hop(i, d)
        if nz - 1 - d < 3:
            fold1(nz - 1 - d)
    for w in range(nz - 1, 3):
        fold1(w)
    ox1().wait_recv()
    ro[0] = plus(ro[0], mo[xi, :, :, 0:hw])
    oy2().start()
    oy1().wait_recv()
    ro[1] = plus(ro[1], mo[:, yi, :, hw:dm])
    ox2().start()
    for i in range(2):
        end(i)
    for w in range(3):
        fold2(w)
    oy2().wait_recv()
    oo[:, 0:hw] = so[0].astype(f32) + ro[0, yi].astype(f32)
    ox2().wait_recv()
    oo[:, hw:dm] = so[1].astype(f32) + ro[1, xi].astype(f32)

    fw = cu.shape[2]
    for w in range(3):
        for d in range(1, nt):
            tp(w, d, False).wait_recv()
    for j in range(3):
        for h in range(2):
            for o in range(0, nt, 2):
                lo = j * 2 * HD + h * HD
                both = jnp.concatenate([cq[o, :, lo : lo + HD], cq[o + 1, :, lo : lo + HD]], axis=1)
                at = j * dm + h * hw + o * HD
                oq[:, at : at + 2 * HD] = both.astype(f32)
    osum[...] = jnp.sum(cq[:, :, 6 * HD :].astype(f32), axis=0)
    for o in range(nt):
        ou[:, o * fw : (o + 1) * fw] = cu[o].astype(f32)
        od[:, o * fw : (o + 1) * fw] = cd[o].astype(f32)

    for i in range(2):

        @pl.when(ki != yi)
        def _():
            swap(i).wait()

        for z in range(nz):
            share(i, z, 1 - ki).wait_send()
        for d in range(1, nz):

            @pl.when(zi + d < nz)
            def _():
                up_copy(i, zi + d).wait_send()

            @pl.when(zi - d >= 0)
            def _():
                dn_copy(i, zi - d).wait_send()

    for w in range(3):
        x1(w, True).wait_send()
        for c in y1(w, 1 - yi):
            c.wait_send()
        y2(w).wait_send()
        x2(w).wait_send()
        for d in range(1, nt):
            tp(w, d, True).wait_send()
    ox1().wait_send()
    oy1().wait_send()
    oy2().wait_send()
    ox2().wait_send()


def scatter_all(nz, a0, a1, mq, mu, md, mo):
    bf, f32 = jnp.bfloat16, jnp.float32
    nt, rows, dm = a0.shape
    piece, qw = mq.shape[3:]
    fw = mu.shape[4]
    vm = pl.BlockSpec(memory_space=pltpu.VMEM)
    dma = pltpu.SemaphoreType.DMA
    shape = jax.ShapeDtypeStruct
    widths = (qw, fw, fw)
    return pl.pallas_call(
        functools.partial(scatter_kernel, nz, 2),
        out_shape=(
            shape((rows, dm), bf),
            shape((rows, dm), bf),
            shape((piece, 3 * dm), f32),
            shape((piece, fw * nt), f32),
            shape((piece, fw * nt), f32),
            shape((piece, dm), f32),
            shape((piece, LANES), f32),
        ),
        in_specs=[vm] * 6,
        out_specs=(vm,) * 7,
        scratch_shapes=[
            pltpu.VMEM((2, nz, rows, dm), bf),
            pltpu.VMEM((2, nz, rows, dm), bf),
            pltpu.VMEM((2, nz, rows, dm), bf),
            pltpu.VMEM((2, rows, dm), bf),
        ]
        + [pltpu.VMEM((2, nz, 2, piece, w), bf) for w in widths]
        + [pltpu.VMEM((nt, piece, w), bf) for w in widths]
        + [pltpu.VMEM((nt, piece, w), bf) for w in widths]
        + [pltpu.VMEM((2, 2, piece, dm // 2), bf), pltpu.VMEM((2, piece, dm // 2), bf)]
        + [dma((2, nz)) for _ in range(6)]
        + [dma((2,)), dma((2,))]
        + [dma((4,)), dma((4,)), dma((4, 2)), dma((4, 2))]
        + [dma((4,)) for _ in range(4)]
        + [dma((3, nt)), dma((3, nt))],
        compiler_params=pltpu.CompilerParams(
            collective_id=1, has_side_effects=True, vmem_limit_bytes=56 * 1024 * 1024
        ),
    )(a0, a1, mq, mu, md, mo)


def routed(
    layer_in,
    grad_out,
    pair_of_rank,
    ln1_gain,
    ln1_bias,
    ln2_gain,
    ln2_bias,
    w_qkv,
    b_qkv,
    w_out,
    b_out,
    w_up,
    b_up,
    w_down,
    b_down,
):
    f32 = jnp.float32
    bf = jnp.bfloat16
    nctx = lax.axis_size("ctx")
    ndev = nctx * lax.axis_size("fsdp")
    nz = nctx // 2
    t = lax.rem(lax.axis_index("fsdp"), 2) * nz + lax.div(lax.axis_index("ctx"), 2)
    width2, dmodel = layer_in.shape[2:]
    blk = width2 // 2
    ff = w_up.shape[1]
    qw = 2 * HD
    fw = ff // nctx
    piece = dmodel // ndev
    scale = 1.0 / math.sqrt(HD)

    vectors = (ln1_gain, ln1_bias, ln2_gain, ln2_bias, b_out, b_down, b_qkv, b_up)
    x_own = layer_in.reshape(width2, dmodel)
    g_own = grad_out.reshape(width2, dmodel)
    x_all, g_all, wq, wu, wd, wo = gather_all(
        nz, x_own, g_own, w_qkv, w_up, w_down, w_out, *vectors
    )
    rows = nctx * width2
    x_all = x_all.reshape(rows, dmodel)
    g_all = g_all.reshape(rows, dmodel)
    wq = wq.reshape(dmodel, -1)
    wq_c = wq[:, : 3 * qw]
    got = wq[:, 3 * qw :].reshape(ndev, piece, LANES).astype(f32)
    wu_c = wu.reshape(dmodel, fw)
    wd_c = wd.reshape(dmodel, fw)
    wo_c = wo.reshape(qw, dmodel)

    fulls = [got[:, i, : v.shape[0]].reshape(-1) for i, v in enumerate(vectors)]
    gain1, bias1, gain2, bias2, bo, bd, bq, bu = fulls
    bq_c = lax.dynamic_slice_in_dim(bq.reshape(3, 2, nctx, HD), t, 1, axis=2).reshape(1, 3 * qw)
    bu_c = lax.dynamic_slice_in_dim(bu, t * fw, fw).reshape(1, fw)

    offsets = jnp.arange(blk, dtype=jnp.int32)
    slot_a = pair_of_rank[:, None] * blk + offsets[None, :]
    slot_b = (2 * nctx - 1 - pair_of_rank)[:, None] * blk + offsets[None, :]
    places = jnp.concatenate([slot_a, slot_b], axis=1).reshape(rows)

    def hat_of(xf):
        row_mean = jnp.mean(xf, axis=-1, keepdims=True)
        centred = xf - row_mean
        rstd = lax.rsqrt(jnp.mean(centred * centred, axis=-1, keepdims=True) + EPS)
        return centred * rstd, rstd

    hat, _ = hat_of(x_all.astype(f32))
    norm1 = (hat * gain1 + bias1).astype(bf)
    norm2 = (hat * gain2 + bias2).astype(bf)
    qkv = jnp.dot(norm1, wq_c, preferred_element_type=f32) + bq_c
    cosine, sine_low, sine_high = turn_tables(places, qw)
    query = headed(turn(qkv[:, :qw], cosine, sine_low, sine_high).astype(bf), 2)
    key = headed(turn(qkv[:, qw : 2 * qw], cosine, sine_low, sine_high).astype(bf), 2)
    value = headed(qkv[:, 2 * qw :].astype(bf), 2)
    visible = places[None, :] <= places[:, None]
    score = jnp.where(visible[None], bdot("hqd,hkd->hqk", query, key) * scale, NEG)
    top = jnp.max(score, axis=-1, keepdims=True)
    weight = jnp.exp(score - top)
    total = jnp.sum(weight, axis=-1, keepdims=True)
    mixed = bdot("hqk,hkd->hqd", weight.astype(bf), value)
    context = (mixed / total).astype(bf)
    lse = top + jnp.log(total)
    ctx_c = joined(context)

    pre = jnp.dot(norm2, wu_c, preferred_element_type=f32) + bu_c
    hidden = gelu_value(pre).astype(bf)
    part = rdot(hidden, wd_c) + jnp.dot(ctx_c, wo_c, preferred_element_type=f32)

    dhidden = jnp.dot(g_all, wd_c, preferred_element_type=f32)
    dpre = dhidden * gelu_slope(pre)
    dpre_b = dpre.astype(bf)
    dnorm2 = rdot(dpre_b, wu_c)
    dctx = headed(rdot(g_all, wo_c).astype(bf), 2)
    delta = jnp.sum(dctx.astype(f32) * context.astype(f32), axis=-1, keepdims=True)
    prob = jnp.exp(score - lse)
    dprob = bdot("hqd,hkd->hqk", dctx, value)
    ds = (scale * prob * (dprob - delta)).astype(bf)
    dquery = joined(bdot("hqk,hkd->hqd", ds, key))
    dkey = joined(bdot("hqk,hqd->hkd", ds, query))
    dvalue = joined(bdot("hqk,hqd->hkd", prob.astype(bf), dctx))
    dqkv = jnp.concatenate(
        [
            turn(dquery, cosine, -sine_low, -sine_high),
            turn(dkey, cosine, -sine_low, -sine_high),
            dvalue,
        ],
        axis=1,
    )
    dqkv_b = dqkv.astype(bf)
    dnorm1 = rdot(dqkv_b, wq_c)
    gsum = (dnorm1 * gain1 + dnorm2 * gain2).astype(bf)
    g_ownf = g_own.astype(f32)

    sum_q = lax.dynamic_update_slice_in_dim(
        jnp.zeros((3, 2, nctx, HD), f32), jnp.sum(dqkv, axis=0).reshape(3, 2, 1, HD), t, axis=2
    ).reshape(ndev, -1)
    sum_u = lax.dynamic_update_slice_in_dim(
        jnp.zeros((ff,), f32), jnp.sum(dpre, axis=0), t * fw, axis=0
    ).reshape(ndev, -1)
    sums = [
        jnp.sum(dnorm1 * hat, axis=0).reshape(ndev, -1),
        jnp.sum(dnorm1, axis=0).reshape(ndev, -1),
        jnp.sum(dnorm2 * hat, axis=0).reshape(ndev, -1),
        jnp.sum(dnorm2, axis=0).reshape(ndev, -1),
        jnp.sum(g_ownf, axis=0).reshape(ndev, -1),
        sum_q,
        sum_u,
    ]
    sums = jnp.stack([jnp.pad(v, ((0, 0), (0, LANES - v.shape[1]))) for v in sums], axis=1)
    sums = jnp.pad(sums, ((0, 0), (0, piece - sums.shape[1]), (0, 0))).reshape(dmodel, LANES)

    lead = (2, nctx, 2, piece)
    fwd, gsum, grad_qkv, grad_up, grad_down, grad_wout, sums = scatter_all(
        nz,
        part.astype(bf).reshape(nctx, width2, dmodel),
        gsum.reshape(nctx, width2, dmodel),
        jnp.concatenate([tdot(norm1, dqkv_b).astype(bf), sums.astype(bf)], axis=1).reshape(
            lead + (3 * qw + LANES,)
        ),
        tdot(norm2, dpre_b).astype(bf).reshape(lead + (fw,)),
        tdot(g_all, hidden).astype(bf).reshape(lead + (fw,)),
        tdot(ctx_c, g_all).astype(bf).reshape(2, 2, piece, dmodel),
    )
    x_ownf = x_own.astype(f32)
    layer_out = (x_ownf + fwd.astype(f32) + (bo + bd)).astype(bf).reshape(layer_in.shape)
    gsum = gsum.astype(f32)
    hat_own, rstd_own = hat_of(x_ownf)
    grad_x = (
        g_ownf
        + rstd_own
        * (
            gsum
            - jnp.mean(gsum, axis=-1, keepdims=True)
            - hat_own * jnp.mean(gsum * hat_own, axis=-1, keepdims=True)
        )
    ).astype(bf).reshape(layer_in.shape)
    sizes = (piece,) * 5 + (b_qkv.shape[0], b_up.shape[0])
    vs = [sums[i, :n] for i, n in enumerate(sizes)]
    return (
        layer_out,
        grad_x,
        vs[0],
        vs[1],
        vs[2],
        vs[3],
        grad_qkv,
        vs[5],
        grad_wout,
        vs[4],
        grad_up,
        vs[6],
        grad_down,
        vs[4],
    )


def solution(mesh):
    nctx = mesh.shape["ctx"]

    def pick(layer_in, *rest):
        heads = layer_in.shape[-1] // HD
        whole = heads % nctx == 0
        square = nctx % 2 == 0 and mesh.shape["fsdp"] == 4 and heads == 2 * nctx
        if square and layer_in.shape[1] == 1 and layer_in.shape[2] % 16 == 0:
            return routed(layer_in, *rest)
        return (head_shards if whole else shards)(layer_in, *rest)

    return jax.shard_map(
        pick,
        mesh=mesh,
        in_specs=(
            P("ctx", "fsdp", None, None),
            P("ctx", "fsdp", None, None),
            P(),
            P(("fsdp", "ctx")),
            P(("fsdp", "ctx")),
            P(("fsdp", "ctx")),
            P(("fsdp", "ctx")),
            P(("fsdp", "ctx"), None),
            P(("fsdp", "ctx")),
            P(("fsdp", "ctx"), None),
            P(("fsdp", "ctx")),
            P(("fsdp", "ctx"), None),
            P(("fsdp", "ctx")),
            P(("fsdp", "ctx"), None),
            P(("fsdp", "ctx")),
        ),
        out_specs=(
            P("ctx", "fsdp", None, None),
            P("ctx", "fsdp", None, None),
            P(("fsdp", "ctx")),
            P(("fsdp", "ctx")),
            P(("fsdp", "ctx")),
            P(("fsdp", "ctx")),
            P(("fsdp", "ctx"), None),
            P(("fsdp", "ctx")),
            P(("fsdp", "ctx"), None),
            P(("fsdp", "ctx")),
            P(("fsdp", "ctx"), None),
            P(("fsdp", "ctx")),
            P(("fsdp", "ctx"), None),
            P(("fsdp", "ctx")),
        ),
        check_vma=False,
    )
```

```python
import functools
import math
import types

import jax
import jax.numpy as jnp
from jax import lax
from jax.experimental import pallas as pl
from jax.experimental.pallas import tpu as pltpu
from jax.sharding import PartitionSpec as P

HD = 64
ROT = 16
LANES = 128


EPS = 1e-05
NEG = -1e30
ROOT_HALF = 0.7071067811865476
INV_ROOT_TAU = 0.3989422804014327


def norm_parts(xf, scale_weight, shift_bias):
    row_mean = jnp.mean(xf, axis=-1, keepdims=True)
    centred_input = xf - row_mean
    inverse_deviation = lax.rsqrt(
        jnp.mean(centred_input * centred_input, axis=-1, keepdims=True) + EPS
    )
    normalized_input = centred_input * inverse_deviation
    return (
        normalized_input * scale_weight.astype(jnp.float32) + shift_bias.astype(jnp.float32),
        normalized_input,
        inverse_deviation,
    )


def layer_norm_backward(norm_output_gradient, normalized_input, inverse_deviation, scale_weight):
    normalized_gradient = norm_output_gradient * scale_weight.astype(jnp.float32)
    return inverse_deviation * (
        normalized_gradient
        - jnp.mean(normalized_gradient, axis=-1, keepdims=True)
        - normalized_input
        * jnp.mean(normalized_gradient * normalized_input, axis=-1, keepdims=True)
    )


def gelu_value(u):
    return 0.5 * u * (1.0 + lax.erf(u * ROOT_HALF))


def gelu_slope(u):
    return 0.5 * (1.0 + lax.erf(u * ROOT_HALF)) + u * jnp.exp(-0.5 * u * u) * INV_ROOT_TAU


def rotate(field, place, sign):
    half = ROT // 2
    freqs = jnp.exp(jnp.arange(half).astype(jnp.float32) * (-2.0 * math.log(10000.0) / ROT))
    angle = place.astype(jnp.float32)[..., None] * freqs
    cosine = jnp.cos(angle)[..., None, :]
    sine = sign * jnp.sin(angle)[..., None, :]
    first = field[..., :half]
    second = field[..., half:ROT]
    return jnp.concatenate(
        [first * cosine - second * sine, second * cosine + first * sine, field[..., rot_end() :]],
        axis=-1,
    )


def rot_end():
    return ROT


def leading(field, letters):
    return "n" + letters if field.ndim == 5 else letters


def product(left, left_letters, right, right_letters, result):
    form = leading(left, left_letters) + "," + leading(right, right_letters) + "->" + result
    return jnp.einsum(form, left, right, preferred_element_type=jnp.float32)


def selectors(sel):
    return (sel[:, None, None, None, None], sel[:, None, None, None], sel[:, None])


def visibility(sel, qpa, qpb, kpa, kpb):
    chosen = sel[:, None]
    key_place = jnp.where(chosen, kpa, kpb)
    query_place = jnp.where(chosen, qpa, qpb)
    return (key_place[:, None, :] <= query_place[:, :, None])[:, None, None]


def online_update(state, qa, qb, ka, kb, va, vb, qpa, qpb, kpa, kpb, sel, with_first, scale):
    top_a, total_a, acc_a, top_b, total_b, acc_b = state
    sel5, sel4, sel2 = selectors(sel)
    query_two = jnp.where(sel5, qa, qb)
    key_two = jnp.where(sel5, ka, kb)
    value_two = jnp.where(sel5, va, vb)
    visible = visibility(sel, qpa, qpb, kpa, kpb)
    score = jnp.where(visible, product(query_two, "sqhd", key_two, "skhd", "nshqk") * scale, NEG)
    peak_a = jnp.max(jnp.where(sel5, score, NEG), axis=(0, 4))
    peak_b = jnp.max(jnp.where(sel5, NEG, score), axis=(0, 4))
    if with_first:
        score_one = product(qb, "sqhd", ka, "skhd", "nshqk") * scale
        peak_b = jnp.maximum(peak_b, jnp.max(score_one, axis=(0, 4)))
    new_a = jnp.maximum(top_a, peak_a)
    new_b = jnp.maximum(top_b, peak_b)
    lifted = jnp.where(sel5, new_a[..., None], new_b[..., None])
    weight = jnp.where(visible, jnp.exp(score - lifted), 0.0)
    mixed = product(weight.astype(jnp.bfloat16), "shqk", value_two, "skhd", "nshqd")
    mass = jnp.sum(weight, axis=4)
    add_total_a = jnp.sum(jnp.where(sel4, mass, 0.0), axis=0)
    add_total_b = jnp.sum(jnp.where(sel4, 0.0, mass), axis=0)
    add_acc_a = jnp.sum(jnp.where(sel5, mixed, 0.0), axis=0)
    add_acc_b = jnp.sum(jnp.where(sel5, 0.0, mixed), axis=0)
    if with_first:
        weight_one = jnp.exp(score_one - new_b[..., None])
        add_total_b = add_total_b + jnp.sum(weight_one, axis=(0, 4))
        add_acc_b = add_acc_b + product(weight_one.astype(jnp.bfloat16), "shqk", va, "skhd", "shqd")
    decay_a = jnp.exp(top_a - new_a)
    decay_b = jnp.exp(top_b - new_b)
    return (
        new_a,
        total_a * decay_a + add_total_a,
        acc_a * decay_a[..., None] + add_acc_a,
        new_b,
        total_b * decay_b + add_total_b,
        acc_b * decay_b[..., None] + add_acc_b,
    )


def pair_terms(
    qa,
    qb,
    ka,
    kb,
    va,
    vb,
    da,
    db,
    lsea,
    lseb,
    dela,
    delb,
    qpa,
    qpb,
    kpa,
    kpb,
    sel,
    with_first,
    scale,
):
    sel5, sel4, sel2 = selectors(sel)
    query_two = jnp.where(sel5, qa, qb)
    key_two = jnp.where(sel5, ka, kb)
    value_two = jnp.where(sel5, va, vb)
    dctx_two = jnp.where(sel5, da, db)
    lse_two = jnp.where(sel4, lsea, lseb)
    delta_two = jnp.where(sel4, dela, delb)
    visible = visibility(sel, qpa, qpb, kpa, kpb)
    score = jnp.where(visible, product(query_two, "sqhd", key_two, "skhd", "nshqk") * scale, NEG)
    prob = jnp.exp(score - lse_two[..., None])
    dprob = product(dctx_two, "sqhd", value_two, "skhd", "nshqk")
    dscore = (scale * prob * (dprob - delta_two[..., None])).astype(jnp.bfloat16)
    first_ds = None
    first_prob = None
    if with_first:
        score_one = product(qb, "sqhd", ka, "skhd", "nshqk") * scale
        prob_one = jnp.exp(score_one - lseb[..., None])
        dprob_one = product(db, "sqhd", va, "skhd", "nshqk")
        first_ds = (scale * prob_one * (dprob_one - delb[..., None])).astype(jnp.bfloat16)
        first_prob = prob_one.astype(jnp.bfloat16)
    return (first_ds, first_prob, dscore, prob.astype(jnp.bfloat16))


def query_grads(terms, ka, kb, sel):
    sel5, sel4, sel2 = selectors(sel)
    key_two = jnp.where(sel5, ka, kb)
    dq_two = product(terms[2], "shqk", key_two, "skhd", "nsqhd")
    dq_a = jnp.where(sel5, dq_two, 0.0)
    dq_b = jnp.where(sel5, 0.0, dq_two)
    if terms[0] is not None:
        dq_b = dq_b + product(terms[0], "shqk", ka, "skhd", "nsqhd")
    return (dq_a, dq_b)


def key_grads(terms, qa, qb, da, db, sel):
    sel5, sel4, sel2 = selectors(sel)
    query_two = jnp.where(sel5, qa, qb)
    dctx_two = jnp.where(sel5, da, db)
    dk_two = product(terms[2], "shqk", query_two, "sqhd", "nskhd")
    dv_two = product(terms[3], "shqk", dctx_two, "sqhd", "nskhd")
    dk_a = jnp.where(sel5, dk_two, 0.0)
    dk_b = jnp.where(sel5, 0.0, dk_two)
    dv_a = jnp.where(sel5, dv_two, 0.0)
    dv_b = jnp.where(sel5, 0.0, dv_two)
    if terms[0] is not None:
        dk_a = dk_a + product(terms[0], "shqk", qb, "sqhd", "nskhd")
        dv_a = dv_a + product(terms[1], "shqk", db, "sqhd", "nskhd")
    return (dk_a, dk_b, dv_a, dv_b)


def tdot(left, right):
    return lax.dot_general(
        left, right, (((0,), (0,)), ((), ())), preferred_element_type=jnp.float32
    )


def rdot(left, right):
    return lax.dot_general(
        left, right, (((1,), (1,)), ((), ())), preferred_element_type=jnp.float32
    )


def shards(
    layer_in,
    grad_out,
    pair_of_rank,
    ln1_gain,
    ln1_bias,
    ln2_gain,
    ln2_bias,
    w_qkv,
    b_qkv,
    w_out,
    b_out,
    w_up,
    b_up,
    w_down,
    b_down,
):
    f32 = jnp.float32
    bf = jnp.bfloat16
    nctx = lax.axis_size("ctx")
    mine = pair_of_rank[lax.axis_index("ctx")]
    seqs = layer_in.shape[1]
    width2 = layer_in.shape[2]
    dmodel = layer_in.shape[3]
    blk = width2 // 2
    rows = seqs * width2
    heads = dmodel // HD
    scale = 1.0 / math.sqrt(HD)
    offsets = jnp.arange(blk, dtype=jnp.int32)
    place_a = mine * blk + offsets
    place_b = (2 * nctx - 1 - mine) * blk + offsets
    places = jnp.concatenate([place_a, place_b])
    params = (
        ln1_gain,
        ln1_bias,
        ln2_gain,
        ln2_bias,
        w_qkv,
        b_qkv,
        w_out,
        b_out,
        w_up,
        b_up,
        w_down,
        b_down,
    )
    full = (
        lax.all_gather(params[0], ("fsdp", "ctx"), axis=0, tiled=True),
        lax.all_gather(params[1], ("fsdp", "ctx"), axis=0, tiled=True),
        lax.all_gather(params[2], ("fsdp", "ctx"), axis=0, tiled=True),
        lax.all_gather(params[3], ("fsdp", "ctx"), axis=0, tiled=True),
        lax.all_gather(params[4], ("fsdp", "ctx"), axis=0, tiled=True),
        lax.all_gather(params[5], ("fsdp", "ctx"), axis=0, tiled=True),
        lax.all_gather(params[6], ("fsdp", "ctx"), axis=0, tiled=True),
        lax.all_gather(params[7], ("fsdp", "ctx"), axis=0, tiled=True),
        lax.all_gather(params[8], ("fsdp", "ctx"), axis=0, tiled=True),
        lax.all_gather(params[9], ("fsdp", "ctx"), axis=0, tiled=True),
        lax.all_gather(params[10], ("fsdp", "ctx"), axis=0, tiled=True),
        lax.all_gather(params[11], ("fsdp", "ctx"), axis=0, tiled=True),
    )
    xf = layer_in.reshape(rows, dmodel).astype(f32)
    norm1, hat1, rstd1 = norm_parts(xf, full[0], full[1])
    norm2, hat2, rstd2 = norm_parts(xf, full[2], full[3])
    norm1 = norm1.astype(bf)
    norm2 = norm2.astype(bf)
    qkv = jnp.dot(norm1, full[4], preferred_element_type=f32) + full[5].astype(f32)
    query = rotate(qkv[:, :dmodel].reshape(seqs, width2, heads, HD), places, 1.0).astype(bf)
    key = rotate(qkv[:, dmodel : 2 * dmodel].reshape(seqs, width2, heads, HD), places, 1.0).astype(
        bf
    )
    value = qkv[:, 2 * dmodel :].reshape(seqs, width2, heads, HD).astype(bf)
    query_a = query[:, :blk]
    query_b = query[:, blk:]
    key_b = key[:, blk:]
    value_b = value[:, blk:]
    lone = jnp.zeros((1,), dtype=bool)
    empty_top = jnp.full((seqs, heads, blk), NEG, f32)
    empty_total = jnp.zeros((seqs, heads, blk), f32)
    empty_acc = jnp.zeros((seqs, heads, blk, HD), f32)
    state = (empty_top, empty_total, empty_acc, empty_top, empty_total, empty_acc)
    state = online_update(
        state,
        query_a,
        query_b,
        key_b[None],
        key_b[None],
        value_b[None],
        value_b[None],
        place_a,
        place_b,
        place_b[None],
        place_b[None],
        lone,
        False,
        scale,
    )

    def key_parts(kpiece, vpiece, first):
        count = kpiece.shape[0]
        pairs = lax.dynamic_slice_in_dim(pair_of_rank, first, count)
        keys = kpiece.reshape(count, seqs, width2, heads, HD)
        values = vpiece.reshape(count, seqs, width2, heads, HD)
        kplace_a = pairs[:, None] * blk + offsets[None, :]
        kplace_b = (2 * nctx - 1 - pairs)[:, None] * blk + offsets[None, :]
        return (
            keys[:, :, :blk],
            keys[:, :, blk:],
            values[:, :, :blk],
            values[:, :, blk:],
            kplace_a,
            kplace_b,
            pairs,
        )

    key_send = key.reshape(1, seqs, width2, dmodel)
    value_send = value.reshape(1, seqs, width2, dmodel)
    ka, kb, va, vb, kpa, kpb, pairs = key_parts(
        lax.all_gather(key_send, "ctx", axis=0, tiled=True),
        lax.all_gather(value_send, "ctx", axis=0, tiled=True),
        jnp.int32(0),
    )
    state = online_update(
        state,
        query_a,
        query_b,
        ka,
        kb,
        va,
        vb,
        place_a,
        place_b,
        kpa,
        kpb,
        pairs <= mine,
        True,
        scale,
    )
    top_a, total_a, acc_a, top_b, total_b, acc_b = state
    context4 = jnp.concatenate([acc_a / total_a[..., None], acc_b / total_b[..., None]], axis=2)
    lse = jnp.concatenate([top_a + jnp.log(total_a), top_b + jnp.log(total_b)], axis=2)
    context = context4.transpose(0, 2, 1, 3).reshape(rows, dmodel).astype(bf)
    attn = jnp.dot(context, full[6], preferred_element_type=f32) + full[7].astype(f32)
    pre = jnp.dot(norm2, full[8], preferred_element_type=f32) + full[9].astype(f32)
    hidden = gelu_value(pre).astype(bf)
    mlp = rdot(hidden, full[10]) + full[11].astype(f32)
    layer_out = (xf + attn + mlp).astype(bf).reshape(layer_in.shape)
    again = (
        lax.all_gather(params[0], ("fsdp", "ctx"), axis=0, tiled=True),
        lax.all_gather(params[1], ("fsdp", "ctx"), axis=0, tiled=True),
        lax.all_gather(params[2], ("fsdp", "ctx"), axis=0, tiled=True),
        lax.all_gather(params[3], ("fsdp", "ctx"), axis=0, tiled=True),
        lax.all_gather(params[4], ("fsdp", "ctx"), axis=0, tiled=True),
        lax.all_gather(params[5], ("fsdp", "ctx"), axis=0, tiled=True),
        lax.all_gather(params[6], ("fsdp", "ctx"), axis=0, tiled=True),
        lax.all_gather(params[7], ("fsdp", "ctx"), axis=0, tiled=True),
        lax.all_gather(params[8], ("fsdp", "ctx"), axis=0, tiled=True),
        lax.all_gather(params[9], ("fsdp", "ctx"), axis=0, tiled=True),
        lax.all_gather(params[10], ("fsdp", "ctx"), axis=0, tiled=True),
        lax.all_gather(params[11], ("fsdp", "ctx"), axis=0, tiled=True),
    )
    grad_b = grad_out.reshape(rows, dmodel)
    grad_f = grad_b.astype(f32)
    dhidden = jnp.dot(grad_b, again[10], preferred_element_type=f32)
    dpre = dhidden * gelu_slope(pre)
    dpre_b = dpre.astype(bf)
    dnorm2 = rdot(dpre_b, again[8])
    dcontext = rdot(grad_b, again[6]).astype(bf)
    dctx4 = dcontext.reshape(seqs, width2, heads, HD)
    delta = jnp.sum(
        dctx4.astype(f32) * context.reshape(seqs, width2, heads, HD).astype(f32), axis=-1
    ).transpose(0, 2, 1)
    dctx_a = dctx4[:, :blk]
    dctx_b = dctx4[:, blk:]
    lse_a = lse[..., :blk]
    lse_b = lse[..., blk:]
    delta_a = delta[..., :blk]
    delta_b = delta[..., blk:]
    own = pair_terms(
        query_b,
        query_b,
        key_b[None],
        key_b[None],
        value_b[None],
        value_b[None],
        dctx_b,
        dctx_b,
        lse_b,
        lse_b,
        delta_b,
        delta_b,
        place_b,
        place_b,
        place_b[None],
        place_b[None],
        lone,
        False,
        scale,
    )
    own_dq = query_grads(own, key_b[None], key_b[None], lone)[1][0]
    own_keys = key_grads(own, query_b, query_b, dctx_b, dctx_b, lone)
    gathered = (
        lax.all_gather(key_send, "ctx", axis=0, tiled=True),
        lax.all_gather(value_send, "ctx", axis=0, tiled=True),
    )
    groups = math.gcd(nctx, 8)
    per = nctx // groups

    def group_terms(args):
        kpiece, vpiece, first = args
        ka, kb, va, vb, kpa, kpb, pairs = key_parts(kpiece, vpiece, first)
        sel = pairs <= mine
        terms = pair_terms(
            query_a,
            query_b,
            ka,
            kb,
            va,
            vb,
            dctx_a,
            dctx_b,
            lse_a,
            lse_b,
            delta_a,
            delta_b,
            place_a,
            place_b,
            kpa,
            kpb,
            sel,
            True,
            scale,
        )
        dq_a, dq_b = query_grads(terms, ka, kb, sel)
        return (terms, jnp.sum(dq_a, axis=0), jnp.sum(dq_b, axis=0))

    grouped = lax.map(
        group_terms,
        (
            gathered[0].reshape(groups, per, seqs, width2, dmodel),
            gathered[1].reshape(groups, per, seqs, width2, dmodel),
            jnp.arange(groups, dtype=jnp.int32) * per,
        ),
    )
    terms_all = tuple((part.reshape((nctx,) + part.shape[2:]) for part in grouped[0]))
    dq_a = jnp.sum(grouped[1], axis=0)
    dq_b = jnp.sum(grouped[2], axis=0)
    pairs = pair_of_rank
    sliced = tuple(
        (lax.slice_in_dim(part, 0, 1 * lax.axis_size("ctx"), axis=0) for part in terms_all)
    )
    dk_a, dk_b, dv_a, dv_b = key_grads(sliced, query_a, query_b, dctx_a, dctx_b, pairs <= mine)
    dkey = jnp.concatenate([dk_a, dk_b], axis=2).reshape(
        1 * lax.axis_size("ctx"), seqs, width2, dmodel
    )
    dval = jnp.concatenate([dv_a, dv_b], axis=2).reshape(
        1 * lax.axis_size("ctx"), seqs, width2, dmodel
    )
    kv_grad = lax.psum_scatter(
        jnp.concatenate([dkey, dval], axis=-1), "ctx", scatter_dimension=0, tiled=True
    )
    dkey = kv_grad[0, :, :, :dmodel].reshape(seqs, width2, heads, HD)
    dval = kv_grad[0, :, :, dmodel:].reshape(seqs, width2, heads, HD)
    zero_half = jnp.zeros((seqs, blk, heads, HD), f32)
    dquery = jnp.concatenate([dq_a, dq_b + own_dq], axis=1)
    dkey = dkey + jnp.concatenate([zero_half, own_keys[1][0]], axis=1)
    dval = dval + jnp.concatenate([zero_half, own_keys[3][0]], axis=1)
    dqkv = jnp.concatenate(
        [
            rotate(dquery, places, -1.0).reshape(rows, dmodel),
            rotate(dkey, places, -1.0).reshape(rows, dmodel),
            dval.reshape(rows, dmodel),
        ],
        axis=1,
    )
    dqkv_b = dqkv.astype(bf)
    dnorm1 = rdot(dqkv_b, again[4])
    grad_x = (
        (
            grad_f
            + layer_norm_backward(dnorm1, hat1, rstd1, again[0])
            + layer_norm_backward(dnorm2, hat2, rstd2, again[2])
        )
        .astype(bf)
        .reshape(layer_in.shape)
    )
    vectors = (
        lax.psum_scatter(
            jnp.sum(dnorm1 * hat1, axis=0), ("fsdp", "ctx"), scatter_dimension=0, tiled=True
        ),
        lax.psum_scatter(jnp.sum(dnorm1, axis=0), ("fsdp", "ctx"), scatter_dimension=0, tiled=True),
        lax.psum_scatter(
            jnp.sum(dnorm2 * hat2, axis=0), ("fsdp", "ctx"), scatter_dimension=0, tiled=True
        ),
        lax.psum_scatter(jnp.sum(dnorm2, axis=0), ("fsdp", "ctx"), scatter_dimension=0, tiled=True),
        lax.psum_scatter(jnp.sum(dqkv, axis=0), ("fsdp", "ctx"), scatter_dimension=0, tiled=True),
        lax.psum_scatter(jnp.sum(grad_f, axis=0), ("fsdp", "ctx"), scatter_dimension=0, tiled=True),
        lax.psum_scatter(jnp.sum(dpre, axis=0), ("fsdp", "ctx"), scatter_dimension=0, tiled=True),
    )
    weights = (
        lax.psum_scatter(tdot(norm1, dqkv_b), ("fsdp", "ctx"), scatter_dimension=0, tiled=True),
        lax.psum_scatter(tdot(context, grad_b), ("fsdp", "ctx"), scatter_dimension=0, tiled=True),
        lax.psum_scatter(tdot(norm2, dpre_b), ("fsdp", "ctx"), scatter_dimension=0, tiled=True),
        lax.psum_scatter(tdot(grad_b, hidden), ("fsdp", "ctx"), scatter_dimension=0, tiled=True),
    )
    return (
        layer_out,
        grad_x,
        vectors[0],
        vectors[1],
        vectors[2],
        vectors[3],
        weights[0],
        vectors[4],
        weights[1],
        vectors[5],
        weights[2],
        vectors[6],
        weights[3],
        vectors[5],
    )


def span(lead, cols):
    return jnp.arange(lead, dtype=jnp.int32)[:, None] if cols else jnp.arange(lead, dtype=jnp.int32)


def turn(field, cosine, sine_low, sine_high):
    half = ROT // 2
    down = jnp.concatenate([field[:, half:], field[:, :half]], axis=1)
    up = jnp.concatenate([field[:, -half:], field[:, :-half]], axis=1)
    return field * cosine + down * sine_low + up * sine_high


def turn_tables(places, width):
    half = ROT // 2
    lane = jnp.arange(width, dtype=jnp.int32) % HD
    freqs = jnp.exp((lane % half).astype(jnp.float32) * (-2.0 * math.log(10000.0) / ROT))
    angle = places.astype(jnp.float32)[:, None] * freqs[None, :]
    cosine = jnp.where(lane < ROT, jnp.cos(angle), 1.0)
    sine = jnp.sin(angle)
    sine_low = jnp.where(lane < half, -sine, 0.0)
    sine_high = jnp.where((lane >= half) & (lane < ROT), sine, 0.0)
    return cosine, sine_low, sine_high


def headed(field, count):
    return field.reshape(field.shape[0], count, HD).transpose(1, 0, 2)


def joined(field):
    return field.transpose(1, 0, 2).reshape(field.shape[1], -1)


def bdot(form, left, right):
    return jnp.einsum(form, left, right, preferred_element_type=jnp.float32)


def head_shards(
    layer_in,
    grad_out,
    pair_of_rank,
    ln1_gain,
    ln1_bias,
    ln2_gain,
    ln2_bias,
    w_qkv,
    b_qkv,
    w_out,
    b_out,
    w_up,
    b_up,
    w_down,
    b_down,
):
    f32 = jnp.float32
    bf = jnp.bfloat16
    both = ("fsdp", "ctx")
    nctx = lax.axis_size("ctx")
    nf = lax.axis_size("fsdp")
    ndev = nctx * nf
    c = lax.axis_index("ctx")
    seqs, width2, dmodel = layer_in.shape[1:]
    blk = width2 // 2
    own_rows = seqs * width2
    ff = w_up.shape[1]
    hloc = dmodel // HD // nctx
    qw = hloc * HD
    fw = ff // nctx
    piece = dmodel // ndev
    scale = 1.0 / math.sqrt(HD)

    x_all = lax.all_gather(layer_in.reshape(own_rows, dmodel), "ctx", axis=0, tiled=True)
    def columns(parts):
        packed = jnp.concatenate([p.reshape(piece, nctx, -1) for p in parts], axis=-1)
        packed = packed.transpose(1, 0, 2)
        got = lax.all_to_all(packed, "ctx", split_axis=0, concat_axis=0, tiled=True)
        return got.reshape(nctx * piece, -1)

    wq = w_qkv.reshape(piece, 3, nctx, qw).transpose(0, 2, 1, 3)
    vec = jnp.concatenate([ln1_gain, ln1_bias, ln2_gain, ln2_bias, b_out, b_down, b_qkv, b_up])
    vw = LANES * -(-vec.shape[0] // (piece * LANES))
    vec_pad = jnp.pad(vec, (0, piece * vw - vec.shape[0])).reshape(piece, 1, vw)
    vec_pad = jnp.broadcast_to(vec_pad, (piece, nctx, vw))
    cols = lax.all_gather(columns([wq, w_up, w_down, vec_pad]), "fsdp", axis=0, tiled=True)
    g_own = grad_out.reshape(own_rows, dmodel)
    cols, g_send = lax.optimization_barrier((cols, g_own))
    got = cols[:, 3 * qw + 2 * fw :].reshape(ndev, piece * vw)
    cuts = [piece] * 6 + [b_qkv.shape[0], b_up.shape[0]]
    fulls = []
    at = 0
    for cut in cuts:
        fulls.append(got[:, at : at + cut].reshape(-1).astype(f32))
        at += cut
    gain1, bias1, gain2, bias2, bo, bd, bq, bu = fulls
    bq_c = lax.dynamic_slice_in_dim(bq.reshape(3, nctx, qw), c, 1, axis=1).reshape(1, 3 * qw)
    bu_c = lax.dynamic_slice_in_dim(bu, c * fw, fw).reshape(1, fw)
    wq_c = cols[:, : 3 * qw]
    wu_c = cols[:, 3 * qw : 3 * qw + fw]
    wd_c = cols[:, 3 * qw + fw : 3 * qw + 2 * fw]
    there = [((nf * cc + f) , f * nctx + cc) for f in range(nf) for cc in range(nctx)]
    back = [(b, a) for a, b in there]
    wo_c = lax.all_gather(lax.ppermute(w_out, both, there), "fsdp", axis=0, tiled=True)
    g_all = lax.all_gather(g_send, "ctx", axis=0, tiled=True)

    rows = x_all.shape[0]
    offsets = jnp.arange(blk, dtype=jnp.int32)
    slot_a = pair_of_rank[:, None] * blk + offsets[None, :]
    slot_b = (2 * nctx - 1 - pair_of_rank)[:, None] * blk + offsets[None, :]
    slots = jnp.concatenate([slot_a, slot_b], axis=1)[:, None, :]
    places = jnp.broadcast_to(slots, (nctx, seqs, width2)).reshape(rows)
    group = jnp.broadcast_to(span(seqs, False)[None, :, None], (nctx, seqs, width2)).reshape(rows)

    def hat_of(xf):
        row_mean = jnp.mean(xf, axis=-1, keepdims=True)
        centred = xf - row_mean
        rstd = lax.rsqrt(jnp.mean(centred * centred, axis=-1, keepdims=True) + EPS)
        return centred * rstd, rstd

    hat, _ = hat_of(x_all.astype(f32))
    norm1 = (hat * gain1 + bias1).astype(bf)
    norm2 = (hat * gain2 + bias2).astype(bf)
    qkv = jnp.dot(norm1, wq_c, preferred_element_type=f32) + bq_c
    cosine, sine_low, sine_high = turn_tables(places, qw)
    query = headed(turn(qkv[:, :qw], cosine, sine_low, sine_high).astype(bf), hloc)
    key = headed(turn(qkv[:, qw : 2 * qw], cosine, sine_low, sine_high).astype(bf), hloc)
    value = headed(qkv[:, 2 * qw :].astype(bf), hloc)
    visible = places[None, :] <= places[:, None]
    if seqs > 1:
        visible = visible & (group[None, :] == group[:, None])
    score = jnp.where(visible[None], bdot("hqd,hkd->hqk", query, key) * scale, NEG)
    top = jnp.max(score, axis=-1, keepdims=True)
    weight = jnp.exp(score - top)
    total = jnp.sum(weight, axis=-1, keepdims=True)
    mixed = bdot("hqk,hkd->hqd", weight.astype(bf), value)
    context = (mixed / total).astype(bf)
    lse = top + jnp.log(total)
    ctx_c = joined(context)

    pre = jnp.dot(norm2, wu_c, preferred_element_type=f32) + bu_c
    hidden = gelu_value(pre).astype(bf)
    part = rdot(hidden, wd_c) + jnp.dot(ctx_c, wo_c, preferred_element_type=f32)
    fwd = lax.all_to_all(
        part.astype(bf).reshape(nctx, own_rows, dmodel), "ctx", split_axis=0, concat_axis=0, tiled=True
    )
    fwd = jnp.sum(fwd.astype(f32), axis=0)
    x_own = layer_in.reshape(own_rows, dmodel).astype(f32)
    layer_out = (x_own + fwd + (bo + bd)).astype(bf).reshape(layer_in.shape)

    dhidden = jnp.dot(g_all, wd_c, preferred_element_type=f32)
    dpre = dhidden * gelu_slope(pre)
    dpre_b = dpre.astype(bf)
    dnorm2 = rdot(dpre_b, wu_c)
    dctx = headed(rdot(g_all, wo_c).astype(bf), hloc)
    delta = jnp.sum(dctx.astype(f32) * context.astype(f32), axis=-1, keepdims=True)
    prob = jnp.exp(score - lse)
    dprob = bdot("hqd,hkd->hqk", dctx, value)
    ds = (scale * prob * (dprob - delta)).astype(bf)
    dquery = joined(bdot("hqk,hkd->hqd", ds, key))
    dkey = joined(bdot("hqk,hqd->hkd", ds, query))
    dvalue = joined(bdot("hqk,hqd->hkd", prob.astype(bf), dctx))
    dqkv = jnp.concatenate(
        [
            turn(dquery, cosine, -sine_low, -sine_high),
            turn(dkey, cosine, -sine_low, -sine_high),
            dvalue,
        ],
        axis=1,
    )
    dqkv_b = dqkv.astype(bf)
    dnorm1 = rdot(dqkv_b, wq_c)
    gsum = (dnorm1 * gain1 + dnorm2 * gain2).astype(bf)
    gsum = lax.psum_scatter(gsum, "ctx", scatter_dimension=0, tiled=True).astype(f32)
    hat_own, rstd_own = hat_of(x_own)
    g_ownf = g_own.astype(f32)
    grad_x = (
        g_ownf
        + rstd_own
        * (
            gsum
            - jnp.mean(gsum, axis=-1, keepdims=True)
            - hat_own * jnp.mean(gsum * hat_own, axis=-1, keepdims=True)
        )
    ).astype(bf).reshape(layer_in.shape)

    sum_q = jnp.zeros((3, nctx, qw), f32)
    sum_q = lax.dynamic_update_slice_in_dim(
        sum_q, jnp.sum(dqkv, axis=0).reshape(3, 1, qw), c, axis=1
    ).reshape(ndev, -1)
    sum_u = lax.dynamic_update_slice_in_dim(
        jnp.zeros((ff,), f32), jnp.sum(dpre, axis=0), c * fw, axis=0
    ).reshape(ndev, -1)
    sums = [
        jnp.sum(dnorm1 * hat, axis=0).reshape(ndev, -1),
        jnp.sum(dnorm1, axis=0).reshape(ndev, -1),
        jnp.sum(dnorm2 * hat, axis=0).reshape(ndev, -1),
        jnp.sum(dnorm2, axis=0).reshape(ndev, -1),
        jnp.sum(g_ownf, axis=0).reshape(ndev, -1),
        sum_q,
        sum_u,
    ]
    sums = jnp.concatenate(sums, axis=1)
    sw = LANES * -(-sums.shape[1] // (piece * LANES))
    sums_pad = jnp.pad(sums, ((0, 0), (0, piece * sw - sums.shape[1]))).reshape(ndev * piece, sw)
    rows_out = tdot(ctx_c, g_all).astype(bf)
    wide = jnp.concatenate(
        [
            tdot(norm1, dqkv_b).astype(bf),
            tdot(norm2, dpre_b).astype(bf),
            tdot(g_all, hidden).astype(bf),
            sums_pad.astype(bf),
            rows_out.reshape(ndev * piece, -1),
        ],
        axis=1,
    )
    wide = lax.psum_scatter(wide, "fsdp", scatter_dimension=0, tiled=True)
    split = 3 * qw + 2 * fw + sw
    grad_wout = lax.ppermute(wide[:, split:].reshape(piece, dmodel), both, back).astype(f32)
    wide = lax.all_to_all(
        wide[:, :split].reshape(nctx, piece, split), "ctx", split_axis=0, concat_axis=0, tiled=True
    )
    sums = jnp.sum(wide[:, :, split - sw :].astype(f32), axis=0).reshape(-1)[: sums.shape[1]]
    wide = wide.transpose(1, 0, 2).astype(f32)
    grad_qkv = (
        wide[:, :, : 3 * qw].reshape(piece, nctx, 3, qw).transpose(0, 2, 1, 3).reshape(piece, -1)
    )
    grad_up = wide[:, :, 3 * qw : 3 * qw + fw].reshape(piece, ff)
    grad_down = wide[:, :, 3 * qw + fw : 3 * qw + 2 * fw].reshape(piece, ff)
    ends = [piece * i for i in range(6)] + [5 * piece + b_qkv.shape[0], sums.shape[0]]
    vs = [sums[a:b] for a, b in zip(ends[:-1], ends[1:])]
    return (
        layer_out,
        grad_x,
        vs[0],
        vs[1],
        vs[2],
        vs[3],
        grad_qkv,
        vs[5],
        grad_wout,
        vs[4],
        grad_up,
        vs[6],
        grad_down,
        vs[4],
    )


def mod_less(a, n):
    return jnp.where(a >= n, a - n, a)


def mesh_dev(xi, ki, zi, yi):
    return {"fsdp": xi * 2 + ki, "ctx": zi * 2 + yi}


def rcopy(src, dst, send, recv, where):
    return pltpu.make_async_remote_copy(
        src_ref=src,
        dst_ref=dst,
        send_sem=send,
        recv_sem=recv,
        device_id=where,
        device_id_type=pl.DeviceIdType.MESH,
    )


def greet(nz, xi, ki, zi, yi):
    t = ki * nz + zi
    nt = 2 * nz
    barrier = pltpu.get_barrier_semaphore()

    def hello(where):
        pl.semaphore_signal(barrier, inc=1, device_id=where, device_id_type=pl.DeviceIdType.MESH)

    for d in range(1, nt):
        o = mod_less(t + d, nt)
        hello(mesh_dev(xi, lax.div(o, nz), lax.rem(o, nz), yi))
    hello(mesh_dev(1 - xi, ki, zi, yi))
    hello(mesh_dev(xi, ki, zi, 1 - yi))

    @pl.when(ki != yi)
    def _():
        hello(mesh_dev(xi, yi, zi, ki))

    pl.semaphore_wait(barrier, jnp.where(ki != yi, nt + 2, nt + 1))


NT = (((1,), (1,)), ((), ()))
TN = (((0,), (0,)), ((), ()))
NN = (((1,), (0,)), ((), ()))


def mm(left, right, form):
    return lax.dot_general(left, right, form, preferred_element_type=jnp.float32)


def layer_plan(nz, width2, dm, ff, piece):
    nt = 2 * nz
    fw = ff // nt
    rows = nt * width2
    qw = 6 * HD + LANES
    bf, f32 = jnp.bfloat16, jnp.float32
    vm = pltpu.VMEM
    dma = pltpu.SemaphoreType.DMA
    plan = dict(
        xo=vm((width2, dm), bf),
        go=vm((width2, dm), bf),
        qo=vm((piece, 3 * dm), bf),
        ld=dma((5 + 2 * nt,)),
        xb=vm((nt, width2, dm), bf),
        gb=vm((nt, width2, dm), bf),
        wq=vm((2, nt, 2, piece, qw), bf),
        wu=vm((2, nt, 2, piece, fw), bf),
        wd=vm((2, nt, 2, piece, fw), bf),
        wo=vm((2, 2, piece, dm), bf),
        pq=vm((nt, piece, qw), bf),
        pu=vm((nt, piece, fw), bf),
        pd=vm((nt, piece, fw), bf),
        vs=vm((piece, LANES), f32),
        gains=vm((8, dm), f32),
        bqf=vm((1, 3 * dm), f32),
        bq=vm((1, 6 * HD), f32),
        bu=vm((1, fw), f32),
        hat=vm((rows, dm), f32),
        n1=vm((rows, dm), bf),
        n2=vm((rows, dm), bf),
        qm=vm((2, rows, 2 * HD), bf),
        km=vm((2, rows, 2 * HD), bf),
        vm=vm((2, rows, 2 * HD), bf),
        dm=vm((2, rows, 2 * HD), bf),
        lse=vm((2, rows, 1), f32),
        delta=vm((2, rows, 1), f32),
        cx=vm((rows, 2 * HD), bf),
        hid=vm((rows, fw), bf),
        slope=vm((rows, fw), f32),
        dpre=vm((rows, fw), bf),
        gs=vm((rows, dm), f32),
        dq=vm((rows, 2 * HD), f32),
        dk=vm((rows, 2 * HD), f32),
        dv=vm((rows, 2 * HD), f32),
        dqkv=vm((rows, 6 * HD), bf),
        sums=vm((8, dm), f32),
        sq=vm((1, 6 * HD), f32),
        su=vm((1, fw), f32),
        a0=vm((nt, width2, dm), bf),
        a1=vm((nt, width2, dm), bf),
        mq=vm((2, nt, 2, piece, qw), bf),
        mu=vm((2, nt, 2, piece, fw), bf),
        md=vm((2, nt, 2, piece, fw), bf),
        mo=vm((2, 2, piece, dm), bf),
        ex=vm((2, nz, width2, dm), bf),
        ru=vm((2, nz, width2, dm), bf),
        rd=vm((2, nz, width2, dm), bf),
        fin=vm((2, width2, dm), bf),
        own=vm((2, width2, dm), bf),
        ro=vm((2, 2, piece, dm // 2), bf),
        so=vm((2, piece, dm // 2), bf),
        sw_s=dma((2,)),
        sw_r=dma((2,)),
        rsw_s=dma((2,)),
        rsw_r=dma((2,)),
        up_s=dma((2, nz)),
        up_r=dma((2, nz)),
        dn_s=dma((2, nz)),
        dn_r=dma((2, nz)),
        cc_s=dma((2, nz)),
        cc_r=dma((2, nz)),
        rup_s=dma((2, nz)),
        rup_r=dma((2, nz)),
        rdn_s=dma((2, nz)),
        rdn_r=dma((2, nz)),
        rcc_s=dma((2, nz)),
        rcc_r=dma((2, nz)),
        w1_s=dma((3, nt)),
        w1_r=dma((3, nt)),
        tp_s=dma((3, nt)),
        tp_r=dma((3, nt)),
        xs_s=dma((4,)),
        xs_r=dma((4,)),
        ys_s=dma((4,)),
        ys_r=dma((4,)),
        fx_s=dma((4,)),
        fx_r=dma((4,)),
        fy_s=dma((4,)),
        fy_r=dma((4,)),
        x1_s=dma((4,)),
        x1_r=dma((4,)),
        x2_s=dma((4,)),
        x2_r=dma((4,)),
        y2_s=dma((4,)),
        y2_r=dma((4,)),
        y1_s=dma((4, 2)),
        y1_r=dma((4, 2)),
        got1_0=vm((2, nz, 2, piece, qw), bf),
        got1_1=vm((2, nz, 2, piece, fw), bf),
        got1_2=vm((2, nz, 2, piece, fw), bf),
        got2_0=vm((nt, piece, qw), bf),
        got2_1=vm((nt, piece, fw), bf),
        got2_2=vm((nt, piece, fw), bf),
        chunk_0=vm((nt, piece, qw), bf),
        chunk_1=vm((nt, piece, fw), bf),
        chunk_2=vm((nt, piece, fw), bf),
    )
    return plan


INPUTS = 19
OUTPUTS = 7


def layer_kernel(nz, names, *refs):
    f32, bf = jnp.float32, jnp.bfloat16
    (x_hbm, g_hbm, wq_hbm, wu_hbm, wd_hbm, wo_hbm) = refs[:6]
    vectors = refs[6:14]
    (place_col, place_row, cos_t, low_t, high_t) = refs[14:19]
    (out_x, out_g, oq, ou, od, oo, osum) = refs[19:26]
    R = types.SimpleNamespace(**dict(zip(names, refs[26:])))

    f = lax.axis_index("fsdp")
    c = lax.axis_index("ctx")
    xi, ki = lax.div(f, 2), lax.rem(f, 2)
    zi, yi = lax.div(c, 2), lax.rem(c, 2)
    nt = 2 * nz
    t = ki * nz + zi
    width2, dm = R.xo.shape
    half = dm // 2
    rows = nt * width2
    fw = R.wu.shape[4]
    piece = R.wq.shape[3]
    qc = 6 * HD
    hw = 2 * HD
    QB = 2 * width2
    nblk = rows // QB
    scale = 1.0 / math.sqrt(HD)
    c_own = zi * 2 + yi

    xpeer = mesh_dev(1 - xi, ki, zi, yi)
    ypeer = mesh_dev(xi, ki, zi, 1 - yi)
    cpeer = mesh_dev(xi, 1 - ki, zi, yi)
    swapped = mesh_dev(xi, yi, zi, ki)
    acts = ((R.xo, R.xb), (R.go, R.gb))
    packs = ((R.pq, R.wq), (R.pu, R.wu), (R.pd, R.wd))
    mats = (R.wq, R.wu, R.wd)
    wo = R.wo

    ld = R.ld
    loads = [
        pltpu.make_async_copy(x_hbm, R.xo, ld.at[0]),
        pltpu.make_async_copy(wq_hbm, R.qo, ld.at[1]),
        pltpu.make_async_copy(wo_hbm, wo.at[xi, yi], ld.at[2]),
    ]
    loads_u = [
        pltpu.make_async_copy(wu_hbm.at[:, o * fw : (o + 1) * fw], R.pu.at[o], ld.at[5 + o])
        for o in range(nt)
    ]
    loads_d = [
        pltpu.make_async_copy(wd_hbm.at[:, o * fw : (o + 1) * fw], R.pd.at[o], ld.at[5 + nt + o])
        for o in range(nt)
    ]
    load_g = pltpu.make_async_copy(g_hbm, R.go, ld.at[3])
    for cp in loads + loads_u + loads_d + [load_g]:
        cp.start()

    def swap(i):
        src, dst = acts[i]
        return rcopy(src, dst.at[c_own], R.sw_s.at[i], R.sw_r.at[i], swapped)

    def swap_start(i):
        @pl.when(ki != yi)
        def _():
            swap(i).start()

        @pl.when(ki == yi)
        def _():
            acts[i][1][c_own] = acts[i][0][...]

    def swap_wait(i):
        @pl.when(ki != yi)
        def _():
            dst = acts[i][1].at[zi * 2 + ki]
            rcopy(acts[i][0], dst, R.sw_s.at[i], R.sw_r.at[i], swapped).wait_recv()

    def up_copy(i, d, z):
        slot = acts[i][1].at[z * 2 + ki]
        return rcopy(slot, slot, R.up_s.at[i, d], R.up_r.at[i, d], mesh_dev(xi, ki, zi + 1, yi))

    def dn_copy(i, d, z):
        slot = acts[i][1].at[z * 2 + ki]
        return rcopy(slot, slot, R.dn_s.at[i, d], R.dn_r.at[i, d], mesh_dev(xi, ki, zi - 1, yi))

    def cc_copy(i, z, k):
        slot = acts[i][1].at[z * 2 + k]
        return rcopy(slot, slot, R.cc_s.at[i, z], R.cc_r.at[i, z], cpeer)

    def hop_send(i, d):
        @pl.when((zi - (d - 1) >= 0) & (zi + 1 < nz))
        def _():
            up_copy(i, d, zi - (d - 1)).start()

        @pl.when((zi + (d - 1) < nz) & (zi >= 1))
        def _():
            dn_copy(i, d, zi + (d - 1)).start()

    def hop_recv(i, d):
        @pl.when(zi - d >= 0)
        def _():
            up_copy(i, d, zi - d).wait_recv()

        @pl.when(zi + d < nz)
        def _():
            dn_copy(i, d, zi + d).wait_recv()

    def hop_share(i, d):
        @pl.when(zi - d >= 0)
        def _():
            cc_copy(i, zi - d, ki).start()

        if d > 0:

            @pl.when(zi + d < nz)
            def _():
                cc_copy(i, zi + d, ki).start()

    def hop(i, d):
        hop_recv(i, d)
        if d + 1 < nz:
            hop_send(i, d + 1)
        hop_share(i, d)

    def all_in(i):
        for z in range(nz):
            cc_copy(i, z, 1 - ki).wait_recv()

    def w1(w, d, own):
        pack, dst = packs[w]
        o = mod_less(t + d, nt) if own else t
        s = t if own else mod_less(t + nt - d, nt)
        return rcopy(
            pack.at[o],
            dst.at[xi, s, yi],
            R.w1_s.at[w, d],
            R.w1_r.at[w, d],
            mesh_dev(xi, lax.div(o, nz), lax.rem(o, nz), yi) if own else xpeer,
        )

    def w1_start(w):
        for d in range(1, nt):
            w1(w, d, True).start()
        packs[w][1][xi, t, yi] = packs[w][0][t]

    def w1_wait(w):
        for d in range(1, nt):
            w1(w, d, False).wait_recv()

    def own_view(w, xx, yy):
        return mats[w].at[xx, :, yy] if w < 3 else wo.at[xx, yy]

    def half_view(w, h, xx, yy):
        if w < 3:
            return mats[w].at[xx, h * nz : (h + 1) * nz, yy]
        return wo.at[xx, yy, :, h * half : (h + 1) * half]

    def plane_x(w, xx):
        v = own_view(w, xx, yi)
        return rcopy(v, v, R.xs_s.at[w], R.xs_r.at[w], xpeer)

    def plane_y(w, yy):
        v = own_view(w, xi, yy)
        return rcopy(v, v, R.ys_s.at[w], R.ys_r.at[w], ypeer)

    def forward_y(w, xx, yy):
        v = half_view(w, 0, xx, yy)
        return rcopy(v, v, R.fy_s.at[w], R.fy_r.at[w], ypeer)

    def forward_x(w, xx, yy):
        v = half_view(w, 1, xx, yy)
        return rcopy(v, v, R.fx_s.at[w], R.fx_r.at[w], xpeer)

    def plane_start(w):
        plane_x(w, xi).start()
        plane_y(w, yi).start()

    def plane_forward(w):
        plane_x(w, 1 - xi).wait_recv()
        forward_y(w, 1 - xi, yi).start()
        plane_y(w, 1 - yi).wait_recv()
        forward_x(w, xi, 1 - yi).start()

    def plane_wait(w):
        forward_y(w, 1 - xi, 1 - yi).wait_recv()
        forward_x(w, 1 - xi, 1 - yi).wait_recv()

    parts = (R.a0, R.a1)
    ex, ru, rd, fin, own = R.ex, R.ru, R.rd, R.fin, R.own
    grads = (R.mq, R.mu, R.md)
    mo, ro, so = R.mo, R.ro, R.so
    got1 = (R.got1_0, R.got1_1, R.got1_2)
    got2 = (R.got2_0, R.got2_1, R.got2_2)
    chunks = (R.chunk_0, R.chunk_1, R.chunk_2)

    def plus(a, b):
        return (a.astype(f32) + b.astype(f32)).astype(bf)

    def share(i, z):
        return rcopy(
            parts[i].at[z * 2 + (1 - ki)],
            ex.at[i, z],
            R.rcc_s.at[i, z],
            R.rcc_r.at[i, z],
            cpeer,
        )

    def rup(i, z):
        return rcopy(
            ex.at[i, z],
            ru.at[i, z],
            R.rup_s.at[i, z],
            R.rup_r.at[i, z],
            mesh_dev(xi, ki, zi + 1, yi),
        )

    def rdn(i, z):
        return rcopy(
            ex.at[i, z],
            rd.at[i, z],
            R.rdn_s.at[i, z],
            R.rdn_r.at[i, z],
            mesh_dev(xi, ki, zi - 1, yi),
        )

    def rswap(i):
        return rcopy(fin.at[i], own.at[i], R.rsw_s.at[i], R.rsw_r.at[i], swapped)

    def x1(w):
        return rcopy(
            grads[w].at[1 - xi, 0:nz], got1[w].at[0], R.x1_s.at[w], R.x1_r.at[w], xpeer
        )

    def y1(w):
        return [
            rcopy(
                grads[w].at[xx, nz:nt, 1 - yi],
                got1[w].at[1, :, xx],
                R.y1_s.at[w, xx],
                R.y1_r.at[w, xx],
                ypeer,
            )
            for xx in range(2)
        ]

    def y2(w):
        return rcopy(
            got1[w].at[0, :, 1 - yi], got2[w].at[0:nz], R.y2_s.at[w], R.y2_r.at[w], ypeer
        )

    def x2(w):
        return rcopy(
            got1[w].at[1, :, 1 - xi], got2[w].at[nz:nt], R.x2_s.at[w], R.x2_r.at[w], xpeer
        )

    def tp(w, d, mine):
        o = mod_less(t + d, nt) if mine else t
        s = t if mine else mod_less(t + nt - d, nt)
        return rcopy(
            got2[w].at[o],
            chunks[w].at[s],
            R.tp_s.at[w, d],
            R.tp_r.at[w, d],
            mesh_dev(xi, lax.div(o, nz), lax.rem(o, nz), yi) if mine else xpeer,
        )

    def ox1():
        return rcopy(
            mo.at[1 - xi, :, :, 0:half], ro.at[0], R.x1_s.at[3], R.x1_r.at[3], xpeer
        )

    def oy1():
        return rcopy(
            mo.at[:, 1 - yi, :, half:dm], ro.at[1], R.y1_s.at[3, 0], R.y1_r.at[3, 0], ypeer
        )

    def oy2():
        return rcopy(ro.at[0, 1 - yi], so.at[0], R.y2_s.at[3], R.y2_r.at[3], ypeer)

    def ox2():
        return rcopy(ro.at[1, 1 - xi], so.at[1], R.x2_s.at[3], R.x2_r.at[3], xpeer)

    def grad_start(w):
        x1(w).start()
        for cp in y1(w):
            cp.start()

    def fold(i):
        for z in range(nz):
            share(i, z).wait_recv()
            ex[i, z] = plus(ex[i, z], parts[i][z * 2 + ki])

    def rhop(i, d):
        @pl.when(zi + d < nz)
        def _():
            z = zi + d

            @pl.when(zi > 0)
            def _():
                rup(i, z).wait_recv()
                ex[i, z] = plus(ex[i, z], ru[i, z])

            rup(i, z).start()

        @pl.when(zi - d >= 0)
        def _():
            z = zi - d

            @pl.when(zi < nz - 1)
            def _():
                rdn(i, z).wait_recv()
                ex[i, z] = plus(ex[i, z], rd[i, z])

            rdn(i, z).start()

    def rend(i):
        @pl.when(zi > 0)
        def _():
            rup(i, zi).wait_recv()
            ex[i, zi] = plus(ex[i, zi], ru[i, zi])

        @pl.when(zi < nz - 1)
        def _():
            rdn(i, zi).wait_recv()
            ex[i, zi] = plus(ex[i, zi], rd[i, zi])

        @pl.when(ki != yi)
        def _():
            fin[i] = ex[i, zi]
            rswap(i).start()

        @pl.when(ki == yi)
        def _():
            own[i] = ex[i, zi]

    def fold1(w):
        x1(w).wait_recv()
        got1[w][0] = plus(got1[w][0], grads[w][xi, 0:nz])
        y2(w).start()
        for cp in y1(w):
            cp.wait_recv()
        for xx in range(2):
            got1[w][1, :, xx] = plus(got1[w][1, :, xx], grads[w][xx, nz:nt, yi])
        x2(w).start()

    def fold2(w):
        y2(w).wait_recv()
        got2[w][0:nz] = plus(got2[w][0:nz], got1[w][0, :, yi])
        x2(w).wait_recv()
        got2[w][nz:nt] = plus(got2[w][nz:nt], got1[w][1, :, xi])
        for d in range(1, nt):
            tp(w, d, True).start()
        chunks[w][t] = got2[w][t]

    lane = lax.broadcasted_iota(jnp.int32, (1, hw), 1)
    first = lane < HD
    gains = R.gains
    hat, n1, n2 = R.hat, R.n1, R.n2
    qm, km, vm, dcm = R.qm, R.km, R.vm, R.dm
    lse, delta, cx = R.lse, R.delta, R.cx
    hid, slope, dpre_s, gs = R.hid, R.slope, R.dpre, R.gs
    dq, dk, dv, dqkv = R.dq, R.dk, R.dv, R.dqkv
    sums, sq, su = R.sums, R.sq, R.su

    def block(i):
        return pl.ds(pl.multiple_of(i * QB, QB), QB)

    def act(ref, i):
        return ref[pl.ds(2 * i, 2)].reshape(QB, dm)

    def masked(value):
        return jnp.where(first, value, 0), jnp.where(first, 0, value)

    def hats(xf):
        mean = jnp.mean(xf, axis=-1, keepdims=True)
        centred = xf - mean
        rstd = lax.rsqrt(jnp.mean(centred * centred, axis=-1, keepdims=True) + EPS)
        return centred * rstd, rstd

    def hat_step(i, _):
        hat[block(i)] = hats(act(R.xb, i).astype(f32))[0]
        return 0

    def vectors_in():
        wq = R.wq
        per = LANES // piece

        def tile(r):
            a, b, e = r // (2 * nt), (r // 2) % nt, r % 2
            return wq[a, b, e, :, qc:].astype(f32)

        n = nt * 4
        for j in range(n // per):
            tiles = [tile(j * per + m) for m in range(per)]
            gains[:, j * LANES : (j + 1) * LANES] = jnp.concatenate(
                [v[0:8, 0:piece] for v in tiles], axis=1
            )
            bw = 3 * piece
            R.bqf[:, j * per * bw : (j + 1) * per * bw] = jnp.concatenate(
                [v[6:7, 0:bw] for v in tiles], axis=1
            )
        here = lax.div(t, 2) * LANES
        odd = lax.rem(t, 2) == 1
        for p in range(3):
            out = []
            for h in range(2):
                at = pl.multiple_of(here + (p * dm + h * half), LANES)
                v = R.bqf[:, pl.ds(at, LANES)]
                out.append(jnp.where(odd, v[:, HD:], v[:, :HD]))
            R.bq[:, p * hw : (p + 1) * hw] = jnp.concatenate(out, axis=1)
        for j in range(fw // LANES):
            r = t * (fw // LANES) + j
            v = wq[lax.div(r, 2 * nt), lax.rem(lax.div(r, 2), nt), lax.rem(r, 2), :, qc:]
            R.bu[:, j * LANES : (j + 1) * LANES] = v.astype(f32)[7:8]

    def turned(field, b, sign):
        down = pltpu.roll(field, hw - ROT // 2, 1)
        up = pltpu.roll(field, ROT // 2, 1)
        return field * cos_t[b] + sign * (down * low_t[b] + up * high_t[b])

    def qkv_step(i, _):
        b = block(i)
        h = hat[b]
        n1[b] = (h * gains[0:1] + gains[1:2]).astype(bf)
        n2[b] = (h * gains[2:3] + gains[3:4]).astype(bf)
        w = R.wq[:, :, :, :, 0:qc].reshape(dm, qc)
        qkv = mm(n1[b], w, NN) + R.bq[...]
        q = turned(qkv[:, 0:hw], b, 1.0).astype(bf).astype(f32) * scale
        k = turned(qkv[:, hw : 2 * hw], b, 1.0)
        v = qkv[:, 2 * hw : 3 * hw]
        for ref, value in ((qm, q), (km, k), (vm, v)):
            one, two = masked(value)
            ref[0, b] = one.astype(bf)
            ref[1, b] = two.astype(bf)
        return 0

    def attend_step(i, _):
        b = block(i)
        visible = place_row[...] <= place_col[b]
        ctx = jnp.zeros((QB, hw), f32)
        for h in range(2):
            s = jnp.where(visible, mm(qm[h, b], km[h], NT), NEG)
            top = jnp.max(s, axis=-1, keepdims=True)
            e = jnp.exp(s - top)
            total = jnp.sum(e, axis=-1, keepdims=True)
            ctx = ctx + mm(e.astype(bf), vm[h], NN) / total
            lse[h, b] = top + jnp.log(total)
        cx[b] = ctx.astype(bf)
        return 0

    def up_step(i, _):
        b = block(i)
        pre = mm(n2[b], R.wu[...].reshape(dm, fw), NN) + R.bu[...]
        bell = 0.5 * (1.0 + lax.erf(pre * ROOT_HALF))
        hid[b] = (pre * bell).astype(bf)
        slope[b] = bell + pre * jnp.exp(-0.5 * pre * pre) * INV_ROOT_TAU
        return 0

    def down_step(i, _):
        b = block(i)
        out = mm(hid[b], R.wd[...].reshape(dm, fw), NT)
        out = out + mm(cx[b], wo[...].reshape(hw, dm), NN)
        R.a0[pl.ds(2 * i, 2)] = out.astype(bf).reshape(2, width2, dm)
        return 0

    def back_step(i, _):
        b = block(i)
        g = act(R.gb, i)
        dpre = mm(g, R.wd[...].reshape(dm, fw), NN) * slope[b]
        su[...] += jnp.sum(dpre, axis=0, keepdims=True)
        dpre_s[b] = dpre.astype(bf)
        dn2 = mm(dpre_s[b], R.wu[...].reshape(dm, fw), NT)
        sums[2:3] += jnp.sum(dn2 * hat[b], axis=0, keepdims=True)
        sums[3:4] += jnp.sum(dn2, axis=0, keepdims=True)
        gs[b] = dn2 * gains[2:3]
        dctx = mm(g, wo[...].reshape(hw, dm), NT).astype(bf).astype(f32)
        prod = dctx * cx[b].astype(f32)
        for h, (d, p) in enumerate(zip(masked(dctx), masked(prod))):
            dcm[h, b] = d.astype(bf)
            delta[h, b] = jnp.sum(p, axis=-1, keepdims=True)
        return 0

    def rows_of(ref, i):
        return ref.at[lax.div(i, 2), pl.ds(pl.multiple_of(lax.rem(i, 2) * nz, nz), nz)]

    def outer_step(i, _):
        cols = pl.ds(pl.multiple_of(i * QB, QB), QB)
        gt = R.gb[:, :, cols].reshape(rows, QB)
        out = mm(gt, hid[...], TN)
        rows_of(R.md, i)[...] = out.astype(bf).reshape(nz, 2, piece, fw)
        wide = mm(cx[...], gt, TN).astype(bf)
        mo[:, :, :, cols] = wide.reshape(2, 2, piece, QB)
        return 0

    def outer_up_step(i, _):
        cols = pl.ds(pl.multiple_of(i * QB, QB), QB)
        out = mm(n2[:, cols], dpre_s[...], TN)
        rows_of(R.mu, i)[...] = out.astype(bf).reshape(nz, 2, piece, fw)
        return 0

    def attend_back_step(i, _):
        b = block(i)
        visible = place_row[...] <= place_col[b]
        acc = jnp.zeros((QB, hw), f32)
        for h in range(2):
            s = jnp.where(visible, mm(qm[h, b], km[h], NT), NEG)
            p = jnp.exp(s - lse[h, b])
            dp = mm(dcm[h, b], vm[h], NT)
            ds = (p * (dp - delta[h, b])).astype(bf)
            acc = acc + mm(ds, km[h], NN)
            dk[...] += mm(ds, qm[h, b], TN)
            dv[...] += mm(p.astype(bf), dcm[h, b], TN)
        dq[b] = acc * scale
        return 0

    def dqkv_step(i, _):
        b = block(i)
        fields = (turned(dq[b], b, -1.0), turned(dk[b], b, -1.0), dv[b])
        for j, v in enumerate(fields):
            sq[:, j * hw : (j + 1) * hw] += jnp.sum(v, axis=0, keepdims=True)
            dqkv[b, j * hw : (j + 1) * hw] = v.astype(bf)
        w = R.wq[:, :, :, :, 0:qc].reshape(dm, qc)
        dn1 = mm(dqkv[b], w, NT)
        sums[0:1] += jnp.sum(dn1 * hat[b], axis=0, keepdims=True)
        sums[1:2] += jnp.sum(dn1, axis=0, keepdims=True)
        out = (dn1 * gains[0:1] + gs[b]).astype(bf)
        R.a1[pl.ds(2 * i, 2)] = out.reshape(2, width2, dm)
        return 0

    def outer_qkv_step(i, _):
        cols = pl.ds(pl.multiple_of(i * QB, QB), QB)
        out = mm(n1[:, cols], dqkv[...], TN)
        view = R.mq.at[lax.div(i, 2), pl.ds(pl.multiple_of(lax.rem(i, 2) * nz, nz), nz), :, :, 0:qc]
        view[...] = out.astype(bf).reshape(nz, 2, piece, qc)
        return 0

    def sums_out():
        low = jnp.concatenate(
            [sq[:, j * hw : (j + 1) * hw] for j in range(3)]
            + [su[:, j * LANES : (j + 1) * LANES] for j in range(fw // LANES)]
            + [jnp.zeros((piece - 8 - 3 - fw // LANES, LANES), f32)],
            axis=0,
        )
        for r in range(nt * 4):
            one = sums[:, r * piece : (r + 1) * piece]
            one = jnp.concatenate([one, jnp.zeros((8, LANES - piece), f32)], axis=1)
            tile = jnp.concatenate([one, low], axis=0).astype(bf)
            R.mq[r // (2 * nt), (r // 2) % nt, r % 2, :, qc:] = tile

    vs = R.vs
    vs[...] = jnp.zeros_like(vs)
    for i, v in enumerate(vectors):
        vs[i : i + 1, 0 : v.shape[1]] = v[...].astype(f32)
    small = vs[...].astype(bf)
    loads[1].wait()
    for o in range(nt):
        pieces = []
        for p in range(3):
            base = p * dm + o * HD
            for at in (base, base + half):
                pieces.append(R.qo[:, at : at + HD])
        for j in range(3):
            R.pq[o, :, j * hw : (j + 1) * hw] = jnp.concatenate(pieces[2 * j : 2 * j + 2], axis=1)
        R.pq[o, :, qc:] = small
    for ref in (sums, sq, su, dk, dv):
        ref[...] = jnp.zeros_like(ref)
    loads[0].wait()
    loads[2].wait()
    load_g.wait()

    greet(nz, xi, ki, zi, yi)

    swap_start(0)
    w1_start(0)
    swap_wait(0)
    hop_send(0, 1)
    hop_share(0, 0)
    plane_start(3)
    for cp in loads_u:
        cp.wait()
    w1_start(1)
    hop(0, 1)
    w1_wait(0)
    plane_start(0)
    for d in range(2, nz):
        hop(0, d)
    plane_forward(0)
    swap_start(1)
    for cp in loads_d:
        cp.wait()
    w1_start(2)
    sums[4:5] = jnp.sum(R.go[...].astype(f32), axis=0, keepdims=True)
    all_in(0)
    lax.fori_loop(0, nblk, hat_step, 0)
    swap_wait(1)
    hop_send(1, 1)
    hop_share(1, 0)
    w1_wait(1)
    plane_start(1)
    plane_forward(3)
    plane_wait(0)
    vectors_in()
    lax.fori_loop(0, nblk, qkv_step, 0)
    plane_forward(1)
    w1_wait(2)
    plane_start(2)
    hop(1, 1)
    lax.fori_loop(0, nblk // 2, attend_step, 0)
    for d in range(2, nz):
        hop(1, d)
    lax.fori_loop(nblk // 2, nblk, attend_step, 0)
    plane_forward(2)
    plane_wait(1)
    lax.fori_loop(0, nblk, up_step, 0)
    plane_wait(2)
    plane_wait(3)
    lax.fori_loop(0, nblk, down_step, 0)
    for z in range(nz):
        share(0, z).start()
    all_in(1)
    lax.fori_loop(0, nblk, back_step, 0)
    fold(0)
    rhop(0, nz - 1)
    lax.fori_loop(0, nblk, outer_step, 0)
    grad_start(2)
    ox1().start()
    oy1().start()
    for d in range(nz - 2, nz - 3, -1):
        rhop(0, d)
    lax.fori_loop(0, nblk, outer_up_step, 0)
    grad_start(1)
    for d in range(nz - 3, 0, -1):
        rhop(0, d)
    lax.fori_loop(0, nblk // 2, attend_back_step, 0)
    rend(0)
    fold1(2)
    lax.fori_loop(nblk // 2, nblk, attend_back_step, 0)
    fold1(1)
    lax.fori_loop(0, nblk, dqkv_step, 0)
    for z in range(nz):
        share(1, z).start()
    fold2(2)
    lax.fori_loop(0, nblk, outer_qkv_step, 0)
    sums_out()
    grad_start(0)
    fold(1)
    rhop(1, nz - 1)
    ox1().wait_recv()
    ro[0] = plus(ro[0], mo[xi, :, :, 0:half])
    oy2().start()
    oy1().wait_recv()
    ro[1] = plus(ro[1], mo[:, yi, :, half:dm])
    ox2().start()
    fold2(1)
    fold1(0)
    for d in range(nz - 2, 0, -1):
        rhop(1, d)
    fold2(0)
    rend(1)

    @pl.when(ki != yi)
    def _():
        rswap(0).wait_recv()

    x_own = R.xo[...].astype(f32)
    out_x[...] = (x_own + own[0].astype(f32) + (gains[4:5] + gains[5:6])).astype(bf)
    oy2().wait_recv()
    oo[:, 0:half] = so[0].astype(f32) + ro[0, yi].astype(f32)
    ox2().wait_recv()
    oo[:, half:dm] = so[1].astype(f32) + ro[1, xi].astype(f32)
    for w in (2, 1):
        for d in range(1, nt):
            tp(w, d, False).wait_recv()
        ref = (None, ou, od)[w]
        for o in range(nt):
            ref[:, o * fw : (o + 1) * fw] = chunks[w][o].astype(f32)
    hat_own, rstd_own = hats(x_own)

    @pl.when(ki != yi)
    def _():
        rswap(1).wait_recv()

    gsum = own[1].astype(f32)
    out_g[...] = (
        R.go[...].astype(f32)
        + rstd_own
        * (
            gsum
            - jnp.mean(gsum, axis=-1, keepdims=True)
            - hat_own * jnp.mean(gsum * hat_own, axis=-1, keepdims=True)
        )
    ).astype(bf)
    for d in range(1, nt):
        tp(0, d, False).wait_recv()
    cq = chunks[0]
    for j in range(3):
        for h in range(2):
            for o in range(0, nt, 2):
                lo = j * hw + h * HD
                both = jnp.concatenate([cq[o, :, lo : lo + HD], cq[o + 1, :, lo : lo + HD]], axis=1)
                at = j * dm + h * half + o * HD
                oq[:, at : at + hw] = both.astype(f32)
    for o in range(nt):
        osum[o] = cq[o, :, qc:].astype(f32)[0:16]

    for i in range(2):

        @pl.when(ki != yi)
        def _():
            swap(i).wait_send()
            rswap(i).wait_send()

        for d in range(1, nz):

            @pl.when((zi - (d - 1) >= 0) & (zi + 1 < nz))
            def _():
                up_copy(i, d, zi - (d - 1)).wait_send()

            @pl.when((zi + (d - 1) < nz) & (zi >= 1))
            def _():
                dn_copy(i, d, zi + (d - 1)).wait_send()

            @pl.when(zi + d < nz)
            def _():
                rup(i, zi + d).wait_send()

            @pl.when(zi - d >= 0)
            def _():
                rdn(i, zi - d).wait_send()

        for z in range(nz):
            cc_copy(i, z, ki).wait_send()
            share(i, z).wait_send()
    for w in range(3):
        for d in range(1, nt):
            w1(w, d, True).wait_send()
            tp(w, d, True).wait_send()
        x1(w).wait_send()
        for cp in y1(w):
            cp.wait_send()
        y2(w).wait_send()
        x2(w).wait_send()
    for w in range(4):
        plane_x(w, xi).wait_send()
        plane_y(w, yi).wait_send()
        forward_y(w, 1 - xi, yi).wait_send()
        forward_x(w, xi, 1 - yi).wait_send()
    ox1().wait_send()
    oy1().wait_send()
    oy2().wait_send()
    ox2().wait_send()


def routed(
    layer_in,
    grad_out,
    pair_of_rank,
    ln1_gain,
    ln1_bias,
    ln2_gain,
    ln2_bias,
    w_qkv,
    b_qkv,
    w_out,
    b_out,
    w_up,
    b_up,
    w_down,
    b_down,
):
    f32 = jnp.float32
    bf = jnp.bfloat16
    nctx = lax.axis_size("ctx")
    nz = nctx // 2
    r = lax.axis_index("fsdp") * nctx + lax.axis_index("ctx")
    width2, dmodel = layer_in.shape[2:]
    blk = width2 // 2
    ff = w_up.shape[1]
    piece = w_qkv.shape[0]
    rows = nctx * width2

    offsets = jnp.arange(blk, dtype=jnp.int32)
    slot_a = pair_of_rank[:, None] * blk + offsets[None, :]
    slot_b = (2 * nctx - 1 - pair_of_rank)[:, None] * blk + offsets[None, :]
    places = jnp.concatenate([slot_a, slot_b], axis=1).reshape(rows)
    tables = turn_tables(places, 2 * HD)

    plan = layer_plan(nz, width2, dmodel, ff, piece)
    vectors = (ln1_gain, ln1_bias, ln2_gain, ln2_bias, b_out, b_down, b_qkv, b_up)
    vm = pl.BlockSpec(memory_space=pltpu.VMEM)
    anywhere = pl.BlockSpec(memory_space=pl.ANY)
    shape = jax.ShapeDtypeStruct
    layer_out, grad_x, grad_qkv, grad_up, grad_down, grad_wout, sums = pl.pallas_call(
        functools.partial(layer_kernel, nz, tuple(plan)),
        out_shape=(
            shape((width2, dmodel), bf),
            shape((width2, dmodel), bf),
            shape((piece, 3 * dmodel), f32),
            shape((piece, ff), f32),
            shape((piece, ff), f32),
            shape((piece, dmodel), f32),
            shape((nctx, 16, LANES), f32),
        ),
        in_specs=[anywhere] * 6 + [vm] * 13,
        out_specs=(vm,) * 7,
        scratch_shapes=list(plan.values()),
        compiler_params=pltpu.CompilerParams(
            collective_id=0, has_side_effects=True, vmem_limit_bytes=60 * 1024 * 1024
        ),
    )(
        layer_in.reshape(width2, dmodel),
        grad_out.reshape(width2, dmodel),
        w_qkv,
        w_up,
        w_down,
        w_out,
        *[v.reshape(1, -1) for v in vectors],
        places.reshape(rows, 1),
        places.reshape(1, rows),
        *tables,
    )
    total = jnp.sum(sums, axis=0)
    vs = [total[i, :piece] for i in range(5)]
    nq = b_qkv.shape[0]
    all_q = sums[:, 8:11].reshape(nctx, 3, 2, HD).transpose(1, 2, 0, 3).reshape(-1)
    all_u = sums[:, 11 : 11 + ff // nctx // LANES].reshape(-1)
    grad_bq = lax.dynamic_slice_in_dim(all_q, r * nq, nq)
    grad_bu = lax.dynamic_slice_in_dim(all_u, r * b_up.shape[0], b_up.shape[0])
    return (
        layer_out.reshape(layer_in.shape),
        grad_x.reshape(layer_in.shape),
        vs[0],
        vs[1],
        vs[2],
        vs[3],
        grad_qkv,
        grad_bq,
        grad_wout,
        vs[4],
        grad_up,
        grad_bu,
        grad_down,
        vs[4],
    )


def solution(mesh):
    nctx = mesh.shape["ctx"]

    def pick(layer_in, *rest):
        heads = layer_in.shape[-1] // HD
        whole = heads % nctx == 0
        square = nctx % 2 == 0 and mesh.shape["fsdp"] == 4 and heads == 2 * nctx
        if square and layer_in.shape[1] == 1 and layer_in.shape[-1] == 8 * layer_in.shape[2] == nctx * layer_in.shape[2]:
            return routed(layer_in, *rest)
        return (head_shards if whole else shards)(layer_in, *rest)

    return jax.shard_map(
        pick,
        mesh=mesh,
        in_specs=(
            P("ctx", "fsdp", None, None),
            P("ctx", "fsdp", None, None),
            P(),
            P(("fsdp", "ctx")),
            P(("fsdp", "ctx")),
            P(("fsdp", "ctx")),
            P(("fsdp", "ctx")),
            P(("fsdp", "ctx"), None),
            P(("fsdp", "ctx")),
            P(("fsdp", "ctx"), None),
            P(("fsdp", "ctx")),
            P(("fsdp", "ctx"), None),
            P(("fsdp", "ctx")),
            P(("fsdp", "ctx"), None),
            P(("fsdp", "ctx")),
        ),
        out_specs=(
            P("ctx", "fsdp", None, None),
            P("ctx", "fsdp", None, None),
            P(("fsdp", "ctx")),
            P(("fsdp", "ctx")),
            P(("fsdp", "ctx")),
            P(("fsdp", "ctx")),
            P(("fsdp", "ctx"), None),
            P(("fsdp", "ctx")),
            P(("fsdp", "ctx"), None),
            P(("fsdp", "ctx")),
            P(("fsdp", "ctx"), None),
            P(("fsdp", "ctx")),
            P(("fsdp", "ctx"), None),
            P(("fsdp", "ctx")),
        ),
        check_vma=False,
    )
```

```python
import functools
import math
import types

import jax
import jax.numpy as jnp
from jax import lax
from jax.experimental import pallas as pl
from jax.experimental.pallas import tpu as pltpu
from jax.sharding import PartitionSpec as P

HD = 64
ROT = 16
LANES = 128


EPS = 1e-05
NEG = -1e30
ROOT_HALF = 0.7071067811865476
INV_ROOT_TAU = 0.3989422804014327


def norm_parts(xf, scale_weight, shift_bias):
    row_mean = jnp.mean(xf, axis=-1, keepdims=True)
    centred_input = xf - row_mean
    inverse_deviation = lax.rsqrt(
        jnp.mean(centred_input * centred_input, axis=-1, keepdims=True) + EPS
    )
    normalized_input = centred_input * inverse_deviation
    return (
        normalized_input * scale_weight.astype(jnp.float32) + shift_bias.astype(jnp.float32),
        normalized_input,
        inverse_deviation,
    )


def layer_norm_backward(norm_output_gradient, normalized_input, inverse_deviation, scale_weight):
    normalized_gradient = norm_output_gradient * scale_weight.astype(jnp.float32)
    return inverse_deviation * (
        normalized_gradient
        - jnp.mean(normalized_gradient, axis=-1, keepdims=True)
        - normalized_input
        * jnp.mean(normalized_gradient * normalized_input, axis=-1, keepdims=True)
    )


def gelu_value(u):
    return 0.5 * u * (1.0 + lax.erf(u * ROOT_HALF))


def gelu_slope(u):
    return 0.5 * (1.0 + lax.erf(u * ROOT_HALF)) + u * jnp.exp(-0.5 * u * u) * INV_ROOT_TAU


def rotate(field, place, sign):
    half = ROT // 2
    freqs = jnp.exp(jnp.arange(half).astype(jnp.float32) * (-2.0 * math.log(10000.0) / ROT))
    angle = place.astype(jnp.float32)[..., None] * freqs
    cosine = jnp.cos(angle)[..., None, :]
    sine = sign * jnp.sin(angle)[..., None, :]
    first = field[..., :half]
    second = field[..., half:ROT]
    return jnp.concatenate(
        [first * cosine - second * sine, second * cosine + first * sine, field[..., rot_end() :]],
        axis=-1,
    )


def rot_end():
    return ROT


def leading(field, letters):
    return "n" + letters if field.ndim == 5 else letters


def product(left, left_letters, right, right_letters, result):
    form = leading(left, left_letters) + "," + leading(right, right_letters) + "->" + result
    return jnp.einsum(form, left, right, preferred_element_type=jnp.float32)


def selectors(sel):
    return (sel[:, None, None, None, None], sel[:, None, None, None], sel[:, None])


def visibility(sel, qpa, qpb, kpa, kpb):
    chosen = sel[:, None]
    key_place = jnp.where(chosen, kpa, kpb)
    query_place = jnp.where(chosen, qpa, qpb)
    return (key_place[:, None, :] <= query_place[:, :, None])[:, None, None]


def online_update(state, qa, qb, ka, kb, va, vb, qpa, qpb, kpa, kpb, sel, with_first, scale):
    top_a, total_a, acc_a, top_b, total_b, acc_b = state
    sel5, sel4, sel2 = selectors(sel)
    query_two = jnp.where(sel5, qa, qb)
    key_two = jnp.where(sel5, ka, kb)
    value_two = jnp.where(sel5, va, vb)
    visible = visibility(sel, qpa, qpb, kpa, kpb)
    score = jnp.where(visible, product(query_two, "sqhd", key_two, "skhd", "nshqk") * scale, NEG)
    peak_a = jnp.max(jnp.where(sel5, score, NEG), axis=(0, 4))
    peak_b = jnp.max(jnp.where(sel5, NEG, score), axis=(0, 4))
    if with_first:
        score_one = product(qb, "sqhd", ka, "skhd", "nshqk") * scale
        peak_b = jnp.maximum(peak_b, jnp.max(score_one, axis=(0, 4)))
    new_a = jnp.maximum(top_a, peak_a)
    new_b = jnp.maximum(top_b, peak_b)
    lifted = jnp.where(sel5, new_a[..., None], new_b[..., None])
    weight = jnp.where(visible, jnp.exp(score - lifted), 0.0)
    mixed = product(weight.astype(jnp.bfloat16), "shqk", value_two, "skhd", "nshqd")
    mass = jnp.sum(weight, axis=4)
    add_total_a = jnp.sum(jnp.where(sel4, mass, 0.0), axis=0)
    add_total_b = jnp.sum(jnp.where(sel4, 0.0, mass), axis=0)
    add_acc_a = jnp.sum(jnp.where(sel5, mixed, 0.0), axis=0)
    add_acc_b = jnp.sum(jnp.where(sel5, 0.0, mixed), axis=0)
    if with_first:
        weight_one = jnp.exp(score_one - new_b[..., None])
        add_total_b = add_total_b + jnp.sum(weight_one, axis=(0, 4))
        add_acc_b = add_acc_b + product(weight_one.astype(jnp.bfloat16), "shqk", va, "skhd", "shqd")
    decay_a = jnp.exp(top_a - new_a)
    decay_b = jnp.exp(top_b - new_b)
    return (
        new_a,
        total_a * decay_a + add_total_a,
        acc_a * decay_a[..., None] + add_acc_a,
        new_b,
        total_b * decay_b + add_total_b,
        acc_b * decay_b[..., None] + add_acc_b,
    )


def pair_terms(
    qa,
    qb,
    ka,
    kb,
    va,
    vb,
    da,
    db,
    lsea,
    lseb,
    dela,
    delb,
    qpa,
    qpb,
    kpa,
    kpb,
    sel,
    with_first,
    scale,
):
    sel5, sel4, sel2 = selectors(sel)
    query_two = jnp.where(sel5, qa, qb)
    key_two = jnp.where(sel5, ka, kb)
    value_two = jnp.where(sel5, va, vb)
    dctx_two = jnp.where(sel5, da, db)
    lse_two = jnp.where(sel4, lsea, lseb)
    delta_two = jnp.where(sel4, dela, delb)
    visible = visibility(sel, qpa, qpb, kpa, kpb)
    score = jnp.where(visible, product(query_two, "sqhd", key_two, "skhd", "nshqk") * scale, NEG)
    prob = jnp.exp(score - lse_two[..., None])
    dprob = product(dctx_two, "sqhd", value_two, "skhd", "nshqk")
    dscore = (scale * prob * (dprob - delta_two[..., None])).astype(jnp.bfloat16)
    first_ds = None
    first_prob = None
    if with_first:
        score_one = product(qb, "sqhd", ka, "skhd", "nshqk") * scale
        prob_one = jnp.exp(score_one - lseb[..., None])
        dprob_one = product(db, "sqhd", va, "skhd", "nshqk")
        first_ds = (scale * prob_one * (dprob_one - delb[..., None])).astype(jnp.bfloat16)
        first_prob = prob_one.astype(jnp.bfloat16)
    return (first_ds, first_prob, dscore, prob.astype(jnp.bfloat16))


def query_grads(terms, ka, kb, sel):
    sel5, sel4, sel2 = selectors(sel)
    key_two = jnp.where(sel5, ka, kb)
    dq_two = product(terms[2], "shqk", key_two, "skhd", "nsqhd")
    dq_a = jnp.where(sel5, dq_two, 0.0)
    dq_b = jnp.where(sel5, 0.0, dq_two)
    if terms[0] is not None:
        dq_b = dq_b + product(terms[0], "shqk", ka, "skhd", "nsqhd")
    return (dq_a, dq_b)


def key_grads(terms, qa, qb, da, db, sel):
    sel5, sel4, sel2 = selectors(sel)
    query_two = jnp.where(sel5, qa, qb)
    dctx_two = jnp.where(sel5, da, db)
    dk_two = product(terms[2], "shqk", query_two, "sqhd", "nskhd")
    dv_two = product(terms[3], "shqk", dctx_two, "sqhd", "nskhd")
    dk_a = jnp.where(sel5, dk_two, 0.0)
    dk_b = jnp.where(sel5, 0.0, dk_two)
    dv_a = jnp.where(sel5, dv_two, 0.0)
    dv_b = jnp.where(sel5, 0.0, dv_two)
    if terms[0] is not None:
        dk_a = dk_a + product(terms[0], "shqk", qb, "sqhd", "nskhd")
        dv_a = dv_a + product(terms[1], "shqk", db, "sqhd", "nskhd")
    return (dk_a, dk_b, dv_a, dv_b)


def tdot(left, right):
    return lax.dot_general(
        left, right, (((0,), (0,)), ((), ())), preferred_element_type=jnp.float32
    )


def rdot(left, right):
    return lax.dot_general(
        left, right, (((1,), (1,)), ((), ())), preferred_element_type=jnp.float32
    )


def shards(
    layer_in,
    grad_out,
    pair_of_rank,
    ln1_gain,
    ln1_bias,
    ln2_gain,
    ln2_bias,
    w_qkv,
    b_qkv,
    w_out,
    b_out,
    w_up,
    b_up,
    w_down,
    b_down,
):
    f32 = jnp.float32
    bf = jnp.bfloat16
    nctx = lax.axis_size("ctx")
    mine = pair_of_rank[lax.axis_index("ctx")]
    seqs = layer_in.shape[1]
    width2 = layer_in.shape[2]
    dmodel = layer_in.shape[3]
    blk = width2 // 2
    rows = seqs * width2
    heads = dmodel // HD
    scale = 1.0 / math.sqrt(HD)
    offsets = jnp.arange(blk, dtype=jnp.int32)
    place_a = mine * blk + offsets
    place_b = (2 * nctx - 1 - mine) * blk + offsets
    places = jnp.concatenate([place_a, place_b])
    params = (
        ln1_gain,
        ln1_bias,
        ln2_gain,
        ln2_bias,
        w_qkv,
        b_qkv,
        w_out,
        b_out,
        w_up,
        b_up,
        w_down,
        b_down,
    )
    full = (
        lax.all_gather(params[0], ("fsdp", "ctx"), axis=0, tiled=True),
        lax.all_gather(params[1], ("fsdp", "ctx"), axis=0, tiled=True),
        lax.all_gather(params[2], ("fsdp", "ctx"), axis=0, tiled=True),
        lax.all_gather(params[3], ("fsdp", "ctx"), axis=0, tiled=True),
        lax.all_gather(params[4], ("fsdp", "ctx"), axis=0, tiled=True),
        lax.all_gather(params[5], ("fsdp", "ctx"), axis=0, tiled=True),
        lax.all_gather(params[6], ("fsdp", "ctx"), axis=0, tiled=True),
        lax.all_gather(params[7], ("fsdp", "ctx"), axis=0, tiled=True),
        lax.all_gather(params[8], ("fsdp", "ctx"), axis=0, tiled=True),
        lax.all_gather(params[9], ("fsdp", "ctx"), axis=0, tiled=True),
        lax.all_gather(params[10], ("fsdp", "ctx"), axis=0, tiled=True),
        lax.all_gather(params[11], ("fsdp", "ctx"), axis=0, tiled=True),
    )
    xf = layer_in.reshape(rows, dmodel).astype(f32)
    norm1, hat1, rstd1 = norm_parts(xf, full[0], full[1])
    norm2, hat2, rstd2 = norm_parts(xf, full[2], full[3])
    norm1 = norm1.astype(bf)
    norm2 = norm2.astype(bf)
    qkv = jnp.dot(norm1, full[4], preferred_element_type=f32) + full[5].astype(f32)
    query = rotate(qkv[:, :dmodel].reshape(seqs, width2, heads, HD), places, 1.0).astype(bf)
    key = rotate(qkv[:, dmodel : 2 * dmodel].reshape(seqs, width2, heads, HD), places, 1.0).astype(
        bf
    )
    value = qkv[:, 2 * dmodel :].reshape(seqs, width2, heads, HD).astype(bf)
    query_a = query[:, :blk]
    query_b = query[:, blk:]
    key_b = key[:, blk:]
    value_b = value[:, blk:]
    lone = jnp.zeros((1,), dtype=bool)
    empty_top = jnp.full((seqs, heads, blk), NEG, f32)
    empty_total = jnp.zeros((seqs, heads, blk), f32)
    empty_acc = jnp.zeros((seqs, heads, blk, HD), f32)
    state = (empty_top, empty_total, empty_acc, empty_top, empty_total, empty_acc)
    state = online_update(
        state,
        query_a,
        query_b,
        key_b[None],
        key_b[None],
        value_b[None],
        value_b[None],
        place_a,
        place_b,
        place_b[None],
        place_b[None],
        lone,
        False,
        scale,
    )

    def key_parts(kpiece, vpiece, first):
        count = kpiece.shape[0]
        pairs = lax.dynamic_slice_in_dim(pair_of_rank, first, count)
        keys = kpiece.reshape(count, seqs, width2, heads, HD)
        values = vpiece.reshape(count, seqs, width2, heads, HD)
        kplace_a = pairs[:, None] * blk + offsets[None, :]
        kplace_b = (2 * nctx - 1 - pairs)[:, None] * blk + offsets[None, :]
        return (
            keys[:, :, :blk],
            keys[:, :, blk:],
            values[:, :, :blk],
            values[:, :, blk:],
            kplace_a,
            kplace_b,
            pairs,
        )

    key_send = key.reshape(1, seqs, width2, dmodel)
    value_send = value.reshape(1, seqs, width2, dmodel)
    ka, kb, va, vb, kpa, kpb, pairs = key_parts(
        lax.all_gather(key_send, "ctx", axis=0, tiled=True),
        lax.all_gather(value_send, "ctx", axis=0, tiled=True),
        jnp.int32(0),
    )
    state = online_update(
        state,
        query_a,
        query_b,
        ka,
        kb,
        va,
        vb,
        place_a,
        place_b,
        kpa,
        kpb,
        pairs <= mine,
        True,
        scale,
    )
    top_a, total_a, acc_a, top_b, total_b, acc_b = state
    context4 = jnp.concatenate([acc_a / total_a[..., None], acc_b / total_b[..., None]], axis=2)
    lse = jnp.concatenate([top_a + jnp.log(total_a), top_b + jnp.log(total_b)], axis=2)
    context = context4.transpose(0, 2, 1, 3).reshape(rows, dmodel).astype(bf)
    attn = jnp.dot(context, full[6], preferred_element_type=f32) + full[7].astype(f32)
    pre = jnp.dot(norm2, full[8], preferred_element_type=f32) + full[9].astype(f32)
    hidden = gelu_value(pre).astype(bf)
    mlp = rdot(hidden, full[10]) + full[11].astype(f32)
    layer_out = (xf + attn + mlp).astype(bf).reshape(layer_in.shape)
    again = (
        lax.all_gather(params[0], ("fsdp", "ctx"), axis=0, tiled=True),
        lax.all_gather(params[1], ("fsdp", "ctx"), axis=0, tiled=True),
        lax.all_gather(params[2], ("fsdp", "ctx"), axis=0, tiled=True),
        lax.all_gather(params[3], ("fsdp", "ctx"), axis=0, tiled=True),
        lax.all_gather(params[4], ("fsdp", "ctx"), axis=0, tiled=True),
        lax.all_gather(params[5], ("fsdp", "ctx"), axis=0, tiled=True),
        lax.all_gather(params[6], ("fsdp", "ctx"), axis=0, tiled=True),
        lax.all_gather(params[7], ("fsdp", "ctx"), axis=0, tiled=True),
        lax.all_gather(params[8], ("fsdp", "ctx"), axis=0, tiled=True),
        lax.all_gather(params[9], ("fsdp", "ctx"), axis=0, tiled=True),
        lax.all_gather(params[10], ("fsdp", "ctx"), axis=0, tiled=True),
        lax.all_gather(params[11], ("fsdp", "ctx"), axis=0, tiled=True),
    )
    grad_b = grad_out.reshape(rows, dmodel)
    grad_f = grad_b.astype(f32)
    dhidden = jnp.dot(grad_b, again[10], preferred_element_type=f32)
    dpre = dhidden * gelu_slope(pre)
    dpre_b = dpre.astype(bf)
    dnorm2 = rdot(dpre_b, again[8])
    dcontext = rdot(grad_b, again[6]).astype(bf)
    dctx4 = dcontext.reshape(seqs, width2, heads, HD)
    delta = jnp.sum(
        dctx4.astype(f32) * context.reshape(seqs, width2, heads, HD).astype(f32), axis=-1
    ).transpose(0, 2, 1)
    dctx_a = dctx4[:, :blk]
    dctx_b = dctx4[:, blk:]
    lse_a = lse[..., :blk]
    lse_b = lse[..., blk:]
    delta_a = delta[..., :blk]
    delta_b = delta[..., blk:]
    own = pair_terms(
        query_b,
        query_b,
        key_b[None],
        key_b[None],
        value_b[None],
        value_b[None],
        dctx_b,
        dctx_b,
        lse_b,
        lse_b,
        delta_b,
        delta_b,
        place_b,
        place_b,
        place_b[None],
        place_b[None],
        lone,
        False,
        scale,
    )
    own_dq = query_grads(own, key_b[None], key_b[None], lone)[1][0]
    own_keys = key_grads(own, query_b, query_b, dctx_b, dctx_b, lone)
    gathered = (
        lax.all_gather(key_send, "ctx", axis=0, tiled=True),
        lax.all_gather(value_send, "ctx", axis=0, tiled=True),
    )
    groups = math.gcd(nctx, 8)
    per = nctx // groups

    def group_terms(args):
        kpiece, vpiece, first = args
        ka, kb, va, vb, kpa, kpb, pairs = key_parts(kpiece, vpiece, first)
        sel = pairs <= mine
        terms = pair_terms(
            query_a,
            query_b,
            ka,
            kb,
            va,
            vb,
            dctx_a,
            dctx_b,
            lse_a,
            lse_b,
            delta_a,
            delta_b,
            place_a,
            place_b,
            kpa,
            kpb,
            sel,
            True,
            scale,
        )
        dq_a, dq_b = query_grads(terms, ka, kb, sel)
        return (terms, jnp.sum(dq_a, axis=0), jnp.sum(dq_b, axis=0))

    grouped = lax.map(
        group_terms,
        (
            gathered[0].reshape(groups, per, seqs, width2, dmodel),
            gathered[1].reshape(groups, per, seqs, width2, dmodel),
            jnp.arange(groups, dtype=jnp.int32) * per,
        ),
    )
    terms_all = tuple((part.reshape((nctx,) + part.shape[2:]) for part in grouped[0]))
    dq_a = jnp.sum(grouped[1], axis=0)
    dq_b = jnp.sum(grouped[2], axis=0)
    pairs = pair_of_rank
    sliced = tuple(
        (lax.slice_in_dim(part, 0, 1 * lax.axis_size("ctx"), axis=0) for part in terms_all)
    )
    dk_a, dk_b, dv_a, dv_b = key_grads(sliced, query_a, query_b, dctx_a, dctx_b, pairs <= mine)
    dkey = jnp.concatenate([dk_a, dk_b], axis=2).reshape(
        1 * lax.axis_size("ctx"), seqs, width2, dmodel
    )
    dval = jnp.concatenate([dv_a, dv_b], axis=2).reshape(
        1 * lax.axis_size("ctx"), seqs, width2, dmodel
    )
    kv_grad = lax.psum_scatter(
        jnp.concatenate([dkey, dval], axis=-1), "ctx", scatter_dimension=0, tiled=True
    )
    dkey = kv_grad[0, :, :, :dmodel].reshape(seqs, width2, heads, HD)
    dval = kv_grad[0, :, :, dmodel:].reshape(seqs, width2, heads, HD)
    zero_half = jnp.zeros((seqs, blk, heads, HD), f32)
    dquery = jnp.concatenate([dq_a, dq_b + own_dq], axis=1)
    dkey = dkey + jnp.concatenate([zero_half, own_keys[1][0]], axis=1)
    dval = dval + jnp.concatenate([zero_half, own_keys[3][0]], axis=1)
    dqkv = jnp.concatenate(
        [
            rotate(dquery, places, -1.0).reshape(rows, dmodel),
            rotate(dkey, places, -1.0).reshape(rows, dmodel),
            dval.reshape(rows, dmodel),
        ],
        axis=1,
    )
    dqkv_b = dqkv.astype(bf)
    dnorm1 = rdot(dqkv_b, again[4])
    grad_x = (
        (
            grad_f
            + layer_norm_backward(dnorm1, hat1, rstd1, again[0])
            + layer_norm_backward(dnorm2, hat2, rstd2, again[2])
        )
        .astype(bf)
        .reshape(layer_in.shape)
    )
    vectors = (
        lax.psum_scatter(
            jnp.sum(dnorm1 * hat1, axis=0), ("fsdp", "ctx"), scatter_dimension=0, tiled=True
        ),
        lax.psum_scatter(jnp.sum(dnorm1, axis=0), ("fsdp", "ctx"), scatter_dimension=0, tiled=True),
        lax.psum_scatter(
            jnp.sum(dnorm2 * hat2, axis=0), ("fsdp", "ctx"), scatter_dimension=0, tiled=True
        ),
        lax.psum_scatter(jnp.sum(dnorm2, axis=0), ("fsdp", "ctx"), scatter_dimension=0, tiled=True),
        lax.psum_scatter(jnp.sum(dqkv, axis=0), ("fsdp", "ctx"), scatter_dimension=0, tiled=True),
        lax.psum_scatter(jnp.sum(grad_f, axis=0), ("fsdp", "ctx"), scatter_dimension=0, tiled=True),
        lax.psum_scatter(jnp.sum(dpre, axis=0), ("fsdp", "ctx"), scatter_dimension=0, tiled=True),
    )
    weights = (
        lax.psum_scatter(tdot(norm1, dqkv_b), ("fsdp", "ctx"), scatter_dimension=0, tiled=True),
        lax.psum_scatter(tdot(context, grad_b), ("fsdp", "ctx"), scatter_dimension=0, tiled=True),
        lax.psum_scatter(tdot(norm2, dpre_b), ("fsdp", "ctx"), scatter_dimension=0, tiled=True),
        lax.psum_scatter(tdot(grad_b, hidden), ("fsdp", "ctx"), scatter_dimension=0, tiled=True),
    )
    return (
        layer_out,
        grad_x,
        vectors[0],
        vectors[1],
        vectors[2],
        vectors[3],
        weights[0],
        vectors[4],
        weights[1],
        vectors[5],
        weights[2],
        vectors[6],
        weights[3],
        vectors[5],
    )


def span(lead, cols):
    return jnp.arange(lead, dtype=jnp.int32)[:, None] if cols else jnp.arange(lead, dtype=jnp.int32)


def turn(field, cosine, sine_low, sine_high):
    half = ROT // 2
    down = jnp.concatenate([field[:, half:], field[:, :half]], axis=1)
    up = jnp.concatenate([field[:, -half:], field[:, :-half]], axis=1)
    return field * cosine + down * sine_low + up * sine_high


def turn_tables(places, width):
    half = ROT // 2
    lane = jnp.arange(width, dtype=jnp.int32) % HD
    freqs = jnp.exp((lane % half).astype(jnp.float32) * (-2.0 * math.log(10000.0) / ROT))
    angle = places.astype(jnp.float32)[:, None] * freqs[None, :]
    cosine = jnp.where(lane < ROT, jnp.cos(angle), 1.0)
    sine = jnp.sin(angle)
    sine_low = jnp.where(lane < half, -sine, 0.0)
    sine_high = jnp.where((lane >= half) & (lane < ROT), sine, 0.0)
    return cosine, sine_low, sine_high


def headed(field, count):
    return field.reshape(field.shape[0], count, HD).transpose(1, 0, 2)


def joined(field):
    return field.transpose(1, 0, 2).reshape(field.shape[1], -1)


def bdot(form, left, right):
    return jnp.einsum(form, left, right, preferred_element_type=jnp.float32)


def head_shards(
    layer_in,
    grad_out,
    pair_of_rank,
    ln1_gain,
    ln1_bias,
    ln2_gain,
    ln2_bias,
    w_qkv,
    b_qkv,
    w_out,
    b_out,
    w_up,
    b_up,
    w_down,
    b_down,
):
    f32 = jnp.float32
    bf = jnp.bfloat16
    both = ("fsdp", "ctx")
    nctx = lax.axis_size("ctx")
    nf = lax.axis_size("fsdp")
    ndev = nctx * nf
    c = lax.axis_index("ctx")
    seqs, width2, dmodel = layer_in.shape[1:]
    blk = width2 // 2
    own_rows = seqs * width2
    ff = w_up.shape[1]
    hloc = dmodel // HD // nctx
    qw = hloc * HD
    fw = ff // nctx
    piece = dmodel // ndev
    scale = 1.0 / math.sqrt(HD)

    x_all = lax.all_gather(layer_in.reshape(own_rows, dmodel), "ctx", axis=0, tiled=True)
    def columns(parts):
        packed = jnp.concatenate([p.reshape(piece, nctx, -1) for p in parts], axis=-1)
        packed = packed.transpose(1, 0, 2)
        got = lax.all_to_all(packed, "ctx", split_axis=0, concat_axis=0, tiled=True)
        return got.reshape(nctx * piece, -1)

    wq = w_qkv.reshape(piece, 3, nctx, qw).transpose(0, 2, 1, 3)
    vec = jnp.concatenate([ln1_gain, ln1_bias, ln2_gain, ln2_bias, b_out, b_down, b_qkv, b_up])
    vw = LANES * -(-vec.shape[0] // (piece * LANES))
    vec_pad = jnp.pad(vec, (0, piece * vw - vec.shape[0])).reshape(piece, 1, vw)
    vec_pad = jnp.broadcast_to(vec_pad, (piece, nctx, vw))
    cols = lax.all_gather(columns([wq, w_up, w_down, vec_pad]), "fsdp", axis=0, tiled=True)
    g_own = grad_out.reshape(own_rows, dmodel)
    cols, g_send = lax.optimization_barrier((cols, g_own))
    got = cols[:, 3 * qw + 2 * fw :].reshape(ndev, piece * vw)
    cuts = [piece] * 6 + [b_qkv.shape[0], b_up.shape[0]]
    fulls = []
    at = 0
    for cut in cuts:
        fulls.append(got[:, at : at + cut].reshape(-1).astype(f32))
        at += cut
    gain1, bias1, gain2, bias2, bo, bd, bq, bu = fulls
    bq_c = lax.dynamic_slice_in_dim(bq.reshape(3, nctx, qw), c, 1, axis=1).reshape(1, 3 * qw)
    bu_c = lax.dynamic_slice_in_dim(bu, c * fw, fw).reshape(1, fw)
    wq_c = cols[:, : 3 * qw]
    wu_c = cols[:, 3 * qw : 3 * qw + fw]
    wd_c = cols[:, 3 * qw + fw : 3 * qw + 2 * fw]
    there = [((nf * cc + f) , f * nctx + cc) for f in range(nf) for cc in range(nctx)]
    back = [(b, a) for a, b in there]
    wo_c = lax.all_gather(lax.ppermute(w_out, both, there), "fsdp", axis=0, tiled=True)
    g_all = lax.all_gather(g_send, "ctx", axis=0, tiled=True)

    rows = x_all.shape[0]
    offsets = jnp.arange(blk, dtype=jnp.int32)
    slot_a = pair_of_rank[:, None] * blk + offsets[None, :]
    slot_b = (2 * nctx - 1 - pair_of_rank)[:, None] * blk + offsets[None, :]
    slots = jnp.concatenate([slot_a, slot_b], axis=1)[:, None, :]
    places = jnp.broadcast_to(slots, (nctx, seqs, width2)).reshape(rows)
    group = jnp.broadcast_to(span(seqs, False)[None, :, None], (nctx, seqs, width2)).reshape(rows)

    def hat_of(xf):
        row_mean = jnp.mean(xf, axis=-1, keepdims=True)
        centred = xf - row_mean
        rstd = lax.rsqrt(jnp.mean(centred * centred, axis=-1, keepdims=True) + EPS)
        return centred * rstd, rstd

    hat, _ = hat_of(x_all.astype(f32))
    norm1 = (hat * gain1 + bias1).astype(bf)
    norm2 = (hat * gain2 + bias2).astype(bf)
    qkv = jnp.dot(norm1, wq_c, preferred_element_type=f32) + bq_c
    cosine, sine_low, sine_high = turn_tables(places, qw)
    query = headed(turn(qkv[:, :qw], cosine, sine_low, sine_high).astype(bf), hloc)
    key = headed(turn(qkv[:, qw : 2 * qw], cosine, sine_low, sine_high).astype(bf), hloc)
    value = headed(qkv[:, 2 * qw :].astype(bf), hloc)
    visible = places[None, :] <= places[:, None]
    if seqs > 1:
        visible = visible & (group[None, :] == group[:, None])
    score = jnp.where(visible[None], bdot("hqd,hkd->hqk", query, key) * scale, NEG)
    top = jnp.max(score, axis=-1, keepdims=True)
    weight = jnp.exp(score - top)
    total = jnp.sum(weight, axis=-1, keepdims=True)
    mixed = bdot("hqk,hkd->hqd", weight.astype(bf), value)
    context = (mixed / total).astype(bf)
    lse = top + jnp.log(total)
    ctx_c = joined(context)

    pre = jnp.dot(norm2, wu_c, preferred_element_type=f32) + bu_c
    hidden = gelu_value(pre).astype(bf)
    part = rdot(hidden, wd_c) + jnp.dot(ctx_c, wo_c, preferred_element_type=f32)
    fwd = lax.all_to_all(
        part.astype(bf).reshape(nctx, own_rows, dmodel), "ctx", split_axis=0, concat_axis=0, tiled=True
    )
    fwd = jnp.sum(fwd.astype(f32), axis=0)
    x_own = layer_in.reshape(own_rows, dmodel).astype(f32)
    layer_out = (x_own + fwd + (bo + bd)).astype(bf).reshape(layer_in.shape)

    dhidden = jnp.dot(g_all, wd_c, preferred_element_type=f32)
    dpre = dhidden * gelu_slope(pre)
    dpre_b = dpre.astype(bf)
    dnorm2 = rdot(dpre_b, wu_c)
    dctx = headed(rdot(g_all, wo_c).astype(bf), hloc)
    delta = jnp.sum(dctx.astype(f32) * context.astype(f32), axis=-1, keepdims=True)
    prob = jnp.exp(score - lse)
    dprob = bdot("hqd,hkd->hqk", dctx, value)
    ds = (scale * prob * (dprob - delta)).astype(bf)
    dquery = joined(bdot("hqk,hkd->hqd", ds, key))
    dkey = joined(bdot("hqk,hqd->hkd", ds, query))
    dvalue = joined(bdot("hqk,hqd->hkd", prob.astype(bf), dctx))
    dqkv = jnp.concatenate(
        [
            turn(dquery, cosine, -sine_low, -sine_high),
            turn(dkey, cosine, -sine_low, -sine_high),
            dvalue,
        ],
        axis=1,
    )
    dqkv_b = dqkv.astype(bf)
    dnorm1 = rdot(dqkv_b, wq_c)
    gsum = (dnorm1 * gain1 + dnorm2 * gain2).astype(bf)
    gsum = lax.psum_scatter(gsum, "ctx", scatter_dimension=0, tiled=True).astype(f32)
    hat_own, rstd_own = hat_of(x_own)
    g_ownf = g_own.astype(f32)
    grad_x = (
        g_ownf
        + rstd_own
        * (
            gsum
            - jnp.mean(gsum, axis=-1, keepdims=True)
            - hat_own * jnp.mean(gsum * hat_own, axis=-1, keepdims=True)
        )
    ).astype(bf).reshape(layer_in.shape)

    sum_q = jnp.zeros((3, nctx, qw), f32)
    sum_q = lax.dynamic_update_slice_in_dim(
        sum_q, jnp.sum(dqkv, axis=0).reshape(3, 1, qw), c, axis=1
    ).reshape(ndev, -1)
    sum_u = lax.dynamic_update_slice_in_dim(
        jnp.zeros((ff,), f32), jnp.sum(dpre, axis=0), c * fw, axis=0
    ).reshape(ndev, -1)
    sums = [
        jnp.sum(dnorm1 * hat, axis=0).reshape(ndev, -1),
        jnp.sum(dnorm1, axis=0).reshape(ndev, -1),
        jnp.sum(dnorm2 * hat, axis=0).reshape(ndev, -1),
        jnp.sum(dnorm2, axis=0).reshape(ndev, -1),
        jnp.sum(g_ownf, axis=0).reshape(ndev, -1),
        sum_q,
        sum_u,
    ]
    sums = jnp.concatenate(sums, axis=1)
    sw = LANES * -(-sums.shape[1] // (piece * LANES))
    sums_pad = jnp.pad(sums, ((0, 0), (0, piece * sw - sums.shape[1]))).reshape(ndev * piece, sw)
    rows_out = tdot(ctx_c, g_all).astype(bf)
    wide = jnp.concatenate(
        [
            tdot(norm1, dqkv_b).astype(bf),
            tdot(norm2, dpre_b).astype(bf),
            tdot(g_all, hidden).astype(bf),
            sums_pad.astype(bf),
            rows_out.reshape(ndev * piece, -1),
        ],
        axis=1,
    )
    wide = lax.psum_scatter(wide, "fsdp", scatter_dimension=0, tiled=True)
    split = 3 * qw + 2 * fw + sw
    grad_wout = lax.ppermute(wide[:, split:].reshape(piece, dmodel), both, back).astype(f32)
    wide = lax.all_to_all(
        wide[:, :split].reshape(nctx, piece, split), "ctx", split_axis=0, concat_axis=0, tiled=True
    )
    sums = jnp.sum(wide[:, :, split - sw :].astype(f32), axis=0).reshape(-1)[: sums.shape[1]]
    wide = wide.transpose(1, 0, 2).astype(f32)
    grad_qkv = (
        wide[:, :, : 3 * qw].reshape(piece, nctx, 3, qw).transpose(0, 2, 1, 3).reshape(piece, -1)
    )
    grad_up = wide[:, :, 3 * qw : 3 * qw + fw].reshape(piece, ff)
    grad_down = wide[:, :, 3 * qw + fw : 3 * qw + 2 * fw].reshape(piece, ff)
    ends = [piece * i for i in range(6)] + [5 * piece + b_qkv.shape[0], sums.shape[0]]
    vs = [sums[a:b] for a, b in zip(ends[:-1], ends[1:])]
    return (
        layer_out,
        grad_x,
        vs[0],
        vs[1],
        vs[2],
        vs[3],
        grad_qkv,
        vs[5],
        grad_wout,
        vs[4],
        grad_up,
        vs[6],
        grad_down,
        vs[4],
    )


def mod_less(a, n):
    return jnp.where(a >= n, a - n, a)


def mesh_dev(xi, ki, zi, yi):
    return {"fsdp": xi * 2 + ki, "ctx": zi * 2 + yi}


def rcopy(src, dst, send, recv, where):
    return pltpu.make_async_remote_copy(
        src_ref=src,
        dst_ref=dst,
        send_sem=send,
        recv_sem=recv,
        device_id=where,
        device_id_type=pl.DeviceIdType.MESH,
    )


def greet(nz, xi, ki, zi, yi):
    t = ki * nz + zi
    nt = 2 * nz
    barrier = pltpu.get_barrier_semaphore()

    def hello(where):
        pl.semaphore_signal(barrier, inc=1, device_id=where, device_id_type=pl.DeviceIdType.MESH)

    for d in range(1, nt):
        o = mod_less(t + d, nt)
        hello(mesh_dev(xi, lax.div(o, nz), lax.rem(o, nz), yi))
    hello(mesh_dev(1 - xi, ki, zi, yi))
    hello(mesh_dev(xi, ki, zi, 1 - yi))

    @pl.when(ki != yi)
    def _():
        for z in range(nz):
            hello(mesh_dev(xi, yi, z, ki))

    pl.semaphore_wait(barrier, jnp.where(ki != yi, nt + 1 + nz, nt + 1))


STEPS = (-2, -1, 1, 2)
DIRECT_OUT = (False, True)


NT = (((1,), (1,)), ((), ()))
TN = (((0,), (0,)), ((), ()))
NN = (((1,), (0,)), ((), ()))


def mm(left, right, form):
    return lax.dot_general(left, right, form, preferred_element_type=jnp.float32)


def layer_plan(nz, width2, dm, ff, piece):
    nt = 2 * nz
    fw = ff // nt
    rows = nt * width2
    qw = 6 * HD + LANES
    bf, f32 = jnp.bfloat16, jnp.float32
    vm = pltpu.VMEM
    dma = pltpu.SemaphoreType.DMA
    plan = dict(
        xo=vm((width2, dm), bf),
        go=vm((width2, dm), bf),
        qo=vm((piece, 3 * dm), bf),
        ld=dma((5 + 2 * nt,)),
        xb=vm((nt, width2, dm), bf),
        gb=vm((nt, width2, dm), bf),
        wq=vm((2, nt, 2, piece, qw), bf),
        wu=vm((2, nt, 2, piece, fw), bf),
        wd=vm((2, nt, 2, piece, fw), bf),
        wo=vm((2, 2, piece, dm), bf),
        pq=vm((nt, piece, qw), bf),
        pu=vm((nt, piece, fw), bf),
        pd=vm((nt, piece, fw), bf),
        vs=vm((piece, LANES), f32),
        gains=vm((8, dm), f32),
        bqf=vm((1, 3 * dm), f32),
        bq=vm((1, 6 * HD), f32),
        bu=vm((1, fw), f32),
        hat=vm((rows, dm), f32),
        n1=vm((rows, dm), bf),
        n2=vm((rows, dm), bf),
        qm=vm((2, rows, 2 * HD), bf),
        km=vm((2, rows, 2 * HD), bf),
        vm=vm((2, rows, 2 * HD), bf),
        dm=vm((2, rows, 2 * HD), bf),
        lse=vm((2, rows, 1), f32),
        delta=vm((2, rows, 1), f32),
        cx=vm((rows, 2 * HD), bf),
        hid=vm((rows, fw), bf),
        slope=vm((rows, fw), f32),
        dpre=vm((rows, fw), bf),
        gs=vm((rows, dm), f32),
        dq=vm((rows, 2 * HD), f32),
        dk=vm((rows, 2 * HD), f32),
        dv=vm((rows, 2 * HD), f32),
        dqkv=vm((rows, 6 * HD), bf),
        sums=vm((8, dm), f32),
        sq=vm((1, 6 * HD), f32),
        su=vm((1, fw), f32),
        a0=vm((nt, width2, dm), bf),
        a1=vm((nt, width2, dm), bf),
        mq=vm((2, nt, 2, piece, qw), bf),
        mu=vm((2, nt, 2, piece, fw), bf),
        md=vm((2, nt, 2, piece, fw), bf),
        mo=vm((2, 2, piece, dm), bf),
        ex=vm((2, nz, width2, dm), bf),
        rcv=vm((2, 5, width2, dm), bf),
        cmb=vm((2, 2, width2, dm), bf),
        fin=vm((2, width2, dm), bf),
        own=vm((2, width2, dm), f32),
        pcol=vm((rows, 1), jnp.int32),
        prow=vm((1, rows), jnp.int32),
        cos=vm((rows, 2 * HD), f32),
        low=vm((rows, 2 * HD), f32),
        high=vm((rows, 2 * HD), f32),
        ro=vm((2, 2, piece, dm // 2), bf),
        so=vm((2, piece, dm // 2), bf),
        sw_s=dma((2,)),
        sw_r=dma((2,)),
        rsw_s=dma((2,)),
        rsw_r=dma((2,)),
        up_s=dma((2, nz)),
        up_r=dma((2, nz)),
        dn_s=dma((2, nz)),
        dn_r=dma((2, nz)),
        cc_s=dma((2, nz)),
        cc_r=dma((2, nz)),
        rn_s=dma((2, 4)),
        rn_r=dma((2, 4)),
        rf_s=dma((2, 2)),
        rf_r=dma((2, 2)),
        rcc_s=dma((2, nz)),
        rcc_r=dma((2, nz)),
        w1_s=dma((3, nt)),
        w1_r=dma((3, nt)),
        tp_s=dma((3, nt)),
        tp_r=dma((3, nt)),
        xs_s=dma((4,)),
        xs_r=dma((4,)),
        ys_s=dma((4,)),
        ys_r=dma((4,)),
        fx_s=dma((4,)),
        fx_r=dma((4,)),
        fy_s=dma((4,)),
        fy_r=dma((4,)),
        x1_s=dma((4,)),
        x1_r=dma((4,)),
        x2_s=dma((4,)),
        x2_r=dma((4,)),
        y2_s=dma((4,)),
        y2_r=dma((4,)),
        y1_s=dma((4, 2)),
        y1_r=dma((4, 2)),
        got1_0=vm((2, nz, 2, piece, qw), bf),
        got1_1=vm((2, nz, 2, piece, fw), bf),
        got1_2=vm((2, nz, 2, piece, fw), bf),
        got2_0=vm((nt, piece, qw), bf),
        got2_1=vm((nt, piece, fw), bf),
        got2_2=vm((nt, piece, fw), bf),
        chunk_0=vm((nt, piece, qw), bf),
        chunk_1=vm((nt, piece, fw), bf),
        chunk_2=vm((nt, piece, fw), bf),
    )
    return plan


def layer_kernel(nz, names, *refs):
    f32, bf = jnp.float32, jnp.bfloat16
    (x_hbm, g_hbm, wq_hbm, wu_hbm, wd_hbm, wo_hbm) = refs[:6]
    vectors = refs[6:14]
    pairs = refs[14]
    (out_x, out_g, oq, ou, od, oo, osum) = refs[15:22]
    R = types.SimpleNamespace(**dict(zip(names, refs[22:])))

    f = lax.axis_index("fsdp")
    c = lax.axis_index("ctx")
    xi, ki = lax.div(f, 2), lax.rem(f, 2)
    zi, yi = lax.div(c, 2), lax.rem(c, 2)
    nt = 2 * nz
    t = ki * nz + zi
    width2, dm = R.xo.shape
    half = dm // 2
    rows = nt * width2
    fw = R.wu.shape[4]
    piece = R.wq.shape[3]
    qc = 6 * HD
    hw = 2 * HD
    QB = 2 * width2
    nblk = rows // QB
    scale = 1.0 / math.sqrt(HD)
    c_own = zi * 2 + yi

    xpeer = mesh_dev(1 - xi, ki, zi, yi)
    ypeer = mesh_dev(xi, ki, zi, 1 - yi)
    cpeer = mesh_dev(xi, 1 - ki, zi, yi)
    swapped = mesh_dev(xi, yi, zi, ki)
    acts = ((R.xo, R.xb), (R.go, R.gb))
    packs = ((R.pq, R.wq), (R.pu, R.wu), (R.pd, R.wd))
    mats = (R.wq, R.wu, R.wd)
    wo = R.wo

    ld = R.ld
    loads = [
        pltpu.make_async_copy(x_hbm, R.xo, ld.at[0]),
        pltpu.make_async_copy(wq_hbm, R.qo, ld.at[1]),
        pltpu.make_async_copy(wo_hbm, wo.at[xi, yi], ld.at[2]),
    ]
    loads_u = [
        pltpu.make_async_copy(wu_hbm.at[:, o * fw : (o + 1) * fw], R.pu.at[o], ld.at[5 + o])
        for o in range(nt)
    ]
    loads_d = [
        pltpu.make_async_copy(wd_hbm.at[:, o * fw : (o + 1) * fw], R.pd.at[o], ld.at[5 + nt + o])
        for o in range(nt)
    ]
    load_g = pltpu.make_async_copy(g_hbm, R.go, ld.at[3])
    for cp in loads + loads_u + loads_d + [load_g]:
        cp.start()

    def swap(i):
        src, dst = acts[i]
        return rcopy(src, dst.at[c_own], R.sw_s.at[i], R.sw_r.at[i], swapped)

    def swap_start(i):
        @pl.when(ki != yi)
        def _():
            swap(i).start()

        @pl.when(ki == yi)
        def _():
            acts[i][1][c_own] = acts[i][0][...]

    def swap_wait(i):
        @pl.when(ki != yi)
        def _():
            dst = acts[i][1].at[zi * 2 + ki]
            rcopy(acts[i][0], dst, R.sw_s.at[i], R.sw_r.at[i], swapped).wait_recv()

    def inside(z):
        return (z >= 0) & (z < nz)

    def up_copy(i, d, z):
        slot = acts[i][1].at[z * 2 + ki]
        return rcopy(slot, slot, R.up_s.at[i, d], R.up_r.at[i, d], mesh_dev(xi, ki, zi + 1, yi))

    def dn_copy(i, d, z):
        slot = acts[i][1].at[z * 2 + ki]
        return rcopy(slot, slot, R.dn_s.at[i, d], R.dn_r.at[i, d], mesh_dev(xi, ki, zi - 1, yi))

    def cc_copy(i, z, k):
        slot = acts[i][1].at[z * 2 + k]
        return rcopy(slot, slot, R.cc_s.at[i, z], R.cc_r.at[i, z], cpeer)

    def pass_on(i, *steps):
        for step in steps:

            @pl.when(inside(zi - step))
            def _():
                cc_copy(i, zi - step, ki).start()

    def hop_send(i, d):
        @pl.when(inside(zi - (d - 1)) & inside(zi + 1))
        def _():
            up_copy(i, d, zi - (d - 1)).start()

        @pl.when(inside(zi + (d - 1)) & inside(zi - 1))
        def _():
            dn_copy(i, d, zi + (d - 1)).start()

    def hop(i, d):
        @pl.when(inside(zi - d))
        def _():
            up_copy(i, d, zi - d).wait_recv()

        @pl.when(inside(zi + d))
        def _():
            dn_copy(i, d, zi + d).wait_recv()

        if d + 1 < nz:
            hop_send(i, d + 1)
        pass_on(i, -d, d)

    def first_hop(i):
        swap_wait(i)
        hop_send(i, 1)
        pass_on(i, 0)

    def all_in(i):
        for z in range(nz):
            cc_copy(i, z, 1 - ki).wait_recv()

    def w1(w, d, own):
        pack, dst = packs[w]
        o = mod_less(t + d, nt) if own else t
        s = t if own else mod_less(t + nt - d, nt)
        return rcopy(
            pack.at[o],
            dst.at[xi, s, yi],
            R.w1_s.at[w, d],
            R.w1_r.at[w, d],
            mesh_dev(xi, lax.div(o, nz), lax.rem(o, nz), yi) if own else xpeer,
        )

    def w1_start(w):
        for d in range(1, nt):
            w1(w, d, True).start()
        packs[w][1][xi, t, yi] = packs[w][0][t]

    def w1_wait(w):
        for d in range(1, nt):
            w1(w, d, False).wait_recv()

    def own_view(w, xx, yy):
        return mats[w].at[xx, :, yy] if w < 3 else wo.at[xx, yy]

    def half_view(w, h, xx, yy):
        if w < 3:
            return mats[w].at[xx, h * nz : (h + 1) * nz, yy]
        return wo.at[xx, yy, :, h * half : (h + 1) * half]

    def plane_x(w, xx):
        v = own_view(w, xx, yi)
        return rcopy(v, v, R.xs_s.at[w], R.xs_r.at[w], xpeer)

    def plane_y(w, yy):
        v = own_view(w, xi, yy)
        return rcopy(v, v, R.ys_s.at[w], R.ys_r.at[w], ypeer)

    def forward_y(w, xx, yy):
        v = half_view(w, 0, xx, yy)
        return rcopy(v, v, R.fy_s.at[w], R.fy_r.at[w], ypeer)

    def forward_x(w, xx, yy):
        v = half_view(w, 1, xx, yy)
        return rcopy(v, v, R.fx_s.at[w], R.fx_r.at[w], xpeer)

    def plane_start(w):
        plane_x(w, xi).start()
        plane_y(w, yi).start()

    def plane_forward(w):
        plane_x(w, 1 - xi).wait_recv()
        forward_y(w, 1 - xi, yi).start()
        plane_y(w, 1 - yi).wait_recv()
        forward_x(w, xi, 1 - yi).start()

    def plane_wait(w):
        forward_y(w, 1 - xi, 1 - yi).wait_recv()
        forward_x(w, 1 - xi, 1 - yi).wait_recv()

    parts = (R.a0, R.a1)
    ex, rcv, cmb, fin, own = R.ex, R.rcv, R.cmb, R.fin, R.own
    grads = (R.mq, R.mu, R.md)
    mo, ro, so = R.mo, R.ro, R.so
    got1 = (R.got1_0, R.got1_1, R.got1_2)
    got2 = (R.got2_0, R.got2_1, R.got2_2)
    chunks = (R.chunk_0, R.chunk_1, R.chunk_2)

    def plus(a, b):
        return (a.astype(f32) + b.astype(f32)).astype(bf)

    def share(i, z):
        return rcopy(
            parts[i].at[z * 2 + (1 - ki)],
            ex.at[i, z],
            R.rcc_s.at[i, z],
            R.rcc_r.at[i, z],
            cpeer,
        )

    def rnear(i, n):
        z = zi + STEPS[n]
        where = mesh_dev(xi, yi, z, ki) if DIRECT_OUT[i] else mesh_dev(xi, ki, z, yi)
        return rcopy(ex.at[i, z], rcv.at[i, n], R.rn_s.at[i, n], R.rn_r.at[i, n], where)

    def rfar(i, up):
        step = 1 if up else -1
        m = 0 if up else 1
        return rcopy(
            ex.at[i, zi + 3 * step],
            cmb.at[i, m],
            R.rf_s.at[i, m],
            R.rf_r.at[i, m],
            mesh_dev(xi, ki, zi + step, yi),
        )

    def rswap(i):
        return rcopy(fin.at[i], rcv.at[i, 4], R.rsw_s.at[i], R.rsw_r.at[i], swapped)

    def x1(w):
        return rcopy(
            grads[w].at[1 - xi, 0:nz], got1[w].at[0], R.x1_s.at[w], R.x1_r.at[w], xpeer
        )

    def y1(w):
        return [
            rcopy(
                grads[w].at[xx, nz:nt, 1 - yi],
                got1[w].at[1, :, xx],
                R.y1_s.at[w, xx],
                R.y1_r.at[w, xx],
                ypeer,
            )
            for xx in range(2)
        ]

    def y2(w):
        return rcopy(
            got1[w].at[0, :, 1 - yi], got2[w].at[0:nz], R.y2_s.at[w], R.y2_r.at[w], ypeer
        )

    def x2(w):
        return rcopy(
            got1[w].at[1, :, 1 - xi], got2[w].at[nz:nt], R.x2_s.at[w], R.x2_r.at[w], xpeer
        )

    def tp(w, d, mine):
        o = mod_less(t + d, nt) if mine else t
        s = t if mine else mod_less(t + nt - d, nt)
        return rcopy(
            got2[w].at[o],
            chunks[w].at[s],
            R.tp_s.at[w, d],
            R.tp_r.at[w, d],
            mesh_dev(xi, lax.div(o, nz), lax.rem(o, nz), yi) if mine else xpeer,
        )

    def ox1():
        return rcopy(
            mo.at[1 - xi, :, :, 0:half], ro.at[0], R.x1_s.at[3], R.x1_r.at[3], xpeer
        )

    def oy1():
        return rcopy(
            mo.at[:, 1 - yi, :, half:dm], ro.at[1], R.y1_s.at[3, 0], R.y1_r.at[3, 0], ypeer
        )

    def oy2():
        return rcopy(ro.at[0, 1 - yi], so.at[0], R.y2_s.at[3], R.y2_r.at[3], ypeer)

    def ox2():
        return rcopy(ro.at[1, 1 - xi], so.at[1], R.x2_s.at[3], R.x2_r.at[3], xpeer)

    def grad_start(w):
        x1(w).start()
        for cp in y1(w):
            cp.start()

    def fold(i):
        for z in range(nz):
            share(i, z).wait_recv()
            ex[i, z] = plus(ex[i, z], parts[i][z * 2 + ki])

    def rstart(i):
        for up, step in ((True, 1), (False, -1)):

            @pl.when(inside(zi + 3 * step))
            def _():
                rfar(i, up).start()

            @pl.when(inside(zi + 2 * step) & jnp.logical_not(inside(zi - step)))
            def _():
                rnear(i, 3 if up else 0).start()

            @pl.when(inside(zi + step))
            def _():
                rnear(i, 2 if up else 1).start()

        if DIRECT_OUT[i]:

            @pl.when(ki != yi)
            def _():
                fin[i] = ex[i, zi]
                rswap(i).start()

    def rjoin(i):
        for up, step in ((True, 1), (False, -1)):

            @pl.when(inside(zi + 2 * step) & inside(zi - step))
            def _():
                m = 0 if up else 1
                z = zi + 2 * step
                there = mesh_dev(xi, ki, zi - step, yi)
                rcopy(
                    ex.at[i, z], cmb.at[i, m], R.rf_s.at[i, m], R.rf_r.at[i, m], there
                ).wait_recv()
                ex[i, z] = plus(ex[i, z], cmb[i, m])
                rnear(i, 3 if up else 0).start()

    def swapped_in(i):
        rcopy(fin.at[i], rcv.at[i, 4], R.rsw_s.at[i], R.rsw_r.at[i], swapped).wait_recv()

    def rnears(i):
        for n in range(4):

            @pl.when(inside(zi - STEPS[n]))
            def _():
                rcopy(
                    fin.at[i], rcv.at[i, n], R.rn_s.at[i, n], R.rn_r.at[i, n], cpeer
                ).wait_recv()
                own[i] += rcv[i, n].astype(f32)

    def rend(i):
        if DIRECT_OUT[i]:

            @pl.when(ki != yi)
            def _():
                swapped_in(i)
                own[i] = rcv[i, 4].astype(f32)

            @pl.when(ki == yi)
            def _():
                own[i] = ex[i, zi].astype(f32)

            rnears(i)
        else:
            own[i] = ex[i, zi].astype(f32)
            rnears(i)

            @pl.when(ki != yi)
            def _():
                fin[i] = own[i].astype(bf)
                rswap(i).start()

    def rlast(i):
        if not DIRECT_OUT[i]:

            @pl.when(ki != yi)
            def _():
                swapped_in(i)
                own[i] = rcv[i, 4].astype(f32)

    def fold1(w):
        x1(w).wait_recv()
        got1[w][0] = plus(got1[w][0], grads[w][xi, 0:nz])
        y2(w).start()
        for cp in y1(w):
            cp.wait_recv()
        for xx in range(2):
            got1[w][1, :, xx] = plus(got1[w][1, :, xx], grads[w][xx, nz:nt, yi])
        x2(w).start()

    def fold2(w):
        y2(w).wait_recv()
        got2[w][0:nz] = plus(got2[w][0:nz], got1[w][0, :, yi])
        x2(w).wait_recv()
        got2[w][nz:nt] = plus(got2[w][nz:nt], got1[w][1, :, xi])
        for d in range(1, nt):
            tp(w, d, True).start()
        chunks[w][t] = got2[w][t]

    lane = lax.broadcasted_iota(jnp.int32, (1, hw), 1)
    first = lane < HD
    gains = R.gains
    hat, n1, n2 = R.hat, R.n1, R.n2
    place_col, place_row, cos_t, low_t, high_t = R.pcol, R.prow, R.cos, R.low, R.high
    qm, km, vm, dcm = R.qm, R.km, R.vm, R.dm
    lse, delta, cx = R.lse, R.delta, R.cx
    hid, slope, dpre_s, gs = R.hid, R.slope, R.dpre, R.gs
    dq, dk, dv, dqkv = R.dq, R.dk, R.dv, R.dqkv
    sums, sq, su = R.sums, R.sq, R.su

    def block(i):
        return pl.ds(pl.multiple_of(i * QB, QB), QB)

    def act(ref, i):
        return ref[pl.ds(2 * i, 2)].reshape(QB, dm)

    def masked(value):
        return jnp.where(first, value, 0), jnp.where(first, 0, value)

    def hats(xf):
        mean = jnp.mean(xf, axis=-1, keepdims=True)
        centred = xf - mean
        rstd = lax.rsqrt(jnp.mean(centred * centred, axis=-1, keepdims=True) + EPS)
        return centred * rstd, rstd

    def table_step(i, _):
        blk = width2 // 2
        p = pairs[i]

        def place_of(j):
            return jnp.where(j < blk, p * blk + j, (2 * nt - 1 - p) * blk + j - blk)

        at = pl.ds(pl.multiple_of(i * width2, width2), width2)
        place = place_of(lax.broadcasted_iota(jnp.int32, (width2, 1), 0))
        place_col[at] = place
        place_row[:, at] = place_of(lax.broadcasted_iota(jnp.int32, (1, width2), 1))
        turn_lane = lane & (HD - 1)
        step = (turn_lane & (ROT // 2 - 1)).astype(f32)
        angle = place.astype(f32) * jnp.exp(step * (-2.0 * math.log(10000.0) / ROT))
        sine = jnp.sin(angle)
        cos_t[at] = jnp.where(turn_lane < ROT, jnp.cos(angle), 1.0)
        low_t[at] = jnp.where(turn_lane < ROT // 2, -sine, 0.0)
        high_t[at] = jnp.where((turn_lane >= ROT // 2) & (turn_lane < ROT), sine, 0.0)
        return 0

    def hat_step(i, _):
        hat[block(i)] = hats(act(R.xb, i).astype(f32))[0]
        return 0

    def vectors_in():
        wq = R.wq
        per = LANES // piece

        def tile(r):
            a, b, e = r // (2 * nt), (r // 2) % nt, r % 2
            return wq[a, b, e, :, qc:].astype(f32)

        n = nt * 4
        for j in range(n // per):
            tiles = [tile(j * per + m) for m in range(per)]
            gains[:, j * LANES : (j + 1) * LANES] = jnp.concatenate(
                [v[0:8, 0:piece] for v in tiles], axis=1
            )
            bw = 3 * piece
            R.bqf[:, j * per * bw : (j + 1) * per * bw] = jnp.concatenate(
                [v[6:7, 0:bw] for v in tiles], axis=1
            )
        here = lax.div(t, 2) * LANES
        odd = lax.rem(t, 2) == 1
        for p in range(3):
            out = []
            for h in range(2):
                at = pl.multiple_of(here + (p * dm + h * half), LANES)
                v = R.bqf[:, pl.ds(at, LANES)]
                out.append(jnp.where(odd, v[:, HD:], v[:, :HD]))
            R.bq[:, p * hw : (p + 1) * hw] = jnp.concatenate(out, axis=1)
        for j in range(fw // LANES):
            r = t * (fw // LANES) + j
            v = wq[lax.div(r, 2 * nt), lax.rem(lax.div(r, 2), nt), lax.rem(r, 2), :, qc:]
            R.bu[:, j * LANES : (j + 1) * LANES] = v.astype(f32)[7:8]

    def turned(field, b, sign):
        down = pltpu.roll(field, hw - ROT // 2, 1)
        up = pltpu.roll(field, ROT // 2, 1)
        return field * cos_t[b] + sign * (down * low_t[b] + up * high_t[b])

    def qkv_step(i, _):
        b = block(i)
        h = hat[b]
        n1[b] = (h * gains[0:1] + gains[1:2]).astype(bf)
        n2[b] = (h * gains[2:3] + gains[3:4]).astype(bf)
        w = R.wq[:, :, :, :, 0:qc].reshape(dm, qc)
        qkv = mm(n1[b], w, NN) + R.bq[...]
        q = turned(qkv[:, 0:hw], b, 1.0).astype(bf).astype(f32) * scale
        k = turned(qkv[:, hw : 2 * hw], b, 1.0)
        v = qkv[:, 2 * hw : 3 * hw]
        for ref, value in ((qm, q), (km, k), (vm, v)):
            one, two = masked(value)
            ref[0, b] = one.astype(bf)
            ref[1, b] = two.astype(bf)
        return 0

    def attend_step(i, _):
        b = block(i)
        visible = place_row[...] <= place_col[b]
        ctx = jnp.zeros((QB, hw), f32)
        for h in range(2):
            s = jnp.where(visible, mm(qm[h, b], km[h], NT), NEG)
            top = jnp.max(s, axis=-1, keepdims=True)
            e = jnp.exp(s - top)
            total = jnp.sum(e, axis=-1, keepdims=True)
            ctx = ctx + mm(e.astype(bf), vm[h], NN) / total
            lse[h, b] = top + jnp.log(total)
        cx[b] = ctx.astype(bf)
        return 0

    def up_step(i, _):
        b = block(i)
        pre = mm(n2[b], R.wu[...].reshape(dm, fw), NN) + R.bu[...]
        bell = 0.5 * (1.0 + lax.erf(pre * ROOT_HALF))
        hid[b] = (pre * bell).astype(bf)
        slope[b] = bell + pre * jnp.exp(-0.5 * pre * pre) * INV_ROOT_TAU
        return 0

    def down_step(i, _):
        b = block(i)
        out = mm(hid[b], R.wd[...].reshape(dm, fw), NT)
        out = out + mm(cx[b], wo[...].reshape(hw, dm), NN)
        R.a0[pl.ds(2 * i, 2)] = out.astype(bf).reshape(2, width2, dm)
        return 0

    def back_step(i, _):
        b = block(i)
        g = act(R.gb, i)
        dpre = mm(g, R.wd[...].reshape(dm, fw), NN) * slope[b]
        su[...] += jnp.sum(dpre, axis=0, keepdims=True)
        dpre_s[b] = dpre.astype(bf)
        dn2 = mm(dpre_s[b], R.wu[...].reshape(dm, fw), NT)
        sums[2:3] += jnp.sum(dn2 * hat[b], axis=0, keepdims=True)
        sums[3:4] += jnp.sum(dn2, axis=0, keepdims=True)
        gs[b] = dn2 * gains[2:3]
        dctx = mm(g, wo[...].reshape(hw, dm), NT).astype(bf).astype(f32)
        prod = dctx * cx[b].astype(f32)
        for h, (d, p) in enumerate(zip(masked(dctx), masked(prod))):
            dcm[h, b] = d.astype(bf)
            delta[h, b] = jnp.sum(p, axis=-1, keepdims=True)
        return 0

    def rows_of(ref, i):
        return ref.at[lax.div(i, 2), pl.ds(pl.multiple_of(lax.rem(i, 2) * nz, nz), nz)]

    def outer_step(i, _):
        cols = pl.ds(pl.multiple_of(i * QB, QB), QB)
        gt = R.gb[:, :, cols].reshape(rows, QB)
        out = mm(gt, hid[...], TN)
        rows_of(R.md, i)[...] = out.astype(bf).reshape(nz, 2, piece, fw)
        wide = mm(cx[...], gt, TN).astype(bf)
        mo[:, :, :, cols] = wide.reshape(2, 2, piece, QB)
        return 0

    def outer_up_step(i, _):
        cols = pl.ds(pl.multiple_of(i * QB, QB), QB)
        out = mm(n2[:, cols], dpre_s[...], TN)
        rows_of(R.mu, i)[...] = out.astype(bf).reshape(nz, 2, piece, fw)
        return 0

    def attend_back_step(i, _):
        b = block(i)
        visible = place_row[...] <= place_col[b]
        acc = jnp.zeros((QB, hw), f32)
        for h in range(2):
            s = jnp.where(visible, mm(qm[h, b], km[h], NT), NEG)
            p = jnp.exp(s - lse[h, b])
            dp = mm(dcm[h, b], vm[h], NT)
            ds = (p * (dp - delta[h, b])).astype(bf)
            acc = acc + mm(ds, km[h], NN)
            dk[...] += mm(ds, qm[h, b], TN)
            dv[...] += mm(p.astype(bf), dcm[h, b], TN)
        dq[b] = acc * scale
        return 0

    def dqkv_step(i, _):
        b = block(i)
        fields = (turned(dq[b], b, -1.0), turned(dk[b], b, -1.0), dv[b])
        for j, v in enumerate(fields):
            sq[:, j * hw : (j + 1) * hw] += jnp.sum(v, axis=0, keepdims=True)
            dqkv[b, j * hw : (j + 1) * hw] = v.astype(bf)
        w = R.wq[:, :, :, :, 0:qc].reshape(dm, qc)
        dn1 = mm(dqkv[b], w, NT)
        sums[0:1] += jnp.sum(dn1 * hat[b], axis=0, keepdims=True)
        sums[1:2] += jnp.sum(dn1, axis=0, keepdims=True)
        out = (dn1 * gains[0:1] + gs[b]).astype(bf)
        R.a1[pl.ds(2 * i, 2)] = out.reshape(2, width2, dm)
        return 0

    def outer_qkv_step(i, _):
        cols = pl.ds(pl.multiple_of(i * QB, QB), QB)
        out = mm(n1[:, cols], dqkv[...], TN)
        view = R.mq.at[lax.div(i, 2), pl.ds(pl.multiple_of(lax.rem(i, 2) * nz, nz), nz), :, :, 0:qc]
        view[...] = out.astype(bf).reshape(nz, 2, piece, qc)
        return 0

    def sums_out():
        low = jnp.concatenate(
            [sq[:, j * hw : (j + 1) * hw] for j in range(3)]
            + [su[:, j * LANES : (j + 1) * LANES] for j in range(fw // LANES)]
            + [jnp.zeros((piece - 8 - 3 - fw // LANES, LANES), f32)],
            axis=0,
        )
        for r in range(nt * 4):
            one = sums[:, r * piece : (r + 1) * piece]
            one = jnp.concatenate([one, jnp.zeros((8, LANES - piece), f32)], axis=1)
            tile = jnp.concatenate([one, low], axis=0).astype(bf)
            R.mq[r // (2 * nt), (r // 2) % nt, r % 2, :, qc:] = tile

    vs = R.vs
    vs[...] = jnp.zeros_like(vs)
    for i, v in enumerate(vectors):
        vs[i : i + 1, 0 : v.shape[1]] = v[...].astype(f32)
    small = vs[...].astype(bf)
    loads[1].wait()
    for o in range(nt):
        pieces = []
        for p in range(3):
            base = p * dm + o * HD
            for at in (base, base + half):
                pieces.append(R.qo[:, at : at + HD])
        for j in range(3):
            R.pq[o, :, j * hw : (j + 1) * hw] = jnp.concatenate(pieces[2 * j : 2 * j + 2], axis=1)
        R.pq[o, :, qc:] = small
    for ref in (sums, sq, su, dk, dv):
        ref[...] = jnp.zeros_like(ref)
    loads[0].wait()
    loads[2].wait()

    greet(nz, xi, ki, zi, yi)

    swap_start(0)
    w1_start(0)
    load_g.wait()
    swap_start(1)
    first_hop(0)
    plane_start(3)
    for cp in loads_u:
        cp.wait()
    w1_start(1)
    for cp in loads_d:
        cp.wait()
    w1_start(2)
    lax.fori_loop(0, nt, table_step, 0)
    sums[4:5] = jnp.sum(R.go[...].astype(f32), axis=0, keepdims=True)
    hop(0, 1)
    w1_wait(0)
    plane_start(0)
    first_hop(1)
    hop(0, 2)
    hop(1, 1)
    w1_wait(1)
    plane_start(1)
    plane_forward(0)
    hop(0, 3)
    hop(1, 2)
    w1_wait(2)
    plane_start(2)
    plane_forward(3)
    all_in(0)
    lax.fori_loop(0, nblk, hat_step, 0)
    plane_wait(0)
    vectors_in()
    lax.fori_loop(0, nblk, qkv_step, 0)
    plane_forward(1)
    lax.fori_loop(0, nblk // 2, attend_step, 0)
    plane_forward(2)
    lax.fori_loop(nblk // 2, nblk, attend_step, 0)
    plane_wait(1)
    hop(1, 3)
    lax.fori_loop(0, nblk, up_step, 0)
    plane_wait(2)
    plane_wait(3)
    lax.fori_loop(0, nblk, down_step, 0)
    for z in range(nz):
        share(0, z).start()
    all_in(1)
    lax.fori_loop(0, nblk, back_step, 0)
    fold(0)
    rstart(0)
    lax.fori_loop(0, nblk, outer_step, 0)
    grad_start(2)
    ox1().start()
    oy1().start()
    lax.fori_loop(0, nblk, outer_up_step, 0)
    grad_start(1)
    rjoin(0)
    lax.fori_loop(0, nblk // 2, attend_back_step, 0)
    fold1(2)
    lax.fori_loop(nblk // 2, nblk, attend_back_step, 0)
    lax.fori_loop(0, nblk, dqkv_step, 0)
    for z in range(nz):
        share(1, z).start()
    lax.fori_loop(0, nblk, outer_qkv_step, 0)
    sums_out()
    grad_start(0)
    fold(1)
    rstart(1)
    fold1(1)
    fold2(2)
    rend(0)
    ox1().wait_recv()
    ro[0] = plus(ro[0], mo[xi, :, :, 0:half])
    oy2().start()
    oy1().wait_recv()
    ro[1] = plus(ro[1], mo[:, yi, :, half:dm])
    ox2().start()
    fold1(0)
    fold2(1)
    rjoin(1)
    fold2(0)
    rlast(0)

    x_own = R.xo[...].astype(f32)
    out_x[...] = (x_own + own[0] + (gains[4:5] + gains[5:6])).astype(bf)
    oy2().wait_recv()
    oo[:, 0:half] = so[0].astype(f32) + ro[0, yi].astype(f32)
    ox2().wait_recv()
    oo[:, half:dm] = so[1].astype(f32) + ro[1, xi].astype(f32)
    for w in (2, 1):
        for d in range(1, nt):
            tp(w, d, False).wait_recv()
        ref = (None, ou, od)[w]
        for o in range(nt):
            ref[:, o * fw : (o + 1) * fw] = chunks[w][o].astype(f32)
    hat_own, rstd_own = hats(x_own)

    rend(1)
    gsum = own[1]
    out_g[...] = (
        R.go[...].astype(f32)
        + rstd_own
        * (
            gsum
            - jnp.mean(gsum, axis=-1, keepdims=True)
            - hat_own * jnp.mean(gsum * hat_own, axis=-1, keepdims=True)
        )
    ).astype(bf)
    for d in range(1, nt):
        tp(0, d, False).wait_recv()
    cq = chunks[0]
    for j in range(3):
        for h in range(2):
            for o in range(0, nt, 2):
                lo = j * hw + h * HD
                both = jnp.concatenate([cq[o, :, lo : lo + HD], cq[o + 1, :, lo : lo + HD]], axis=1)
                at = j * dm + h * half + o * HD
                oq[:, at : at + hw] = both.astype(f32)
    for o in range(nt):
        osum[o] = cq[o, :, qc:].astype(f32)[0:16]

    for i in range(2):

        @pl.when(ki != yi)
        def _():
            swap(i).wait_send()
            rswap(i).wait_send()

        for d in range(1, nz):

            @pl.when(inside(zi - (d - 1)) & inside(zi + 1))
            def _():
                up_copy(i, d, zi - (d - 1)).wait_send()

            @pl.when(inside(zi + (d - 1)) & inside(zi - 1))
            def _():
                dn_copy(i, d, zi + (d - 1)).wait_send()

        for n in range(4):

            @pl.when(inside(zi + STEPS[n]))
            def _():
                rnear(i, n).wait_send()

        for up, step in ((True, 1), (False, -1)):

            @pl.when(inside(zi + 3 * step))
            def _():
                rfar(i, up).wait_send()

        for z in range(nz):
            cc_copy(i, z, ki).wait_send()
            share(i, z).wait_send()
    for w in range(3):
        for d in range(1, nt):
            w1(w, d, True).wait_send()
            tp(w, d, True).wait_send()
        x1(w).wait_send()
        for cp in y1(w):
            cp.wait_send()
        y2(w).wait_send()
        x2(w).wait_send()
    for w in range(4):
        plane_x(w, xi).wait_send()
        plane_y(w, yi).wait_send()
        forward_y(w, 1 - xi, yi).wait_send()
        forward_x(w, xi, 1 - yi).wait_send()
    ox1().wait_send()
    oy1().wait_send()
    oy2().wait_send()
    ox2().wait_send()


def finish_kernel(dm, nq, fw, *refs):
    big, sums, outs, small = refs[:6], refs[6], refs[7:13], refs[13:21]
    flat = refs[21]
    for a, b in zip(big, outs):
        b[...] = a[...]
    nt = sums.shape[0]
    half = dm // 2
    r = lax.axis_index("fsdp") * lax.axis_size("ctx") + lax.axis_index("ctx")
    total = sums[0, 0:8]
    for o in range(1, nt):
        total = total + sums[o, 0:8]
    for i, row in enumerate((0, 1, 2, 3, 4, 4)):
        small[i][...] = total[row : row + 1, 0 : small[i].shape[1]]
    flat[:, 3 * dm :] = jnp.zeros((1, LANES), jnp.float32)
    for j in range(3):
        for h in range(2):
            for o in range(0, nt, 2):
                pair = [sums[o + e, 8 + j : 9 + j, h * HD : (h + 1) * HD] for e in range(2)]
                at = j * dm + h * half + o * HD
                flat[:, at : at + 2 * HD] = jnp.concatenate(pair, axis=1)
    begin = r * nq
    chunk = lax.div(begin, LANES)
    wide = flat[:, pl.ds(pl.multiple_of(chunk * LANES, LANES), 2 * LANES)]
    shift = begin - chunk * LANES
    unit = math.gcd(nq, LANES)
    mine = wide[:, 0:nq]
    for at in range(unit, LANES, unit):
        mine = jnp.where(shift == at, wide[:, at : at + nq], mine)
    small[6][...] = mine
    per = fw // LANES
    row = 11 + lax.rem(r, per)
    small[7][...] = sums[lax.div(r, per), pl.ds(row, 1)]


def finish(arrays, sums, nq, fw, dm):
    vm = pl.BlockSpec(memory_space=pltpu.VMEM)
    f32 = jnp.float32
    shape = jax.ShapeDtypeStruct
    piece = arrays[2].shape[0]
    smalls = [piece] * 6 + [nq, LANES]
    return pl.pallas_call(
        functools.partial(finish_kernel, dm, nq, fw),
        out_shape=[shape(a.shape, a.dtype) for a in arrays] + [shape((1, n), f32) for n in smalls],
        in_specs=[vm] * 7,
        out_specs=[vm] * 14,
        scratch_shapes=[pltpu.VMEM((1, 3 * dm + LANES), f32)],
        compiler_params=pltpu.CompilerParams(vmem_limit_bytes=60 * 1024 * 1024),
    )(*arrays, sums)


def routed(
    layer_in,
    grad_out,
    pair_of_rank,
    ln1_gain,
    ln1_bias,
    ln2_gain,
    ln2_bias,
    w_qkv,
    b_qkv,
    w_out,
    b_out,
    w_up,
    b_up,
    w_down,
    b_down,
):
    f32 = jnp.float32
    bf = jnp.bfloat16
    nctx = lax.axis_size("ctx")
    nz = nctx // 2
    width2, dmodel = layer_in.shape[2:]
    ff = w_up.shape[1]
    piece = w_qkv.shape[0]
    plan = layer_plan(nz, width2, dmodel, ff, piece)
    vectors = (ln1_gain, ln1_bias, ln2_gain, ln2_bias, b_out, b_down, b_qkv, b_up)
    vm = pl.BlockSpec(memory_space=pltpu.VMEM)
    anywhere = pl.BlockSpec(memory_space=pl.ANY)
    shape = jax.ShapeDtypeStruct
    layer_out, grad_x, grad_qkv, grad_up, grad_down, grad_wout, sums = pl.pallas_call(
        functools.partial(layer_kernel, nz, tuple(plan)),
        out_shape=(
            shape((width2, dmodel), bf),
            shape((width2, dmodel), bf),
            shape((piece, 3 * dmodel), f32),
            shape((piece, ff), f32),
            shape((piece, ff), f32),
            shape((piece, dmodel), f32),
            shape((nctx, 16, LANES), f32),
        ),
        in_specs=[anywhere] * 6 + [vm] * 8 + [pl.BlockSpec(memory_space=pltpu.SMEM)],
        out_specs=(vm,) * 7,
        scratch_shapes=list(plan.values()),
        compiler_params=pltpu.CompilerParams(
            collective_id=0, has_side_effects=True, vmem_limit_bytes=60 * 1024 * 1024
        ),
    )(
        layer_in.reshape(width2, dmodel),
        grad_out.reshape(width2, dmodel),
        w_qkv,
        w_up,
        w_down,
        w_out,
        *[v.reshape(1, -1) for v in vectors],
        pair_of_rank,
    )
    done = finish(
        (layer_out, grad_x, grad_qkv, grad_up, grad_down, grad_wout),
        sums,
        b_qkv.shape[0],
        ff // nctx,
        dmodel,
    )
    layer_out, grad_x, grad_qkv, grad_up, grad_down, grad_wout = done[:6]
    vs = [v.reshape(-1) for v in done[6:]]
    return (
        layer_out.reshape(layer_in.shape),
        grad_x.reshape(layer_in.shape),
        vs[0],
        vs[1],
        vs[2],
        vs[3],
        grad_qkv,
        vs[6],
        grad_wout,
        vs[4],
        grad_up,
        vs[7],
        grad_down,
        vs[5],
    )


def solution(mesh):
    nctx = mesh.shape["ctx"]

    def pick(layer_in, *rest):
        heads = layer_in.shape[-1] // HD
        whole = heads % nctx == 0
        square = nctx % 2 == 0 and mesh.shape["fsdp"] == 4 and heads == 2 * nctx
        if square and layer_in.shape[1] == 1 and layer_in.shape[-1] == 8 * layer_in.shape[2] == nctx * layer_in.shape[2]:
            return routed(layer_in, *rest)
        return (head_shards if whole else shards)(layer_in, *rest)

    return jax.shard_map(
        pick,
        mesh=mesh,
        in_specs=(
            P("ctx", "fsdp", None, None),
            P("ctx", "fsdp", None, None),
            P(),
            P(("fsdp", "ctx")),
            P(("fsdp", "ctx")),
            P(("fsdp", "ctx")),
            P(("fsdp", "ctx")),
            P(("fsdp", "ctx"), None),
            P(("fsdp", "ctx")),
            P(("fsdp", "ctx"), None),
            P(("fsdp", "ctx")),
            P(("fsdp", "ctx"), None),
            P(("fsdp", "ctx")),
            P(("fsdp", "ctx"), None),
            P(("fsdp", "ctx")),
        ),
        out_specs=(
            P("ctx", "fsdp", None, None),
            P("ctx", "fsdp", None, None),
            P(("fsdp", "ctx")),
            P(("fsdp", "ctx")),
            P(("fsdp", "ctx")),
            P(("fsdp", "ctx")),
            P(("fsdp", "ctx"), None),
            P(("fsdp", "ctx")),
            P(("fsdp", "ctx"), None),
            P(("fsdp", "ctx")),
            P(("fsdp", "ctx"), None),
            P(("fsdp", "ctx")),
            P(("fsdp", "ctx"), None),
            P(("fsdp", "ctx")),
        ),
        check_vma=False,
    )
```

```python
import functools
import math
import types

import jax
import jax.numpy as jnp
from jax import lax
from jax.experimental import pallas as pl
from jax.experimental.pallas import tpu as pltpu
from jax.sharding import PartitionSpec as P

HD = 64
ROT = 16
LANES = 128


EPS = 1e-05
NEG = -1e30
ROOT_HALF = 0.7071067811865476
INV_ROOT_TAU = 0.3989422804014327


def norm_parts(xf, scale_weight, shift_bias):
    row_mean = jnp.mean(xf, axis=-1, keepdims=True)
    centred_input = xf - row_mean
    inverse_deviation = lax.rsqrt(
        jnp.mean(centred_input * centred_input, axis=-1, keepdims=True) + EPS
    )
    normalized_input = centred_input * inverse_deviation
    return (
        normalized_input * scale_weight.astype(jnp.float32) + shift_bias.astype(jnp.float32),
        normalized_input,
        inverse_deviation,
    )


def layer_norm_backward(norm_output_gradient, normalized_input, inverse_deviation, scale_weight):
    normalized_gradient = norm_output_gradient * scale_weight.astype(jnp.float32)
    return inverse_deviation * (
        normalized_gradient
        - jnp.mean(normalized_gradient, axis=-1, keepdims=True)
        - normalized_input
        * jnp.mean(normalized_gradient * normalized_input, axis=-1, keepdims=True)
    )


def gelu_value(u):
    return 0.5 * u * (1.0 + lax.erf(u * ROOT_HALF))


def gelu_slope(u):
    return 0.5 * (1.0 + lax.erf(u * ROOT_HALF)) + u * jnp.exp(-0.5 * u * u) * INV_ROOT_TAU


def rotate(field, place, sign):
    half = ROT // 2
    freqs = jnp.exp(jnp.arange(half).astype(jnp.float32) * (-2.0 * math.log(10000.0) / ROT))
    angle = place.astype(jnp.float32)[..., None] * freqs
    cosine = jnp.cos(angle)[..., None, :]
    sine = sign * jnp.sin(angle)[..., None, :]
    first = field[..., :half]
    second = field[..., half:ROT]
    return jnp.concatenate(
        [first * cosine - second * sine, second * cosine + first * sine, field[..., rot_end() :]],
        axis=-1,
    )


def rot_end():
    return ROT


def leading(field, letters):
    return "n" + letters if field.ndim == 5 else letters


def product(left, left_letters, right, right_letters, result):
    form = leading(left, left_letters) + "," + leading(right, right_letters) + "->" + result
    return jnp.einsum(form, left, right, preferred_element_type=jnp.float32)


def selectors(sel):
    return (sel[:, None, None, None, None], sel[:, None, None, None], sel[:, None])


def visibility(sel, qpa, qpb, kpa, kpb):
    chosen = sel[:, None]
    key_place = jnp.where(chosen, kpa, kpb)
    query_place = jnp.where(chosen, qpa, qpb)
    return (key_place[:, None, :] <= query_place[:, :, None])[:, None, None]


def online_update(state, qa, qb, ka, kb, va, vb, qpa, qpb, kpa, kpb, sel, with_first, scale):
    top_a, total_a, acc_a, top_b, total_b, acc_b = state
    sel5, sel4, sel2 = selectors(sel)
    query_two = jnp.where(sel5, qa, qb)
    key_two = jnp.where(sel5, ka, kb)
    value_two = jnp.where(sel5, va, vb)
    visible = visibility(sel, qpa, qpb, kpa, kpb)
    score = jnp.where(visible, product(query_two, "sqhd", key_two, "skhd", "nshqk") * scale, NEG)
    peak_a = jnp.max(jnp.where(sel5, score, NEG), axis=(0, 4))
    peak_b = jnp.max(jnp.where(sel5, NEG, score), axis=(0, 4))
    if with_first:
        score_one = product(qb, "sqhd", ka, "skhd", "nshqk") * scale
        peak_b = jnp.maximum(peak_b, jnp.max(score_one, axis=(0, 4)))
    new_a = jnp.maximum(top_a, peak_a)
    new_b = jnp.maximum(top_b, peak_b)
    lifted = jnp.where(sel5, new_a[..., None], new_b[..., None])
    weight = jnp.where(visible, jnp.exp(score - lifted), 0.0)
    mixed = product(weight.astype(jnp.bfloat16), "shqk", value_two, "skhd", "nshqd")
    mass = jnp.sum(weight, axis=4)
    add_total_a = jnp.sum(jnp.where(sel4, mass, 0.0), axis=0)
    add_total_b = jnp.sum(jnp.where(sel4, 0.0, mass), axis=0)
    add_acc_a = jnp.sum(jnp.where(sel5, mixed, 0.0), axis=0)
    add_acc_b = jnp.sum(jnp.where(sel5, 0.0, mixed), axis=0)
    if with_first:
        weight_one = jnp.exp(score_one - new_b[..., None])
        add_total_b = add_total_b + jnp.sum(weight_one, axis=(0, 4))
        add_acc_b = add_acc_b + product(weight_one.astype(jnp.bfloat16), "shqk", va, "skhd", "shqd")
    decay_a = jnp.exp(top_a - new_a)
    decay_b = jnp.exp(top_b - new_b)
    return (
        new_a,
        total_a * decay_a + add_total_a,
        acc_a * decay_a[..., None] + add_acc_a,
        new_b,
        total_b * decay_b + add_total_b,
        acc_b * decay_b[..., None] + add_acc_b,
    )


def pair_terms(
    qa,
    qb,
    ka,
    kb,
    va,
    vb,
    da,
    db,
    lsea,
    lseb,
    dela,
    delb,
    qpa,
    qpb,
    kpa,
    kpb,
    sel,
    with_first,
    scale,
):
    sel5, sel4, sel2 = selectors(sel)
    query_two = jnp.where(sel5, qa, qb)
    key_two = jnp.where(sel5, ka, kb)
    value_two = jnp.where(sel5, va, vb)
    dctx_two = jnp.where(sel5, da, db)
    lse_two = jnp.where(sel4, lsea, lseb)
    delta_two = jnp.where(sel4, dela, delb)
    visible = visibility(sel, qpa, qpb, kpa, kpb)
    score = jnp.where(visible, product(query_two, "sqhd", key_two, "skhd", "nshqk") * scale, NEG)
    prob = jnp.exp(score - lse_two[..., None])
    dprob = product(dctx_two, "sqhd", value_two, "skhd", "nshqk")
    dscore = (scale * prob * (dprob - delta_two[..., None])).astype(jnp.bfloat16)
    first_ds = None
    first_prob = None
    if with_first:
        score_one = product(qb, "sqhd", ka, "skhd", "nshqk") * scale
        prob_one = jnp.exp(score_one - lseb[..., None])
        dprob_one = product(db, "sqhd", va, "skhd", "nshqk")
        first_ds = (scale * prob_one * (dprob_one - delb[..., None])).astype(jnp.bfloat16)
        first_prob = prob_one.astype(jnp.bfloat16)
    return (first_ds, first_prob, dscore, prob.astype(jnp.bfloat16))


def query_grads(terms, ka, kb, sel):
    sel5, sel4, sel2 = selectors(sel)
    key_two = jnp.where(sel5, ka, kb)
    dq_two = product(terms[2], "shqk", key_two, "skhd", "nsqhd")
    dq_a = jnp.where(sel5, dq_two, 0.0)
    dq_b = jnp.where(sel5, 0.0, dq_two)
    if terms[0] is not None:
        dq_b = dq_b + product(terms[0], "shqk", ka, "skhd", "nsqhd")
    return (dq_a, dq_b)


def key_grads(terms, qa, qb, da, db, sel):
    sel5, sel4, sel2 = selectors(sel)
    query_two = jnp.where(sel5, qa, qb)
    dctx_two = jnp.where(sel5, da, db)
    dk_two = product(terms[2], "shqk", query_two, "sqhd", "nskhd")
    dv_two = product(terms[3], "shqk", dctx_two, "sqhd", "nskhd")
    dk_a = jnp.where(sel5, dk_two, 0.0)
    dk_b = jnp.where(sel5, 0.0, dk_two)
    dv_a = jnp.where(sel5, dv_two, 0.0)
    dv_b = jnp.where(sel5, 0.0, dv_two)
    if terms[0] is not None:
        dk_a = dk_a + product(terms[0], "shqk", qb, "sqhd", "nskhd")
        dv_a = dv_a + product(terms[1], "shqk", db, "sqhd", "nskhd")
    return (dk_a, dk_b, dv_a, dv_b)


def tdot(left, right):
    return lax.dot_general(
        left, right, (((0,), (0,)), ((), ())), preferred_element_type=jnp.float32
    )


def rdot(left, right):
    return lax.dot_general(
        left, right, (((1,), (1,)), ((), ())), preferred_element_type=jnp.float32
    )


def shards(
    layer_in,
    grad_out,
    pair_of_rank,
    ln1_gain,
    ln1_bias,
    ln2_gain,
    ln2_bias,
    w_qkv,
    b_qkv,
    w_out,
    b_out,
    w_up,
    b_up,
    w_down,
    b_down,
):
    f32 = jnp.float32
    bf = jnp.bfloat16
    nctx = lax.axis_size("ctx")
    mine = pair_of_rank[lax.axis_index("ctx")]
    seqs = layer_in.shape[1]
    width2 = layer_in.shape[2]
    dmodel = layer_in.shape[3]
    blk = width2 // 2
    rows = seqs * width2
    heads = dmodel // HD
    scale = 1.0 / math.sqrt(HD)
    offsets = jnp.arange(blk, dtype=jnp.int32)
    place_a = mine * blk + offsets
    place_b = (2 * nctx - 1 - mine) * blk + offsets
    places = jnp.concatenate([place_a, place_b])
    params = (
        ln1_gain,
        ln1_bias,
        ln2_gain,
        ln2_bias,
        w_qkv,
        b_qkv,
        w_out,
        b_out,
        w_up,
        b_up,
        w_down,
        b_down,
    )
    full = (
        lax.all_gather(params[0], ("fsdp", "ctx"), axis=0, tiled=True),
        lax.all_gather(params[1], ("fsdp", "ctx"), axis=0, tiled=True),
        lax.all_gather(params[2], ("fsdp", "ctx"), axis=0, tiled=True),
        lax.all_gather(params[3], ("fsdp", "ctx"), axis=0, tiled=True),
        lax.all_gather(params[4], ("fsdp", "ctx"), axis=0, tiled=True),
        lax.all_gather(params[5], ("fsdp", "ctx"), axis=0, tiled=True),
        lax.all_gather(params[6], ("fsdp", "ctx"), axis=0, tiled=True),
        lax.all_gather(params[7], ("fsdp", "ctx"), axis=0, tiled=True),
        lax.all_gather(params[8], ("fsdp", "ctx"), axis=0, tiled=True),
        lax.all_gather(params[9], ("fsdp", "ctx"), axis=0, tiled=True),
        lax.all_gather(params[10], ("fsdp", "ctx"), axis=0, tiled=True),
        lax.all_gather(params[11], ("fsdp", "ctx"), axis=0, tiled=True),
    )
    xf = layer_in.reshape(rows, dmodel).astype(f32)
    norm1, hat1, rstd1 = norm_parts(xf, full[0], full[1])
    norm2, hat2, rstd2 = norm_parts(xf, full[2], full[3])
    norm1 = norm1.astype(bf)
    norm2 = norm2.astype(bf)
    qkv = jnp.dot(norm1, full[4], preferred_element_type=f32) + full[5].astype(f32)
    query = rotate(qkv[:, :dmodel].reshape(seqs, width2, heads, HD), places, 1.0).astype(bf)
    key = rotate(qkv[:, dmodel : 2 * dmodel].reshape(seqs, width2, heads, HD), places, 1.0).astype(
        bf
    )
    value = qkv[:, 2 * dmodel :].reshape(seqs, width2, heads, HD).astype(bf)
    query_a = query[:, :blk]
    query_b = query[:, blk:]
    key_b = key[:, blk:]
    value_b = value[:, blk:]
    lone = jnp.zeros((1,), dtype=bool)
    empty_top = jnp.full((seqs, heads, blk), NEG, f32)
    empty_total = jnp.zeros((seqs, heads, blk), f32)
    empty_acc = jnp.zeros((seqs, heads, blk, HD), f32)
    state = (empty_top, empty_total, empty_acc, empty_top, empty_total, empty_acc)
    state = online_update(
        state,
        query_a,
        query_b,
        key_b[None],
        key_b[None],
        value_b[None],
        value_b[None],
        place_a,
        place_b,
        place_b[None],
        place_b[None],
        lone,
        False,
        scale,
    )

    def key_parts(kpiece, vpiece, first):
        count = kpiece.shape[0]
        pairs = lax.dynamic_slice_in_dim(pair_of_rank, first, count)
        keys = kpiece.reshape(count, seqs, width2, heads, HD)
        values = vpiece.reshape(count, seqs, width2, heads, HD)
        kplace_a = pairs[:, None] * blk + offsets[None, :]
        kplace_b = (2 * nctx - 1 - pairs)[:, None] * blk + offsets[None, :]
        return (
            keys[:, :, :blk],
            keys[:, :, blk:],
            values[:, :, :blk],
            values[:, :, blk:],
            kplace_a,
            kplace_b,
            pairs,
        )

    key_send = key.reshape(1, seqs, width2, dmodel)
    value_send = value.reshape(1, seqs, width2, dmodel)
    ka, kb, va, vb, kpa, kpb, pairs = key_parts(
        lax.all_gather(key_send, "ctx", axis=0, tiled=True),
        lax.all_gather(value_send, "ctx", axis=0, tiled=True),
        jnp.int32(0),
    )
    state = online_update(
        state,
        query_a,
        query_b,
        ka,
        kb,
        va,
        vb,
        place_a,
        place_b,
        kpa,
        kpb,
        pairs <= mine,
        True,
        scale,
    )
    top_a, total_a, acc_a, top_b, total_b, acc_b = state
    context4 = jnp.concatenate([acc_a / total_a[..., None], acc_b / total_b[..., None]], axis=2)
    lse = jnp.concatenate([top_a + jnp.log(total_a), top_b + jnp.log(total_b)], axis=2)
    context = context4.transpose(0, 2, 1, 3).reshape(rows, dmodel).astype(bf)
    attn = jnp.dot(context, full[6], preferred_element_type=f32) + full[7].astype(f32)
    pre = jnp.dot(norm2, full[8], preferred_element_type=f32) + full[9].astype(f32)
    hidden = gelu_value(pre).astype(bf)
    mlp = rdot(hidden, full[10]) + full[11].astype(f32)
    layer_out = (xf + attn + mlp).astype(bf).reshape(layer_in.shape)
    again = (
        lax.all_gather(params[0], ("fsdp", "ctx"), axis=0, tiled=True),
        lax.all_gather(params[1], ("fsdp", "ctx"), axis=0, tiled=True),
        lax.all_gather(params[2], ("fsdp", "ctx"), axis=0, tiled=True),
        lax.all_gather(params[3], ("fsdp", "ctx"), axis=0, tiled=True),
        lax.all_gather(params[4], ("fsdp", "ctx"), axis=0, tiled=True),
        lax.all_gather(params[5], ("fsdp", "ctx"), axis=0, tiled=True),
        lax.all_gather(params[6], ("fsdp", "ctx"), axis=0, tiled=True),
        lax.all_gather(params[7], ("fsdp", "ctx"), axis=0, tiled=True),
        lax.all_gather(params[8], ("fsdp", "ctx"), axis=0, tiled=True),
        lax.all_gather(params[9], ("fsdp", "ctx"), axis=0, tiled=True),
        lax.all_gather(params[10], ("fsdp", "ctx"), axis=0, tiled=True),
        lax.all_gather(params[11], ("fsdp", "ctx"), axis=0, tiled=True),
    )
    grad_b = grad_out.reshape(rows, dmodel)
    grad_f = grad_b.astype(f32)
    dhidden = jnp.dot(grad_b, again[10], preferred_element_type=f32)
    dpre = dhidden * gelu_slope(pre)
    dpre_b = dpre.astype(bf)
    dnorm2 = rdot(dpre_b, again[8])
    dcontext = rdot(grad_b, again[6]).astype(bf)
    dctx4 = dcontext.reshape(seqs, width2, heads, HD)
    delta = jnp.sum(
        dctx4.astype(f32) * context.reshape(seqs, width2, heads, HD).astype(f32), axis=-1
    ).transpose(0, 2, 1)
    dctx_a = dctx4[:, :blk]
    dctx_b = dctx4[:, blk:]
    lse_a = lse[..., :blk]
    lse_b = lse[..., blk:]
    delta_a = delta[..., :blk]
    delta_b = delta[..., blk:]
    own = pair_terms(
        query_b,
        query_b,
        key_b[None],
        key_b[None],
        value_b[None],
        value_b[None],
        dctx_b,
        dctx_b,
        lse_b,
        lse_b,
        delta_b,
        delta_b,
        place_b,
        place_b,
        place_b[None],
        place_b[None],
        lone,
        False,
        scale,
    )
    own_dq = query_grads(own, key_b[None], key_b[None], lone)[1][0]
    own_keys = key_grads(own, query_b, query_b, dctx_b, dctx_b, lone)
    gathered = (
        lax.all_gather(key_send, "ctx", axis=0, tiled=True),
        lax.all_gather(value_send, "ctx", axis=0, tiled=True),
    )
    groups = math.gcd(nctx, 8)
    per = nctx // groups

    def group_terms(args):
        kpiece, vpiece, first = args
        ka, kb, va, vb, kpa, kpb, pairs = key_parts(kpiece, vpiece, first)
        sel = pairs <= mine
        terms = pair_terms(
            query_a,
            query_b,
            ka,
            kb,
            va,
            vb,
            dctx_a,
            dctx_b,
            lse_a,
            lse_b,
            delta_a,
            delta_b,
            place_a,
            place_b,
            kpa,
            kpb,
            sel,
            True,
            scale,
        )
        dq_a, dq_b = query_grads(terms, ka, kb, sel)
        return (terms, jnp.sum(dq_a, axis=0), jnp.sum(dq_b, axis=0))

    grouped = lax.map(
        group_terms,
        (
            gathered[0].reshape(groups, per, seqs, width2, dmodel),
            gathered[1].reshape(groups, per, seqs, width2, dmodel),
            jnp.arange(groups, dtype=jnp.int32) * per,
        ),
    )
    terms_all = tuple((part.reshape((nctx,) + part.shape[2:]) for part in grouped[0]))
    dq_a = jnp.sum(grouped[1], axis=0)
    dq_b = jnp.sum(grouped[2], axis=0)
    pairs = pair_of_rank
    sliced = tuple(
        (lax.slice_in_dim(part, 0, 1 * lax.axis_size("ctx"), axis=0) for part in terms_all)
    )
    dk_a, dk_b, dv_a, dv_b = key_grads(sliced, query_a, query_b, dctx_a, dctx_b, pairs <= mine)
    dkey = jnp.concatenate([dk_a, dk_b], axis=2).reshape(
        1 * lax.axis_size("ctx"), seqs, width2, dmodel
    )
    dval = jnp.concatenate([dv_a, dv_b], axis=2).reshape(
        1 * lax.axis_size("ctx"), seqs, width2, dmodel
    )
    kv_grad = lax.psum_scatter(
        jnp.concatenate([dkey, dval], axis=-1), "ctx", scatter_dimension=0, tiled=True
    )
    dkey = kv_grad[0, :, :, :dmodel].reshape(seqs, width2, heads, HD)
    dval = kv_grad[0, :, :, dmodel:].reshape(seqs, width2, heads, HD)
    zero_half = jnp.zeros((seqs, blk, heads, HD), f32)
    dquery = jnp.concatenate([dq_a, dq_b + own_dq], axis=1)
    dkey = dkey + jnp.concatenate([zero_half, own_keys[1][0]], axis=1)
    dval = dval + jnp.concatenate([zero_half, own_keys[3][0]], axis=1)
    dqkv = jnp.concatenate(
        [
            rotate(dquery, places, -1.0).reshape(rows, dmodel),
            rotate(dkey, places, -1.0).reshape(rows, dmodel),
            dval.reshape(rows, dmodel),
        ],
        axis=1,
    )
    dqkv_b = dqkv.astype(bf)
    dnorm1 = rdot(dqkv_b, again[4])
    grad_x = (
        (
            grad_f
            + layer_norm_backward(dnorm1, hat1, rstd1, again[0])
            + layer_norm_backward(dnorm2, hat2, rstd2, again[2])
        )
        .astype(bf)
        .reshape(layer_in.shape)
    )
    vectors = (
        lax.psum_scatter(
            jnp.sum(dnorm1 * hat1, axis=0), ("fsdp", "ctx"), scatter_dimension=0, tiled=True
        ),
        lax.psum_scatter(jnp.sum(dnorm1, axis=0), ("fsdp", "ctx"), scatter_dimension=0, tiled=True),
        lax.psum_scatter(
            jnp.sum(dnorm2 * hat2, axis=0), ("fsdp", "ctx"), scatter_dimension=0, tiled=True
        ),
        lax.psum_scatter(jnp.sum(dnorm2, axis=0), ("fsdp", "ctx"), scatter_dimension=0, tiled=True),
        lax.psum_scatter(jnp.sum(dqkv, axis=0), ("fsdp", "ctx"), scatter_dimension=0, tiled=True),
        lax.psum_scatter(jnp.sum(grad_f, axis=0), ("fsdp", "ctx"), scatter_dimension=0, tiled=True),
        lax.psum_scatter(jnp.sum(dpre, axis=0), ("fsdp", "ctx"), scatter_dimension=0, tiled=True),
    )
    weights = (
        lax.psum_scatter(tdot(norm1, dqkv_b), ("fsdp", "ctx"), scatter_dimension=0, tiled=True),
        lax.psum_scatter(tdot(context, grad_b), ("fsdp", "ctx"), scatter_dimension=0, tiled=True),
        lax.psum_scatter(tdot(norm2, dpre_b), ("fsdp", "ctx"), scatter_dimension=0, tiled=True),
        lax.psum_scatter(tdot(grad_b, hidden), ("fsdp", "ctx"), scatter_dimension=0, tiled=True),
    )
    return (
        layer_out,
        grad_x,
        vectors[0],
        vectors[1],
        vectors[2],
        vectors[3],
        weights[0],
        vectors[4],
        weights[1],
        vectors[5],
        weights[2],
        vectors[6],
        weights[3],
        vectors[5],
    )


def span(lead, cols):
    return jnp.arange(lead, dtype=jnp.int32)[:, None] if cols else jnp.arange(lead, dtype=jnp.int32)


def turn(field, cosine, sine_low, sine_high):
    half = ROT // 2
    down = jnp.concatenate([field[:, half:], field[:, :half]], axis=1)
    up = jnp.concatenate([field[:, -half:], field[:, :-half]], axis=1)
    return field * cosine + down * sine_low + up * sine_high


def turn_tables(places, width):
    half = ROT // 2
    lane = jnp.arange(width, dtype=jnp.int32) % HD
    freqs = jnp.exp((lane % half).astype(jnp.float32) * (-2.0 * math.log(10000.0) / ROT))
    angle = places.astype(jnp.float32)[:, None] * freqs[None, :]
    cosine = jnp.where(lane < ROT, jnp.cos(angle), 1.0)
    sine = jnp.sin(angle)
    sine_low = jnp.where(lane < half, -sine, 0.0)
    sine_high = jnp.where((lane >= half) & (lane < ROT), sine, 0.0)
    return cosine, sine_low, sine_high


def headed(field, count):
    return field.reshape(field.shape[0], count, HD).transpose(1, 0, 2)


def joined(field):
    return field.transpose(1, 0, 2).reshape(field.shape[1], -1)


def bdot(form, left, right):
    return jnp.einsum(form, left, right, preferred_element_type=jnp.float32)


def head_shards(
    layer_in,
    grad_out,
    pair_of_rank,
    ln1_gain,
    ln1_bias,
    ln2_gain,
    ln2_bias,
    w_qkv,
    b_qkv,
    w_out,
    b_out,
    w_up,
    b_up,
    w_down,
    b_down,
):
    f32 = jnp.float32
    bf = jnp.bfloat16
    both = ("fsdp", "ctx")
    nctx = lax.axis_size("ctx")
    nf = lax.axis_size("fsdp")
    ndev = nctx * nf
    c = lax.axis_index("ctx")
    seqs, width2, dmodel = layer_in.shape[1:]
    blk = width2 // 2
    own_rows = seqs * width2
    ff = w_up.shape[1]
    hloc = dmodel // HD // nctx
    qw = hloc * HD
    fw = ff // nctx
    piece = dmodel // ndev
    scale = 1.0 / math.sqrt(HD)

    x_all = lax.all_gather(layer_in.reshape(own_rows, dmodel), "ctx", axis=0, tiled=True)
    def columns(parts):
        packed = jnp.concatenate([p.reshape(piece, nctx, -1) for p in parts], axis=-1)
        packed = packed.transpose(1, 0, 2)
        got = lax.all_to_all(packed, "ctx", split_axis=0, concat_axis=0, tiled=True)
        return got.reshape(nctx * piece, -1)

    wq = w_qkv.reshape(piece, 3, nctx, qw).transpose(0, 2, 1, 3)
    vec = jnp.concatenate([ln1_gain, ln1_bias, ln2_gain, ln2_bias, b_out, b_down, b_qkv, b_up])
    vw = LANES * -(-vec.shape[0] // (piece * LANES))
    vec_pad = jnp.pad(vec, (0, piece * vw - vec.shape[0])).reshape(piece, 1, vw)
    vec_pad = jnp.broadcast_to(vec_pad, (piece, nctx, vw))
    cols = lax.all_gather(columns([wq, w_up, w_down, vec_pad]), "fsdp", axis=0, tiled=True)
    g_own = grad_out.reshape(own_rows, dmodel)
    cols, g_send = lax.optimization_barrier((cols, g_own))
    got = cols[:, 3 * qw + 2 * fw :].reshape(ndev, piece * vw)
    cuts = [piece] * 6 + [b_qkv.shape[0], b_up.shape[0]]
    fulls = []
    at = 0
    for cut in cuts:
        fulls.append(got[:, at : at + cut].reshape(-1).astype(f32))
        at += cut
    gain1, bias1, gain2, bias2, bo, bd, bq, bu = fulls
    bq_c = lax.dynamic_slice_in_dim(bq.reshape(3, nctx, qw), c, 1, axis=1).reshape(1, 3 * qw)
    bu_c = lax.dynamic_slice_in_dim(bu, c * fw, fw).reshape(1, fw)
    wq_c = cols[:, : 3 * qw]
    wu_c = cols[:, 3 * qw : 3 * qw + fw]
    wd_c = cols[:, 3 * qw + fw : 3 * qw + 2 * fw]
    there = [((nf * cc + f) , f * nctx + cc) for f in range(nf) for cc in range(nctx)]
    back = [(b, a) for a, b in there]
    wo_c = lax.all_gather(lax.ppermute(w_out, both, there), "fsdp", axis=0, tiled=True)
    g_all = lax.all_gather(g_send, "ctx", axis=0, tiled=True)

    rows = x_all.shape[0]
    offsets = jnp.arange(blk, dtype=jnp.int32)
    slot_a = pair_of_rank[:, None] * blk + offsets[None, :]
    slot_b = (2 * nctx - 1 - pair_of_rank)[:, None] * blk + offsets[None, :]
    slots = jnp.concatenate([slot_a, slot_b], axis=1)[:, None, :]
    places = jnp.broadcast_to(slots, (nctx, seqs, width2)).reshape(rows)
    group = jnp.broadcast_to(span(seqs, False)[None, :, None], (nctx, seqs, width2)).reshape(rows)

    def hat_of(xf):
        row_mean = jnp.mean(xf, axis=-1, keepdims=True)
        centred = xf - row_mean
        rstd = lax.rsqrt(jnp.mean(centred * centred, axis=-1, keepdims=True) + EPS)
        return centred * rstd, rstd

    hat, _ = hat_of(x_all.astype(f32))
    norm1 = (hat * gain1 + bias1).astype(bf)
    norm2 = (hat * gain2 + bias2).astype(bf)
    qkv = jnp.dot(norm1, wq_c, preferred_element_type=f32) + bq_c
    cosine, sine_low, sine_high = turn_tables(places, qw)
    query = headed(turn(qkv[:, :qw], cosine, sine_low, sine_high).astype(bf), hloc)
    key = headed(turn(qkv[:, qw : 2 * qw], cosine, sine_low, sine_high).astype(bf), hloc)
    value = headed(qkv[:, 2 * qw :].astype(bf), hloc)
    visible = places[None, :] <= places[:, None]
    if seqs > 1:
        visible = visible & (group[None, :] == group[:, None])
    score = jnp.where(visible[None], bdot("hqd,hkd->hqk", query, key) * scale, NEG)
    top = jnp.max(score, axis=-1, keepdims=True)
    weight = jnp.exp(score - top)
    total = jnp.sum(weight, axis=-1, keepdims=True)
    mixed = bdot("hqk,hkd->hqd", weight.astype(bf), value)
    context = (mixed / total).astype(bf)
    lse = top + jnp.log(total)
    ctx_c = joined(context)

    pre = jnp.dot(norm2, wu_c, preferred_element_type=f32) + bu_c
    hidden = gelu_value(pre).astype(bf)
    part = rdot(hidden, wd_c) + jnp.dot(ctx_c, wo_c, preferred_element_type=f32)
    fwd = lax.all_to_all(
        part.astype(bf).reshape(nctx, own_rows, dmodel), "ctx", split_axis=0, concat_axis=0, tiled=True
    )
    fwd = jnp.sum(fwd.astype(f32), axis=0)
    x_own = layer_in.reshape(own_rows, dmodel).astype(f32)
    layer_out = (x_own + fwd + (bo + bd)).astype(bf).reshape(layer_in.shape)

    dhidden = jnp.dot(g_all, wd_c, preferred_element_type=f32)
    dpre = dhidden * gelu_slope(pre)
    dpre_b = dpre.astype(bf)
    dnorm2 = rdot(dpre_b, wu_c)
    dctx = headed(rdot(g_all, wo_c).astype(bf), hloc)
    delta = jnp.sum(dctx.astype(f32) * context.astype(f32), axis=-1, keepdims=True)
    prob = jnp.exp(score - lse)
    dprob = bdot("hqd,hkd->hqk", dctx, value)
    ds = (scale * prob * (dprob - delta)).astype(bf)
    dquery = joined(bdot("hqk,hkd->hqd", ds, key))
    dkey = joined(bdot("hqk,hqd->hkd", ds, query))
    dvalue = joined(bdot("hqk,hqd->hkd", prob.astype(bf), dctx))
    dqkv = jnp.concatenate(
        [
            turn(dquery, cosine, -sine_low, -sine_high),
            turn(dkey, cosine, -sine_low, -sine_high),
            dvalue,
        ],
        axis=1,
    )
    dqkv_b = dqkv.astype(bf)
    dnorm1 = rdot(dqkv_b, wq_c)
    gsum = (dnorm1 * gain1 + dnorm2 * gain2).astype(bf)
    gsum = lax.psum_scatter(gsum, "ctx", scatter_dimension=0, tiled=True).astype(f32)
    hat_own, rstd_own = hat_of(x_own)
    g_ownf = g_own.astype(f32)
    grad_x = (
        g_ownf
        + rstd_own
        * (
            gsum
            - jnp.mean(gsum, axis=-1, keepdims=True)
            - hat_own * jnp.mean(gsum * hat_own, axis=-1, keepdims=True)
        )
    ).astype(bf).reshape(layer_in.shape)

    sum_q = jnp.zeros((3, nctx, qw), f32)
    sum_q = lax.dynamic_update_slice_in_dim(
        sum_q, jnp.sum(dqkv, axis=0).reshape(3, 1, qw), c, axis=1
    ).reshape(ndev, -1)
    sum_u = lax.dynamic_update_slice_in_dim(
        jnp.zeros((ff,), f32), jnp.sum(dpre, axis=0), c * fw, axis=0
    ).reshape(ndev, -1)
    sums = [
        jnp.sum(dnorm1 * hat, axis=0).reshape(ndev, -1),
        jnp.sum(dnorm1, axis=0).reshape(ndev, -1),
        jnp.sum(dnorm2 * hat, axis=0).reshape(ndev, -1),
        jnp.sum(dnorm2, axis=0).reshape(ndev, -1),
        jnp.sum(g_ownf, axis=0).reshape(ndev, -1),
        sum_q,
        sum_u,
    ]
    sums = jnp.concatenate(sums, axis=1)
    sw = LANES * -(-sums.shape[1] // (piece * LANES))
    sums_pad = jnp.pad(sums, ((0, 0), (0, piece * sw - sums.shape[1]))).reshape(ndev * piece, sw)
    rows_out = tdot(ctx_c, g_all).astype(bf)
    wide = jnp.concatenate(
        [
            tdot(norm1, dqkv_b).astype(bf),
            tdot(norm2, dpre_b).astype(bf),
            tdot(g_all, hidden).astype(bf),
            sums_pad.astype(bf),
            rows_out.reshape(ndev * piece, -1),
        ],
        axis=1,
    )
    wide = lax.psum_scatter(wide, "fsdp", scatter_dimension=0, tiled=True)
    split = 3 * qw + 2 * fw + sw
    grad_wout = lax.ppermute(wide[:, split:].reshape(piece, dmodel), both, back).astype(f32)
    wide = lax.all_to_all(
        wide[:, :split].reshape(nctx, piece, split), "ctx", split_axis=0, concat_axis=0, tiled=True
    )
    sums = jnp.sum(wide[:, :, split - sw :].astype(f32), axis=0).reshape(-1)[: sums.shape[1]]
    wide = wide.transpose(1, 0, 2).astype(f32)
    grad_qkv = (
        wide[:, :, : 3 * qw].reshape(piece, nctx, 3, qw).transpose(0, 2, 1, 3).reshape(piece, -1)
    )
    grad_up = wide[:, :, 3 * qw : 3 * qw + fw].reshape(piece, ff)
    grad_down = wide[:, :, 3 * qw + fw : 3 * qw + 2 * fw].reshape(piece, ff)
    ends = [piece * i for i in range(6)] + [5 * piece + b_qkv.shape[0], sums.shape[0]]
    vs = [sums[a:b] for a, b in zip(ends[:-1], ends[1:])]
    return (
        layer_out,
        grad_x,
        vs[0],
        vs[1],
        vs[2],
        vs[3],
        grad_qkv,
        vs[5],
        grad_wout,
        vs[4],
        grad_up,
        vs[6],
        grad_down,
        vs[4],
    )


def mod_less(a, n):
    return jnp.where(a >= n, a - n, a)


def mesh_dev(xi, ki, zi, yi):
    return {"fsdp": xi * 2 + ki, "ctx": zi * 2 + yi}


def rcopy(src, dst, send, recv, where):
    return pltpu.make_async_remote_copy(
        src_ref=src,
        dst_ref=dst,
        send_sem=send,
        recv_sem=recv,
        device_id=where,
        device_id_type=pl.DeviceIdType.MESH,
    )


def greet(nz, xi, ki, zi, yi):
    t = ki * nz + zi
    nt = 2 * nz
    barrier = pltpu.get_barrier_semaphore()

    def hello(where):
        pl.semaphore_signal(barrier, inc=1, device_id=where, device_id_type=pl.DeviceIdType.MESH)

    for d in range(1, nt):
        o = mod_less(t + d, nt)
        hello(mesh_dev(xi, lax.div(o, nz), lax.rem(o, nz), yi))
    hello(mesh_dev(1 - xi, ki, zi, yi))
    hello(mesh_dev(xi, ki, zi, 1 - yi))

    @pl.when(ki != yi)
    def _():
        for z in range(nz):
            hello(mesh_dev(xi, yi, z, ki))

    return lambda: pl.semaphore_wait(barrier, jnp.where(ki != yi, nt + 1 + nz, nt + 1))


STEPS = (-2, -1, 1, 2)
DIRECT_OUT = (False, True)


NT = (((1,), (1,)), ((), ()))
TN = (((0,), (0,)), ((), ()))
NN = (((1,), (0,)), ((), ()))


def mm(left, right, form):
    return lax.dot_general(left, right, form, preferred_element_type=jnp.float32)


def layer_plan(nz, width2, dm, ff, piece):
    nt = 2 * nz
    fw = ff // nt
    rows = nt * width2
    qw = 6 * HD + LANES
    bf, f32 = jnp.bfloat16, jnp.float32
    vm = pltpu.VMEM
    dma = pltpu.SemaphoreType.DMA
    plan = dict(
        xo=vm((width2, dm), bf),
        go=vm((width2, dm), bf),
        qo=vm((piece, 3 * dm), bf),
        ld=dma((5 + 2 * nt,)),
        xb=vm((nt, width2, dm), bf),
        gb=vm((nt, width2, dm), bf),
        wq=vm((2, nt, 2, piece, qw), bf),
        wu=vm((2, nt, 2, piece, fw), bf),
        wd=vm((2, nt, 2, piece, fw), bf),
        wo=vm((2, 2, piece, dm), bf),
        pq=vm((nt, piece, qw), bf),
        pu=vm((nt, piece, fw), bf),
        pd=vm((nt, piece, fw), bf),
        vs=vm((piece, LANES), f32),
        gains=vm((8, dm), f32),
        bqf=vm((1, 3 * dm), f32),
        bq=vm((1, 6 * HD), f32),
        bu=vm((1, fw), f32),
        hat=vm((rows, dm), f32),
        n1=vm((rows, dm), bf),
        n2=vm((rows, dm), bf),
        qm=vm((2, rows, 2 * HD), bf),
        km=vm((2, rows, 2 * HD), bf),
        vm=vm((2, rows, 2 * HD), bf),
        dm=vm((2, rows, 2 * HD), bf),
        lse=vm((2, rows, 1), f32),
        delta=vm((2, rows, 1), f32),
        cx=vm((rows, 2 * HD), bf),
        hid=vm((rows, fw), bf),
        slope=vm((rows, fw), f32),
        dpre=vm((rows, fw), bf),
        gs=vm((rows, dm), f32),
        dq=vm((rows, 2 * HD), f32),
        dk=vm((rows, 2 * HD), f32),
        dv=vm((rows, 2 * HD), f32),
        dqkv=vm((rows, 6 * HD), bf),
        sums=vm((8, dm), f32),
        sq=vm((1, 6 * HD), f32),
        su=vm((1, fw), f32),
        a0=vm((nt, width2, dm), bf),
        a1=vm((nt, width2, dm), bf),
        mq=vm((2, nt, 2, piece, qw), bf),
        mu=vm((2, nt, 2, piece, fw), bf),
        md=vm((2, nt, 2, piece, fw), bf),
        mo=vm((2, 2, piece, dm), bf),
        ex=vm((2, nz, width2, dm), bf),
        rcv=vm((2, 5, width2, dm), bf),
        cmb=vm((2, 2, width2, dm), bf),
        fin=vm((2, width2, dm), bf),
        own=vm((2, width2, dm), f32),
        pcol=vm((rows, 1), jnp.int32),
        prow=vm((1, rows), jnp.int32),
        cos=vm((rows, 2 * HD), f32),
        low=vm((rows, 2 * HD), f32),
        high=vm((rows, 2 * HD), f32),
        ro=vm((2, 2, piece, dm // 2), bf),
        so=vm((2, piece, dm // 2), bf),
        sw_s=dma((2,)),
        sw_r=dma((2,)),
        rsw_s=dma((2,)),
        rsw_r=dma((2,)),
        up_s=dma((2, nz)),
        up_r=dma((2, nz)),
        dn_s=dma((2, nz)),
        dn_r=dma((2, nz)),
        cc_s=dma((2, nz)),
        cc_r=dma((2, nz)),
        rn_s=dma((2, 4)),
        rn_r=dma((2, 4)),
        rf_s=dma((2, 2)),
        rf_r=dma((2, 2)),
        rcc_s=dma((2, nz)),
        rcc_r=dma((2, nz)),
        w1_s=dma((3, nt)),
        w1_r=dma((3, nt)),
        tp_s=dma((3, nt)),
        tp_r=dma((3, nt)),
        xs_s=dma((4,)),
        xs_r=dma((4,)),
        ys_s=dma((4,)),
        ys_r=dma((4,)),
        fx_s=dma((4,)),
        fx_r=dma((4,)),
        fy_s=dma((4,)),
        fy_r=dma((4,)),
        x1_s=dma((4,)),
        x1_r=dma((4,)),
        x2_s=dma((4,)),
        x2_r=dma((4,)),
        y2_s=dma((4,)),
        y2_r=dma((4,)),
        y1_s=dma((4, 2)),
        y1_r=dma((4, 2)),
        got1_0=vm((2, nz, 2, piece, qw), bf),
        got1_1=vm((2, nz, 2, piece, fw), bf),
        got1_2=vm((2, nz, 2, piece, fw), bf),
        got2_0=vm((nt, piece, qw), bf),
        got2_1=vm((nt, piece, fw), bf),
        got2_2=vm((nt, piece, fw), bf),
        chunk_0=vm((nt, piece, qw), bf),
        chunk_1=vm((nt, piece, fw), bf),
        chunk_2=vm((nt, piece, fw), bf),
    )
    return plan


def layer_kernel(nz, names, *refs):
    f32, bf = jnp.float32, jnp.bfloat16
    (x_hbm, g_hbm, wq_hbm, wu_hbm, wd_hbm, wo_hbm) = refs[:6]
    vectors = refs[6:14]
    pairs = refs[14]
    (out_x, out_g, oq, ou, od, oo, osum) = refs[15:22]
    R = types.SimpleNamespace(**dict(zip(names, refs[22:])))

    f = lax.axis_index("fsdp")
    c = lax.axis_index("ctx")
    xi, ki = lax.div(f, 2), lax.rem(f, 2)
    zi, yi = lax.div(c, 2), lax.rem(c, 2)
    nt = 2 * nz
    t = ki * nz + zi
    width2, dm = R.xo.shape
    half = dm // 2
    rows = nt * width2
    fw = R.wu.shape[4]
    piece = R.wq.shape[3]
    qc = 6 * HD
    hw = 2 * HD
    QB = 2 * width2
    nblk = rows // QB
    RB = 2 * width2
    rblk = rows // RB
    scale = 1.0 / math.sqrt(HD)
    c_own = zi * 2 + yi

    xpeer = mesh_dev(1 - xi, ki, zi, yi)
    ypeer = mesh_dev(xi, ki, zi, 1 - yi)
    cpeer = mesh_dev(xi, 1 - ki, zi, yi)
    swapped = mesh_dev(xi, yi, zi, ki)
    acts = ((R.xo, R.xb), (R.go, R.gb))
    packs = ((R.pq, R.wq), (R.pu, R.wu), (R.pd, R.wd))
    mats = (R.wq, R.wu, R.wd)
    wo = R.wo

    ld = R.ld
    loads = [
        pltpu.make_async_copy(x_hbm, R.xo, ld.at[0]),
        pltpu.make_async_copy(wq_hbm, R.qo, ld.at[1]),
        pltpu.make_async_copy(wo_hbm, wo.at[xi, yi], ld.at[2]),
    ]
    loads_u = [
        pltpu.make_async_copy(wu_hbm.at[:, o * fw : (o + 1) * fw], R.pu.at[o], ld.at[5 + o])
        for o in range(nt)
    ]
    loads_d = [
        pltpu.make_async_copy(wd_hbm.at[:, o * fw : (o + 1) * fw], R.pd.at[o], ld.at[5 + nt + o])
        for o in range(nt)
    ]
    load_g = pltpu.make_async_copy(g_hbm, R.go, ld.at[3])
    for cp in loads + loads_u + loads_d + [load_g]:
        cp.start()

    def swap(i):
        src, dst = acts[i]
        return rcopy(src, dst.at[c_own], R.sw_s.at[i], R.sw_r.at[i], swapped)

    def swap_start(i):
        @pl.when(ki != yi)
        def _():
            swap(i).start()

        @pl.when(ki == yi)
        def _():
            acts[i][1][c_own] = acts[i][0][...]

    def swap_wait(i):
        @pl.when(ki != yi)
        def _():
            dst = acts[i][1].at[zi * 2 + ki]
            rcopy(acts[i][0], dst, R.sw_s.at[i], R.sw_r.at[i], swapped).wait_recv()

    def inside(z):
        return (z >= 0) & (z < nz)

    def up_copy(i, d, z):
        slot = acts[i][1].at[z * 2 + ki]
        return rcopy(slot, slot, R.up_s.at[i, d], R.up_r.at[i, d], mesh_dev(xi, ki, zi + 1, yi))

    def dn_copy(i, d, z):
        slot = acts[i][1].at[z * 2 + ki]
        return rcopy(slot, slot, R.dn_s.at[i, d], R.dn_r.at[i, d], mesh_dev(xi, ki, zi - 1, yi))

    def cc_copy(i, z, k):
        slot = acts[i][1].at[z * 2 + k]
        return rcopy(slot, slot, R.cc_s.at[i, z], R.cc_r.at[i, z], cpeer)

    def pass_on(i, *steps):
        for step in steps:

            @pl.when(inside(zi - step))
            def _():
                cc_copy(i, zi - step, ki).start()

    def hop_send(i, d):
        @pl.when(inside(zi - (d - 1)) & inside(zi + 1))
        def _():
            up_copy(i, d, zi - (d - 1)).start()

        @pl.when(inside(zi + (d - 1)) & inside(zi - 1))
        def _():
            dn_copy(i, d, zi + (d - 1)).start()

    def hop(i, d):
        @pl.when(inside(zi - d))
        def _():
            up_copy(i, d, zi - d).wait_recv()

        @pl.when(inside(zi + d))
        def _():
            dn_copy(i, d, zi + d).wait_recv()

        if d + 1 < nz:
            hop_send(i, d + 1)
        pass_on(i, -d, d)

    def first_hop(i):
        swap_wait(i)
        hop_send(i, 1)
        pass_on(i, 0)

    def all_in(i):
        for z in range(nz):
            cc_copy(i, z, 1 - ki).wait_recv()

    def w1(w, d, own):
        pack, dst = packs[w]
        o = mod_less(t + d, nt) if own else t
        s = t if own else mod_less(t + nt - d, nt)
        return rcopy(
            pack.at[o],
            dst.at[xi, s, yi],
            R.w1_s.at[w, d],
            R.w1_r.at[w, d],
            mesh_dev(xi, lax.div(o, nz), lax.rem(o, nz), yi) if own else xpeer,
        )

    def w1_start(w):
        for d in range(1, nt):
            w1(w, d, True).start()
        packs[w][1][xi, t, yi] = packs[w][0][t]

    def w1_wait(w):
        for d in range(1, nt):
            w1(w, d, False).wait_recv()

    def own_view(w, xx, yy):
        return mats[w].at[xx, :, yy] if w < 3 else wo.at[xx, yy]

    def half_view(w, h, xx, yy):
        if w < 3:
            return mats[w].at[xx, h * nz : (h + 1) * nz, yy]
        return wo.at[xx, yy, :, h * half : (h + 1) * half]

    def plane_x(w, xx):
        v = own_view(w, xx, yi)
        return rcopy(v, v, R.xs_s.at[w], R.xs_r.at[w], xpeer)

    def plane_y(w, yy):
        v = own_view(w, xi, yy)
        return rcopy(v, v, R.ys_s.at[w], R.ys_r.at[w], ypeer)

    def forward_y(w, xx, yy):
        v = half_view(w, 0, xx, yy)
        return rcopy(v, v, R.fy_s.at[w], R.fy_r.at[w], ypeer)

    def forward_x(w, xx, yy):
        v = half_view(w, 1, xx, yy)
        return rcopy(v, v, R.fx_s.at[w], R.fx_r.at[w], xpeer)

    def plane_start(w):
        plane_x(w, xi).start()
        plane_y(w, yi).start()

    def plane_forward(w):
        plane_x(w, 1 - xi).wait_recv()
        forward_y(w, 1 - xi, yi).start()
        plane_y(w, 1 - yi).wait_recv()
        forward_x(w, xi, 1 - yi).start()

    def plane_wait(w):
        forward_y(w, 1 - xi, 1 - yi).wait_recv()
        forward_x(w, 1 - xi, 1 - yi).wait_recv()

    parts = (R.a0, R.a1)
    ex, rcv, cmb, fin, own = R.ex, R.rcv, R.cmb, R.fin, R.own
    grads = (R.mq, R.mu, R.md)
    mo, ro, so = R.mo, R.ro, R.so
    got1 = (R.got1_0, R.got1_1, R.got1_2)
    got2 = (R.got2_0, R.got2_1, R.got2_2)
    chunks = (R.chunk_0, R.chunk_1, R.chunk_2)

    def plus(a, b):
        return (a.astype(f32) + b.astype(f32)).astype(bf)

    def share(i, z):
        return rcopy(
            parts[i].at[z * 2 + (1 - ki)],
            ex.at[i, z],
            R.rcc_s.at[i, z],
            R.rcc_r.at[i, z],
            cpeer,
        )

    def rnear(i, n):
        z = zi + STEPS[n]
        where = mesh_dev(xi, yi, z, ki) if DIRECT_OUT[i] else mesh_dev(xi, ki, z, yi)
        return rcopy(ex.at[i, z], rcv.at[i, n], R.rn_s.at[i, n], R.rn_r.at[i, n], where)

    def rfar(i, up):
        step = 1 if up else -1
        m = 0 if up else 1
        return rcopy(
            ex.at[i, zi + 3 * step],
            cmb.at[i, m],
            R.rf_s.at[i, m],
            R.rf_r.at[i, m],
            mesh_dev(xi, ki, zi + step, yi),
        )

    def rswap(i):
        return rcopy(fin.at[i], rcv.at[i, 4], R.rsw_s.at[i], R.rsw_r.at[i], swapped)

    def x1(w):
        return rcopy(
            grads[w].at[1 - xi, 0:nz], got1[w].at[0], R.x1_s.at[w], R.x1_r.at[w], xpeer
        )

    def y1(w):
        return [
            rcopy(
                grads[w].at[xx, nz:nt, 1 - yi],
                got1[w].at[1, :, xx],
                R.y1_s.at[w, xx],
                R.y1_r.at[w, xx],
                ypeer,
            )
            for xx in range(2)
        ]

    def y2(w):
        return rcopy(
            got1[w].at[0, :, 1 - yi], got2[w].at[0:nz], R.y2_s.at[w], R.y2_r.at[w], ypeer
        )

    def x2(w):
        return rcopy(
            got1[w].at[1, :, 1 - xi], got2[w].at[nz:nt], R.x2_s.at[w], R.x2_r.at[w], xpeer
        )

    def tp(w, d, mine):
        o = mod_less(t + d, nt) if mine else t
        s = t if mine else mod_less(t + nt - d, nt)
        return rcopy(
            got2[w].at[o],
            chunks[w].at[s],
            R.tp_s.at[w, d],
            R.tp_r.at[w, d],
            mesh_dev(xi, lax.div(o, nz), lax.rem(o, nz), yi) if mine else xpeer,
        )

    def ox1():
        return rcopy(
            mo.at[1 - xi, :, :, 0:half], ro.at[0], R.x1_s.at[3], R.x1_r.at[3], xpeer
        )

    def oy1():
        return rcopy(
            mo.at[:, 1 - yi, :, half:dm], ro.at[1], R.y1_s.at[3, 0], R.y1_r.at[3, 0], ypeer
        )

    def oy2():
        return rcopy(ro.at[0, 1 - yi], so.at[0], R.y2_s.at[3], R.y2_r.at[3], ypeer)

    def ox2():
        return rcopy(ro.at[1, 1 - xi], so.at[1], R.x2_s.at[3], R.x2_r.at[3], xpeer)

    def grad_start(w):
        x1(w).start()
        for cp in y1(w):
            cp.start()

    def fold(i):
        for z in range(nz):
            share(i, z).wait_recv()
            ex[i, z] = plus(ex[i, z], parts[i][z * 2 + ki])

    def rstart(i):
        for up, step in ((True, 1), (False, -1)):

            @pl.when(inside(zi + 3 * step))
            def _():
                rfar(i, up).start()

            @pl.when(inside(zi + 2 * step) & jnp.logical_not(inside(zi - step)))
            def _():
                rnear(i, 3 if up else 0).start()

            @pl.when(inside(zi + step))
            def _():
                rnear(i, 2 if up else 1).start()

        if DIRECT_OUT[i]:

            @pl.when(ki != yi)
            def _():
                fin[i] = ex[i, zi]
                rswap(i).start()

    def rjoin(i):
        for up, step in ((True, 1), (False, -1)):

            @pl.when(inside(zi + 2 * step) & inside(zi - step))
            def _():
                m = 0 if up else 1
                z = zi + 2 * step
                there = mesh_dev(xi, ki, zi - step, yi)
                rcopy(
                    ex.at[i, z], cmb.at[i, m], R.rf_s.at[i, m], R.rf_r.at[i, m], there
                ).wait_recv()
                ex[i, z] = plus(ex[i, z], cmb[i, m])
                rnear(i, 3 if up else 0).start()

    def swapped_in(i):
        rcopy(fin.at[i], rcv.at[i, 4], R.rsw_s.at[i], R.rsw_r.at[i], swapped).wait_recv()

    def rnears(i):
        for n in range(4):

            @pl.when(inside(zi - STEPS[n]))
            def _():
                rcopy(
                    fin.at[i], rcv.at[i, n], R.rn_s.at[i, n], R.rn_r.at[i, n], cpeer
                ).wait_recv()
                own[i] += rcv[i, n].astype(f32)

    def rend(i):
        if DIRECT_OUT[i]:

            @pl.when(ki != yi)
            def _():
                swapped_in(i)
                own[i] = rcv[i, 4].astype(f32)

            @pl.when(ki == yi)
            def _():
                own[i] = ex[i, zi].astype(f32)

            rnears(i)
        else:
            own[i] = ex[i, zi].astype(f32)
            rnears(i)

            @pl.when(ki != yi)
            def _():
                fin[i] = own[i].astype(bf)
                rswap(i).start()

    def rlast(i):
        if not DIRECT_OUT[i]:

            @pl.when(ki != yi)
            def _():
                swapped_in(i)
                own[i] = rcv[i, 4].astype(f32)

    def fold1(w):
        x1(w).wait_recv()
        got1[w][0] = plus(got1[w][0], grads[w][xi, 0:nz])
        y2(w).start()
        for cp in y1(w):
            cp.wait_recv()
        for xx in range(2):
            got1[w][1, :, xx] = plus(got1[w][1, :, xx], grads[w][xx, nz:nt, yi])
        x2(w).start()

    def fold2(w):
        y2(w).wait_recv()
        got2[w][0:nz] = plus(got2[w][0:nz], got1[w][0, :, yi])
        x2(w).wait_recv()
        got2[w][nz:nt] = plus(got2[w][nz:nt], got1[w][1, :, xi])
        for d in range(1, nt):
            tp(w, d, True).start()
        chunks[w][t] = got2[w][t]

    lane = lax.broadcasted_iota(jnp.int32, (1, hw), 1)
    first = lane < HD
    gains = R.gains
    hat, n1, n2 = R.hat, R.n1, R.n2
    place_col, place_row, cos_t, low_t, high_t = R.pcol, R.prow, R.cos, R.low, R.high
    qm, km, vm, dcm = R.qm, R.km, R.vm, R.dm
    lse, delta, cx = R.lse, R.delta, R.cx
    hid, slope, dpre_s, gs = R.hid, R.slope, R.dpre, R.gs
    dq, dk, dv, dqkv = R.dq, R.dk, R.dv, R.dqkv
    sums, sq, su = R.sums, R.sq, R.su

    def block(i):
        return pl.ds(pl.multiple_of(i * RB, RB), RB)

    def act(ref, i):
        return ref[pl.ds(2 * i, 2)].reshape(RB, dm)

    def masked(value):
        return jnp.where(first, value, 0), jnp.where(first, 0, value)

    def hats(xf):
        mean = jnp.mean(xf, axis=-1, keepdims=True)
        centred = xf - mean
        rstd = lax.rsqrt(jnp.mean(centred * centred, axis=-1, keepdims=True) + EPS)
        return centred * rstd, rstd

    def table_step(i, _):
        blk = width2 // 2
        p = pairs[i]

        def place_of(j):
            return jnp.where(j < blk, p * blk + j, (2 * nt - 1 - p) * blk + j - blk)

        at = pl.ds(pl.multiple_of(i * width2, width2), width2)
        place = place_of(lax.broadcasted_iota(jnp.int32, (width2, 1), 0))
        place_col[at] = place
        place_row[:, at] = place_of(lax.broadcasted_iota(jnp.int32, (1, width2), 1))
        turn_lane = lane & (HD - 1)
        step = (turn_lane & (ROT // 2 - 1)).astype(f32)
        angle = place.astype(f32) * jnp.exp(step * (-2.0 * math.log(10000.0) / ROT))
        sine = jnp.sin(angle)
        cos_t[at] = jnp.where(turn_lane < ROT, jnp.cos(angle), 1.0)
        low_t[at] = jnp.where(turn_lane < ROT // 2, -sine, 0.0)
        high_t[at] = jnp.where((turn_lane >= ROT // 2) & (turn_lane < ROT), sine, 0.0)
        return 0

    def hat_step(i, _):
        hat[block(i)] = hats(act(R.xb, i).astype(f32))[0]
        return 0

    def vectors_in():
        wq = R.wq
        per = LANES // piece

        def tile(r):
            a, b, e = r // (2 * nt), (r // 2) % nt, r % 2
            return wq[a, b, e, :, qc:].astype(f32)

        n = nt * 4
        for j in range(n // per):
            tiles = [tile(j * per + m) for m in range(per)]
            gains[:, j * LANES : (j + 1) * LANES] = jnp.concatenate(
                [v[0:8, 0:piece] for v in tiles], axis=1
            )
            bw = 3 * piece
            R.bqf[:, j * per * bw : (j + 1) * per * bw] = jnp.concatenate(
                [v[6:7, 0:bw] for v in tiles], axis=1
            )
        here = lax.div(t, 2) * LANES
        odd = lax.rem(t, 2) == 1
        for p in range(3):
            out = []
            for h in range(2):
                at = pl.multiple_of(here + (p * dm + h * half), LANES)
                v = R.bqf[:, pl.ds(at, LANES)]
                out.append(jnp.where(odd, v[:, HD:], v[:, :HD]))
            R.bq[:, p * hw : (p + 1) * hw] = jnp.concatenate(out, axis=1)
        for j in range(fw // LANES):
            r = t * (fw // LANES) + j
            v = wq[lax.div(r, 2 * nt), lax.rem(lax.div(r, 2), nt), lax.rem(r, 2), :, qc:]
            R.bu[:, j * LANES : (j + 1) * LANES] = v.astype(f32)[7:8]

    def turned(field, b, sign):
        down = pltpu.roll(field, hw - ROT // 2, 1)
        up = pltpu.roll(field, ROT // 2, 1)
        return field * cos_t[b] + sign * (down * low_t[b] + up * high_t[b])

    def qkv_step(i, _):
        b = block(i)
        h = hat[b]
        n1[b] = (h * gains[0:1] + gains[1:2]).astype(bf)
        n2[b] = (h * gains[2:3] + gains[3:4]).astype(bf)
        w = R.wq[:, :, :, :, 0:qc].reshape(dm, qc)
        qkv = mm(n1[b], w, NN) + R.bq[...]
        q = turned(qkv[:, 0:hw], b, 1.0).astype(bf).astype(f32) * scale
        k = turned(qkv[:, hw : 2 * hw], b, 1.0)
        v = qkv[:, 2 * hw : 3 * hw]
        for ref, value in ((qm, q), (km, k), (vm, v)):
            one, two = masked(value)
            ref[0, b] = one.astype(bf)
            ref[1, b] = two.astype(bf)
        return 0

    def attend_step(i, _):
        b = block(i)
        visible = place_row[...] <= place_col[b]
        ctx = jnp.zeros((RB, hw), f32)
        for h in range(2):
            s = jnp.where(visible, mm(qm[h, b], km[h], NT), NEG)
            top = jnp.max(s, axis=-1, keepdims=True)
            e = jnp.exp(s - top)
            total = jnp.sum(e, axis=-1, keepdims=True)
            ctx = ctx + mm(e.astype(bf), vm[h], NN) / total
            lse[h, b] = top + jnp.log(total)
        cx[b] = ctx.astype(bf)
        return 0

    def up_step(i, _):
        b = block(i)
        pre = mm(n2[b], R.wu[...].reshape(dm, fw), NN) + R.bu[...]
        bell = 0.5 * (1.0 + lax.erf(pre * ROOT_HALF))
        hid[b] = (pre * bell).astype(bf)
        slope[b] = bell + pre * jnp.exp(-0.5 * pre * pre) * INV_ROOT_TAU
        return 0

    def down_step(i, _):
        b = block(i)
        out = mm(hid[b], R.wd[...].reshape(dm, fw), NT)
        out = out + mm(cx[b], wo[...].reshape(hw, dm), NN)
        R.a0[pl.ds(2 * i, 2)] = out.astype(bf).reshape(2, width2, dm)
        return 0

    def back_step(i, _):
        b = block(i)
        g = act(R.gb, i)
        dpre = mm(g, R.wd[...].reshape(dm, fw), NN) * slope[b]
        su[...] += jnp.sum(dpre, axis=0, keepdims=True)
        dpre_s[b] = dpre.astype(bf)
        dn2 = mm(dpre_s[b], R.wu[...].reshape(dm, fw), NT)
        sums[2:3] += jnp.sum(dn2 * hat[b], axis=0, keepdims=True)
        sums[3:4] += jnp.sum(dn2, axis=0, keepdims=True)
        gs[b] = dn2 * gains[2:3]
        return 0

    def context_step(i, _):
        b = block(i)
        g = act(R.gb, i)
        dctx = mm(g, wo[...].reshape(hw, dm), NT).astype(bf).astype(f32)
        prod = dctx * cx[b].astype(f32)
        for h, (d, p) in enumerate(zip(masked(dctx), masked(prod))):
            dcm[h, b] = d.astype(bf)
            delta[h, b] = jnp.sum(p, axis=-1, keepdims=True)
        return 0

    def rows_of(ref, i):
        return ref.at[lax.div(i, 2), pl.ds(pl.multiple_of(lax.rem(i, 2) * nz, nz), nz)]

    def outer_step(i, _):
        cols = pl.ds(pl.multiple_of(i * QB, QB), QB)
        gt = R.gb[:, :, cols].reshape(rows, QB)
        out = mm(gt, hid[...], TN)
        rows_of(R.md, i)[...] = out.astype(bf).reshape(nz, 2, piece, fw)
        wide = mm(cx[...], gt, TN).astype(bf)
        mo[:, :, :, cols] = wide.reshape(2, 2, piece, QB)
        return 0

    def outer_up_step(i, _):
        cols = pl.ds(pl.multiple_of(i * QB, QB), QB)
        out = mm(n2[:, cols], dpre_s[...], TN)
        rows_of(R.mu, i)[...] = out.astype(bf).reshape(nz, 2, piece, fw)
        return 0

    def attend_back_step(i, _):
        b = block(i)
        visible = place_row[...] <= place_col[b]
        acc = jnp.zeros((RB, hw), f32)
        for h in range(2):
            s = jnp.where(visible, mm(qm[h, b], km[h], NT), NEG)
            p = jnp.exp(s - lse[h, b])
            dp = mm(dcm[h, b], vm[h], NT)
            ds = (p * (dp - delta[h, b])).astype(bf)
            acc = acc + mm(ds, km[h], NN)
            dk[...] += mm(ds, qm[h, b], TN)
            dv[...] += mm(p.astype(bf), dcm[h, b], TN)
        dq[b] = acc * scale
        return 0

    def dqkv_step(i, _):
        b = block(i)
        fields = (turned(dq[b], b, -1.0), turned(dk[b], b, -1.0), dv[b])
        for j, v in enumerate(fields):
            sq[:, j * hw : (j + 1) * hw] += jnp.sum(v, axis=0, keepdims=True)
            dqkv[b, j * hw : (j + 1) * hw] = v.astype(bf)
        w = R.wq[:, :, :, :, 0:qc].reshape(dm, qc)
        dn1 = mm(dqkv[b], w, NT)
        sums[0:1] += jnp.sum(dn1 * hat[b], axis=0, keepdims=True)
        sums[1:2] += jnp.sum(dn1, axis=0, keepdims=True)
        out = (dn1 * gains[0:1] + gs[b]).astype(bf)
        R.a1[pl.ds(2 * i, 2)] = out.reshape(2, width2, dm)
        return 0

    def outer_qkv_step(i, _):
        cols = pl.ds(pl.multiple_of(i * QB, QB), QB)
        out = mm(n1[:, cols], dqkv[...], TN)
        view = R.mq.at[lax.div(i, 2), pl.ds(pl.multiple_of(lax.rem(i, 2) * nz, nz), nz), :, :, 0:qc]
        view[...] = out.astype(bf).reshape(nz, 2, piece, qc)
        return 0

    def sums_out():
        low = jnp.concatenate(
            [sq[:, j * hw : (j + 1) * hw] for j in range(3)]
            + [su[:, j * LANES : (j + 1) * LANES] for j in range(fw // LANES)]
            + [jnp.zeros((piece - 8 - 3 - fw // LANES, LANES), f32)],
            axis=0,
        )
        for r in range(nt * 4):
            one = sums[:, r * piece : (r + 1) * piece]
            one = jnp.concatenate([one, jnp.zeros((8, LANES - piece), f32)], axis=1)
            tile = jnp.concatenate([one, low], axis=0).astype(bf)
            R.mq[r // (2 * nt), (r // 2) % nt, r % 2, :, qc:] = tile

    all_here = greet(nz, xi, ki, zi, yi)
    vs = R.vs
    vs[...] = jnp.zeros_like(vs)
    for i, v in enumerate(vectors):
        vs[i : i + 1, 0 : v.shape[1]] = v[...].astype(f32)
    small = vs[...].astype(bf)
    loads[1].wait()
    for o in range(nt):
        pieces = []
        for p in range(3):
            base = p * dm + o * HD
            for at in (base, base + half):
                pieces.append(R.qo[:, at : at + HD])
        for j in range(3):
            R.pq[o, :, j * hw : (j + 1) * hw] = jnp.concatenate(pieces[2 * j : 2 * j + 2], axis=1)
        R.pq[o, :, qc:] = small
    loads[0].wait()
    all_here()

    swap_start(0)
    w1_start(0)
    load_g.wait()
    swap_start(1)
    first_hop(0)
    loads[2].wait()
    plane_start(3)
    for cp in loads_u:
        cp.wait()
    w1_start(1)
    for cp in loads_d:
        cp.wait()
    w1_start(2)
    for ref in (sums, sq, su, dk, dv):
        ref[...] = jnp.zeros_like(ref)
    lax.fori_loop(0, nt, table_step, 0)
    sums[4:5] = jnp.sum(R.go[...].astype(f32), axis=0, keepdims=True)
    hop(0, 1)
    w1_wait(0)
    plane_start(0)
    first_hop(1)
    hop(0, 2)
    hop(1, 1)
    w1_wait(1)
    plane_start(1)
    plane_forward(0)
    hop(0, 3)
    hop(1, 2)
    w1_wait(2)
    plane_start(2)
    plane_forward(3)
    all_in(0)
    lax.fori_loop(0, rblk, hat_step, 0)
    plane_wait(0)
    vectors_in()
    lax.fori_loop(0, rblk, qkv_step, 0)
    plane_forward(1)
    lax.fori_loop(0, rblk // 2, attend_step, 0)
    plane_forward(2)
    lax.fori_loop(rblk // 2, rblk, attend_step, 0)
    plane_wait(1)
    hop(1, 3)
    lax.fori_loop(0, rblk, up_step, 0)
    plane_wait(2)
    plane_wait(3)
    lax.fori_loop(0, rblk, down_step, 0)
    for z in range(nz):
        share(0, z).start()
    all_in(1)
    lax.fori_loop(0, nblk, outer_step, 0)
    grad_start(2)
    ox1().start()
    oy1().start()
    fold(0)
    rstart(0)
    lax.fori_loop(0, rblk, back_step, 0)
    lax.fori_loop(0, rblk, context_step, 0)
    lax.fori_loop(0, nblk, outer_up_step, 0)
    grad_start(1)
    rjoin(0)
    lax.fori_loop(0, rblk // 2, attend_back_step, 0)
    fold1(2)
    ox1().wait_recv()
    ro[0] = plus(ro[0], mo[xi, :, :, 0:half])
    oy2().start()
    oy1().wait_recv()
    ro[1] = plus(ro[1], mo[:, yi, :, half:dm])
    ox2().start()
    lax.fori_loop(rblk // 2, rblk, attend_back_step, 0)
    fold1(1)
    fold2(2)
    lax.fori_loop(0, rblk, dqkv_step, 0)
    for z in range(nz):
        share(1, z).start()
    fold2(1)
    lax.fori_loop(0, nblk, outer_qkv_step, 0)
    sums_out()
    grad_start(0)
    fold(1)
    rstart(1)
    rend(0)
    rjoin(1)
    fold1(0)
    fold2(0)
    rlast(0)

    x_own = R.xo[...].astype(f32)
    out_x[...] = (x_own + own[0] + (gains[4:5] + gains[5:6])).astype(bf)
    oy2().wait_recv()
    oo[:, 0:half] = so[0].astype(f32) + ro[0, yi].astype(f32)
    ox2().wait_recv()
    oo[:, half:dm] = so[1].astype(f32) + ro[1, xi].astype(f32)
    for w in (2, 1):
        for d in range(1, nt):
            tp(w, d, False).wait_recv()
        ref = (None, ou, od)[w]
        for o in range(nt):
            ref[:, o * fw : (o + 1) * fw] = chunks[w][o].astype(f32)
    hat_own, rstd_own = hats(x_own)

    rend(1)
    gsum = own[1]
    out_g[...] = (
        R.go[...].astype(f32)
        + rstd_own
        * (
            gsum
            - jnp.mean(gsum, axis=-1, keepdims=True)
            - hat_own * jnp.mean(gsum * hat_own, axis=-1, keepdims=True)
        )
    ).astype(bf)
    for d in range(1, nt):
        tp(0, d, False).wait_recv()
    cq = chunks[0]
    for j in range(3):
        for h in range(2):
            for o in range(0, nt, 2):
                lo = j * hw + h * HD
                both = jnp.concatenate([cq[o, :, lo : lo + HD], cq[o + 1, :, lo : lo + HD]], axis=1)
                at = j * dm + h * half + o * HD
                oq[:, at : at + hw] = both.astype(f32)
    for o in range(nt):
        osum[o] = cq[o, :, qc:].astype(f32)[0:16]

    for i in range(2):

        @pl.when(ki != yi)
        def _():
            swap(i).wait_send()
            rswap(i).wait_send()

        for d in range(1, nz):

            @pl.when(inside(zi - (d - 1)) & inside(zi + 1))
            def _():
                up_copy(i, d, zi - (d - 1)).wait_send()

            @pl.when(inside(zi + (d - 1)) & inside(zi - 1))
            def _():
                dn_copy(i, d, zi + (d - 1)).wait_send()

        for n in range(4):

            @pl.when(inside(zi + STEPS[n]))
            def _():
                rnear(i, n).wait_send()

        for up, step in ((True, 1), (False, -1)):

            @pl.when(inside(zi + 3 * step))
            def _():
                rfar(i, up).wait_send()

        for z in range(nz):
            cc_copy(i, z, ki).wait_send()
            share(i, z).wait_send()
    for w in range(3):
        for d in range(1, nt):
            w1(w, d, True).wait_send()
            tp(w, d, True).wait_send()
        x1(w).wait_send()
        for cp in y1(w):
            cp.wait_send()
        y2(w).wait_send()
        x2(w).wait_send()
    for w in range(4):
        plane_x(w, xi).wait_send()
        plane_y(w, yi).wait_send()
        forward_y(w, 1 - xi, yi).wait_send()
        forward_x(w, xi, 1 - yi).wait_send()
    ox1().wait_send()
    oy1().wait_send()
    oy2().wait_send()
    ox2().wait_send()


def finish_kernel(dm, nq, fw, *refs):
    big, sums, outs, small = refs[:6], refs[6], refs[7:13], refs[13:21]
    flat = refs[21]
    for a, b in zip(big, outs):
        b[...] = a[...]
    nt = sums.shape[0]
    half = dm // 2
    r = lax.axis_index("fsdp") * lax.axis_size("ctx") + lax.axis_index("ctx")
    total = sums[0, 0:8]
    for o in range(1, nt):
        total = total + sums[o, 0:8]
    for i, row in enumerate((0, 1, 2, 3, 4, 4)):
        small[i][...] = total[row : row + 1, 0 : small[i].shape[1]]
    flat[:, 3 * dm :] = jnp.zeros((1, LANES), jnp.float32)
    for j in range(3):
        for h in range(2):
            for o in range(0, nt, 2):
                pair = [sums[o + e, 8 + j : 9 + j, h * HD : (h + 1) * HD] for e in range(2)]
                at = j * dm + h * half + o * HD
                flat[:, at : at + 2 * HD] = jnp.concatenate(pair, axis=1)
    begin = r * nq
    chunk = lax.div(begin, LANES)
    wide = flat[:, pl.ds(pl.multiple_of(chunk * LANES, LANES), 2 * LANES)]
    shift = begin - chunk * LANES
    unit = math.gcd(nq, LANES)
    mine = wide[:, 0:nq]
    for at in range(unit, LANES, unit):
        mine = jnp.where(shift == at, wide[:, at : at + nq], mine)
    small[6][...] = mine
    per = fw // LANES
    row = 11 + lax.rem(r, per)
    small[7][...] = sums[lax.div(r, per), pl.ds(row, 1)]


def finish(arrays, sums, nq, fw, dm):
    vm = pl.BlockSpec(memory_space=pltpu.VMEM)
    f32 = jnp.float32
    shape = jax.ShapeDtypeStruct
    piece = arrays[2].shape[0]
    smalls = [piece] * 6 + [nq, LANES]
    return pl.pallas_call(
        functools.partial(finish_kernel, dm, nq, fw),
        out_shape=[shape(a.shape, a.dtype) for a in arrays] + [shape((1, n), f32) for n in smalls],
        in_specs=[vm] * 7,
        out_specs=[vm] * 14,
        scratch_shapes=[pltpu.VMEM((1, 3 * dm + LANES), f32)],
        compiler_params=pltpu.CompilerParams(vmem_limit_bytes=60 * 1024 * 1024),
    )(*arrays, sums)


def routed(
    layer_in,
    grad_out,
    pair_of_rank,
    ln1_gain,
    ln1_bias,
    ln2_gain,
    ln2_bias,
    w_qkv,
    b_qkv,
    w_out,
    b_out,
    w_up,
    b_up,
    w_down,
    b_down,
):
    f32 = jnp.float32
    bf = jnp.bfloat16
    nctx = lax.axis_size("ctx")
    nz = nctx // 2
    width2, dmodel = layer_in.shape[2:]
    ff = w_up.shape[1]
    piece = w_qkv.shape[0]
    plan = layer_plan(nz, width2, dmodel, ff, piece)
    vectors = (ln1_gain, ln1_bias, ln2_gain, ln2_bias, b_out, b_down, b_qkv, b_up)
    vm = pl.BlockSpec(memory_space=pltpu.VMEM)
    anywhere = pl.BlockSpec(memory_space=pl.ANY)
    shape = jax.ShapeDtypeStruct
    layer_out, grad_x, grad_qkv, grad_up, grad_down, grad_wout, sums = pl.pallas_call(
        functools.partial(layer_kernel, nz, tuple(plan)),
        out_shape=(
            shape((width2, dmodel), bf),
            shape((width2, dmodel), bf),
            shape((piece, 3 * dmodel), f32),
            shape((piece, ff), f32),
            shape((piece, ff), f32),
            shape((piece, dmodel), f32),
            shape((nctx, 16, LANES), f32),
        ),
        in_specs=[anywhere] * 6 + [vm] * 8 + [pl.BlockSpec(memory_space=pltpu.SMEM)],
        out_specs=(vm,) * 7,
        scratch_shapes=list(plan.values()),
        compiler_params=pltpu.CompilerParams(
            collective_id=0, has_side_effects=True, vmem_limit_bytes=60 * 1024 * 1024
        ),
    )(
        layer_in.reshape(width2, dmodel),
        grad_out.reshape(width2, dmodel),
        w_qkv,
        w_up,
        w_down,
        w_out,
        *[v.reshape(1, -1) for v in vectors],
        pair_of_rank,
    )
    done = finish(
        (layer_out, grad_x, grad_qkv, grad_up, grad_down, grad_wout),
        sums,
        b_qkv.shape[0],
        ff // nctx,
        dmodel,
    )
    layer_out, grad_x, grad_qkv, grad_up, grad_down, grad_wout = done[:6]
    vs = [v.reshape(-1) for v in done[6:]]
    return (
        layer_out.reshape(layer_in.shape),
        grad_x.reshape(layer_in.shape),
        vs[0],
        vs[1],
        vs[2],
        vs[3],
        grad_qkv,
        vs[6],
        grad_wout,
        vs[4],
        grad_up,
        vs[7],
        grad_down,
        vs[5],
    )


def solution(mesh):
    nctx = mesh.shape["ctx"]

    def pick(layer_in, *rest):
        heads = layer_in.shape[-1] // HD
        whole = heads % nctx == 0
        square = nctx % 2 == 0 and mesh.shape["fsdp"] == 4 and heads == 2 * nctx
        if square and layer_in.shape[1] == 1 and layer_in.shape[-1] == 8 * layer_in.shape[2] == nctx * layer_in.shape[2]:
            return routed(layer_in, *rest)
        return (head_shards if whole else shards)(layer_in, *rest)

    return jax.shard_map(
        pick,
        mesh=mesh,
        in_specs=(
            P("ctx", "fsdp", None, None),
            P("ctx", "fsdp", None, None),
            P(),
            P(("fsdp", "ctx")),
            P(("fsdp", "ctx")),
            P(("fsdp", "ctx")),
            P(("fsdp", "ctx")),
            P(("fsdp", "ctx"), None),
            P(("fsdp", "ctx")),
            P(("fsdp", "ctx"), None),
            P(("fsdp", "ctx")),
            P(("fsdp", "ctx"), None),
            P(("fsdp", "ctx")),
            P(("fsdp", "ctx"), None),
            P(("fsdp", "ctx")),
        ),
        out_specs=(
            P("ctx", "fsdp", None, None),
            P("ctx", "fsdp", None, None),
            P(("fsdp", "ctx")),
            P(("fsdp", "ctx")),
            P(("fsdp", "ctx")),
            P(("fsdp", "ctx")),
            P(("fsdp", "ctx"), None),
            P(("fsdp", "ctx")),
            P(("fsdp", "ctx"), None),
            P(("fsdp", "ctx")),
            P(("fsdp", "ctx"), None),
            P(("fsdp", "ctx")),
            P(("fsdp", "ctx"), None),
            P(("fsdp", "ctx")),
        ),
        check_vma=False,
    )
```

```python
import functools
import math
import types

import jax
import jax.numpy as jnp
from jax import lax
from jax.experimental import pallas as pl
from jax.experimental.pallas import tpu as pltpu
from jax.sharding import PartitionSpec as P

HD = 64
ROT = 16
LANES = 128


EPS = 1e-05
NEG = -1e30
ROOT_HALF = 0.7071067811865476
INV_ROOT_TAU = 0.3989422804014327


def norm_parts(xf, scale_weight, shift_bias):
    row_mean = jnp.mean(xf, axis=-1, keepdims=True)
    centred_input = xf - row_mean
    inverse_deviation = lax.rsqrt(
        jnp.mean(centred_input * centred_input, axis=-1, keepdims=True) + EPS
    )
    normalized_input = centred_input * inverse_deviation
    return (
        normalized_input * scale_weight.astype(jnp.float32) + shift_bias.astype(jnp.float32),
        normalized_input,
        inverse_deviation,
    )


def layer_norm_backward(norm_output_gradient, normalized_input, inverse_deviation, scale_weight):
    normalized_gradient = norm_output_gradient * scale_weight.astype(jnp.float32)
    return inverse_deviation * (
        normalized_gradient
        - jnp.mean(normalized_gradient, axis=-1, keepdims=True)
        - normalized_input
        * jnp.mean(normalized_gradient * normalized_input, axis=-1, keepdims=True)
    )


def gelu_value(u):
    return 0.5 * u * (1.0 + lax.erf(u * ROOT_HALF))


def gelu_slope(u):
    return 0.5 * (1.0 + lax.erf(u * ROOT_HALF)) + u * jnp.exp(-0.5 * u * u) * INV_ROOT_TAU


def rotate(field, place, sign):
    half = ROT // 2
    freqs = jnp.exp(jnp.arange(half).astype(jnp.float32) * (-2.0 * math.log(10000.0) / ROT))
    angle = place.astype(jnp.float32)[..., None] * freqs
    cosine = jnp.cos(angle)[..., None, :]
    sine = sign * jnp.sin(angle)[..., None, :]
    first = field[..., :half]
    second = field[..., half:ROT]
    return jnp.concatenate(
        [first * cosine - second * sine, second * cosine + first * sine, field[..., rot_end() :]],
        axis=-1,
    )


def rot_end():
    return ROT


def leading(field, letters):
    return "n" + letters if field.ndim == 5 else letters


def product(left, left_letters, right, right_letters, result):
    form = leading(left, left_letters) + "," + leading(right, right_letters) + "->" + result
    return jnp.einsum(form, left, right, preferred_element_type=jnp.float32)


def selectors(sel):
    return (sel[:, None, None, None, None], sel[:, None, None, None], sel[:, None])


def visibility(sel, qpa, qpb, kpa, kpb):
    chosen = sel[:, None]
    key_place = jnp.where(chosen, kpa, kpb)
    query_place = jnp.where(chosen, qpa, qpb)
    return (key_place[:, None, :] <= query_place[:, :, None])[:, None, None]


def online_update(state, qa, qb, ka, kb, va, vb, qpa, qpb, kpa, kpb, sel, with_first, scale):
    top_a, total_a, acc_a, top_b, total_b, acc_b = state
    sel5, sel4, sel2 = selectors(sel)
    query_two = jnp.where(sel5, qa, qb)
    key_two = jnp.where(sel5, ka, kb)
    value_two = jnp.where(sel5, va, vb)
    visible = visibility(sel, qpa, qpb, kpa, kpb)
    score = jnp.where(visible, product(query_two, "sqhd", key_two, "skhd", "nshqk") * scale, NEG)
    peak_a = jnp.max(jnp.where(sel5, score, NEG), axis=(0, 4))
    peak_b = jnp.max(jnp.where(sel5, NEG, score), axis=(0, 4))
    if with_first:
        score_one = product(qb, "sqhd", ka, "skhd", "nshqk") * scale
        peak_b = jnp.maximum(peak_b, jnp.max(score_one, axis=(0, 4)))
    new_a = jnp.maximum(top_a, peak_a)
    new_b = jnp.maximum(top_b, peak_b)
    lifted = jnp.where(sel5, new_a[..., None], new_b[..., None])
    weight = jnp.where(visible, jnp.exp(score - lifted), 0.0)
    mixed = product(weight.astype(jnp.bfloat16), "shqk", value_two, "skhd", "nshqd")
    mass = jnp.sum(weight, axis=4)
    add_total_a = jnp.sum(jnp.where(sel4, mass, 0.0), axis=0)
    add_total_b = jnp.sum(jnp.where(sel4, 0.0, mass), axis=0)
    add_acc_a = jnp.sum(jnp.where(sel5, mixed, 0.0), axis=0)
    add_acc_b = jnp.sum(jnp.where(sel5, 0.0, mixed), axis=0)
    if with_first:
        weight_one = jnp.exp(score_one - new_b[..., None])
        add_total_b = add_total_b + jnp.sum(weight_one, axis=(0, 4))
        add_acc_b = add_acc_b + product(weight_one.astype(jnp.bfloat16), "shqk", va, "skhd", "shqd")
    decay_a = jnp.exp(top_a - new_a)
    decay_b = jnp.exp(top_b - new_b)
    return (
        new_a,
        total_a * decay_a + add_total_a,
        acc_a * decay_a[..., None] + add_acc_a,
        new_b,
        total_b * decay_b + add_total_b,
        acc_b * decay_b[..., None] + add_acc_b,
    )


def pair_terms(
    qa,
    qb,
    ka,
    kb,
    va,
    vb,
    da,
    db,
    lsea,
    lseb,
    dela,
    delb,
    qpa,
    qpb,
    kpa,
    kpb,
    sel,
    with_first,
    scale,
):
    sel5, sel4, sel2 = selectors(sel)
    query_two = jnp.where(sel5, qa, qb)
    key_two = jnp.where(sel5, ka, kb)
    value_two = jnp.where(sel5, va, vb)
    dctx_two = jnp.where(sel5, da, db)
    lse_two = jnp.where(sel4, lsea, lseb)
    delta_two = jnp.where(sel4, dela, delb)
    visible = visibility(sel, qpa, qpb, kpa, kpb)
    score = jnp.where(visible, product(query_two, "sqhd", key_two, "skhd", "nshqk") * scale, NEG)
    prob = jnp.exp(score - lse_two[..., None])
    dprob = product(dctx_two, "sqhd", value_two, "skhd", "nshqk")
    dscore = (scale * prob * (dprob - delta_two[..., None])).astype(jnp.bfloat16)
    first_ds = None
    first_prob = None
    if with_first:
        score_one = product(qb, "sqhd", ka, "skhd", "nshqk") * scale
        prob_one = jnp.exp(score_one - lseb[..., None])
        dprob_one = product(db, "sqhd", va, "skhd", "nshqk")
        first_ds = (scale * prob_one * (dprob_one - delb[..., None])).astype(jnp.bfloat16)
        first_prob = prob_one.astype(jnp.bfloat16)
    return (first_ds, first_prob, dscore, prob.astype(jnp.bfloat16))


def query_grads(terms, ka, kb, sel):
    sel5, sel4, sel2 = selectors(sel)
    key_two = jnp.where(sel5, ka, kb)
    dq_two = product(terms[2], "shqk", key_two, "skhd", "nsqhd")
    dq_a = jnp.where(sel5, dq_two, 0.0)
    dq_b = jnp.where(sel5, 0.0, dq_two)
    if terms[0] is not None:
        dq_b = dq_b + product(terms[0], "shqk", ka, "skhd", "nsqhd")
    return (dq_a, dq_b)


def key_grads(terms, qa, qb, da, db, sel):
    sel5, sel4, sel2 = selectors(sel)
    query_two = jnp.where(sel5, qa, qb)
    dctx_two = jnp.where(sel5, da, db)
    dk_two = product(terms[2], "shqk", query_two, "sqhd", "nskhd")
    dv_two = product(terms[3], "shqk", dctx_two, "sqhd", "nskhd")
    dk_a = jnp.where(sel5, dk_two, 0.0)
    dk_b = jnp.where(sel5, 0.0, dk_two)
    dv_a = jnp.where(sel5, dv_two, 0.0)
    dv_b = jnp.where(sel5, 0.0, dv_two)
    if terms[0] is not None:
        dk_a = dk_a + product(terms[0], "shqk", qb, "sqhd", "nskhd")
        dv_a = dv_a + product(terms[1], "shqk", db, "sqhd", "nskhd")
    return (dk_a, dk_b, dv_a, dv_b)


def tdot(left, right):
    return lax.dot_general(
        left, right, (((0,), (0,)), ((), ())), preferred_element_type=jnp.float32
    )


def rdot(left, right):
    return lax.dot_general(
        left, right, (((1,), (1,)), ((), ())), preferred_element_type=jnp.float32
    )


def shards(
    layer_in,
    grad_out,
    pair_of_rank,
    ln1_gain,
    ln1_bias,
    ln2_gain,
    ln2_bias,
    w_qkv,
    b_qkv,
    w_out,
    b_out,
    w_up,
    b_up,
    w_down,
    b_down,
):
    f32 = jnp.float32
    bf = jnp.bfloat16
    nctx = lax.axis_size("ctx")
    mine = pair_of_rank[lax.axis_index("ctx")]
    seqs = layer_in.shape[1]
    width2 = layer_in.shape[2]
    dmodel = layer_in.shape[3]
    blk = width2 // 2
    rows = seqs * width2
    heads = dmodel // HD
    scale = 1.0 / math.sqrt(HD)
    offsets = jnp.arange(blk, dtype=jnp.int32)
    place_a = mine * blk + offsets
    place_b = (2 * nctx - 1 - mine) * blk + offsets
    places = jnp.concatenate([place_a, place_b])
    params = (
        ln1_gain,
        ln1_bias,
        ln2_gain,
        ln2_bias,
        w_qkv,
        b_qkv,
        w_out,
        b_out,
        w_up,
        b_up,
        w_down,
        b_down,
    )
    full = (
        lax.all_gather(params[0], ("fsdp", "ctx"), axis=0, tiled=True),
        lax.all_gather(params[1], ("fsdp", "ctx"), axis=0, tiled=True),
        lax.all_gather(params[2], ("fsdp", "ctx"), axis=0, tiled=True),
        lax.all_gather(params[3], ("fsdp", "ctx"), axis=0, tiled=True),
        lax.all_gather(params[4], ("fsdp", "ctx"), axis=0, tiled=True),
        lax.all_gather(params[5], ("fsdp", "ctx"), axis=0, tiled=True),
        lax.all_gather(params[6], ("fsdp", "ctx"), axis=0, tiled=True),
        lax.all_gather(params[7], ("fsdp", "ctx"), axis=0, tiled=True),
        lax.all_gather(params[8], ("fsdp", "ctx"), axis=0, tiled=True),
        lax.all_gather(params[9], ("fsdp", "ctx"), axis=0, tiled=True),
        lax.all_gather(params[10], ("fsdp", "ctx"), axis=0, tiled=True),
        lax.all_gather(params[11], ("fsdp", "ctx"), axis=0, tiled=True),
    )
    xf = layer_in.reshape(rows, dmodel).astype(f32)
    norm1, hat1, rstd1 = norm_parts(xf, full[0], full[1])
    norm2, hat2, rstd2 = norm_parts(xf, full[2], full[3])
    norm1 = norm1.astype(bf)
    norm2 = norm2.astype(bf)
    qkv = jnp.dot(norm1, full[4], preferred_element_type=f32) + full[5].astype(f32)
    query = rotate(qkv[:, :dmodel].reshape(seqs, width2, heads, HD), places, 1.0).astype(bf)
    key = rotate(qkv[:, dmodel : 2 * dmodel].reshape(seqs, width2, heads, HD), places, 1.0).astype(
        bf
    )
    value = qkv[:, 2 * dmodel :].reshape(seqs, width2, heads, HD).astype(bf)
    query_a = query[:, :blk]
    query_b = query[:, blk:]
    key_b = key[:, blk:]
    value_b = value[:, blk:]
    lone = jnp.zeros((1,), dtype=bool)
    empty_top = jnp.full((seqs, heads, blk), NEG, f32)
    empty_total = jnp.zeros((seqs, heads, blk), f32)
    empty_acc = jnp.zeros((seqs, heads, blk, HD), f32)
    state = (empty_top, empty_total, empty_acc, empty_top, empty_total, empty_acc)
    state = online_update(
        state,
        query_a,
        query_b,
        key_b[None],
        key_b[None],
        value_b[None],
        value_b[None],
        place_a,
        place_b,
        place_b[None],
        place_b[None],
        lone,
        False,
        scale,
    )

    def key_parts(kpiece, vpiece, first):
        count = kpiece.shape[0]
        pairs = lax.dynamic_slice_in_dim(pair_of_rank, first, count)
        keys = kpiece.reshape(count, seqs, width2, heads, HD)
        values = vpiece.reshape(count, seqs, width2, heads, HD)
        kplace_a = pairs[:, None] * blk + offsets[None, :]
        kplace_b = (2 * nctx - 1 - pairs)[:, None] * blk + offsets[None, :]
        return (
            keys[:, :, :blk],
            keys[:, :, blk:],
            values[:, :, :blk],
            values[:, :, blk:],
            kplace_a,
            kplace_b,
            pairs,
        )

    key_send = key.reshape(1, seqs, width2, dmodel)
    value_send = value.reshape(1, seqs, width2, dmodel)
    ka, kb, va, vb, kpa, kpb, pairs = key_parts(
        lax.all_gather(key_send, "ctx", axis=0, tiled=True),
        lax.all_gather(value_send, "ctx", axis=0, tiled=True),
        jnp.int32(0),
    )
    state = online_update(
        state,
        query_a,
        query_b,
        ka,
        kb,
        va,
        vb,
        place_a,
        place_b,
        kpa,
        kpb,
        pairs <= mine,
        True,
        scale,
    )
    top_a, total_a, acc_a, top_b, total_b, acc_b = state
    context4 = jnp.concatenate([acc_a / total_a[..., None], acc_b / total_b[..., None]], axis=2)
    lse = jnp.concatenate([top_a + jnp.log(total_a), top_b + jnp.log(total_b)], axis=2)
    context = context4.transpose(0, 2, 1, 3).reshape(rows, dmodel).astype(bf)
    attn = jnp.dot(context, full[6], preferred_element_type=f32) + full[7].astype(f32)
    pre = jnp.dot(norm2, full[8], preferred_element_type=f32) + full[9].astype(f32)
    hidden = gelu_value(pre).astype(bf)
    mlp = rdot(hidden, full[10]) + full[11].astype(f32)
    layer_out = (xf + attn + mlp).astype(bf).reshape(layer_in.shape)
    again = (
        lax.all_gather(params[0], ("fsdp", "ctx"), axis=0, tiled=True),
        lax.all_gather(params[1], ("fsdp", "ctx"), axis=0, tiled=True),
        lax.all_gather(params[2], ("fsdp", "ctx"), axis=0, tiled=True),
        lax.all_gather(params[3], ("fsdp", "ctx"), axis=0, tiled=True),
        lax.all_gather(params[4], ("fsdp", "ctx"), axis=0, tiled=True),
        lax.all_gather(params[5], ("fsdp", "ctx"), axis=0, tiled=True),
        lax.all_gather(params[6], ("fsdp", "ctx"), axis=0, tiled=True),
        lax.all_gather(params[7], ("fsdp", "ctx"), axis=0, tiled=True),
        lax.all_gather(params[8], ("fsdp", "ctx"), axis=0, tiled=True),
        lax.all_gather(params[9], ("fsdp", "ctx"), axis=0, tiled=True),
        lax.all_gather(params[10], ("fsdp", "ctx"), axis=0, tiled=True),
        lax.all_gather(params[11], ("fsdp", "ctx"), axis=0, tiled=True),
    )
    grad_b = grad_out.reshape(rows, dmodel)
    grad_f = grad_b.astype(f32)
    dhidden = jnp.dot(grad_b, again[10], preferred_element_type=f32)
    dpre = dhidden * gelu_slope(pre)
    dpre_b = dpre.astype(bf)
    dnorm2 = rdot(dpre_b, again[8])
    dcontext = rdot(grad_b, again[6]).astype(bf)
    dctx4 = dcontext.reshape(seqs, width2, heads, HD)
    delta = jnp.sum(
        dctx4.astype(f32) * context.reshape(seqs, width2, heads, HD).astype(f32), axis=-1
    ).transpose(0, 2, 1)
    dctx_a = dctx4[:, :blk]
    dctx_b = dctx4[:, blk:]
    lse_a = lse[..., :blk]
    lse_b = lse[..., blk:]
    delta_a = delta[..., :blk]
    delta_b = delta[..., blk:]
    own = pair_terms(
        query_b,
        query_b,
        key_b[None],
        key_b[None],
        value_b[None],
        value_b[None],
        dctx_b,
        dctx_b,
        lse_b,
        lse_b,
        delta_b,
        delta_b,
        place_b,
        place_b,
        place_b[None],
        place_b[None],
        lone,
        False,
        scale,
    )
    own_dq = query_grads(own, key_b[None], key_b[None], lone)[1][0]
    own_keys = key_grads(own, query_b, query_b, dctx_b, dctx_b, lone)
    gathered = (
        lax.all_gather(key_send, "ctx", axis=0, tiled=True),
        lax.all_gather(value_send, "ctx", axis=0, tiled=True),
    )
    groups = math.gcd(nctx, 8)
    per = nctx // groups

    def group_terms(args):
        kpiece, vpiece, first = args
        ka, kb, va, vb, kpa, kpb, pairs = key_parts(kpiece, vpiece, first)
        sel = pairs <= mine
        terms = pair_terms(
            query_a,
            query_b,
            ka,
            kb,
            va,
            vb,
            dctx_a,
            dctx_b,
            lse_a,
            lse_b,
            delta_a,
            delta_b,
            place_a,
            place_b,
            kpa,
            kpb,
            sel,
            True,
            scale,
        )
        dq_a, dq_b = query_grads(terms, ka, kb, sel)
        return (terms, jnp.sum(dq_a, axis=0), jnp.sum(dq_b, axis=0))

    grouped = lax.map(
        group_terms,
        (
            gathered[0].reshape(groups, per, seqs, width2, dmodel),
            gathered[1].reshape(groups, per, seqs, width2, dmodel),
            jnp.arange(groups, dtype=jnp.int32) * per,
        ),
    )
    terms_all = tuple((part.reshape((nctx,) + part.shape[2:]) for part in grouped[0]))
    dq_a = jnp.sum(grouped[1], axis=0)
    dq_b = jnp.sum(grouped[2], axis=0)
    pairs = pair_of_rank
    sliced = tuple(
        (lax.slice_in_dim(part, 0, 1 * lax.axis_size("ctx"), axis=0) for part in terms_all)
    )
    dk_a, dk_b, dv_a, dv_b = key_grads(sliced, query_a, query_b, dctx_a, dctx_b, pairs <= mine)
    dkey = jnp.concatenate([dk_a, dk_b], axis=2).reshape(
        1 * lax.axis_size("ctx"), seqs, width2, dmodel
    )
    dval = jnp.concatenate([dv_a, dv_b], axis=2).reshape(
        1 * lax.axis_size("ctx"), seqs, width2, dmodel
    )
    kv_grad = lax.psum_scatter(
        jnp.concatenate([dkey, dval], axis=-1), "ctx", scatter_dimension=0, tiled=True
    )
    dkey = kv_grad[0, :, :, :dmodel].reshape(seqs, width2, heads, HD)
    dval = kv_grad[0, :, :, dmodel:].reshape(seqs, width2, heads, HD)
    zero_half = jnp.zeros((seqs, blk, heads, HD), f32)
    dquery = jnp.concatenate([dq_a, dq_b + own_dq], axis=1)
    dkey = dkey + jnp.concatenate([zero_half, own_keys[1][0]], axis=1)
    dval = dval + jnp.concatenate([zero_half, own_keys[3][0]], axis=1)
    dqkv = jnp.concatenate(
        [
            rotate(dquery, places, -1.0).reshape(rows, dmodel),
            rotate(dkey, places, -1.0).reshape(rows, dmodel),
            dval.reshape(rows, dmodel),
        ],
        axis=1,
    )
    dqkv_b = dqkv.astype(bf)
    dnorm1 = rdot(dqkv_b, again[4])
    grad_x = (
        (
            grad_f
            + layer_norm_backward(dnorm1, hat1, rstd1, again[0])
            + layer_norm_backward(dnorm2, hat2, rstd2, again[2])
        )
        .astype(bf)
        .reshape(layer_in.shape)
    )
    vectors = (
        lax.psum_scatter(
            jnp.sum(dnorm1 * hat1, axis=0), ("fsdp", "ctx"), scatter_dimension=0, tiled=True
        ),
        lax.psum_scatter(jnp.sum(dnorm1, axis=0), ("fsdp", "ctx"), scatter_dimension=0, tiled=True),
        lax.psum_scatter(
            jnp.sum(dnorm2 * hat2, axis=0), ("fsdp", "ctx"), scatter_dimension=0, tiled=True
        ),
        lax.psum_scatter(jnp.sum(dnorm2, axis=0), ("fsdp", "ctx"), scatter_dimension=0, tiled=True),
        lax.psum_scatter(jnp.sum(dqkv, axis=0), ("fsdp", "ctx"), scatter_dimension=0, tiled=True),
        lax.psum_scatter(jnp.sum(grad_f, axis=0), ("fsdp", "ctx"), scatter_dimension=0, tiled=True),
        lax.psum_scatter(jnp.sum(dpre, axis=0), ("fsdp", "ctx"), scatter_dimension=0, tiled=True),
    )
    weights = (
        lax.psum_scatter(tdot(norm1, dqkv_b), ("fsdp", "ctx"), scatter_dimension=0, tiled=True),
        lax.psum_scatter(tdot(context, grad_b), ("fsdp", "ctx"), scatter_dimension=0, tiled=True),
        lax.psum_scatter(tdot(norm2, dpre_b), ("fsdp", "ctx"), scatter_dimension=0, tiled=True),
        lax.psum_scatter(tdot(grad_b, hidden), ("fsdp", "ctx"), scatter_dimension=0, tiled=True),
    )
    return (
        layer_out,
        grad_x,
        vectors[0],
        vectors[1],
        vectors[2],
        vectors[3],
        weights[0],
        vectors[4],
        weights[1],
        vectors[5],
        weights[2],
        vectors[6],
        weights[3],
        vectors[5],
    )


def span(lead, cols):
    return jnp.arange(lead, dtype=jnp.int32)[:, None] if cols else jnp.arange(lead, dtype=jnp.int32)


def turn(field, cosine, sine_low, sine_high):
    half = ROT // 2
    down = jnp.concatenate([field[:, half:], field[:, :half]], axis=1)
    up = jnp.concatenate([field[:, -half:], field[:, :-half]], axis=1)
    return field * cosine + down * sine_low + up * sine_high


def turn_tables(places, width):
    half = ROT // 2
    lane = jnp.arange(width, dtype=jnp.int32) % HD
    freqs = jnp.exp((lane % half).astype(jnp.float32) * (-2.0 * math.log(10000.0) / ROT))
    angle = places.astype(jnp.float32)[:, None] * freqs[None, :]
    cosine = jnp.where(lane < ROT, jnp.cos(angle), 1.0)
    sine = jnp.sin(angle)
    sine_low = jnp.where(lane < half, -sine, 0.0)
    sine_high = jnp.where((lane >= half) & (lane < ROT), sine, 0.0)
    return cosine, sine_low, sine_high


def headed(field, count):
    return field.reshape(field.shape[0], count, HD).transpose(1, 0, 2)


def joined(field):
    return field.transpose(1, 0, 2).reshape(field.shape[1], -1)


def bdot(form, left, right):
    return jnp.einsum(form, left, right, preferred_element_type=jnp.float32)


def head_shards(
    layer_in,
    grad_out,
    pair_of_rank,
    ln1_gain,
    ln1_bias,
    ln2_gain,
    ln2_bias,
    w_qkv,
    b_qkv,
    w_out,
    b_out,
    w_up,
    b_up,
    w_down,
    b_down,
):
    f32 = jnp.float32
    bf = jnp.bfloat16
    both = ("fsdp", "ctx")
    nctx = lax.axis_size("ctx")
    nf = lax.axis_size("fsdp")
    ndev = nctx * nf
    c = lax.axis_index("ctx")
    seqs, width2, dmodel = layer_in.shape[1:]
    blk = width2 // 2
    own_rows = seqs * width2
    ff = w_up.shape[1]
    hloc = dmodel // HD // nctx
    qw = hloc * HD
    fw = ff // nctx
    piece = dmodel // ndev
    scale = 1.0 / math.sqrt(HD)

    x_all = lax.all_gather(layer_in.reshape(own_rows, dmodel), "ctx", axis=0, tiled=True)
    def columns(parts):
        packed = jnp.concatenate([p.reshape(piece, nctx, -1) for p in parts], axis=-1)
        packed = packed.transpose(1, 0, 2)
        got = lax.all_to_all(packed, "ctx", split_axis=0, concat_axis=0, tiled=True)
        return got.reshape(nctx * piece, -1)

    wq = w_qkv.reshape(piece, 3, nctx, qw).transpose(0, 2, 1, 3)
    vec = jnp.concatenate([ln1_gain, ln1_bias, ln2_gain, ln2_bias, b_out, b_down, b_qkv, b_up])
    vw = LANES * -(-vec.shape[0] // (piece * LANES))
    vec_pad = jnp.pad(vec, (0, piece * vw - vec.shape[0])).reshape(piece, 1, vw)
    vec_pad = jnp.broadcast_to(vec_pad, (piece, nctx, vw))
    cols = lax.all_gather(columns([wq, w_up, w_down, vec_pad]), "fsdp", axis=0, tiled=True)
    g_own = grad_out.reshape(own_rows, dmodel)
    cols, g_send = lax.optimization_barrier((cols, g_own))
    got = cols[:, 3 * qw + 2 * fw :].reshape(ndev, piece * vw)
    cuts = [piece] * 6 + [b_qkv.shape[0], b_up.shape[0]]
    fulls = []
    at = 0
    for cut in cuts:
        fulls.append(got[:, at : at + cut].reshape(-1).astype(f32))
        at += cut
    gain1, bias1, gain2, bias2, bo, bd, bq, bu = fulls
    bq_c = lax.dynamic_slice_in_dim(bq.reshape(3, nctx, qw), c, 1, axis=1).reshape(1, 3 * qw)
    bu_c = lax.dynamic_slice_in_dim(bu, c * fw, fw).reshape(1, fw)
    wq_c = cols[:, : 3 * qw]
    wu_c = cols[:, 3 * qw : 3 * qw + fw]
    wd_c = cols[:, 3 * qw + fw : 3 * qw + 2 * fw]
    there = [((nf * cc + f) , f * nctx + cc) for f in range(nf) for cc in range(nctx)]
    back = [(b, a) for a, b in there]
    wo_c = lax.all_gather(lax.ppermute(w_out, both, there), "fsdp", axis=0, tiled=True)
    g_all = lax.all_gather(g_send, "ctx", axis=0, tiled=True)

    rows = x_all.shape[0]
    offsets = jnp.arange(blk, dtype=jnp.int32)
    slot_a = pair_of_rank[:, None] * blk + offsets[None, :]
    slot_b = (2 * nctx - 1 - pair_of_rank)[:, None] * blk + offsets[None, :]
    slots = jnp.concatenate([slot_a, slot_b], axis=1)[:, None, :]
    places = jnp.broadcast_to(slots, (nctx, seqs, width2)).reshape(rows)
    group = jnp.broadcast_to(span(seqs, False)[None, :, None], (nctx, seqs, width2)).reshape(rows)

    def hat_of(xf):
        row_mean = jnp.mean(xf, axis=-1, keepdims=True)
        centred = xf - row_mean
        rstd = lax.rsqrt(jnp.mean(centred * centred, axis=-1, keepdims=True) + EPS)
        return centred * rstd, rstd

    hat, _ = hat_of(x_all.astype(f32))
    norm1 = (hat * gain1 + bias1).astype(bf)
    norm2 = (hat * gain2 + bias2).astype(bf)
    qkv = jnp.dot(norm1, wq_c, preferred_element_type=f32) + bq_c
    cosine, sine_low, sine_high = turn_tables(places, qw)
    query = headed(turn(qkv[:, :qw], cosine, sine_low, sine_high).astype(bf), hloc)
    key = headed(turn(qkv[:, qw : 2 * qw], cosine, sine_low, sine_high).astype(bf), hloc)
    value = headed(qkv[:, 2 * qw :].astype(bf), hloc)
    visible = places[None, :] <= places[:, None]
    if seqs > 1:
        visible = visible & (group[None, :] == group[:, None])
    score = jnp.where(visible[None], bdot("hqd,hkd->hqk", query, key) * scale, NEG)
    top = jnp.max(score, axis=-1, keepdims=True)
    weight = jnp.exp(score - top)
    total = jnp.sum(weight, axis=-1, keepdims=True)
    mixed = bdot("hqk,hkd->hqd", weight.astype(bf), value)
    context = (mixed / total).astype(bf)
    lse = top + jnp.log(total)
    ctx_c = joined(context)

    pre = jnp.dot(norm2, wu_c, preferred_element_type=f32) + bu_c
    hidden = gelu_value(pre).astype(bf)
    part = rdot(hidden, wd_c) + jnp.dot(ctx_c, wo_c, preferred_element_type=f32)
    fwd = lax.all_to_all(
        part.astype(bf).reshape(nctx, own_rows, dmodel), "ctx", split_axis=0, concat_axis=0, tiled=True
    )
    fwd = jnp.sum(fwd.astype(f32), axis=0)
    x_own = layer_in.reshape(own_rows, dmodel).astype(f32)
    layer_out = (x_own + fwd + (bo + bd)).astype(bf).reshape(layer_in.shape)

    dhidden = jnp.dot(g_all, wd_c, preferred_element_type=f32)
    dpre = dhidden * gelu_slope(pre)
    dpre_b = dpre.astype(bf)
    dnorm2 = rdot(dpre_b, wu_c)
    dctx = headed(rdot(g_all, wo_c).astype(bf), hloc)
    delta = jnp.sum(dctx.astype(f32) * context.astype(f32), axis=-1, keepdims=True)
    prob = jnp.exp(score - lse)
    dprob = bdot("hqd,hkd->hqk", dctx, value)
    ds = (scale * prob * (dprob - delta)).astype(bf)
    dquery = joined(bdot("hqk,hkd->hqd", ds, key))
    dkey = joined(bdot("hqk,hqd->hkd", ds, query))
    dvalue = joined(bdot("hqk,hqd->hkd", prob.astype(bf), dctx))
    dqkv = jnp.concatenate(
        [
            turn(dquery, cosine, -sine_low, -sine_high),
            turn(dkey, cosine, -sine_low, -sine_high),
            dvalue,
        ],
        axis=1,
    )
    dqkv_b = dqkv.astype(bf)
    dnorm1 = rdot(dqkv_b, wq_c)
    gsum = (dnorm1 * gain1 + dnorm2 * gain2).astype(bf)
    gsum = lax.psum_scatter(gsum, "ctx", scatter_dimension=0, tiled=True).astype(f32)
    hat_own, rstd_own = hat_of(x_own)
    g_ownf = g_own.astype(f32)
    grad_x = (
        g_ownf
        + rstd_own
        * (
            gsum
            - jnp.mean(gsum, axis=-1, keepdims=True)
            - hat_own * jnp.mean(gsum * hat_own, axis=-1, keepdims=True)
        )
    ).astype(bf).reshape(layer_in.shape)

    sum_q = jnp.zeros((3, nctx, qw), f32)
    sum_q = lax.dynamic_update_slice_in_dim(
        sum_q, jnp.sum(dqkv, axis=0).reshape(3, 1, qw), c, axis=1
    ).reshape(ndev, -1)
    sum_u = lax.dynamic_update_slice_in_dim(
        jnp.zeros((ff,), f32), jnp.sum(dpre, axis=0), c * fw, axis=0
    ).reshape(ndev, -1)
    sums = [
        jnp.sum(dnorm1 * hat, axis=0).reshape(ndev, -1),
        jnp.sum(dnorm1, axis=0).reshape(ndev, -1),
        jnp.sum(dnorm2 * hat, axis=0).reshape(ndev, -1),
        jnp.sum(dnorm2, axis=0).reshape(ndev, -1),
        jnp.sum(g_ownf, axis=0).reshape(ndev, -1),
        sum_q,
        sum_u,
    ]
    sums = jnp.concatenate(sums, axis=1)
    sw = LANES * -(-sums.shape[1] // (piece * LANES))
    sums_pad = jnp.pad(sums, ((0, 0), (0, piece * sw - sums.shape[1]))).reshape(ndev * piece, sw)
    rows_out = tdot(ctx_c, g_all).astype(bf)
    wide = jnp.concatenate(
        [
            tdot(norm1, dqkv_b).astype(bf),
            tdot(norm2, dpre_b).astype(bf),
            tdot(g_all, hidden).astype(bf),
            sums_pad.astype(bf),
            rows_out.reshape(ndev * piece, -1),
        ],
        axis=1,
    )
    wide = lax.psum_scatter(wide, "fsdp", scatter_dimension=0, tiled=True)
    split = 3 * qw + 2 * fw + sw
    grad_wout = lax.ppermute(wide[:, split:].reshape(piece, dmodel), both, back).astype(f32)
    wide = lax.all_to_all(
        wide[:, :split].reshape(nctx, piece, split), "ctx", split_axis=0, concat_axis=0, tiled=True
    )
    sums = jnp.sum(wide[:, :, split - sw :].astype(f32), axis=0).reshape(-1)[: sums.shape[1]]
    wide = wide.transpose(1, 0, 2).astype(f32)
    grad_qkv = (
        wide[:, :, : 3 * qw].reshape(piece, nctx, 3, qw).transpose(0, 2, 1, 3).reshape(piece, -1)
    )
    grad_up = wide[:, :, 3 * qw : 3 * qw + fw].reshape(piece, ff)
    grad_down = wide[:, :, 3 * qw + fw : 3 * qw + 2 * fw].reshape(piece, ff)
    ends = [piece * i for i in range(6)] + [5 * piece + b_qkv.shape[0], sums.shape[0]]
    vs = [sums[a:b] for a, b in zip(ends[:-1], ends[1:])]
    return (
        layer_out,
        grad_x,
        vs[0],
        vs[1],
        vs[2],
        vs[3],
        grad_qkv,
        vs[5],
        grad_wout,
        vs[4],
        grad_up,
        vs[6],
        grad_down,
        vs[4],
    )


def mod_less(a, n):
    return jnp.where(a >= n, a - n, a)


def mesh_dev(xi, ki, zi, yi):
    return {"fsdp": xi * 2 + ki, "ctx": zi * 2 + yi}


def rcopy(src, dst, send, recv, where):
    return pltpu.make_async_remote_copy(
        src_ref=src,
        dst_ref=dst,
        send_sem=send,
        recv_sem=recv,
        device_id=where,
        device_id_type=pl.DeviceIdType.MESH,
    )


def greet(nz, xi, ki, zi, yi):
    t = ki * nz + zi
    nt = 2 * nz
    barrier = pltpu.get_barrier_semaphore()

    def hello(where):
        pl.semaphore_signal(barrier, inc=1, device_id=where, device_id_type=pl.DeviceIdType.MESH)

    for d in range(1, nt):
        o = mod_less(t + d, nt)
        hello(mesh_dev(xi, lax.div(o, nz), lax.rem(o, nz), yi))
    hello(mesh_dev(1 - xi, ki, zi, yi))
    hello(mesh_dev(xi, ki, zi, 1 - yi))

    @pl.when(ki != yi)
    def _():
        for z in range(nz):
            hello(mesh_dev(xi, yi, z, ki))

    return lambda: pl.semaphore_wait(barrier, jnp.where(ki != yi, nt + 1 + nz, nt + 1))


STEPS = (-2, -1, 1, 2)
DIRECT_OUT = (False, True)


NT = (((1,), (1,)), ((), ()))
TN = (((0,), (0,)), ((), ()))
NN = (((1,), (0,)), ((), ()))


def mm(left, right, form):
    return lax.dot_general(left, right, form, preferred_element_type=jnp.float32)


def layer_plan(nz, width2, dm, ff, piece):
    nt = 2 * nz
    fw = ff // nt
    rows = nt * width2
    qw = 6 * HD + LANES
    bf, f32 = jnp.bfloat16, jnp.float32
    vm = pltpu.VMEM
    dma = pltpu.SemaphoreType.DMA
    plan = dict(
        xo=vm((width2, dm), bf),
        go=vm((width2, dm), bf),
        qo=vm((piece, 3 * dm), bf),
        ld=dma((5 + 2 * nt,)),
        xb=vm((nt, width2, dm), bf),
        gb=vm((nt, width2, dm), bf),
        wq=vm((2, nt, 2, piece, qw), bf),
        wu=vm((2, nt, 2, piece, fw), bf),
        wd=vm((2, nt, 2, piece, fw), bf),
        wo=vm((2, 2, piece, dm), bf),
        pq=vm((nt, piece, qw), bf),
        pu=vm((nt, piece, fw), bf),
        pd=vm((nt, piece, fw), bf),
        vs=vm((piece, LANES), f32),
        gains=vm((8, dm), f32),
        bqf=vm((1, 3 * dm), f32),
        bq=vm((1, 6 * HD), f32),
        bu=vm((1, fw), f32),
        hat=vm((rows, dm), f32),
        n1=vm((rows, dm), bf),
        n2=vm((rows, dm), bf),
        qm=vm((2, rows, 2 * HD), bf),
        km=vm((2, rows, 2 * HD), bf),
        vm=vm((2, rows, 2 * HD), bf),
        dm=vm((2, rows, 2 * HD), bf),
        lse=vm((2, rows, 1), f32),
        delta=vm((2, rows, 1), f32),
        cx=vm((rows, 2 * HD), bf),
        hid=vm((rows, fw), bf),
        slope=vm((rows, fw), f32),
        dpre=vm((rows, fw), bf),
        gs=vm((rows, dm), f32),
        dq=vm((rows, 2 * HD), f32),
        dk=vm((rows, 2 * HD), f32),
        dv=vm((rows, 2 * HD), f32),
        dqkv=vm((rows, 6 * HD), bf),
        sums=vm((8, dm), f32),
        sq=vm((1, 6 * HD), f32),
        su=vm((1, fw), f32),
        a0=vm((nt, width2, dm), bf),
        a1=vm((nt, width2, dm), bf),
        mq=vm((2, nt, 2, piece, qw), bf),
        mu=vm((2, nt, 2, piece, fw), bf),
        md=vm((2, nt, 2, piece, fw), bf),
        mo=vm((2, 2, piece, dm), bf),
        ex=vm((2, nz, width2, dm), bf),
        rcv=vm((2, 5, width2, dm), bf),
        cmb=vm((2, 2, width2, dm), bf),
        fin=vm((2, width2, dm), bf),
        own=vm((2, width2, dm), f32),
        pcol=vm((rows, 1), jnp.int32),
        prow=vm((1, rows), jnp.int32),
        cos=vm((rows, 2 * HD), f32),
        low=vm((rows, 2 * HD), f32),
        high=vm((rows, 2 * HD), f32),
        ro=vm((2, 2, piece, dm // 2), bf),
        so=vm((2, piece, dm // 2), bf),
        sw_s=dma((2,)),
        sw_r=dma((2,)),
        rsw_s=dma((2,)),
        rsw_r=dma((2,)),
        up_s=dma((2, nz)),
        up_r=dma((2, nz)),
        dn_s=dma((2, nz)),
        dn_r=dma((2, nz)),
        cc_s=dma((2, nz)),
        cc_r=dma((2, nz)),
        rn_s=dma((2, 4)),
        rn_r=dma((2, 4)),
        rf_s=dma((2, 2)),
        rf_r=dma((2, 2)),
        rcc_s=dma((2, nz)),
        rcc_r=dma((2, nz)),
        w1_s=dma((3, nt)),
        w1_r=dma((3, nt)),
        tp_s=dma((3, nt)),
        tp_r=dma((3, nt)),
        xs_s=dma((4,)),
        xs_r=dma((4,)),
        ys_s=dma((4,)),
        ys_r=dma((4,)),
        fx_s=dma((4,)),
        fx_r=dma((4,)),
        fy_s=dma((4,)),
        fy_r=dma((4,)),
        x1_s=dma((4,)),
        x1_r=dma((4,)),
        x2_s=dma((4,)),
        x2_r=dma((4,)),
        y2_s=dma((4,)),
        y2_r=dma((4,)),
        y1_s=dma((4, 2)),
        y1_r=dma((4, 2)),
        got1_0=vm((2, nz, 2, piece, qw), bf),
        got1_1=vm((2, nz, 2, piece, fw), bf),
        got1_2=vm((2, nz, 2, piece, fw), bf),
        got2_0=vm((nt, piece, qw), bf),
        got2_1=vm((nt, piece, fw), bf),
        got2_2=vm((nt, piece, fw), bf),
        chunk_0=vm((nt, piece, qw), bf),
        chunk_1=vm((nt, piece, fw), bf),
        chunk_2=vm((nt, piece, fw), bf),
    )
    return plan


def layer_kernel(nz, names, *refs):
    f32, bf = jnp.float32, jnp.bfloat16
    (x_hbm, g_hbm, wq_hbm, wu_hbm, wd_hbm, wo_hbm) = refs[:6]
    vectors = refs[6:14]
    pairs = refs[14]
    (out_x, out_g, oq, ou, od, oo, osum) = refs[15:22]
    R = types.SimpleNamespace(**dict(zip(names, refs[22:])))

    f = lax.axis_index("fsdp")
    c = lax.axis_index("ctx")
    xi, ki = lax.div(f, 2), lax.rem(f, 2)
    zi, yi = lax.div(c, 2), lax.rem(c, 2)
    nt = 2 * nz
    t = ki * nz + zi
    width2, dm = R.xo.shape
    half = dm // 2
    rows = nt * width2
    fw = R.wu.shape[4]
    piece = R.wq.shape[3]
    qc = 6 * HD
    hw = 2 * HD
    QB = 2 * width2
    nblk = rows // QB
    RB = 2 * width2
    rblk = rows // RB
    scale = 1.0 / math.sqrt(HD)
    c_own = zi * 2 + yi

    xpeer = mesh_dev(1 - xi, ki, zi, yi)
    ypeer = mesh_dev(xi, ki, zi, 1 - yi)
    cpeer = mesh_dev(xi, 1 - ki, zi, yi)
    swapped = mesh_dev(xi, yi, zi, ki)
    acts = ((R.xo, R.xb), (R.go, R.gb))
    packs = ((R.pq, R.wq), (R.pu, R.wu), (R.pd, R.wd))
    mats = (R.wq, R.wu, R.wd)
    wo = R.wo

    ld = R.ld
    loads = [
        pltpu.make_async_copy(x_hbm, R.xo, ld.at[0]),
        pltpu.make_async_copy(wq_hbm, R.qo, ld.at[1]),
        pltpu.make_async_copy(wo_hbm, wo.at[xi, yi], ld.at[2]),
    ]
    loads_u = [
        pltpu.make_async_copy(wu_hbm.at[:, o * fw : (o + 1) * fw], R.pu.at[o], ld.at[5 + o])
        for o in range(nt)
    ]
    loads_d = [
        pltpu.make_async_copy(wd_hbm.at[:, o * fw : (o + 1) * fw], R.pd.at[o], ld.at[5 + nt + o])
        for o in range(nt)
    ]
    load_g = pltpu.make_async_copy(g_hbm, R.go, ld.at[3])
    for cp in loads + [load_g]:
        cp.start()

    def swap(i):
        src, dst = acts[i]
        return rcopy(src, dst.at[c_own], R.sw_s.at[i], R.sw_r.at[i], swapped)

    def swap_start(i):
        @pl.when(ki != yi)
        def _():
            swap(i).start()

        @pl.when(ki == yi)
        def _():
            acts[i][1][c_own] = acts[i][0][...]

    def swap_wait(i):
        @pl.when(ki != yi)
        def _():
            dst = acts[i][1].at[zi * 2 + ki]
            rcopy(acts[i][0], dst, R.sw_s.at[i], R.sw_r.at[i], swapped).wait_recv()

    def inside(z):
        return (z >= 0) & (z < nz)

    def up_copy(i, d, z):
        slot = acts[i][1].at[z * 2 + ki]
        return rcopy(slot, slot, R.up_s.at[i, d], R.up_r.at[i, d], mesh_dev(xi, ki, zi + 1, yi))

    def dn_copy(i, d, z):
        slot = acts[i][1].at[z * 2 + ki]
        return rcopy(slot, slot, R.dn_s.at[i, d], R.dn_r.at[i, d], mesh_dev(xi, ki, zi - 1, yi))

    def cc_copy(i, z, k):
        slot = acts[i][1].at[z * 2 + k]
        return rcopy(slot, slot, R.cc_s.at[i, z], R.cc_r.at[i, z], cpeer)

    def pass_on(i, *steps):
        for step in steps:

            @pl.when(inside(zi - step))
            def _():
                cc_copy(i, zi - step, ki).start()

    def hop_send(i, d):
        @pl.when(inside(zi - (d - 1)) & inside(zi + 1))
        def _():
            up_copy(i, d, zi - (d - 1)).start()

        @pl.when(inside(zi + (d - 1)) & inside(zi - 1))
        def _():
            dn_copy(i, d, zi + (d - 1)).start()

    def hop(i, d):
        @pl.when(inside(zi - d))
        def _():
            up_copy(i, d, zi - d).wait_recv()

        @pl.when(inside(zi + d))
        def _():
            dn_copy(i, d, zi + d).wait_recv()

        if d + 1 < nz:
            hop_send(i, d + 1)
        pass_on(i, -d, d)

    def first_hop(i):
        swap_wait(i)
        hop_send(i, 1)
        pass_on(i, 0)

    def all_in(i):
        for z in range(nz):
            cc_copy(i, z, 1 - ki).wait_recv()

    def w1(w, d, own):
        pack, dst = packs[w]
        o = mod_less(t + d, nt) if own else t
        s = t if own else mod_less(t + nt - d, nt)
        return rcopy(
            pack.at[o],
            dst.at[xi, s, yi],
            R.w1_s.at[w, d],
            R.w1_r.at[w, d],
            mesh_dev(xi, lax.div(o, nz), lax.rem(o, nz), yi) if own else xpeer,
        )

    def w1_start(w):
        for d in range(1, nt):
            w1(w, d, True).start()
        packs[w][1][xi, t, yi] = packs[w][0][t]

    def w1_wait(w):
        for d in range(1, nt):
            w1(w, d, False).wait_recv()

    def own_view(w, xx, yy):
        return mats[w].at[xx, :, yy] if w < 3 else wo.at[xx, yy]

    def half_view(w, h, xx, yy):
        if w < 3:
            return mats[w].at[xx, h * nz : (h + 1) * nz, yy]
        return wo.at[xx, yy, :, h * half : (h + 1) * half]

    def plane_x(w, xx):
        v = own_view(w, xx, yi)
        return rcopy(v, v, R.xs_s.at[w], R.xs_r.at[w], xpeer)

    def plane_y(w, yy):
        v = own_view(w, xi, yy)
        return rcopy(v, v, R.ys_s.at[w], R.ys_r.at[w], ypeer)

    def forward_y(w, xx, yy):
        v = half_view(w, 0, xx, yy)
        return rcopy(v, v, R.fy_s.at[w], R.fy_r.at[w], ypeer)

    def forward_x(w, xx, yy):
        v = half_view(w, 1, xx, yy)
        return rcopy(v, v, R.fx_s.at[w], R.fx_r.at[w], xpeer)

    def plane_start(w):
        plane_x(w, xi).start()
        plane_y(w, yi).start()

    def plane_forward(w):
        plane_x(w, 1 - xi).wait_recv()
        forward_y(w, 1 - xi, yi).start()
        plane_y(w, 1 - yi).wait_recv()
        forward_x(w, xi, 1 - yi).start()

    def plane_wait(w):
        forward_y(w, 1 - xi, 1 - yi).wait_recv()
        forward_x(w, 1 - xi, 1 - yi).wait_recv()

    parts = (R.a0, R.a1)
    ex, rcv, cmb, fin, own = R.ex, R.rcv, R.cmb, R.fin, R.own
    grads = (R.mq, R.mu, R.md)
    mo, ro, so = R.mo, R.ro, R.so
    got1 = (R.got1_0, R.got1_1, R.got1_2)
    got2 = (R.got2_0, R.got2_1, R.got2_2)
    chunks = (R.chunk_0, R.chunk_1, R.chunk_2)

    def plus(a, b):
        return (a.astype(f32) + b.astype(f32)).astype(bf)

    def share(i, z):
        return rcopy(
            parts[i].at[z * 2 + (1 - ki)],
            ex.at[i, z],
            R.rcc_s.at[i, z],
            R.rcc_r.at[i, z],
            cpeer,
        )

    def rnear(i, n):
        z = zi + STEPS[n]
        where = mesh_dev(xi, yi, z, ki) if DIRECT_OUT[i] else mesh_dev(xi, ki, z, yi)
        return rcopy(ex.at[i, z], rcv.at[i, n], R.rn_s.at[i, n], R.rn_r.at[i, n], where)

    def rfar(i, up):
        step = 1 if up else -1
        m = 0 if up else 1
        return rcopy(
            ex.at[i, zi + 3 * step],
            cmb.at[i, m],
            R.rf_s.at[i, m],
            R.rf_r.at[i, m],
            mesh_dev(xi, ki, zi + step, yi),
        )

    def rswap(i):
        return rcopy(fin.at[i], rcv.at[i, 4], R.rsw_s.at[i], R.rsw_r.at[i], swapped)

    def x1(w):
        return rcopy(
            grads[w].at[1 - xi, 0:nz], got1[w].at[0], R.x1_s.at[w], R.x1_r.at[w], xpeer
        )

    def y1(w):
        return [
            rcopy(
                grads[w].at[xx, nz:nt, 1 - yi],
                got1[w].at[1, :, xx],
                R.y1_s.at[w, xx],
                R.y1_r.at[w, xx],
                ypeer,
            )
            for xx in range(2)
        ]

    def y2(w):
        return rcopy(
            got1[w].at[0, :, 1 - yi], got2[w].at[0:nz], R.y2_s.at[w], R.y2_r.at[w], ypeer
        )

    def x2(w):
        return rcopy(
            got1[w].at[1, :, 1 - xi], got2[w].at[nz:nt], R.x2_s.at[w], R.x2_r.at[w], xpeer
        )

    def tp(w, d, mine):
        o = mod_less(t + d, nt) if mine else t
        s = t if mine else mod_less(t + nt - d, nt)
        return rcopy(
            got2[w].at[o],
            chunks[w].at[s],
            R.tp_s.at[w, d],
            R.tp_r.at[w, d],
            mesh_dev(xi, lax.div(o, nz), lax.rem(o, nz), yi) if mine else xpeer,
        )

    def ox1():
        return rcopy(
            mo.at[1 - xi, :, :, 0:half], ro.at[0], R.x1_s.at[3], R.x1_r.at[3], xpeer
        )

    def oy1():
        return rcopy(
            mo.at[:, 1 - yi, :, half:dm], ro.at[1], R.y1_s.at[3, 0], R.y1_r.at[3, 0], ypeer
        )

    def oy2():
        return rcopy(ro.at[0, 1 - yi], so.at[0], R.y2_s.at[3], R.y2_r.at[3], ypeer)

    def ox2():
        return rcopy(ro.at[1, 1 - xi], so.at[1], R.x2_s.at[3], R.x2_r.at[3], xpeer)

    def grad_start(w):
        x1(w).start()
        for cp in y1(w):
            cp.start()

    def fold(i):
        for z in range(nz):
            share(i, z).wait_recv()
            ex[i, z] = plus(ex[i, z], parts[i][z * 2 + ki])

    def rstart(i):
        for up, step in ((True, 1), (False, -1)):

            @pl.when(inside(zi + 3 * step))
            def _():
                rfar(i, up).start()

            @pl.when(inside(zi + 2 * step) & jnp.logical_not(inside(zi - step)))
            def _():
                rnear(i, 3 if up else 0).start()

            @pl.when(inside(zi + step))
            def _():
                rnear(i, 2 if up else 1).start()

        if DIRECT_OUT[i]:

            @pl.when(ki != yi)
            def _():
                fin[i] = ex[i, zi]
                rswap(i).start()

    def rjoin(i):
        for up, step in ((True, 1), (False, -1)):

            @pl.when(inside(zi + 2 * step) & inside(zi - step))
            def _():
                m = 0 if up else 1
                z = zi + 2 * step
                there = mesh_dev(xi, ki, zi - step, yi)
                rcopy(
                    ex.at[i, z], cmb.at[i, m], R.rf_s.at[i, m], R.rf_r.at[i, m], there
                ).wait_recv()
                ex[i, z] = plus(ex[i, z], cmb[i, m])
                rnear(i, 3 if up else 0).start()

    def swapped_in(i):
        rcopy(fin.at[i], rcv.at[i, 4], R.rsw_s.at[i], R.rsw_r.at[i], swapped).wait_recv()

    def rnears(i):
        for n in range(4):

            @pl.when(inside(zi - STEPS[n]))
            def _():
                rcopy(
                    fin.at[i], rcv.at[i, n], R.rn_s.at[i, n], R.rn_r.at[i, n], cpeer
                ).wait_recv()
                own[i] += rcv[i, n].astype(f32)

    def rend(i):
        if DIRECT_OUT[i]:

            @pl.when(ki != yi)
            def _():
                swapped_in(i)
                own[i] = rcv[i, 4].astype(f32)

            @pl.when(ki == yi)
            def _():
                own[i] = ex[i, zi].astype(f32)

            rnears(i)
        else:
            own[i] = ex[i, zi].astype(f32)
            rnears(i)

            @pl.when(ki != yi)
            def _():
                fin[i] = own[i].astype(bf)
                rswap(i).start()

    def rlast(i):
        if not DIRECT_OUT[i]:

            @pl.when(ki != yi)
            def _():
                swapped_in(i)
                own[i] = rcv[i, 4].astype(f32)

    def fold1(w):
        x1(w).wait_recv()
        got1[w][0] = plus(got1[w][0], grads[w][xi, 0:nz])
        y2(w).start()
        for cp in y1(w):
            cp.wait_recv()
        for xx in range(2):
            got1[w][1, :, xx] = plus(got1[w][1, :, xx], grads[w][xx, nz:nt, yi])
        x2(w).start()

    def fold2(w):
        y2(w).wait_recv()
        got2[w][0:nz] = plus(got2[w][0:nz], got1[w][0, :, yi])
        x2(w).wait_recv()
        got2[w][nz:nt] = plus(got2[w][nz:nt], got1[w][1, :, xi])
        for d in range(1, nt):
            tp(w, d, True).start()
        chunks[w][t] = got2[w][t]

    lane = lax.broadcasted_iota(jnp.int32, (1, hw), 1)
    first = lane < HD
    gains = R.gains
    hat, n1, n2 = R.hat, R.n1, R.n2
    place_col, place_row, cos_t, low_t, high_t = R.pcol, R.prow, R.cos, R.low, R.high
    qm, km, vm, dcm = R.qm, R.km, R.vm, R.dm
    lse, delta, cx = R.lse, R.delta, R.cx
    hid, slope, dpre_s, gs = R.hid, R.slope, R.dpre, R.gs
    dq, dk, dv, dqkv = R.dq, R.dk, R.dv, R.dqkv
    sums, sq, su = R.sums, R.sq, R.su

    def block(i):
        return pl.ds(pl.multiple_of(i * RB, RB), RB)

    def act(ref, i):
        return ref[pl.ds(2 * i, 2)].reshape(RB, dm)

    def masked(value):
        return jnp.where(first, value, 0), jnp.where(first, 0, value)

    def hats(xf):
        mean = jnp.mean(xf, axis=-1, keepdims=True)
        centred = xf - mean
        rstd = lax.rsqrt(jnp.mean(centred * centred, axis=-1, keepdims=True) + EPS)
        return centred * rstd, rstd

    def table_step(i, _):
        blk = width2 // 2
        p = pairs[i]

        def place_of(j):
            return jnp.where(j < blk, p * blk + j, (2 * nt - 1 - p) * blk + j - blk)

        at = pl.ds(pl.multiple_of(i * width2, width2), width2)
        place = place_of(lax.broadcasted_iota(jnp.int32, (width2, 1), 0))
        place_col[at] = place
        place_row[:, at] = place_of(lax.broadcasted_iota(jnp.int32, (1, width2), 1))
        turn_lane = lane & (HD - 1)
        step = (turn_lane & (ROT // 2 - 1)).astype(f32)
        angle = place.astype(f32) * jnp.exp(step * (-2.0 * math.log(10000.0) / ROT))
        sine = jnp.sin(angle)
        cos_t[at] = jnp.where(turn_lane < ROT, jnp.cos(angle), 1.0)
        low_t[at] = jnp.where(turn_lane < ROT // 2, -sine, 0.0)
        high_t[at] = jnp.where((turn_lane >= ROT // 2) & (turn_lane < ROT), sine, 0.0)
        return 0

    def hat_step(i, _):
        hat[block(i)] = hats(act(R.xb, i).astype(f32))[0]
        return 0

    def vectors_in():
        wq = R.wq
        per = LANES // piece

        def tile(r):
            a, b, e = r // (2 * nt), (r // 2) % nt, r % 2
            return wq[a, b, e, :, qc:].astype(f32)

        n = nt * 4
        for j in range(n // per):
            tiles = [tile(j * per + m) for m in range(per)]
            gains[:, j * LANES : (j + 1) * LANES] = jnp.concatenate(
                [v[0:8, 0:piece] for v in tiles], axis=1
            )
            bw = 3 * piece
            R.bqf[:, j * per * bw : (j + 1) * per * bw] = jnp.concatenate(
                [v[6:7, 0:bw] for v in tiles], axis=1
            )
        here = lax.div(t, 2) * LANES
        odd = lax.rem(t, 2) == 1
        for p in range(3):
            out = []
            for h in range(2):
                at = pl.multiple_of(here + (p * dm + h * half), LANES)
                v = R.bqf[:, pl.ds(at, LANES)]
                out.append(jnp.where(odd, v[:, HD:], v[:, :HD]))
            R.bq[:, p * hw : (p + 1) * hw] = jnp.concatenate(out, axis=1)
        for j in range(fw // LANES):
            r = t * (fw // LANES) + j
            v = wq[lax.div(r, 2 * nt), lax.rem(lax.div(r, 2), nt), lax.rem(r, 2), :, qc:]
            R.bu[:, j * LANES : (j + 1) * LANES] = v.astype(f32)[7:8]

    def turned(field, b, sign):
        down = pltpu.roll(field, hw - ROT // 2, 1)
        up = pltpu.roll(field, ROT // 2, 1)
        return field * cos_t[b] + sign * (down * low_t[b] + up * high_t[b])

    def qkv_step(i, _):
        b = block(i)
        h = hat[b]
        n1[b] = (h * gains[0:1] + gains[1:2]).astype(bf)
        n2[b] = (h * gains[2:3] + gains[3:4]).astype(bf)
        w = R.wq[:, :, :, :, 0:qc].reshape(dm, qc)
        qkv = mm(n1[b], w, NN) + R.bq[...]
        q = turned(qkv[:, 0:hw], b, 1.0).astype(bf).astype(f32) * scale
        k = turned(qkv[:, hw : 2 * hw], b, 1.0)
        v = qkv[:, 2 * hw : 3 * hw]
        for ref, value in ((qm, q), (km, k), (vm, v)):
            one, two = masked(value)
            ref[0, b] = one.astype(bf)
            ref[1, b] = two.astype(bf)
        return 0

    def attend_step(i, _):
        b = block(i)
        visible = place_row[...] <= place_col[b]
        ctx = jnp.zeros((RB, hw), f32)
        for h in range(2):
            s = jnp.where(visible, mm(qm[h, b], km[h], NT), NEG)
            top = jnp.max(s, axis=-1, keepdims=True)
            e = jnp.exp(s - top)
            total = jnp.sum(e, axis=-1, keepdims=True)
            ctx = ctx + mm(e.astype(bf), vm[h], NN) / total
            lse[h, b] = top + jnp.log(total)
        cx[b] = ctx.astype(bf)
        return 0

    def up_step(i, _):
        b = block(i)
        pre = mm(n2[b], R.wu[...].reshape(dm, fw), NN) + R.bu[...]
        bell = 0.5 * (1.0 + lax.erf(pre * ROOT_HALF))
        hid[b] = (pre * bell).astype(bf)
        slope[b] = bell + pre * jnp.exp(-0.5 * pre * pre) * INV_ROOT_TAU
        return 0

    def down_step(i, _):
        b = block(i)
        out = mm(hid[b], R.wd[...].reshape(dm, fw), NT)
        out = out + mm(cx[b], wo[...].reshape(hw, dm), NN)
        R.a0[pl.ds(2 * i, 2)] = out.astype(bf).reshape(2, width2, dm)
        return 0

    def back_step(i, _):
        b = block(i)
        g = act(R.gb, i)
        dpre = mm(g, R.wd[...].reshape(dm, fw), NN) * slope[b]
        su[...] += jnp.sum(dpre, axis=0, keepdims=True)
        dpre_s[b] = dpre.astype(bf)
        dn2 = mm(dpre_s[b], R.wu[...].reshape(dm, fw), NT)
        sums[2:3] += jnp.sum(dn2 * hat[b], axis=0, keepdims=True)
        sums[3:4] += jnp.sum(dn2, axis=0, keepdims=True)
        gs[b] = dn2 * gains[2:3]
        return 0

    def context_step(i, _):
        b = block(i)
        g = act(R.gb, i)
        dctx = mm(g, wo[...].reshape(hw, dm), NT).astype(bf).astype(f32)
        prod = dctx * cx[b].astype(f32)
        for h, (d, p) in enumerate(zip(masked(dctx), masked(prod))):
            dcm[h, b] = d.astype(bf)
            delta[h, b] = jnp.sum(p, axis=-1, keepdims=True)
        return 0

    def rows_of(ref, i):
        return ref.at[lax.div(i, 2), pl.ds(pl.multiple_of(lax.rem(i, 2) * nz, nz), nz)]

    def outer_step(i, _):
        cols = pl.ds(pl.multiple_of(i * QB, QB), QB)
        gt = R.gb[:, :, cols].reshape(rows, QB)
        out = mm(gt, hid[...], TN)
        rows_of(R.md, i)[...] = out.astype(bf).reshape(nz, 2, piece, fw)
        wide = mm(cx[...], gt, TN).astype(bf)
        mo[:, :, :, cols] = wide.reshape(2, 2, piece, QB)
        return 0

    def outer_up_step(i, _):
        cols = pl.ds(pl.multiple_of(i * QB, QB), QB)
        out = mm(n2[:, cols], dpre_s[...], TN)
        rows_of(R.mu, i)[...] = out.astype(bf).reshape(nz, 2, piece, fw)
        return 0

    def attend_back_step(i, _):
        b = block(i)
        visible = place_row[...] <= place_col[b]
        acc = jnp.zeros((RB, hw), f32)
        for h in range(2):
            s = jnp.where(visible, mm(qm[h, b], km[h], NT), NEG)
            p = jnp.exp(s - lse[h, b])
            dp = mm(dcm[h, b], vm[h], NT)
            ds = (p * (dp - delta[h, b])).astype(bf)
            acc = acc + mm(ds, km[h], NN)
            dk[...] += mm(ds, qm[h, b], TN)
            dv[...] += mm(p.astype(bf), dcm[h, b], TN)
        dq[b] = acc * scale
        return 0

    def dqkv_step(i, _):
        b = block(i)
        fields = (turned(dq[b], b, -1.0), turned(dk[b], b, -1.0), dv[b])
        for j, v in enumerate(fields):
            sq[:, j * hw : (j + 1) * hw] += jnp.sum(v, axis=0, keepdims=True)
            dqkv[b, j * hw : (j + 1) * hw] = v.astype(bf)
        w = R.wq[:, :, :, :, 0:qc].reshape(dm, qc)
        dn1 = mm(dqkv[b], w, NT)
        sums[0:1] += jnp.sum(dn1 * hat[b], axis=0, keepdims=True)
        sums[1:2] += jnp.sum(dn1, axis=0, keepdims=True)
        out = (dn1 * gains[0:1] + gs[b]).astype(bf)
        R.a1[pl.ds(2 * i, 2)] = out.reshape(2, width2, dm)
        return 0

    def outer_qkv_step(i, _):
        cols = pl.ds(pl.multiple_of(i * QB, QB), QB)
        out = mm(n1[:, cols], dqkv[...], TN)
        view = R.mq.at[lax.div(i, 2), pl.ds(pl.multiple_of(lax.rem(i, 2) * nz, nz), nz), :, :, 0:qc]
        view[...] = out.astype(bf).reshape(nz, 2, piece, qc)
        return 0

    def sums_out():
        low = jnp.concatenate(
            [sq[:, j * hw : (j + 1) * hw] for j in range(3)]
            + [su[:, j * LANES : (j + 1) * LANES] for j in range(fw // LANES)]
            + [jnp.zeros((piece - 8 - 3 - fw // LANES, LANES), f32)],
            axis=0,
        )
        for r in range(nt * 4):
            one = sums[:, r * piece : (r + 1) * piece]
            one = jnp.concatenate([one, jnp.zeros((8, LANES - piece), f32)], axis=1)
            tile = jnp.concatenate([one, low], axis=0).astype(bf)
            R.mq[r // (2 * nt), (r // 2) % nt, r % 2, :, qc:] = tile

    all_here = greet(nz, xi, ki, zi, yi)
    loads[0].wait()
    all_here()
    swap_start(0)
    for cp in loads_u + loads_d:
        cp.start()
    vs = R.vs
    vs[...] = jnp.zeros_like(vs)
    for i, v in enumerate(vectors):
        vs[i : i + 1, 0 : v.shape[1]] = v[...].astype(f32)
    small = vs[...].astype(bf)
    loads[1].wait()
    for o in range(nt):
        pieces = []
        for p in range(3):
            base = p * dm + o * HD
            for at in (base, base + half):
                pieces.append(R.qo[:, at : at + HD])
        for j in range(3):
            R.pq[o, :, j * hw : (j + 1) * hw] = jnp.concatenate(pieces[2 * j : 2 * j + 2], axis=1)
        R.pq[o, :, qc:] = small
    w1_start(0)
    load_g.wait()
    swap_start(1)
    first_hop(0)
    loads[2].wait()
    plane_start(3)
    for cp in loads_u:
        cp.wait()
    w1_start(1)
    for cp in loads_d:
        cp.wait()
    w1_start(2)
    for ref in (sums, sq, su, dk, dv):
        ref[...] = jnp.zeros_like(ref)
    lax.fori_loop(0, nt, table_step, 0)
    sums[4:5] = jnp.sum(R.go[...].astype(f32), axis=0, keepdims=True)
    hop(0, 1)
    w1_wait(0)
    plane_start(0)
    first_hop(1)
    hop(0, 2)
    hop(1, 1)
    w1_wait(1)
    plane_start(1)
    plane_forward(0)
    hop(0, 3)
    hop(1, 2)
    w1_wait(2)
    plane_start(2)
    plane_forward(3)
    all_in(0)
    lax.fori_loop(0, rblk, hat_step, 0)
    plane_wait(0)
    vectors_in()
    lax.fori_loop(0, rblk, qkv_step, 0)
    plane_forward(1)
    lax.fori_loop(0, rblk // 2, attend_step, 0)
    plane_forward(2)
    lax.fori_loop(rblk // 2, rblk, attend_step, 0)
    plane_wait(1)
    hop(1, 3)
    lax.fori_loop(0, rblk, up_step, 0)
    plane_wait(2)
    plane_wait(3)
    lax.fori_loop(0, rblk, down_step, 0)
    for z in range(nz):
        share(0, z).start()
    all_in(1)
    lax.fori_loop(0, nblk, outer_step, 0)
    grad_start(2)
    ox1().start()
    oy1().start()
    fold(0)
    rstart(0)
    lax.fori_loop(0, rblk, back_step, 0)
    lax.fori_loop(0, rblk, context_step, 0)
    lax.fori_loop(0, nblk, outer_up_step, 0)
    grad_start(1)
    rjoin(0)
    lax.fori_loop(0, rblk // 2, attend_back_step, 0)
    fold1(2)
    ox1().wait_recv()
    ro[0] = plus(ro[0], mo[xi, :, :, 0:half])
    oy2().start()
    oy1().wait_recv()
    ro[1] = plus(ro[1], mo[:, yi, :, half:dm])
    ox2().start()
    lax.fori_loop(rblk // 2, rblk, attend_back_step, 0)
    fold1(1)
    fold2(2)
    lax.fori_loop(0, rblk, dqkv_step, 0)
    for z in range(nz):
        share(1, z).start()
    fold2(1)
    lax.fori_loop(0, nblk, outer_qkv_step, 0)
    sums_out()
    grad_start(0)
    fold(1)
    rstart(1)
    fold1(0)
    rjoin(1)
    rend(0)
    fold2(0)
    rlast(0)

    x_own = R.xo[...].astype(f32)
    out_x[...] = (x_own + own[0] + (gains[4:5] + gains[5:6])).astype(bf)
    oy2().wait_recv()
    oo[:, 0:half] = so[0].astype(f32) + ro[0, yi].astype(f32)
    ox2().wait_recv()
    oo[:, half:dm] = so[1].astype(f32) + ro[1, xi].astype(f32)
    for w in (2, 1):
        for d in range(1, nt):
            tp(w, d, False).wait_recv()
        ref = (None, ou, od)[w]
        for o in range(nt):
            ref[:, o * fw : (o + 1) * fw] = chunks[w][o]
    hat_own, rstd_own = hats(x_own)

    rend(1)
    gsum = own[1]
    out_g[...] = (
        R.go[...].astype(f32)
        + rstd_own
        * (
            gsum
            - jnp.mean(gsum, axis=-1, keepdims=True)
            - hat_own * jnp.mean(gsum * hat_own, axis=-1, keepdims=True)
        )
    ).astype(bf)
    for d in range(1, nt):
        tp(0, d, False).wait_recv()
    cq = chunks[0]
    for j in range(3):
        for h in range(2):
            for o in range(0, nt, 2):
                lo = j * hw + h * HD
                both = jnp.concatenate([cq[o, :, lo : lo + HD], cq[o + 1, :, lo : lo + HD]], axis=1)
                at = j * dm + h * half + o * HD
                oq[:, at : at + hw] = both
    for o in range(nt):
        osum[o] = cq[o, :, qc:].astype(f32)[0:16]

    for i in range(2):

        @pl.when(ki != yi)
        def _():
            swap(i).wait_send()
            rswap(i).wait_send()

        for d in range(1, nz):

            @pl.when(inside(zi - (d - 1)) & inside(zi + 1))
            def _():
                up_copy(i, d, zi - (d - 1)).wait_send()

            @pl.when(inside(zi + (d - 1)) & inside(zi - 1))
            def _():
                dn_copy(i, d, zi + (d - 1)).wait_send()

        for n in range(4):

            @pl.when(inside(zi + STEPS[n]))
            def _():
                rnear(i, n).wait_send()

        for up, step in ((True, 1), (False, -1)):

            @pl.when(inside(zi + 3 * step))
            def _():
                rfar(i, up).wait_send()

        for z in range(nz):
            cc_copy(i, z, ki).wait_send()
            share(i, z).wait_send()
    for w in range(3):
        for d in range(1, nt):
            w1(w, d, True).wait_send()
            tp(w, d, True).wait_send()
        x1(w).wait_send()
        for cp in y1(w):
            cp.wait_send()
        y2(w).wait_send()
        x2(w).wait_send()
    for w in range(4):
        plane_x(w, xi).wait_send()
        plane_y(w, yi).wait_send()
        forward_y(w, 1 - xi, yi).wait_send()
        forward_x(w, xi, 1 - yi).wait_send()
    ox1().wait_send()
    oy1().wait_send()
    oy2().wait_send()
    ox2().wait_send()


def finish_kernel(dm, nq, fw, *refs):
    big, sums, outs, small = refs[:6], refs[6], refs[7:13], refs[13:21]
    flat = refs[21]
    for a, b in zip(big, outs):
        b[...] = a[...].astype(b.dtype)
    nt = sums.shape[0]
    half = dm // 2
    r = lax.axis_index("fsdp") * lax.axis_size("ctx") + lax.axis_index("ctx")
    total = sums[0, 0:8]
    for o in range(1, nt):
        total = total + sums[o, 0:8]
    for i, row in enumerate((0, 1, 2, 3, 4, 4)):
        small[i][...] = total[row : row + 1, 0 : small[i].shape[1]]
    flat[:, 3 * dm :] = jnp.zeros((1, LANES), jnp.float32)
    for j in range(3):
        for h in range(2):
            for o in range(0, nt, 2):
                pair = [sums[o + e, 8 + j : 9 + j, h * HD : (h + 1) * HD] for e in range(2)]
                at = j * dm + h * half + o * HD
                flat[:, at : at + 2 * HD] = jnp.concatenate(pair, axis=1)
    begin = r * nq
    chunk = lax.div(begin, LANES)
    wide = flat[:, pl.ds(pl.multiple_of(chunk * LANES, LANES), 2 * LANES)]
    shift = begin - chunk * LANES
    unit = math.gcd(nq, LANES)
    mine = wide[:, 0:nq]
    for at in range(unit, LANES, unit):
        mine = jnp.where(shift == at, wide[:, at : at + nq], mine)
    small[6][...] = mine
    per = fw // LANES
    row = 11 + lax.rem(r, per)
    small[7][...] = sums[lax.div(r, per), pl.ds(row, 1)]


def finish(arrays, sums, nq, fw, dm):
    vm = pl.BlockSpec(memory_space=pltpu.VMEM)
    f32 = jnp.float32
    shape = jax.ShapeDtypeStruct
    piece = arrays[2].shape[0]
    smalls = [piece] * 6 + [nq, LANES]
    return pl.pallas_call(
        functools.partial(finish_kernel, dm, nq, fw),
        out_shape=[shape(a.shape, a.dtype) for a in arrays[:2]]
        + [shape(a.shape, f32) for a in arrays[2:]]
        + [shape((1, n), f32) for n in smalls],
        in_specs=[vm] * 7,
        out_specs=[vm] * 14,
        scratch_shapes=[pltpu.VMEM((1, 3 * dm + LANES), f32)],
        compiler_params=pltpu.CompilerParams(vmem_limit_bytes=60 * 1024 * 1024),
    )(*arrays, sums)


def routed(
    layer_in,
    grad_out,
    pair_of_rank,
    ln1_gain,
    ln1_bias,
    ln2_gain,
    ln2_bias,
    w_qkv,
    b_qkv,
    w_out,
    b_out,
    w_up,
    b_up,
    w_down,
    b_down,
):
    f32 = jnp.float32
    bf = jnp.bfloat16
    nctx = lax.axis_size("ctx")
    nz = nctx // 2
    width2, dmodel = layer_in.shape[2:]
    ff = w_up.shape[1]
    piece = w_qkv.shape[0]
    plan = layer_plan(nz, width2, dmodel, ff, piece)
    vectors = (ln1_gain, ln1_bias, ln2_gain, ln2_bias, b_out, b_down, b_qkv, b_up)
    vm = pl.BlockSpec(memory_space=pltpu.VMEM)
    anywhere = pl.BlockSpec(memory_space=pl.ANY)
    shape = jax.ShapeDtypeStruct
    layer_out, grad_x, grad_qkv, grad_up, grad_down, grad_wout, sums = pl.pallas_call(
        functools.partial(layer_kernel, nz, tuple(plan)),
        out_shape=(
            shape((width2, dmodel), bf),
            shape((width2, dmodel), bf),
            shape((piece, 3 * dmodel), bf),
            shape((piece, ff), bf),
            shape((piece, ff), bf),
            shape((piece, dmodel), f32),
            shape((nctx, 16, LANES), f32),
        ),
        in_specs=[anywhere] * 6 + [vm] * 8 + [pl.BlockSpec(memory_space=pltpu.SMEM)],
        out_specs=(vm,) * 7,
        scratch_shapes=list(plan.values()),
        compiler_params=pltpu.CompilerParams(
            collective_id=0, has_side_effects=True, vmem_limit_bytes=60 * 1024 * 1024
        ),
    )(
        layer_in.reshape(width2, dmodel),
        grad_out.reshape(width2, dmodel),
        w_qkv,
        w_up,
        w_down,
        w_out,
        *[v.reshape(1, -1) for v in vectors],
        pair_of_rank,
    )
    done = finish(
        (layer_out, grad_x, grad_qkv, grad_up, grad_down, grad_wout),
        sums,
        b_qkv.shape[0],
        ff // nctx,
        dmodel,
    )
    layer_out, grad_x, grad_qkv, grad_up, grad_down, grad_wout = done[:6]
    vs = [v.reshape(-1) for v in done[6:]]
    return (
        layer_out.reshape(layer_in.shape),
        grad_x.reshape(layer_in.shape),
        vs[0],
        vs[1],
        vs[2],
        vs[3],
        grad_qkv,
        vs[6],
        grad_wout,
        vs[4],
        grad_up,
        vs[7],
        grad_down,
        vs[5],
    )


def solution(mesh):
    nctx = mesh.shape["ctx"]

    def pick(layer_in, *rest):
        heads = layer_in.shape[-1] // HD
        whole = heads % nctx == 0
        square = nctx % 2 == 0 and mesh.shape["fsdp"] == 4 and heads == 2 * nctx
        if square and layer_in.shape[1] == 1 and layer_in.shape[-1] == 8 * layer_in.shape[2] == nctx * layer_in.shape[2]:
            return routed(layer_in, *rest)
        return (head_shards if whole else shards)(layer_in, *rest)

    return jax.shard_map(
        pick,
        mesh=mesh,
        in_specs=(
            P("ctx", "fsdp", None, None),
            P("ctx", "fsdp", None, None),
            P(),
            P(("fsdp", "ctx")),
            P(("fsdp", "ctx")),
            P(("fsdp", "ctx")),
            P(("fsdp", "ctx")),
            P(("fsdp", "ctx"), None),
            P(("fsdp", "ctx")),
            P(("fsdp", "ctx"), None),
            P(("fsdp", "ctx")),
            P(("fsdp", "ctx"), None),
            P(("fsdp", "ctx")),
            P(("fsdp", "ctx"), None),
            P(("fsdp", "ctx")),
        ),
        out_specs=(
            P("ctx", "fsdp", None, None),
            P("ctx", "fsdp", None, None),
            P(("fsdp", "ctx")),
            P(("fsdp", "ctx")),
            P(("fsdp", "ctx")),
            P(("fsdp", "ctx")),
            P(("fsdp", "ctx"), None),
            P(("fsdp", "ctx")),
            P(("fsdp", "ctx"), None),
            P(("fsdp", "ctx")),
            P(("fsdp", "ctx"), None),
            P(("fsdp", "ctx")),
            P(("fsdp", "ctx"), None),
            P(("fsdp", "ctx")),
        ),
        check_vma=False,
    )
```
